32 devices in a mesh: eta: 2 (over x), phi: 4 (over z), replica: 4 (over y, core).
Axes of the slice: x: 2, y: 2, z: 4, core: 2. Of those that a mesh axis runs over, the one named last changes fastest.
Arguments:
- tokens: bfloat16 [4, 64, 128, 768], P('replica', 'eta', 'phi'), may hold values from -6 to 6
- send_pos: int32 [4, 2, 4, 8, 35], P('replica', 'eta', 'phi'), may hold values from 0 to 1024, as said below
- enc_src: int32 [4, 2, 4, 256], P('replica', 'eta', 'phi'), may hold values from 0 to 279, as said below
- window_id: int32 [4, 2, 4, 256], P('replica', 'eta', 'phi'), may hold values from 0 to 3
- enc_cot: bfloat16 [4, 2, 4, 256, 768], P('replica', 'eta', 'phi'), may hold values from -0.0625 to 0.0625
- w_qkv: bfloat16 [768, 2304], replicated, may hold values from -0.21875 to 0.21875
- head_scale: float32 [12], replicated, may hold values from 2 to 12
- w_out: bfloat16 [768, 768], replicated, may hold values from -0.21875 to 0.21875
- w_dec_in: bfloat16 [768, 384], replicated, may hold values from -0.21875 to 0.21875
- mask_token: bfloat16 [384], replicated, may hold values from -4 to 4
- conv_kernel: float32 [7, 7, 384], replicated, may hold values from -0.875 to 0.875
- w_up: bfloat16 [384, 768], replicated, may hold values from -0.3125 to 0.3125
- w_down: bfloat16 [768, 384], replicated, may hold values from -0.21875 to 0.21875
- w_head: bfloat16 [384, 128], replicated, may hold values from -0.3125 to 0.3125
Outputs:
- weight_grads: float32 [3072, 768], P(('eta', 'phi'))
- reconstruction: float32 [4, 64, 128, 128], P('replica', 'eta', 'phi')
The draws below stay inside these ranges and needn't reach their ends.
Inputs may be any that keep to these rules, and one draw needn't show every extreme that they name: send_pos[e,a,b,d,k] is the cell of the k-th visible token that tile (a,b) sends to encoder shard d; 1024 marks an empty slot and empty slots follow the live ones. The visible cells of a tile are whole aligned 2 x 2 blocks, each sent exactly once; every encoder shard receives exactly 256 live slots; some tile fills all 35 slots to some shard. enc_src[e,a,b,r] = s * 35 + k names a live slot (send_pos of tile s towards this shard, slot k); each live slot arriving at the shard appears exactly once.
All inputs are finite; a program needn't handle non-finite values.
Results may differ from the reference program's by a relative error of at most 0.0095.
Values may be sent and summed in bfloat16 or wider, within the bound.
No kernel may reach another device: no remote copies, remote signals or barrier semaphores. Data moves between devices by JAX's collectives and lax.ppermute only.
A program may use at most 128 MiB of HBM per device.

```python
import math
import jax
import jax.numpy as jnp
from jax import lax

D = 768
HEADS = 12
DEC = 384
DEC_FF = 768
PATCH = 128
KERN = 7
TE = 32
TP = 32
EVENTS = 4
GROUP = 8
VIS_DEV = 256
BASE = 29
CAP = 35
NWIN = 4
NE = 64
NP = 128
N_ETA = 2
N_PHI = 4
DEVICES = 32


def tile_tables(key):
    base_key = jax.random.fold_in(key, 11)
    half_cols = TP // 2
    block_count = TE // 2 * half_cols
    tile_len = TE * TP

    def one_event(event_key):
        sub_keys = jax.random.split(event_key, 4)
        offsets = jax.random.permutation(sub_keys[0], GROUP).astype(jnp.int32) % 4
        ranking = jax.random.permutation(sub_keys[1], GROUP).astype(jnp.int32)
        extra_load = (ranking - ranking[GROUP - 1] + 3) % 4
        tile_ids = jnp.arange(GROUP, dtype=jnp.int32)
        shift = (tile_ids[None, :] - tile_ids[:, None]) % GROUP
        counts = BASE + offsets[shift] + extra_load[:, None]
        starts = jnp.cumsum(counts, axis=1) - counts
        orders = jax.vmap(lambda block_key: jax.random.permutation(block_key, block_count).astype(jnp.int32))(jax.random.split(sub_keys[2], GROUP))
        listed = jnp.arange(tile_len, dtype=jnp.int32)
        chosen = orders[:, listed // 4]
        corner = listed % 4
        visible_cells = (2 * (chosen // half_cols) + corner // 2) * TP + 2 * (chosen % half_cols) + corner % 2
        slot_ids = jnp.arange(CAP, dtype=jnp.int32)
        index_rows = jnp.minimum(starts[:, :, None] + slot_ids[None, None, :], tile_len - 1)
        picked = visible_cells[tile_ids[:, None, None], index_rows]
        send_table = jnp.where(slot_ids[None, None, :] < counts[:, :, None], picked, tile_len)
        live_slots = (slot_ids[None, None, :] < counts.T[:, :, None]).reshape(GROUP, GROUP * CAP)
        flat_ids = jnp.arange(GROUP * CAP, dtype=jnp.int32)
        sort_key = jnp.where(live_slots, flat_ids[None, :], flat_ids[None, :] + GROUP * CAP)
        ordered = jnp.argsort(sort_key, axis=1).astype(jnp.int32)[:, :VIS_DEV]
        shuffles = jax.vmap(lambda row_key: jax.random.permutation(row_key, VIS_DEV).astype(jnp.int32))(jax.random.split(sub_keys[3], GROUP))
        sources = jnp.take_along_axis(ordered, shuffles, axis=1)
        return (send_table.reshape(N_ETA, N_PHI, GROUP, CAP).astype(jnp.int32), sources.reshape(N_ETA, N_PHI, VIS_DEV).astype(jnp.int32))
    return jax.vmap(one_event)(jax.random.split(base_key, EVENTS))


def draw_send_pos(key, part):
    return tile_tables(key)[0]


def draw_enc_src(key, part):
    return tile_tables(key)[1]


def place_ends(entries, key, smallest, high):
    extent = entries.shape
    spot = [jax.random.randint(jax.random.fold_in(key, axis), (), 0, extent[axis]) for axis in range(len(extent))]
    entries = entries.at[tuple(spot)].set(smallest)
    longest = extent.index(max(extent))
    spot[longest] = (spot[longest] + 1) % extent[longest]
    return entries.at[tuple(spot)].set(high)


def steps_of(rng, extent, shards, low, high):
    factor_of = 1.0
    for position, parts in shards:
        steps = jax.random.uniform(jax.random.fold_in(jax.random.fold_in(rng, 6), position), (parts,), jnp.float32, low / len(shards), high / len(shards))
        factor_of = factor_of * jnp.repeat(jnp.exp(steps), extent[position] // parts).reshape((-1,) + (1,) * (len(extent) - 1 - position))
    return factor_of


def scatter_about(rng, extent, deviation, limit, cuts=(), kind=jnp.bfloat16):
    level = steps_of(rng, extent, cuts, -0.22, 0.18) if cuts else 1.0
    values = jax.random.normal(rng, extent, jnp.float32) * deviation * level
    return jnp.minimum(jnp.maximum(values, -limit), limit).astype(kind)


def setup_inputs(seed: int = 0) -> dict:
    splits = jax.random.split(jax.random.key(seed), 15)
    tokens = scatter_about(splits[0], (EVENTS, NE, NP, D), 1.0, 6.0, ((0, 4), (1, 2), (2, 4)))
    send_pos = draw_send_pos(jax.random.fold_in(splits[14], 71), 0)
    enc_src = draw_enc_src(jax.random.fold_in(splits[14], 71), 0)
    window_id = place_ends(jax.random.randint(splits[3], (EVENTS, N_ETA, N_PHI, VIS_DEV), 0, NWIN), jax.random.fold_in(splits[3], 1), 0, NWIN - 1).astype(jnp.int32)
    enc_cot = scatter_about(splits[4], (EVENTS, N_ETA, N_PHI, VIS_DEV, D), (VIS_DEV * DEVICES) ** -0.5, 0.0625, ((0, 4), (1, 2), (2, 4)))
    w_qkv = scatter_about(splits[5], (D, 3 * D), D ** -0.5, 0.21875)
    head_scale = jnp.clip(jnp.exp(jax.random.uniform(splits[6], (HEADS,), jnp.float32, math.log(2.0), math.log(12.0))), 2.0, 12.0)
    w_out = scatter_about(splits[7], (D, D), D ** -0.5, 0.21875)
    w_dec_in = scatter_about(splits[8], (D, DEC), D ** -0.5, 0.21875)
    mask_token = scatter_about(splits[9], (DEC,), 1.0, 4.0)
    conv_kernel = scatter_about(splits[10], (KERN, KERN, DEC), (KERN * KERN) ** -0.5, 0.875, (), jnp.float32)
    w_up = scatter_about(splits[11], (DEC, DEC_FF), DEC ** -0.5, 0.3125)
    w_down = scatter_about(splits[12], (DEC_FF, DEC), DEC_FF ** -0.5, 0.21875)
    w_head = scatter_about(splits[13], (DEC, PATCH), DEC ** -0.5, 0.3125)
    return {"tokens": tokens, "send_pos": send_pos, "enc_src": enc_src, "window_id": window_id, "enc_cot": enc_cot, "w_qkv": w_qkv, "head_scale": head_scale, "w_out": w_out, "w_dec_in": w_dec_in, "mask_token": mask_token, "conv_kernel": conv_kernel, "w_up": w_up, "w_down": w_down, "w_head": w_head}


norm_eps = 1e-05
length_eps = 1e-06
highest = lax.Precision.HIGHEST

def plain_norm(values):
    centre = lax.optimization_barrier(jnp.mean(values, axis=-1, keepdims=True))
    centred = values - centre
    spread = lax.optimization_barrier(jnp.mean(centred * centred, axis=-1, keepdims=True))
    return centred * lax.rsqrt(spread + norm_eps)

def encoder_pass(enc_in, window, cotangent, w_qkv, head_scale, w_out):
    row_count, feature_width = enc_in.shape
    head_count = head_scale.shape[0]
    head_size = feature_width // head_count
    normed = plain_norm(enc_in.astype(jnp.float32)).astype(jnp.bfloat16)
    qkv = jnp.dot(normed, w_qkv, preferred_element_type=jnp.float32).reshape(row_count, 3, head_count, head_size)
    query = qkv[:, 0]
    keyed = qkv[:, 1]
    value_low = qkv[:, 2].astype(jnp.bfloat16)
    query_len = jnp.sqrt(lax.optimization_barrier(jnp.sum(query * query, axis=-1, keepdims=True)) + length_eps)
    key_len = jnp.sqrt(lax.optimization_barrier(jnp.sum(keyed * keyed, axis=-1, keepdims=True)) + length_eps)
    query_unit = query / query_len
    key_unit = keyed / key_len
    same_window = window[:, None] == window[None, :]
    scores = jnp.einsum('qhd,khd->hqk', query_unit, key_unit, precision=highest) * head_scale[:, None, None]
    raised = jnp.where(same_window[None], jnp.exp(scores), jnp.zeros((), jnp.float32))
    softmax_weights = raised / lax.optimization_barrier(jnp.sum(raised, axis=-1, keepdims=True))
    softmax_low = softmax_weights.astype(jnp.bfloat16)
    attended = jnp.einsum('hqk,khd->qhd', softmax_low.astype(jnp.float32), value_low.astype(jnp.float32), precision=highest).reshape(row_count, feature_width).astype(jnp.bfloat16)
    enc_out = (enc_in.astype(jnp.float32) + jnp.dot(attended, w_out, preferred_element_type=jnp.float32)).astype(jnp.bfloat16)
    grad_attended = jnp.dot(cotangent, w_out.T, preferred_element_type=jnp.float32).astype(jnp.bfloat16)
    grad_attended = grad_attended.reshape(row_count, head_count, head_size)
    grad_soft = jnp.einsum('qhd,khd->hqk', grad_attended.astype(jnp.float32), value_low.astype(jnp.float32), precision=highest)
    grad_value = jnp.einsum('hqk,qhd->khd', softmax_low.astype(jnp.float32), grad_attended.astype(jnp.float32), precision=highest)
    grad_scores = softmax_weights * (grad_soft - lax.optimization_barrier(jnp.sum(softmax_weights * grad_soft, axis=-1, keepdims=True)))
    grad_scores = grad_scores * head_scale[:, None, None]
    grad_qunit = jnp.einsum('hqk,khd->qhd', grad_scores, key_unit, precision=highest)
    grad_kunit = jnp.einsum('hqk,qhd->khd', grad_scores, query_unit, precision=highest)
    grad_query = (grad_qunit - query_unit * lax.optimization_barrier(jnp.sum(query_unit * grad_qunit, axis=-1, keepdims=True))) / query_len
    grad_key = (grad_kunit - key_unit * lax.optimization_barrier(jnp.sum(key_unit * grad_kunit, axis=-1, keepdims=True))) / key_len
    grad_qkv = jnp.stack([grad_query, grad_key, grad_value], axis=1).reshape(row_count, 3 * feature_width).astype(jnp.bfloat16)
    term = jnp.concatenate([jnp.dot(grad_qkv.T, normed, preferred_element_type=jnp.float32), jnp.dot(cotangent.T, attended, preferred_element_type=jnp.float32)], axis=0)
    return (enc_out, term)

def decoder_pass(dec_grid, conv_kernel, w_up, w_down, w_head):
    kernel_span = conv_kernel.shape[0]
    rim_width = kernel_span // 2
    eta_cells, phi_cells, dec_width = dec_grid.shape
    wrapped = jnp.concatenate([dec_grid[:, phi_cells - rim_width:], dec_grid, dec_grid[:, :rim_width]], axis=1)
    padded = jnp.pad(wrapped, ((rim_width, rim_width), (0, 0), (0, 0)))
    mixed_cells = jnp.zeros((eta_cells, phi_cells, dec_width), jnp.float32)
    for row_shift in range(kernel_span):
        for col_shift in range(kernel_span):
            window_cells = padded[row_shift:row_shift + eta_cells, col_shift:col_shift + phi_cells].astype(jnp.float32)
            mixed_cells = mixed_cells + conv_kernel[row_shift, col_shift] * window_cells
    dec_normed = plain_norm(mixed_cells).astype(jnp.bfloat16).reshape(eta_cells * phi_cells, dec_width)
    hidden = jax.nn.gelu(jnp.dot(dec_normed, w_up, preferred_element_type=jnp.float32), approximate=False).astype(jnp.bfloat16)
    decoded = (dec_grid.reshape(eta_cells * phi_cells, dec_width).astype(jnp.float32) + jnp.dot(hidden, w_down, preferred_element_type=jnp.float32)).astype(jnp.bfloat16)
    return jnp.dot(decoded, w_head, preferred_element_type=jnp.float32).reshape(eta_cells, phi_cells, -1)

def reference(tokens, send_pos, enc_src, window_id, enc_cot, w_qkv, head_scale, w_out, w_dec_in, mask_token, conv_kernel, w_up, w_down, w_head):
    event_count = tokens.shape[0]
    feature_width = tokens.shape[-1]
    dec_width = w_dec_in.shape[1]
    group_size = N_ETA * N_PHI
    slot_count = send_pos.shape[-1]
    tile_len = TE * TP
    tile_rows = tokens.reshape(event_count, N_ETA, TE, N_PHI, TP, feature_width).transpose(0, 1, 3, 2, 4, 5)
    tile_rows = tile_rows.reshape(event_count, group_size, tile_len, feature_width)
    send_table = send_pos.reshape(event_count, group_size, group_size, slot_count)
    sources = enc_src.reshape(event_count, group_size, VIS_DEV)
    source_tile = sources // slot_count
    source_slot = sources % slot_count
    event_ids = jnp.arange(event_count, dtype=jnp.int32)[:, None, None]
    shard_ids = jnp.arange(group_size, dtype=jnp.int32)[None, :, None]
    cell_ids = send_table[event_ids, source_tile, shard_ids, source_slot]
    enc_in = tile_rows[event_ids, source_tile, cell_ids]

    def shard_step(total, item):
        rows_in, window, cotangent = item
        enc_out, term = encoder_pass(rows_in, window, cotangent, w_qkv, head_scale, w_out)
        return (total + term, enc_out)
    weight_grads, enc_out = lax.scan(shard_step, jnp.zeros((4 * feature_width, feature_width), jnp.float32), (enc_in.reshape(event_count * group_size, VIS_DEV, feature_width), window_id.reshape(event_count * group_size, VIS_DEV), enc_cot.reshape(event_count * group_size, VIS_DEV, feature_width)))
    dec_rows = jnp.dot(enc_out.reshape(-1, feature_width), w_dec_in, preferred_element_type=jnp.float32).astype(jnp.bfloat16)
    dec_rows = dec_rows.reshape(event_count, group_size, VIS_DEV, dec_width)
    filled = jnp.zeros((event_count, group_size, tile_len, dec_width), jnp.bfloat16).at[event_ids, source_tile, cell_ids].set(dec_rows)
    seen_cells = jnp.zeros((event_count, group_size, tile_len), jnp.bool_).at[event_ids, source_tile, cell_ids].set(True)
    dec_tiles = jnp.where(seen_cells[..., None], filled, mask_token)
    dec_grid = dec_tiles.reshape(event_count, N_ETA, N_PHI, TE, TP, dec_width).transpose(0, 1, 3, 2, 4, 5)
    dec_grid = dec_grid.reshape(event_count, N_ETA * TE, N_PHI * TP, dec_width)
    reconstruction = lax.map(lambda grid_one: decoder_pass(grid_one, conv_kernel, w_up, w_down, w_head), dec_grid)
    return (weight_grads, reconstruction)
```

```python
import functools

import jax
import jax.numpy as jnp
from jax import lax
from jax.experimental import pallas as pl
from jax.experimental.pallas import tpu as pltpu
from jax.sharding import PartitionSpec as P

norm_eps = 1e-05
length_eps = 1e-06
f32 = jnp.float32
bf16 = jnp.bfloat16
MIB = 1024 * 1024

NN = (((1,), (0,)), ((), ()))
NT = (((1,), (1,)), ((), ()))
TN = (((0,), (0,)), ((), ()))


def mm(a, b, dims=NN):
    return lax.dot_general(a, b, dims, preferred_element_type=f32)


def vmem():
    return pl.BlockSpec(memory_space=pltpu.VMEM)


def smem():
    return pl.BlockSpec(memory_space=pltpu.SMEM)


def call(kernel, name, outs, in_specs, scratch=(), flops=0, nbytes=0, limit=48):
    single = not isinstance(outs, (list, tuple))
    out_list = [outs] if single else list(outs)
    specs = [vmem() for _ in out_list]
    return pl.pallas_call(
        kernel,
        out_shape=out_list[0] if single else tuple(out_list),
        in_specs=in_specs,
        out_specs=specs[0] if single else tuple(specs),
        scratch_shapes=list(scratch),
        compiler_params=pltpu.CompilerParams(vmem_limit_bytes=limit * MIB),
        cost_estimate=pl.CostEstimate(flops=flops, bytes_accessed=nbytes, transcendentals=0),
        name=name,
    )


def sds(shape, dtype):
    return jax.ShapeDtypeStruct(shape, dtype)


def column_of(row):
    return jnp.transpose(jnp.broadcast_to(row, (8, row.shape[1])))[:, 0:1]


def slot_column(pos_ref, wide_ref, padded):
    group, cap = pos_ref.shape
    wide_ref[...] = jnp.full(wide_ref.shape, -1.0, f32)
    wide_ref[:, 0:cap] = pos_ref[...].astype(f32)
    turned = jnp.transpose(wide_ref[...])
    return jnp.concatenate([turned[0:padded, d : d + 1] for d in range(group)], axis=0)


def pick_kernel(padded, pos_ref, tok_ref, out_ref, wide_ref):
    slots = slot_column(pos_ref, wide_ref, padded)
    cells = lax.broadcasted_iota(jnp.int32, (slots.shape[0], tok_ref.shape[0]), 1).astype(f32)
    chosen = (slots == cells).astype(f32).astype(bf16)
    out_ref[...] = mm(chosen, tok_ref[...]).astype(bf16)


def prep_kernel(cot_ref, wout_ref, wqkv_ref, ga_ref, cot_t_ref, wqkv_t_ref):
    ga_ref[...] = mm(wout_ref[...], cot_ref[...], NT).astype(bf16)
    cot_t_ref[...] = jnp.transpose(cot_ref[...])
    wqkv_t_ref[...] = jnp.transpose(wqkv_ref[...])


def forward_kernel(
    cap, padded, src_ref, win_ref, scale_ref, arr_ref, wqkv_t_ref, wout_ref, wdec_ref,
    out_ref, e_ref, p_ref, u_ref, len_ref, v_ref, att_ref,
):
    rows, width = e_ref.shape[1], e_ref.shape[2]
    heads = p_ref.shape[0]
    size = width // heads
    slots = arr_ref.shape[0]
    src = src_ref[...].astype(f32)
    slot_row = src + (padded - cap) * jnp.floor((src + 0.5) * (1.0 / cap))
    slot_col = column_of(slot_row)
    lanes = lax.broadcasted_iota(jnp.int32, (rows, slots), 1).astype(f32)
    pick = (slot_col == lanes).astype(f32).astype(bf16)
    enc_in = mm(pick, arr_ref[...])
    centred = enc_in - jnp.mean(enc_in, axis=-1, keepdims=True)
    spread = jnp.mean(centred * centred, axis=-1, keepdims=True)
    normed = (centred * lax.rsqrt(spread + norm_eps)).astype(bf16)
    e_ref[0] = normed
    u_ref[0:width] = mm(wqkv_t_ref[0:width], normed, NT)
    u_ref[width : 2 * width] = mm(wqkv_t_ref[width : 2 * width], normed, NT)
    v_ref[...] = mm(wqkv_t_ref[2 * width : 3 * width], normed, NT).astype(bf16)
    win = win_ref[...].astype(f32)
    same = column_of(win) == win
    for h in range(heads):
        lo, hi = h * size, (h + 1) * size
        q = u_ref[lo:hi]
        k = u_ref[width + lo : width + hi]
        q_inv = lax.rsqrt(jnp.sum(q * q, axis=0, keepdims=True) + length_eps)
        k_inv = lax.rsqrt(jnp.sum(k * k, axis=0, keepdims=True) + length_eps)
        q = q * q_inv
        k = k * k_inv
        u_ref[lo:hi] = q
        u_ref[width + lo : width + hi] = k
        len_ref[h : h + 1] = q_inv
        len_ref[heads + h : heads + h + 1] = k_inv
        scores = mm(k.astype(bf16), q.astype(bf16), TN)
        raised = jnp.where(same, jnp.exp(scores * scale_ref[h]), 0.0)
        weights = (raised * (1.0 / jnp.sum(raised, axis=0, keepdims=True))).astype(bf16)
        p_ref[h] = weights
        att_ref[lo:hi] = mm(v_ref[lo:hi], weights).astype(bf16)
    attended = jnp.transpose(att_ref[...])
    e_ref[1] = attended
    enc_out = (enc_in + mm(attended, wout_ref[...])).astype(bf16)
    dec = mm(enc_out, wdec_ref[...]).astype(bf16)
    places = lax.broadcasted_iota(jnp.int32, (slots, rows), 0).astype(f32)
    put = (places == slot_row).astype(f32).astype(bf16)
    out_ref[...] = mm(put, dec).astype(bf16)


def backward_kernel(
    split, me_ref, scale_ref, p_ref, u_ref, len_ref, v_ref, ga_ref, cot_t_ref, out_ref
):
    heads = p_ref.shape[0]
    width = v_ref.shape[0]
    size = width // heads
    unit = 32
    if split is not None:
        me = me_ref[0]
        per_shard, per_part = split[0] // unit, split[1] // unit

    def emit(start, block):
        for j in range(block.shape[0] // unit):
            u = (start + j * unit) // unit
            piece = block[j * unit : (j + 1) * unit]
            if split is None:
                out_ref[u * unit : (u + 1) * unit] = piece
            else:
                shard, rest = divmod(u, per_shard)
                part, place = divmod(rest, per_part)
                out_ref[me ^ part, shard, place * unit : (place + 1) * unit] = piece

    for h in range(heads):
        lo, hi = h * size, (h + 1) * size
        ga = ga_ref[lo:hi]
        low = p_ref[h]
        weights = low.astype(f32)
        grad_soft = mm(v_ref[lo:hi], ga, TN)
        part = weights * grad_soft
        total = jnp.sum(part, axis=0, keepdims=True)
        grad_scores = ((part - weights * total) * scale_ref[h]).astype(bf16)
        q = u_ref[lo:hi]
        k = u_ref[width + lo : width + hi]
        grad_v = mm(ga, low, NT)
        grad_q = mm(k.astype(bf16), grad_scores)
        grad_k = mm(q.astype(bf16), grad_scores, NT)
        grad_q = (grad_q - q * jnp.sum(q * grad_q, axis=0, keepdims=True)) * len_ref[h : h + 1]
        grad_k = (grad_k - k * jnp.sum(k * grad_k, axis=0, keepdims=True)) * len_ref[
            heads + h : heads + h + 1
        ]
        emit(lo, grad_q.astype(bf16))
        emit(width + lo, grad_k.astype(bf16))
        emit(2 * width + lo, grad_v.astype(bf16))
    emit(3 * width, cot_t_ref[...])


def term_kernel(
    qkv_shards, place_ref, l0, l1, l2, l3, e01, e2, e3, keep_ref, send_ref
):
    shards, part, rows = l0.shape
    half = shards // 2
    width = keep_ref.shape[-1]
    lhs = (l0, l1, l2, l3)

    def rhs(k, which):
        return (e01[0, which], e01[1, which], e2[which], e3[which])[k]

    def block(lo, hi, which):
        acc = None
        for k in range(4):
            left = lhs[k][lo:hi].reshape((hi - lo) * part, rows)
            step = mm(left, rhs(k, which))
            acc = step if acc is None else acc + step
        return acc.reshape(hi - lo, part, width)

    spans = []
    for lo, hi in ((0, half), (half, shards)):
        cut = min(max(qkv_shards, lo), hi)
        pieces = []
        if cut > lo:
            pieces.append((0, block(lo, cut, 0)))
        if hi > cut:
            pieces.append((cut - lo, block(cut, hi, 1)))
        spans.append(pieces)
    for mine in range(2):

        @pl.when(place_ref[0] == mine)
        def _():
            for at, value in spans[mine]:
                keep_ref[at : at + value.shape[0]] = value
            for at, value in spans[1 - mine]:
                send_ref[at : at + value.shape[0]] = value.astype(bf16)


def line_kernel(place_ref, keep_ref, got_ref, own_ref, send_ref):
    count = keep_ref.shape[0]
    me = place_ref[0]
    for k in range(count):
        at = lax.rem(me + k, count)
        value = keep_ref[at] + got_ref[at].astype(f32)
        if k == 0:
            own_ref[...] = value
        else:
            send_ref[k - 1] = value.astype(bf16)


def close_kernel(own_ref, *refs):
    total = own_ref[...]
    for ref in refs[:-1]:
        total = total + ref[...].astype(f32)
    refs[-1][...] = total.astype(bf16)


def spread_kernel(me_ref, first_ref, second_ref, out_ref):
    me = me_ref[0]
    out_ref[me] = first_ref[0].astype(f32)
    out_ref[me ^ 2] = first_ref[1].astype(f32)
    out_ref[me ^ 1] = second_ref[0].astype(f32)
    out_ref[me ^ 3] = second_ref[1].astype(f32)


def flip(value, axis, bit):
    return lax.ppermute(value, axis, [(i, i ^ bit) for i in range(lax.axis_size(axis))])


def turn(value, axis, k):
    count = lax.axis_size(axis)
    return lax.ppermute(value, axis, [(i, (i + k) % count) for i in range(count)])


def extended(block, sides, width):
    for axis, dim in sides:
        low = turn(lax.slice_in_dim(block, block.shape[dim] - width, None, axis=dim), axis, 1)
        high = turn(lax.slice_in_dim(block, 0, width, axis=dim), axis, -1)
        block = jnp.concatenate([low, block, high], axis=dim)
    return block


def plain_norm(values):
    centre = jnp.mean(values, axis=-1, keepdims=True)
    centred = values - centre
    spread = jnp.mean(centred * centred, axis=-1, keepdims=True)
    return centred * lax.rsqrt(spread + norm_eps)


def summed_slow(left, both, width):
    qkv_rows = left.shape[0] - width
    term = jnp.concatenate([mm(left[:qkv_rows], both[0]), mm(left[qkv_rows:], both[1])], axis=0)
    share = lax.psum_scatter(term, ("eta", "phi", "replica"), scatter_dimension=0, tiled=True)
    return lax.all_gather(share.astype(bf16), "replica", axis=0, tiled=True).astype(f32)


def summed_fast(left, both, width, phi_count):
    shards, part, rows = left.shape[1:]
    pair = jnp.stack([both, flip(both, "replica", 2)])
    e01 = pair
    other = flip(pair, "replica", 1)
    got = [flip(left[k], "replica", k) for k in (1, 2, 3)]
    place = lax.axis_index("eta").astype(jnp.int32).reshape(1)
    keep, send = call(
        functools.partial(term_kernel, shards * 3 // 4),
        "terms",
        [sds((shards // 2, part, width), f32), sds((shards // 2, part, width), bf16)],
        [smem()] + [vmem()] * 7,
        flops=2 * shards * part * width * rows * 4,
        nbytes=8 * MIB,
    )(place, left[0], got[1], got[0], got[2], e01, other[0], other[1])
    arrived = turn(send, "eta", 1)
    line = lax.axis_index("phi").astype(jnp.int32).reshape(1)
    own, outgoing = call(
        line_kernel,
        "line",
        [sds((part, width), f32), sds((phi_count - 1, part, width), bf16)],
        [smem(), vmem(), vmem()],
        flops=shards * part * width,
        nbytes=3 * MIB,
    )(line, keep, arrived)
    pieces = [turn(outgoing[k - 1], "phi", k) for k in range(1, phi_count)]
    mine = call(
        close_kernel,
        "close",
        sds((part, width), bf16),
        [vmem()] * phi_count,
        flops=4 * part * width,
        nbytes=MIB,
    )(own, *pieces)
    first = jnp.stack([mine, flip(mine, "replica", 2)])
    second = flip(first, "replica", 1)
    me = lax.axis_index("replica").astype(jnp.int32).reshape(1)
    whole = call(
        spread_kernel,
        "spread",
        sds((4, part, width), f32),
        [smem(), vmem(), vmem()],
        flops=4 * part * width,
        nbytes=2 * MIB,
    )(me, first, second)
    return whole.reshape(4 * part, width)


def body(
    tokens, send_pos, enc_src, window_id, enc_cot, w_qkv, head_scale, w_out, w_dec_in,
    mask_token, conv_kernel, w_up, w_down, w_head,
):
    eta_cells, phi_cells, width = tokens.shape[1:]
    dec_width = w_dec_in.shape[1]
    tile_len = eta_cells * phi_cells
    eta_count = lax.axis_size("eta")
    phi_count = lax.axis_size("phi")
    replicas = lax.axis_size("replica")
    group = eta_count * phi_count
    cap = send_pos.shape[-1]
    padded = -(-cap // 8) * 8
    slots = group * padded
    rows = enc_cot.shape[-2]
    heads = head_scale.shape[0]
    out_rows = 4 * width
    shard_rows = out_rows // group
    part_rows = shard_rows // replicas
    fast = eta_count == 2 and replicas == 4 and part_rows % 32 == 0

    positions = send_pos.reshape(group, cap)
    outgoing = call(
        functools.partial(pick_kernel, padded),
        "pick",
        sds((slots, width), bf16),
        [vmem(), vmem()],
        scratch=[pltpu.VMEM((group, 128), f32)],
        flops=2 * slots * tile_len * width,
        nbytes=3 * MIB,
    )(positions, tokens.reshape(tile_len, width))
    arrived = lax.all_to_all(
        outgoing.reshape(group, padded, width), ("eta", "phi"), split_axis=0, concat_axis=0,
        tiled=True,
    ).reshape(slots, width)

    cotangent = enc_cot.reshape(rows, width)
    grad_att, cot_t, w_qkv_t = call(
        prep_kernel,
        "prep",
        [sds((width, rows), bf16), sds((width, rows), bf16), sds((3 * width, width), bf16)],
        [vmem()] * 3,
        flops=2 * rows * width * width,
        nbytes=10 * MIB,
    )(cotangent, w_out, w_qkv)

    outbound, both, weights, units, lengths, values = call(
        functools.partial(forward_kernel, cap, padded),
        "forward",
        [
            sds((slots, dec_width), bf16),
            sds((2, rows, width), bf16),
            sds((heads, rows, rows), bf16),
            sds((2 * width, rows), f32),
            sds((2 * heads, rows), f32),
            sds((width, rows), bf16),
        ],
        [vmem(), vmem(), smem(), vmem(), vmem(), vmem(), vmem()],
        scratch=[pltpu.VMEM((width, rows), bf16)],
        flops=2 * rows * width * width * 5,
        nbytes=10 * MIB,
    )(
        enc_src.reshape(1, rows), window_id.reshape(1, rows), head_scale, arrived, w_qkv_t,
        w_out, w_dec_in,
    )
    returned = lax.all_to_all(
        outbound.reshape(group, padded, dec_width), ("eta", "phi"), split_axis=0, concat_axis=0,
        tiled=True,
    )

    me = lax.axis_index("replica").astype(jnp.int32).reshape(1)
    left_shape = (replicas, group, part_rows, rows) if fast else (out_rows, rows)
    left = call(
        functools.partial(backward_kernel, (shard_rows, part_rows) if fast else None),
        "backward",
        sds(left_shape, bf16),
        [smem(), smem()] + [vmem()] * 6,
        flops=2 * rows * rows * width * 5,
        nbytes=10 * MIB,
    )(me, head_scale, weights, units, lengths, values, grad_att, cot_t)
    if fast:
        grad_total = summed_fast(left, both, width, phi_count)
    else:
        grad_total = summed_slow(left, both, width)

    dec_slots = returned[:, :cap].reshape(group * cap, dec_width)
    slot_cells = send_pos.reshape(group * cap)
    filled = jnp.zeros((tile_len, dec_width), bf16).at[slot_cells].set(dec_slots, mode="drop")
    seen_cells = jnp.zeros((tile_len,), jnp.bool_).at[slot_cells].set(True, mode="drop")
    dec_grid = jnp.where(seen_cells[:, None], filled, mask_token).reshape(
        eta_cells, phi_cells, dec_width
    )
    kernel_span = conv_kernel.shape[0]
    rim_width = kernel_span // 2
    full = extended(dec_grid, (("eta", 0), ("phi", 1)), rim_width)
    eta_place = lax.axis_index("eta")
    rim_line = lax.broadcasted_iota(jnp.int32, (eta_cells + 2 * rim_width, 1, 1), 0)
    keep_rim = jnp.logical_and(
        jnp.logical_or(rim_line >= rim_width, eta_place > 0),
        jnp.logical_or(rim_line < eta_cells + rim_width, eta_place < eta_count - 1),
    )
    full = jnp.where(keep_rim, full, jnp.zeros((), full.dtype))
    mixed_cells = jnp.zeros((eta_cells, phi_cells, dec_width), f32)
    for row_shift in range(kernel_span):
        for col_shift in range(kernel_span):
            window_cells = full[
                row_shift : row_shift + eta_cells, col_shift : col_shift + phi_cells
            ].astype(f32)
            mixed_cells = mixed_cells + conv_kernel[row_shift, col_shift] * window_cells
    dec_normed = plain_norm(mixed_cells).astype(bf16).reshape(tile_len, dec_width)
    hidden = jax.nn.gelu(mm(dec_normed, w_up), approximate=False).astype(bf16)
    decoded = (dec_grid.reshape(tile_len, dec_width).astype(f32) + mm(hidden, w_down)).astype(bf16)
    reconstruction = mm(decoded, w_head).reshape(1, eta_cells, phi_cells, -1)
    return (grad_total, reconstruction)


def solution(mesh):
    in_specs = (
        P("replica", "eta", "phi", None),
        P("replica", "eta", "phi", None, None),
        P("replica", "eta", "phi", None),
        P("replica", "eta", "phi", None),
        P("replica", "eta", "phi", None, None),
        P(), P(), P(), P(), P(), P(), P(), P(), P(),
    )
    out_specs = (P(("eta", "phi"), None), P("replica", "eta", "phi", None))
    return jax.shard_map(body, mesh=mesh, in_specs=in_specs, out_specs=out_specs, check_vma=False)
```

```python
import functools

import jax
import jax.numpy as jnp
import numpy as np
from jax import lax
from jax.experimental import pallas as pl
from jax.experimental.pallas import tpu as pltpu
from jax.sharding import PartitionSpec as P

norm_eps = 1e-05
length_eps = 1e-06
f32 = jnp.float32
bf16 = jnp.bfloat16
MIB = 1024 * 1024

NN = (((1,), (0,)), ((), ()))
NT = (((1,), (1,)), ((), ()))
TN = (((0,), (0,)), ((), ()))


def mm(a, b, dims=NN):
    return lax.dot_general(a, b, dims, preferred_element_type=f32)


def vmem():
    return pl.BlockSpec(memory_space=pltpu.VMEM)


def smem():
    return pl.BlockSpec(memory_space=pltpu.SMEM)


def call(kernel, name, outs, in_specs, scratch=(), flops=0, nbytes=0, limit=20):
    single = not isinstance(outs, (list, tuple))
    out_list = [outs] if single else list(outs)
    specs = [vmem() for _ in out_list]
    return pl.pallas_call(
        kernel,
        out_shape=out_list[0] if single else tuple(out_list),
        in_specs=in_specs,
        out_specs=specs[0] if single else tuple(specs),
        scratch_shapes=list(scratch),
        compiler_params=pltpu.CompilerParams(vmem_limit_bytes=limit * MIB),
        cost_estimate=pl.CostEstimate(flops=flops, bytes_accessed=nbytes, transcendentals=0),
        name=name,
    )


def sds(shape, dtype):
    return jax.ShapeDtypeStruct(shape, dtype)


def column_of(row):
    return jnp.transpose(jnp.broadcast_to(row, (8, row.shape[1])))[:, 0:1]


def slot_column(pos_ref, wide_ref, padded):
    group, cap = pos_ref.shape
    wide_ref[...] = jnp.full(wide_ref.shape, -1.0, f32)
    wide_ref[:, 0:cap] = pos_ref[...].astype(f32)
    turned = jnp.transpose(wide_ref[...])
    return jnp.concatenate([turned[0:padded, d : d + 1] for d in range(group)], axis=0)


def pick_kernel(padded, pos_ref, tok_ref, out_ref, wide_ref):
    slots = slot_column(pos_ref, wide_ref, padded)
    cells = lax.broadcasted_iota(jnp.int32, (slots.shape[0], tok_ref.shape[0]), 1).astype(f32)
    chosen = (slots == cells).astype(f32).astype(bf16)
    out_ref[...] = mm(chosen, tok_ref[...]).astype(bf16)


def prep_kernel(cot_ref, wout_ref, wqkv_ref, ga_ref, cot_t_ref, wqkv_t_ref):
    ga_ref[...] = mm(wout_ref[...], cot_ref[...], NT).astype(bf16)
    cot_t_ref[...] = jnp.transpose(cot_ref[...])
    wqkv_t_ref[...] = jnp.transpose(wqkv_ref[...])


def forward_kernel(
    cap, padded, src_ref, win_ref, scale_ref, arr_ref, wqkv_t_ref, wout_ref, wdec_ref,
    out_ref, e_ref, p_ref, u_ref, len_ref, v_ref, att_ref,
):
    rows, width = e_ref.shape[1], e_ref.shape[2]
    heads = p_ref.shape[0]
    size = width // heads
    slots = arr_ref.shape[0]
    src = src_ref[...].astype(f32)
    slot_row = src + (padded - cap) * jnp.floor((src + 0.5) * (1.0 / cap))
    slot_col = column_of(slot_row)
    lanes = lax.broadcasted_iota(jnp.int32, (rows, slots), 1).astype(f32)
    pick = (slot_col == lanes).astype(f32).astype(bf16)
    enc_in = mm(pick, arr_ref[...])
    centred = enc_in - jnp.mean(enc_in, axis=-1, keepdims=True)
    spread = jnp.mean(centred * centred, axis=-1, keepdims=True)
    normed = (centred * lax.rsqrt(spread + norm_eps)).astype(bf16)
    e_ref[0] = normed
    u_ref[0:width] = mm(wqkv_t_ref[0:width], normed, NT)
    u_ref[width : 2 * width] = mm(wqkv_t_ref[width : 2 * width], normed, NT)
    v_ref[...] = mm(wqkv_t_ref[2 * width : 3 * width], normed, NT).astype(bf16)
    win = win_ref[...].astype(f32)
    same = column_of(win) == win
    for h in range(heads):
        lo, hi = h * size, (h + 1) * size
        q = u_ref[lo:hi]
        k = u_ref[width + lo : width + hi]
        q_inv = lax.rsqrt(jnp.sum(q * q, axis=0, keepdims=True) + length_eps)
        k_inv = lax.rsqrt(jnp.sum(k * k, axis=0, keepdims=True) + length_eps)
        q = q * q_inv
        k = k * k_inv
        u_ref[lo:hi] = q
        u_ref[width + lo : width + hi] = k
        len_ref[h : h + 1] = q_inv
        len_ref[heads + h : heads + h + 1] = k_inv
        scores = mm(k.astype(bf16), q.astype(bf16), TN)
        raised = jnp.where(same, jnp.exp(scores * scale_ref[h]), 0.0)
        weights = (raised * (1.0 / jnp.sum(raised, axis=0, keepdims=True))).astype(bf16)
        p_ref[h] = weights
        att_ref[lo:hi] = mm(v_ref[lo:hi], weights).astype(bf16)
    attended = jnp.transpose(att_ref[...])
    e_ref[1] = attended
    enc_out = (enc_in + mm(attended, wout_ref[...])).astype(bf16)
    dec = mm(enc_out, wdec_ref[...]).astype(bf16)
    places = lax.broadcasted_iota(jnp.int32, (slots, rows), 0).astype(f32)
    put = (places == slot_row).astype(f32).astype(bf16)
    out_ref[...] = mm(put, dec).astype(bf16)


def backward_kernel(
    split, me_ref, scale_ref, p_ref, u_ref, len_ref, v_ref, ga_ref, cot_t_ref, out_ref
):
    heads = p_ref.shape[0]
    width = v_ref.shape[0]
    size = width // heads
    unit = 32
    if split is not None:
        me = me_ref[0]
        per_shard, per_part = split[0] // unit, split[1] // unit

    def emit(start, block):
        for j in range(block.shape[0] // unit):
            u = (start + j * unit) // unit
            piece = block[j * unit : (j + 1) * unit]
            if split is None:
                out_ref[u * unit : (u + 1) * unit] = piece
            else:
                shard, rest = divmod(u, per_shard)
                part, place = divmod(rest, per_part)
                out_ref[me ^ part, shard, place * unit : (place + 1) * unit] = piece

    for h in range(heads):
        lo, hi = h * size, (h + 1) * size
        ga = ga_ref[lo:hi]
        low = p_ref[h]
        weights = low.astype(f32)
        grad_soft = mm(v_ref[lo:hi], ga, TN)
        part = weights * grad_soft
        total = jnp.sum(part, axis=0, keepdims=True)
        grad_scores = ((part - weights * total) * scale_ref[h]).astype(bf16)
        q = u_ref[lo:hi]
        k = u_ref[width + lo : width + hi]
        grad_v = mm(ga, low, NT)
        grad_q = mm(k.astype(bf16), grad_scores)
        grad_k = mm(q.astype(bf16), grad_scores, NT)
        grad_q = (grad_q - q * jnp.sum(q * grad_q, axis=0, keepdims=True)) * len_ref[h : h + 1]
        grad_k = (grad_k - k * jnp.sum(k * grad_k, axis=0, keepdims=True)) * len_ref[
            heads + h : heads + h + 1
        ]
        emit(lo, grad_q.astype(bf16))
        emit(width + lo, grad_k.astype(bf16))
        emit(2 * width + lo, grad_v.astype(bf16))
    emit(3 * width, cot_t_ref[...])


def term_kernel(
    qkv_shards, place_ref, l0, l1, l2, l3, e01, e2, e3, keep_ref, send_ref
):
    shards, part, rows = l0.shape
    half = shards // 2
    width = keep_ref.shape[-1]
    lhs = (l0, l1, l2, l3)

    def rhs(k, which):
        return (e01[0, which], e01[1, which], e2[which], e3[which])[k]

    def block(lo, hi, which):
        acc = None
        for k in range(4):
            left = lhs[k][lo:hi].reshape((hi - lo) * part, rows)
            step = mm(left, rhs(k, which))
            acc = step if acc is None else acc + step
        return acc.reshape(hi - lo, part, width)

    spans = []
    for lo, hi in ((0, half), (half, shards)):
        cut = min(max(qkv_shards, lo), hi)
        pieces = []
        if cut > lo:
            pieces.append((0, block(lo, cut, 0)))
        if hi > cut:
            pieces.append((cut - lo, block(cut, hi, 1)))
        spans.append(pieces)
    for mine in range(2):

        @pl.when(place_ref[0] == mine)
        def _():
            for at, value in spans[mine]:
                keep_ref[at : at + value.shape[0]] = value
            for at, value in spans[1 - mine]:
                send_ref[at : at + value.shape[0]] = value.astype(bf16)


def line_kernel(place_ref, keep_ref, got_ref, own_ref, send_ref):
    count = keep_ref.shape[0]
    me = place_ref[0]
    for k in range(count):
        at = lax.rem(me + k, count)
        value = keep_ref[at] + got_ref[at].astype(f32)
        if k == 0:
            own_ref[...] = value
        else:
            send_ref[k - 1] = value.astype(bf16)


def close_kernel(own_ref, *refs):
    total = own_ref[...]
    for ref in refs[:-1]:
        total = total + ref[...].astype(f32)
    refs[-1][...] = total.astype(bf16)


def spread_kernel(me_ref, first_ref, second_ref, out_ref):
    me = me_ref[0]
    out_ref[me] = first_ref[0].astype(f32)
    out_ref[me ^ 2] = first_ref[1].astype(f32)
    out_ref[me ^ 1] = second_ref[0].astype(f32)
    out_ref[me ^ 3] = second_ref[1].astype(f32)


def fill_kernel(padded, place_ref, pos_ref, ids_ref, mask_ref, got_ref, *refs):
    wide_ref = refs[-1]
    slots = slot_column(pos_ref, wide_ref, padded)
    ids = ids_ref[0:1] + place_ref[0].astype(f32) * ids_ref[1:2]
    chosen = (slots == ids).astype(f32).astype(bf16)
    got = got_ref[...]
    values = mm(chosen, got, TN)
    hits = mm(chosen, jnp.ones((got.shape[0], 128), bf16), TN)[:, 0:1]
    values = jnp.where(hits > 0.5, values, mask_ref[...].astype(f32)).astype(bf16)
    at = 0
    for ref in refs[:-1]:
        ref[...] = values[at : at + ref.shape[0]]
        at += ref.shape[0]


def conv_kernel_body(
    shape, span, folded, place_ref, grid_ref, left_ref, right_ref, rims, taps_ref, out_ref,
    full_ref, wide_ref, mixed_ref,
):
    lines, columns = shape
    rim = span // 2
    width = grid_ref.shape[-1]
    lead = 8
    full_ref[rim : rim + lines, lead : lead + columns] = (
        grid_ref[...].astype(f32).reshape(lines, columns, width)
    )
    left = left_ref[...].astype(f32)
    right = right_ref[...].astype(f32)
    for x in range(lines):
        full_ref[rim + x, lead - rim : lead] = left[rim * x : rim * (x + 1)]
        full_ref[rim + x, lead + columns : lead + columns + rim] = right[rim * x : rim * (x + 1)]

    def put(base, edge_ref, first_ref, last_ref):
        edge = edge_ref[...].astype(f32)
        first = first_ref[...].astype(f32)
        last = last_ref[...].astype(f32)
        for i in range(rim):
            full_ref[base + i, lead : lead + columns] = edge[columns * i : columns * (i + 1)]
            full_ref[base + i, lead - rim : lead] = first[rim * i : rim * (i + 1)]
            full_ref[base + i, lead + columns : lead + columns + rim] = last[
                rim * i : rim * (i + 1)
            ]

    if folded:
        far = rim + lines
        base = jnp.where(place_ref[0] == 0, far, 0)
        for i in range(rim):
            full_ref[far - base + i] = jnp.zeros(full_ref.shape[1:], f32)
        put(base, *rims)
    else:
        put(0, *rims[:3])
        put(rim + lines, *rims[3:])
    for t in range(span * span):
        wide_ref[t] = jnp.broadcast_to(taps_ref[t : t + 1], (8, width))
    groups = columns // 8

    for c in range(width // 128):
        cut = slice(c * 128, (c + 1) * 128)

        def step(x, accs, live, cut=cut):
            accs = list(accs)
            for v in range(span):
                at = lead - rim + v
                line = full_ref[x, at : at + columns, cut].reshape(groups, 8, 128)
                for i in live:
                    tap = wide_ref[(span - 1 - i) * span + v, :, cut]
                    accs[i] = accs[i] + line * tap[None]
            return accs

        def store(row, acc, cut=cut):
            at = row * columns
            if not isinstance(row, int):
                at = pl.multiple_of(at, columns)
            mixed_ref[pl.ds(at, columns), cut] = acc.reshape(columns, 128)

        zero = jnp.zeros((groups, 8, 128), f32)
        accs = [zero] * span
        for x in range(span - 1):
            accs = step(x, accs, range(span - 1 - x, span))
            accs = accs[1:] + [zero]

        def middle(x, accs):
            accs = step(x, accs, range(span))
            store(x - (span - 1), accs[0])
            return tuple(accs[1:] + [zero])

        accs = list(lax.fori_loop(span - 1, lines, middle, tuple(accs)))
        for x in range(lines, lines + span - 1):
            accs = step(x, accs, range(0, lines + span - 1 - x))
            store(x - (span - 1), accs[0])
            accs = accs[1:] + [zero]

    mixed = mixed_ref[...]
    centred = mixed - jnp.mean(mixed, axis=-1, keepdims=True)
    spread = jnp.mean(centred * centred, axis=-1, keepdims=True)
    out_ref[...] = (centred * lax.rsqrt(spread + norm_eps)).astype(bf16)


def mix_folded(shape, span, place, grid, left, right, a, b, c, taps, out, full, wide, mixed):
    conv_kernel_body(
        shape, span, True, place, grid, left, right, (a, b, c), taps, out, full, wide, mixed
    )


def mix_open(
    shape, span, place, grid, left, right, a, b, c, d, e, g, taps, out, full, wide, mixed
):
    conv_kernel_body(
        shape, span, False, place, grid, left, right, (a, b, c, d, e, g), taps, out, full, wide,
        mixed,
    )


def feed_kernel(chunk, normed_ref, grid_ref, up_ref, down_ref, head_ref, out_ref):
    for at in range(0, normed_ref.shape[0], chunk):
        rows = slice(at, at + chunk)
        wide = mm(normed_ref[rows], up_ref[...])
        hidden = (0.5 * wide * (1.0 + lax.erf(wide * 0.7071067811865476))).astype(bf16)
        decoded = (grid_ref[rows].astype(f32) + mm(hidden, down_ref[...])).astype(bf16)
        out_ref[rows] = mm(decoded, head_ref[...])


def flip(value, axis, bit):
    return lax.ppermute(value, axis, [(i, i ^ bit) for i in range(lax.axis_size(axis))])


def turn(value, axis, k):
    count = lax.axis_size(axis)
    return lax.ppermute(value, axis, [(i, (i + k) % count) for i in range(count)])


def summed_slow(left, both, width):
    qkv_rows = left.shape[0] - width
    term = jnp.concatenate([mm(left[:qkv_rows], both[0]), mm(left[qkv_rows:], both[1])], axis=0)
    share = lax.psum_scatter(term, ("eta", "phi", "replica"), scatter_dimension=0, tiled=True)
    return lax.all_gather(share.astype(bf16), "replica", axis=0, tiled=True).astype(f32)


def summed_fast(left, both, width, phi_count):
    shards, part, rows = left.shape[1:]
    pair = jnp.stack([both, flip(both, "replica", 2)])
    e01 = pair
    other = flip(pair, "replica", 1)
    got = [flip(left[k], "replica", k) for k in (1, 2, 3)]
    place = lax.axis_index("eta").astype(jnp.int32).reshape(1)
    keep, send = call(
        functools.partial(term_kernel, shards * 3 // 4),
        "terms",
        [sds((shards // 2, part, width), f32), sds((shards // 2, part, width), bf16)],
        [smem()] + [vmem()] * 7,
        flops=2 * shards * part * width * rows * 4,
        nbytes=8 * MIB,
    )(place, left[0], got[1], got[0], got[2], e01, other[0], other[1])
    arrived = turn(send, "eta", 1)
    line = lax.axis_index("phi").astype(jnp.int32).reshape(1)
    own, outgoing = call(
        line_kernel,
        "line",
        [sds((part, width), f32), sds((phi_count - 1, part, width), bf16)],
        [smem(), vmem(), vmem()],
        flops=shards * part * width,
        nbytes=3 * MIB,
    )(line, keep, arrived)
    pieces = [turn(outgoing[k - 1], "phi", k) for k in range(1, phi_count)]
    mine = call(
        close_kernel,
        "close",
        sds((part, width), bf16),
        [vmem()] * phi_count,
        flops=4 * part * width,
        nbytes=MIB,
    )(own, *pieces)
    first = jnp.stack([mine, flip(mine, "replica", 2)])
    second = flip(first, "replica", 1)
    me = lax.axis_index("replica").astype(jnp.int32).reshape(1)
    whole = call(
        spread_kernel,
        "spread",
        sds((4, part, width), f32),
        [smem(), vmem(), vmem()],
        flops=4 * part * width,
        nbytes=2 * MIB,
    )(me, first, second)
    return whole.reshape(4 * part, width)


def body(
    tokens, send_pos, enc_src, window_id, enc_cot, w_qkv, head_scale, w_out, w_dec_in,
    mask_token, conv_kernel, w_up, w_down, w_head,
):
    eta_cells, phi_cells, width = tokens.shape[1:]
    dec_width = w_dec_in.shape[1]
    tile_len = eta_cells * phi_cells
    eta_count = lax.axis_size("eta")
    phi_count = lax.axis_size("phi")
    replicas = lax.axis_size("replica")
    group = eta_count * phi_count
    cap = send_pos.shape[-1]
    padded = -(-cap // 8) * 8
    slots = group * padded
    rows = enc_cot.shape[-2]
    heads = head_scale.shape[0]
    out_rows = 4 * width
    shard_rows = out_rows // group
    part_rows = shard_rows // replicas
    fast = eta_count == 2 and replicas == 4 and part_rows % 32 == 0

    positions = send_pos.reshape(group, cap)
    outgoing = call(
        functools.partial(pick_kernel, padded),
        "pick",
        sds((slots, width), bf16),
        [vmem(), vmem()],
        scratch=[pltpu.VMEM((group, 128), f32)],
        flops=2 * slots * tile_len * width,
        nbytes=3 * MIB,
    )(positions, tokens.reshape(tile_len, width))
    arrived = lax.all_to_all(
        outgoing.reshape(group, padded, width), ("eta", "phi"), split_axis=0, concat_axis=0,
        tiled=True,
    ).reshape(slots, width)

    cotangent = enc_cot.reshape(rows, width)
    grad_att, cot_t, w_qkv_t = call(
        prep_kernel,
        "prep",
        [sds((width, rows), bf16), sds((width, rows), bf16), sds((3 * width, width), bf16)],
        [vmem()] * 3,
        flops=2 * rows * width * width,
        nbytes=10 * MIB,
    )(cotangent, w_out, w_qkv)

    outbound, both, weights, units, lengths, values = call(
        functools.partial(forward_kernel, cap, padded),
        "forward",
        [
            sds((slots, dec_width), bf16),
            sds((2, rows, width), bf16),
            sds((heads, rows, rows), bf16),
            sds((2 * width, rows), f32),
            sds((2 * heads, rows), f32),
            sds((width, rows), bf16),
        ],
        [vmem(), vmem(), smem(), vmem(), vmem(), vmem(), vmem()],
        scratch=[pltpu.VMEM((width, rows), bf16)],
        flops=2 * rows * width * width * 5,
        nbytes=10 * MIB,
    )(
        enc_src.reshape(1, rows), window_id.reshape(1, rows), head_scale, arrived, w_qkv_t,
        w_out, w_dec_in,
    )
    returned = lax.all_to_all(
        outbound.reshape(group, padded, dec_width), ("eta", "phi"), split_axis=0, concat_axis=0,
        tiled=True,
    )

    me = lax.axis_index("replica").astype(jnp.int32).reshape(1)
    left_shape = (replicas, group, part_rows, rows) if fast else (out_rows, rows)
    left = call(
        functools.partial(backward_kernel, (shard_rows, part_rows) if fast else None),
        "backward",
        sds(left_shape, bf16),
        [smem(), smem()] + [vmem()] * 6,
        flops=2 * rows * rows * width * 5,
        nbytes=10 * MIB,
    )(me, head_scale, weights, units, lengths, values, grad_att, cot_t)
    left, returned = lax.optimization_barrier((left, returned))
    if fast:
        grad_total = summed_fast(left, both, width, phi_count)
    else:
        grad_total = summed_slow(left, both, width)

    span = conv_kernel.shape[0]
    rim = span // 2
    folded = eta_count == 2
    eta_place = lax.axis_index("eta").astype(jnp.int32).reshape(1)
    lines = np.arange(eta_cells)[:, None]
    columns = np.arange(phi_cells)[None, :]
    cell = lines * phi_cells + columns
    parts = [cell]
    moves = [0]
    if folded:
        edge = cell[eta_cells - rim :]
        parts += [cell[:, :rim], cell[:, -rim:], edge, edge[:, :rim], edge[:, -rim:]]
        moves += [0, 0] + [-(eta_cells - rim) * phi_cells] * 3
    sizes = [-(-p.size // 16) * 16 for p in parts]
    ids = np.full((2, -(-sum(sizes) // 128) * 128), -7.0, np.float32)
    ids[1] = 0
    at = 0
    for p, size, move in zip(parts, sizes, moves):
        ids[0, at : at + p.size] = p.reshape(-1)
        ids[1, at : at + p.size] = move
        at += size
    filled = call(
        functools.partial(fill_kernel, padded),
        "fill",
        [sds((size, dec_width), bf16) for size in sizes],
        [smem()] + [vmem()] * 4,
        scratch=[pltpu.VMEM((group, 128), f32)],
        flops=2 * slots * ids.shape[1] * (dec_width + 128),
        nbytes=3 * MIB,
    )(
        eta_place, positions, jnp.asarray(ids), mask_token.reshape(1, dec_width),
        returned.reshape(slots, dec_width),
    )
    dec_grid = filled[0]
    plane = ("eta", "phi")

    def shifted(value, by):
        pairs = [
            (e * phi_count + p, (1 - e) * phi_count + (p + by) % phi_count)
            for e in range(2)
            for p in range(phi_count)
        ]
        return lax.ppermute(value, plane, pairs)

    if folded:
        _, first, last, edge, edge_first, edge_last = filled
        left = turn(last, "phi", 1)
        right = turn(first, "phi", -1)
        rims = (shifted(edge, 0), shifted(edge_last, 1), shifted(edge_first, -1))
    else:
        box = dec_grid.reshape(eta_cells, phi_cells, dec_width)
        down = [(i, i + 1) for i in range(eta_count - 1)]
        up = [(i + 1, i) for i in range(eta_count - 1)]
        top = lax.ppermute(box[eta_cells - rim :], "eta", down)
        bottom = lax.ppermute(box[:rim], "eta", up)
        box = jnp.concatenate([top, box, bottom], axis=0)
        low = turn(box[:, phi_cells - rim :], "phi", 1)
        high = turn(box[:, :rim], "phi", -1)

        def flat(value):
            return value.reshape(-1, dec_width)

        far = eta_cells + rim
        left, right = flat(low[rim:far]), flat(high[rim:far])
        rims = (
            flat(top), flat(low[:rim]), flat(high[:rim]),
            flat(bottom), flat(low[far:]), flat(high[far:]),
        )
    normed_cells = call(
        functools.partial(mix_folded if folded else mix_open, (eta_cells, phi_cells), span),
        "mix",
        sds((tile_len, dec_width), bf16),
        [smem()] + [vmem()] * (4 + len(rims)),
        scratch=[
            pltpu.VMEM((eta_cells + 2 * rim, phi_cells + 16, dec_width), f32),
            pltpu.VMEM((span * span, 8, dec_width), f32),
            pltpu.VMEM((tile_len, dec_width), f32),
        ],
        flops=400 * 2 * span * span * tile_len * dec_width,
        nbytes=3 * MIB,
    )(eta_place, dec_grid, left, right, *rims, conv_kernel.reshape(span * span, dec_width))
    reconstruction = call(
        functools.partial(feed_kernel, 256),
        "feed",
        sds((tile_len, w_head.shape[1]), f32),
        [vmem()] * 5,
        flops=2 * tile_len * dec_width * (2 * w_up.shape[1] + w_head.shape[1]),
        nbytes=4 * MIB,
    )(normed_cells, dec_grid, w_up, w_down, w_head).reshape(1, eta_cells, phi_cells, -1)
    return (grad_total, reconstruction)


def solution(mesh):
    in_specs = (
        P("replica", "eta", "phi", None),
        P("replica", "eta", "phi", None, None),
        P("replica", "eta", "phi", None),
        P("replica", "eta", "phi", None),
        P("replica", "eta", "phi", None, None),
        P(), P(), P(), P(), P(), P(), P(), P(), P(),
    )
    out_specs = (P(("eta", "phi"), None), P("replica", "eta", "phi", None))
    return jax.shard_map(body, mesh=mesh, in_specs=in_specs, out_specs=out_specs, check_vma=False)
```

```python
import functools

import jax
import jax.numpy as jnp
import numpy as np
from jax import lax
from jax.experimental import pallas as pl
from jax.experimental.pallas import tpu as pltpu
from jax.sharding import PartitionSpec as P

norm_eps = 1e-05
length_eps = 1e-06
f32 = jnp.float32
bf16 = jnp.bfloat16
MIB = 1024 * 1024

NN = (((1,), (0,)), ((), ()))
NT = (((1,), (1,)), ((), ()))
TN = (((0,), (0,)), ((), ()))


def mm(a, b, dims=NN):
    return lax.dot_general(a, b, dims, preferred_element_type=f32)


def vmem():
    return pl.BlockSpec(memory_space=pltpu.VMEM)


def smem():
    return pl.BlockSpec(memory_space=pltpu.SMEM)


def call(kernel, name, outs, in_specs, scratch=(), flops=0, nbytes=0, limit=20):
    single = not isinstance(outs, (list, tuple))
    out_list = [outs] if single else list(outs)
    specs = [vmem() for _ in out_list]
    return pl.pallas_call(
        kernel,
        out_shape=out_list[0] if single else tuple(out_list),
        in_specs=in_specs,
        out_specs=specs[0] if single else tuple(specs),
        scratch_shapes=list(scratch),
        compiler_params=pltpu.CompilerParams(vmem_limit_bytes=limit * MIB),
        cost_estimate=pl.CostEstimate(flops=flops, bytes_accessed=nbytes, transcendentals=0),
        name=name,
    )


def sds(shape, dtype):
    return jax.ShapeDtypeStruct(shape, dtype)


def column_of(row):
    return jnp.transpose(jnp.broadcast_to(row, (8, row.shape[1])))[:, 0:1]


def slot_column(pos_ref, wide_ref, padded):
    group, cap = pos_ref.shape
    wide_ref[...] = jnp.full(wide_ref.shape, -1.0, f32)
    wide_ref[:, 0:cap] = pos_ref[...].astype(f32)
    turned = jnp.transpose(wide_ref[...])
    return jnp.concatenate([turned[0:padded, d : d + 1] for d in range(group)], axis=0)


def pick_kernel(padded, pos_ref, tok_ref, out_ref, wide_ref):
    slots = slot_column(pos_ref, wide_ref, padded)
    cells = lax.broadcasted_iota(jnp.int32, (slots.shape[0], tok_ref.shape[0]), 1).astype(f32)
    chosen = (slots == cells).astype(f32).astype(bf16)
    out_ref[...] = mm(chosen, tok_ref[...]).astype(bf16)


def prep_kernel(split, cot_ref, wout_ref, wqkv_ref, ga_ref, wqkv_t_ref, *refs):
    ga_ref[...] = mm(wout_ref[...], cot_ref[...], NT).astype(bf16)
    emit(split, refs[-1], 0, jnp.transpose(cot_ref[...]))
    deal(split, refs[-1], refs[:-1])
    wqkv_t_ref[...] = jnp.transpose(wqkv_ref[...])


def project_kernel(
    cap, padded, src_ref, arr_ref, wqkv_t_ref, normed_ref, enc_ref, u_ref, len_ref, v_ref,
    place_ref,
):
    rows, width = normed_ref.shape
    heads = len_ref.shape[0] // 2
    size = width // heads
    slots = arr_ref.shape[0]
    src = src_ref[...].astype(f32)
    slot_row = src + (padded - cap) * jnp.floor((src + 0.5) * (1.0 / cap))
    place_ref[...] = slot_row
    slot_col = column_of(slot_row)
    lanes = lax.broadcasted_iota(jnp.int32, (rows, slots), 1).astype(f32)
    pick = (slot_col == lanes).astype(f32).astype(bf16)
    enc_in = mm(pick, arr_ref[...])
    enc_ref[...] = enc_in.astype(bf16)
    centred = enc_in - jnp.mean(enc_in, axis=-1, keepdims=True)
    spread = jnp.mean(centred * centred, axis=-1, keepdims=True)
    normed = (centred * lax.rsqrt(spread + norm_eps)).astype(bf16)
    normed_ref[...] = normed
    for t in range(2):
        raw = mm(wqkv_t_ref[t * width : (t + 1) * width], normed, NT)
        for h in range(heads):
            part = raw[h * size : (h + 1) * size]
            inv = lax.rsqrt(jnp.sum(part * part, axis=0, keepdims=True) + length_eps)
            at = t * width + h * size
            u_ref[at : at + size] = part * inv
            len_ref[t * heads + h : t * heads + h + 1] = inv
    v_ref[...] = mm(wqkv_t_ref[2 * width : 3 * width], normed, NT).astype(bf16)


def encode_kernel(
    split, win_ref, scale_ref, place_ref, enc_ref, u_ref, len_ref, v_ref, ga_ref, wout_ref,
    wdec_ref, out_ref, e_ref, *refs,
):
    left_refs = refs[:-3]
    p_ref, att_ref, left_ref = refs[-3:]
    rows, width = e_ref.shape
    heads = p_ref.shape[0]
    size = width // heads
    slots = out_ref.shape[0]
    win = win_ref[...].astype(f32)
    same = column_of(win) == win
    for h in range(heads):
        lo, hi = h * size, (h + 1) * size
        q = u_ref[lo:hi].astype(bf16)
        k = u_ref[width + lo : width + hi].astype(bf16)
        scores = mm(k, q, TN)
        raised = jnp.where(same, jnp.exp(scores * scale_ref[h]), 0.0)
        weights = (raised * (1.0 / jnp.sum(raised, axis=0, keepdims=True))).astype(bf16)
        p_ref[h] = weights
        att_ref[lo:hi] = mm(v_ref[lo:hi], weights).astype(bf16)
    attended = jnp.transpose(att_ref[...])
    e_ref[...] = attended
    enc_out = (enc_ref[...].astype(f32) + mm(attended, wout_ref[...])).astype(bf16)
    dec = mm(enc_out, wdec_ref[...]).astype(bf16)
    places = lax.broadcasted_iota(jnp.int32, (slots, rows), 0).astype(f32)
    put = (places == place_ref[...]).astype(f32).astype(bf16)
    out_ref[...] = mm(put, dec).astype(bf16)
    for h in range(heads):
        lo, hi = h * size, (h + 1) * size
        ga = ga_ref[lo:hi]
        low = p_ref[h]
        weights = low.astype(f32)
        grad_soft = mm(v_ref[lo:hi], ga, TN)
        part = weights * grad_soft
        total = jnp.sum(part, axis=0, keepdims=True)
        grad_scores = ((part - weights * total) * scale_ref[h]).astype(bf16)
        q = u_ref[lo:hi]
        k = u_ref[width + lo : width + hi]
        grad_v = mm(ga, low, NT)
        grad_q = mm(k.astype(bf16), grad_scores)
        grad_k = mm(q.astype(bf16), grad_scores, NT)
        grad_q = (grad_q - q * jnp.sum(q * grad_q, axis=0, keepdims=True)) * len_ref[h : h + 1]
        grad_k = (grad_k - k * jnp.sum(k * grad_k, axis=0, keepdims=True)) * len_ref[
            heads + h : heads + h + 1
        ]
        emit(split, left_ref, lo, grad_q.astype(bf16))
        emit(split, left_ref, width + lo, grad_k.astype(bf16))
        emit(split, left_ref, 2 * width + lo, grad_v.astype(bf16))
    deal(split, left_ref, left_refs)


def deal(split, left_ref, left_refs):
    if split is None:
        left_refs[0][...] = left_ref[...]
        return
    me = lax.axis_index("replica")
    for n, ref in enumerate(left_refs):
        ref[...] = left_ref[me ^ n]


def emit(split, out_ref, start, block):
    if split is None:
        out_ref[start : start + block.shape[0]] = block
        return
    unit = 32
    per_shard, per_part = split[0] // unit, split[1] // unit
    for j in range(block.shape[0] // unit):
        shard, rest = divmod(start // unit + j, per_shard)
        part, place = divmod(rest, per_part)
        out_ref[part, shard, place * unit : (place + 1) * unit] = block[
            j * unit : (j + 1) * unit
        ]


def term_kernel(columns, *refs):
    lefts, cots, normed, attended = refs[0:4], refs[4:8], refs[8:12], refs[12:16]
    keep_ref, send_ref = refs[16:]
    qkv, part, rows = lefts[0].shape
    shards = qkv + cots[0].shape[0]
    half = shards // 2
    cut = slice(*columns)
    width = columns[1] - columns[0]

    def block(left, lo, hi, right):
        acc = None
        for ref, e in zip(left, right):
            step = mm(ref[lo:hi].reshape((hi - lo) * part, rows), e[:, cut])
            acc = step if acc is None else acc + step
        return acc.reshape(hi - lo, part, width)

    first = [(0, block(lefts, 0, half, normed))]
    second = [
        (0, block(lefts, half, qkv, normed)),
        (qkv - half, block(cots, 0, shards - qkv, attended)),
    ]
    spans = (first, second)
    for mine in range(2):

        @pl.when(lax.axis_index("eta") == mine)
        def _():
            for at, value in spans[mine]:
                keep_ref[at : at + value.shape[0]] = value
            for at, value in spans[1 - mine]:
                send_ref[at : at + value.shape[0]] = value.astype(bf16)


def line_kernel(keep_ref, got_ref, own_ref, *send_refs):
    count = keep_ref.shape[0]
    me = lax.axis_index("phi")
    own_ref[...] = keep_ref[me] + got_ref[me].astype(f32)
    for k, ref in enumerate(send_refs):
        at = lax.rem(me + k + 1, count)
        ref[...] = (keep_ref[at] + got_ref[at].astype(f32)).astype(bf16)


def close_kernel(count, *refs):
    width = refs[0].shape[-1]
    for n in range((len(refs) - 1) // count):
        total = refs[n * count][...]
        for ref in refs[n * count + 1 : (n + 1) * count]:
            total = total + ref[...].astype(f32)
        refs[-1][:, n * width : (n + 1) * width] = total.astype(bf16)


def spread_kernel(own_ref, one_ref, two_ref, three_ref, out_ref):
    me = lax.axis_index("replica")
    for n, ref in enumerate((own_ref, one_ref, two_ref, three_ref)):
        out_ref[me ^ n] = ref[...].astype(f32)


def tie(values, *others):
    return lax.optimization_barrier((values, others))[0]


def fill_kernel(padded, pos_ref, ids_ref, mask_ref, got_ref, *refs):
    wide_ref = refs[-1]
    slots = slot_column(pos_ref, wide_ref, padded)
    ids = ids_ref[0:1] + lax.axis_index("eta").astype(f32) * ids_ref[1:2]
    chosen = (slots == ids).astype(f32).astype(bf16)
    got = got_ref[...]
    values = mm(chosen, got, TN)
    hits = mm(chosen, jnp.ones((got.shape[0], 128), bf16), TN)[:, 0:1]
    values = jnp.where(hits > 0.5, values, mask_ref[...].astype(f32)).astype(bf16)
    at = 0
    for ref in refs[:-1]:
        ref[...] = values[at : at + ref.shape[0]]
        at += ref.shape[0]


def conv_kernel_body(
    shape, span, folded, grid_ref, left_ref, right_ref, rims, taps_ref, out_ref,
    full_ref, wide_ref, mixed_ref,
):
    lines, columns = shape
    rim = span // 2
    width = grid_ref.shape[-1]
    lead = 8
    full_ref[rim : rim + lines, lead : lead + columns] = (
        grid_ref[...].astype(f32).reshape(lines, columns, width)
    )
    left = left_ref[...].astype(f32)
    right = right_ref[...].astype(f32)
    for x in range(lines):
        full_ref[rim + x, lead - rim : lead] = left[rim * x : rim * (x + 1)]
        full_ref[rim + x, lead + columns : lead + columns + rim] = right[rim * x : rim * (x + 1)]

    def put(base, edge_ref, first_ref, last_ref):
        edge = edge_ref[...].astype(f32)
        first = first_ref[...].astype(f32)
        last = last_ref[...].astype(f32)
        for i in range(rim):
            full_ref[base + i, lead : lead + columns] = edge[columns * i : columns * (i + 1)]
            full_ref[base + i, lead - rim : lead] = first[rim * i : rim * (i + 1)]
            full_ref[base + i, lead + columns : lead + columns + rim] = last[
                rim * i : rim * (i + 1)
            ]

    if folded:
        far = rim + lines
        base = jnp.where(lax.axis_index("eta") == 0, far, 0)
        for i in range(rim):
            full_ref[far - base + i] = jnp.zeros(full_ref.shape[1:], f32)
        put(base, *rims)
    else:
        put(0, *rims[:3])
        put(rim + lines, *rims[3:])
    for t in range(span * span):
        wide_ref[t] = jnp.broadcast_to(taps_ref[t // span, t % span : t % span + 1], (8, width))
    groups = columns // 8

    for c in range(width // 128):
        cut = slice(c * 128, (c + 1) * 128)

        def step(x, accs, live, cut=cut):
            accs = list(accs)
            for v in range(span):
                at = lead - rim + v
                line = full_ref[x, at : at + columns, cut].reshape(groups, 8, 128)
                for i in live:
                    tap = wide_ref[(span - 1 - i) * span + v, :, cut]
                    accs[i] = accs[i] + line * tap[None]
            return accs

        def store(row, acc, cut=cut):
            at = row * columns
            if not isinstance(row, int):
                at = pl.multiple_of(at, columns)
            mixed_ref[pl.ds(at, columns), cut] = acc.reshape(columns, 128)

        zero = jnp.zeros((groups, 8, 128), f32)
        accs = [zero] * span
        for x in range(span - 1):
            accs = step(x, accs, range(span - 1 - x, span))
            accs = accs[1:] + [zero]

        def middle(x, accs):
            accs = step(x, accs, range(span))
            store(x - (span - 1), accs[0])
            return tuple(accs[1:] + [zero])

        accs = list(lax.fori_loop(span - 1, lines, middle, tuple(accs)))
        for x in range(lines, lines + span - 1):
            accs = step(x, accs, range(0, lines + span - 1 - x))
            store(x - (span - 1), accs[0])
            accs = accs[1:] + [zero]

    mixed = mixed_ref[...]
    centred = mixed - jnp.mean(mixed, axis=-1, keepdims=True)
    spread = jnp.mean(centred * centred, axis=-1, keepdims=True)
    out_ref[...] = (centred * lax.rsqrt(spread + norm_eps)).astype(bf16)


def mix_folded(shape, span, grid, left, right, a, b, c, taps, out, full, wide, mixed):
    conv_kernel_body(
        shape, span, True, grid, left, right, (a, b, c), taps, out, full, wide, mixed
    )


def mix_open(
    shape, span, grid, left, right, a, b, c, d, e, g, taps, out, full, wide, mixed
):
    conv_kernel_body(
        shape, span, False, grid, left, right, (a, b, c, d, e, g), taps, out, full, wide,
        mixed,
    )


def feed_kernel(chunk, normed_ref, grid_ref, up_ref, down_ref, head_ref, out_ref):
    for at in range(0, normed_ref.shape[0], chunk):
        rows = slice(at, at + chunk)
        wide = mm(normed_ref[rows], up_ref[...])
        hidden = (0.5 * wide * (1.0 + lax.erf(wide * 0.7071067811865476))).astype(bf16)
        decoded = (grid_ref[rows].astype(f32) + mm(hidden, down_ref[...])).astype(bf16)
        out_ref[rows] = mm(decoded, head_ref[...])


def flip(value, axis, bit):
    return lax.ppermute(value, axis, [(i, i ^ bit) for i in range(lax.axis_size(axis))])


def turn(value, axis, k):
    count = lax.axis_size(axis)
    return lax.ppermute(value, axis, [(i, (i + k) % count) for i in range(count)])


def summed_slow(left, cot_t, normed, attended):
    term = jnp.concatenate([mm(left, normed), mm(cot_t, attended)], axis=0)
    share = lax.psum_scatter(term, ("eta", "phi", "replica"), scatter_dimension=0, tiled=True)
    return lax.all_gather(share.astype(bf16), "replica", axis=0, tiled=True).astype(f32)


def body(
    tokens, send_pos, enc_src, window_id, enc_cot, w_qkv, head_scale, w_out, w_dec_in,
    mask_token, conv_kernel, w_up, w_down, w_head,
):
    eta_cells, phi_cells, width = tokens.shape[1:]
    dec_width = w_dec_in.shape[1]
    tile_len = eta_cells * phi_cells
    eta_count = lax.axis_size("eta")
    phi_count = lax.axis_size("phi")
    replicas = lax.axis_size("replica")
    group = eta_count * phi_count
    cap = send_pos.shape[-1]
    padded = -(-cap // 8) * 8
    slots = group * padded
    rows = enc_cot.shape[-2]
    heads = head_scale.shape[0]
    out_rows = 4 * width
    shard_rows = out_rows // group
    part_rows = shard_rows // replicas
    fast = (
        eta_count == 2
        and replicas == 4
        and part_rows % 32 == 0
        and width % shard_rows == 0
        and 3 * width // shard_rows >= group // 2
    )

    positions = send_pos.reshape(group, cap)
    outgoing = call(
        functools.partial(pick_kernel, padded),
        "pick",
        sds((slots, width), bf16),
        [vmem(), vmem()],
        scratch=[pltpu.VMEM((group, 128), f32)],
        flops=2 * slots * tile_len * width,
        nbytes=3 * MIB,
        limit=8,
    )(positions, tokens.reshape(tile_len, width))
    arrived = lax.all_to_all(
        outgoing.reshape(group, padded, width), ("eta", "phi"), split_axis=0, concat_axis=0,
        tiled=True,
    ).reshape(slots, width)

    cotangent = enc_cot.reshape(rows, width)
    split = (shard_rows, part_rows) if fast else None
    pieces = replicas if fast else 1
    cot_part = (width // shard_rows, part_rows, rows) if fast else (width, rows)
    left_part = (3 * width // shard_rows, part_rows, rows) if fast else (3 * width, rows)
    cot_whole = (replicas,) + cot_part if fast else cot_part
    left_whole = (replicas,) + left_part if fast else left_part
    grad_att, w_qkv_t, *cots = call(
        functools.partial(prep_kernel, split),
        "prep",
        [sds((width, rows), bf16), sds((3 * width, width), bf16)]
        + [sds(cot_part, bf16)] * pieces,
        [vmem()] * 3,
        scratch=[pltpu.VMEM(cot_whole, bf16)],
        flops=2 * rows * width * width,
        nbytes=10 * MIB,
        limit=10,
    )(cotangent, w_out, w_qkv)
    if fast:
        cots = [cots[0]] + [flip(cots[k], "replica", k) for k in range(1, 4)]
        arrived = tie(arrived, cots)

    normed, enc_in, units, lengths, values, places = call(
        functools.partial(project_kernel, cap, padded),
        "project",
        [
            sds((rows, width), bf16),
            sds((rows, width), bf16),
            sds((2 * width, rows), f32),
            sds((2 * heads, rows), f32),
            sds((width, rows), bf16),
            sds((1, rows), f32),
        ],
        [vmem()] * 3,
        flops=2 * rows * width * width * 4,
        nbytes=8 * MIB,
        limit=10,
    )(enc_src.reshape(1, rows), arrived, w_qkv_t)
    if fast:
        normed_y = flip(normed, "replica", 2)

    outbound, attended, *lefts = call(
        functools.partial(encode_kernel, split),
        "encode",
        [sds((slots, dec_width), bf16), sds((rows, width), bf16)]
        + [sds(left_part, bf16)] * pieces,
        [vmem(), smem()] + [vmem()] * 8,
        scratch=[
            pltpu.VMEM((heads, rows, rows), bf16),
            pltpu.VMEM((width, rows), bf16),
            pltpu.VMEM(left_whole, bf16),
        ],
        flops=2 * rows * width * width * 10,
        nbytes=8 * MIB,
        limit=14,
    )(
        window_id.reshape(1, rows), head_scale, places, enc_in, units, lengths, values, grad_att,
        w_out, w_dec_in,
    )
    returned = lax.all_to_all(
        outbound.reshape(group, padded, dec_width), ("eta", "phi"), split_axis=0, concat_axis=0,
        tiled=True,
    )
    if fast:
        lefts = [lefts[0]] + [flip(lefts[k], "replica", k) for k in range(1, 4)]
        attended_y = flip(attended, "replica", 2)
        normed_y = tie(normed_y, attended)
        right = [normed, flip(normed, "replica", 1), normed_y, flip(normed_y, "replica", 1)]
        right += [
            attended, flip(attended, "replica", 1), attended_y, flip(attended_y, "replica", 1),
        ]
    else:
        grad_total = summed_slow(lefts[0], cots[0], normed, attended)

    span = conv_kernel.shape[0]
    rim = span // 2
    folded = eta_count == 2
    lines = np.arange(eta_cells)[:, None]
    columns = np.arange(phi_cells)[None, :]
    cell = lines * phi_cells + columns
    parts = [cell]
    moves = [0]
    if folded:
        edge = cell[eta_cells - rim :]
        parts += [cell[:, :rim], cell[:, -rim:], edge, edge[:, :rim], edge[:, -rim:]]
        moves += [0, 0] + [-(eta_cells - rim) * phi_cells] * 3
    sizes = [-(-p.size // 16) * 16 for p in parts]
    ids = np.full((2, -(-sum(sizes) // 128) * 128), -7.0, np.float32)
    ids[1] = 0
    at = 0
    for p, size, move in zip(parts, sizes, moves):
        ids[0, at : at + p.size] = p.reshape(-1)
        ids[1, at : at + p.size] = move
        at += size
    filled = call(
        functools.partial(fill_kernel, padded),
        "fill",
        [sds((size, dec_width), bf16) for size in sizes],
        [vmem()] * 4,
        scratch=[pltpu.VMEM((group, 128), f32)],
        flops=2 * slots * ids.shape[1] * (dec_width + 128),
        nbytes=3 * MIB,
        limit=12,
    )(
        positions, jnp.asarray(ids), mask_token.reshape(1, dec_width),
        returned.reshape(slots, dec_width),
    )
    dec_grid = filled[0]
    plane = ("eta", "phi")

    def shifted(value, by):
        pairs = [
            (e * phi_count + p, (1 - e) * phi_count + (p + by) % phi_count)
            for e in range(2)
            for p in range(phi_count)
        ]
        return lax.ppermute(value, plane, pairs)

    if folded:
        _, first, last, edge, edge_first, edge_last = filled
        left_halo = turn(last, "phi", 1)
        right_halo = turn(first, "phi", -1)
        rims = (shifted(edge, 0), shifted(edge_last, 1), shifted(edge_first, -1))
    else:
        box = dec_grid.reshape(eta_cells, phi_cells, dec_width)
        down = [(i, i + 1) for i in range(eta_count - 1)]
        up = [(i + 1, i) for i in range(eta_count - 1)]
        top = lax.ppermute(box[eta_cells - rim :], "eta", down)
        bottom = lax.ppermute(box[:rim], "eta", up)
        box = jnp.concatenate([top, box, bottom], axis=0)
        low = turn(box[:, phi_cells - rim :], "phi", 1)
        high = turn(box[:, :rim], "phi", -1)

        def flat(value):
            return value.reshape(-1, dec_width)

        far = eta_cells + rim
        left_halo, right_halo = flat(low[rim:far]), flat(high[rim:far])
        rims = (
            flat(top), flat(low[:rim]), flat(high[:rim]),
            flat(bottom), flat(low[far:]), flat(high[far:]),
        )
    if fast:
        lefts, cots, right = tie((lefts, cots, right), filled)
        chunk = width // 2
        half = group // 2
        kept, sent = [], []
        for c in range(2):
            keep, send = call(
                functools.partial(term_kernel, (c * chunk, (c + 1) * chunk)),
                "terms%d" % c,
                [sds((half, part_rows, chunk), f32), sds((half, part_rows, chunk), bf16)],
                [vmem()] * 16,
                flops=2 * out_rows * chunk * rows,
                nbytes=8 * MIB,
                limit=10,
            )(*lefts, *cots, *right)
            kept.append(keep)
            sent.append(turn(send, "eta", 1))
        left, right_halo, rims = tie((left_halo, right_halo, rims), kept)
    else:
        left = left_halo
    normed_cells = call(
        functools.partial(mix_folded if folded else mix_open, (eta_cells, phi_cells), span),
        "mix",
        sds((tile_len, dec_width), bf16),
        [vmem()] * (4 + len(rims)),
        scratch=[
            pltpu.VMEM((eta_cells + 2 * rim, phi_cells + 16, dec_width), f32),
            pltpu.VMEM((span * span, 8, dec_width), f32),
            pltpu.VMEM((tile_len, dec_width), f32),
        ],
        flops=200 * 2 * span * span * tile_len * dec_width,
        nbytes=3 * MIB,
        limit=16,
    )(dec_grid, left, right_halo, *rims, conv_kernel)
    if fast:
        summed = []
        for c in range(2):
            own, *outs = call(
                line_kernel,
                "line%d" % c,
                [sds((part_rows, chunk), f32)] + [sds((part_rows, chunk), bf16)] * (phi_count - 1),
                [vmem()] * 2,
                flops=half * part_rows * chunk,
                nbytes=2 * MIB,
                limit=4,
            )(kept[c], tie(sent[c], normed_cells))
            summed.append([own] + [turn(outs[k], "phi", k + 1) for k in range(phi_count - 1)])
            normed_cells = tie(normed_cells, own)
    reconstruction = call(
        functools.partial(feed_kernel, 256),
        "feed",
        sds((tile_len, w_head.shape[1]), f32),
        [vmem()] * 5,
        flops=2 * tile_len * dec_width * (2 * w_up.shape[1] + w_head.shape[1]),
        nbytes=4 * MIB,
        limit=12,
    )(normed_cells, dec_grid, w_up, w_down, w_head).reshape(1, eta_cells, phi_cells, -1)
    if fast:
        summed = tie(summed, reconstruction)
        mine = call(
            functools.partial(close_kernel, phi_count),
            "close",
            sds((part_rows, width), bf16),
            [vmem()] * (2 * phi_count),
            flops=4 * part_rows * width,
            nbytes=MIB,
            limit=4,
        )(*summed[0], *summed[1])
        mine_y = flip(mine, "replica", 2)
        grad_total = call(
            spread_kernel,
            "spread",
            sds((replicas, part_rows, width), f32),
            [vmem()] * 4,
            flops=4 * part_rows * width,
            nbytes=2 * MIB,
            limit=4,
        )(
            mine, flip(mine, "replica", 1), mine_y, flip(mine_y, "replica", 1),
        ).reshape(shard_rows, width)
    return (grad_total, reconstruction)


def solution(mesh):
    in_specs = (
        P("replica", "eta", "phi", None),
        P("replica", "eta", "phi", None, None),
        P("replica", "eta", "phi", None),
        P("replica", "eta", "phi", None),
        P("replica", "eta", "phi", None, None),
        P(), P(), P(), P(), P(), P(), P(), P(), P(),
    )
    out_specs = (P(("eta", "phi"), None), P("replica", "eta", "phi", None))
    return jax.shard_map(body, mesh=mesh, in_specs=in_specs, out_specs=out_specs, check_vma=False)
```

```python
import functools

import jax
import jax.numpy as jnp
import numpy as np
from jax import lax
from jax.experimental import pallas as pl
from jax.experimental.pallas import tpu as pltpu
from jax.sharding import PartitionSpec as P

norm_eps = 1e-05
length_eps = 1e-06
f32 = jnp.float32
bf16 = jnp.bfloat16
MIB = 1024 * 1024

NN = (((1,), (0,)), ((), ()))
NT = (((1,), (1,)), ((), ()))
TN = (((0,), (0,)), ((), ()))


def mm(a, b, dims=NN):
    return lax.dot_general(a, b, dims, preferred_element_type=f32)


def vmem():
    return pl.BlockSpec(memory_space=pltpu.VMEM)


def smem():
    return pl.BlockSpec(memory_space=pltpu.SMEM)


def call(kernel, name, outs, in_specs, scratch=(), flops=0, nbytes=0, limit=20):
    single = not isinstance(outs, (list, tuple))
    out_list = [outs] if single else list(outs)
    specs = [vmem() for _ in out_list]
    return pl.pallas_call(
        kernel,
        out_shape=out_list[0] if single else tuple(out_list),
        in_specs=in_specs,
        out_specs=specs[0] if single else tuple(specs),
        scratch_shapes=list(scratch),
        compiler_params=pltpu.CompilerParams(vmem_limit_bytes=limit * MIB),
        cost_estimate=pl.CostEstimate(flops=1000, bytes_accessed=1000, transcendentals=0),
        name=name,
    )


def sds(shape, dtype):
    return jax.ShapeDtypeStruct(shape, dtype)


def column_of(row):
    return jnp.transpose(jnp.broadcast_to(row, (8, row.shape[1])))[:, 0:1]


def slot_column(pos_ref, wide_ref, padded):
    group, cap = pos_ref.shape
    wide_ref[...] = jnp.full(wide_ref.shape, -1.0, f32)
    wide_ref[:, 0:cap] = pos_ref[...].astype(f32)
    turned = jnp.transpose(wide_ref[...])
    return jnp.concatenate([turned[0:padded, d : d + 1] for d in range(group)], axis=0)


def pick_kernel(padded, pos_ref, tok_ref, out_ref, wide_ref):
    slots = slot_column(pos_ref, wide_ref, padded)
    cells = lax.broadcasted_iota(jnp.int32, (slots.shape[0], tok_ref.shape[0]), 1).astype(f32)
    chosen = (slots == cells).astype(f32).astype(bf16)
    out_ref[...] = mm(chosen, tok_ref[...]).astype(bf16)


def prep_kernel(split, cot_ref, wout_ref, wqkv_ref, ga_ref, wqkv_t_ref, *refs):
    ga_ref[...] = mm(wout_ref[...], cot_ref[...], NT).astype(bf16)
    emit(split, refs[-1], 0, jnp.transpose(cot_ref[...]))
    deal(split, refs[-1], refs[:-1])
    wqkv_t_ref[...] = jnp.transpose(wqkv_ref[...])


def project_kernel(
    cap, padded, src_ref, arr_ref, wqkv_hbm, normed_ref, enc_ref, u_ref, len_ref, v_ref,
    place_ref, wqkv_t_ref, sems,
):
    rows, width = normed_ref.shape
    copies = []
    for t in range(3):
        cut = slice(t * width, (t + 1) * width)
        copies.append(
            pltpu.make_async_copy(wqkv_hbm.at[cut], wqkv_t_ref.at[cut], sems.at[t])
        )
        copies[-1].start()
    heads = len_ref.shape[0] // 2
    size = width // heads
    slots = arr_ref.shape[0]
    src = src_ref[...].astype(f32)
    slot_row = src + (padded - cap) * jnp.floor((src + 0.5) * (1.0 / cap))
    place_ref[...] = slot_row
    slot_col = column_of(slot_row)
    lanes = lax.broadcasted_iota(jnp.int32, (rows, slots), 1).astype(f32)
    pick = (slot_col == lanes).astype(f32).astype(bf16)
    enc_in = mm(pick, arr_ref[...])
    enc_ref[...] = enc_in.astype(bf16)
    centred = enc_in - jnp.mean(enc_in, axis=-1, keepdims=True)
    spread = jnp.mean(centred * centred, axis=-1, keepdims=True)
    normed = (centred * lax.rsqrt(spread + norm_eps)).astype(bf16)
    normed_ref[...] = normed
    for t in range(2):
        copies[t].wait()
        raw = mm(wqkv_t_ref[t * width : (t + 1) * width], normed, NT)
        for h in range(heads):
            part = raw[h * size : (h + 1) * size]
            inv = lax.rsqrt(jnp.sum(part * part, axis=0, keepdims=True) + length_eps)
            at = t * width + h * size
            u_ref[at : at + size] = part * inv
            len_ref[t * heads + h : t * heads + h + 1] = inv
    copies[2].wait()
    v_ref[...] = mm(wqkv_t_ref[2 * width : 3 * width], normed, NT).astype(bf16)


def encode_kernel(
    split, win_ref, scale_ref, place_ref, enc_ref, u_ref, len_ref, v_ref, ga_ref, wout_ref,
    wdec_ref, normed_ref, out_ref, *refs,
):
    peer_refs = refs[:-3]
    p_ref, att_ref, left_ref = refs[-3:]
    rows, width = enc_ref.shape
    heads = p_ref.shape[0]
    size = width // heads
    slots = out_ref.shape[0]
    win = win_ref[...].astype(f32)
    same = column_of(win) == win
    for h in range(heads):
        lo, hi = h * size, (h + 1) * size
        q = u_ref[lo:hi].astype(bf16)
        k = u_ref[width + lo : width + hi].astype(bf16)
        scores = mm(k, q, TN)
        raised = jnp.where(same, jnp.exp(scores * scale_ref[h]), 0.0)
        weights = (raised * (1.0 / jnp.sum(raised, axis=0, keepdims=True))).astype(bf16)
        p_ref[h] = weights
        att_ref[lo:hi] = mm(v_ref[lo:hi], weights).astype(bf16)
    attended = jnp.transpose(att_ref[...])
    enc_out = (enc_ref[...].astype(f32) + mm(attended, wout_ref[...])).astype(bf16)
    dec = mm(enc_out, wdec_ref[...]).astype(bf16)
    places = lax.broadcasted_iota(jnp.int32, (slots, rows), 0).astype(f32)
    put = (places == place_ref[...]).astype(f32).astype(bf16)
    out_ref[...] = mm(put, dec).astype(bf16)
    for h in range(heads):
        lo, hi = h * size, (h + 1) * size
        ga = ga_ref[lo:hi]
        low = p_ref[h]
        weights = low.astype(f32)
        grad_soft = mm(v_ref[lo:hi], ga, TN)
        part = weights * grad_soft
        total = jnp.sum(part, axis=0, keepdims=True)
        grad_scores = ((part - weights * total) * scale_ref[h]).astype(bf16)
        q = u_ref[lo:hi]
        k = u_ref[width + lo : width + hi]
        grad_v = mm(ga, low, NT)
        grad_q = mm(k.astype(bf16), grad_scores)
        grad_k = mm(q.astype(bf16), grad_scores, NT)
        grad_q = (grad_q - q * jnp.sum(q * grad_q, axis=0, keepdims=True)) * len_ref[h : h + 1]
        grad_k = (grad_k - k * jnp.sum(k * grad_k, axis=0, keepdims=True)) * len_ref[
            heads + h : heads + h + 1
        ]
        emit_wide(split, left_ref, lo, grad_q.astype(bf16))
        emit_wide(split, left_ref, width + lo, grad_k.astype(bf16))
        emit_wide(split, left_ref, 2 * width + lo, grad_v.astype(bf16))
    if split is None:
        peer_refs[0][...] = left_ref[...]
        peer_refs[1][...] = attended
        return
    me = lax.axis_index("replica")
    deep = left_ref.shape[1]
    for n, ref in enumerate(peer_refs):
        ref[0:deep] = left_ref[me ^ n]
        if n == 2:
            ref[deep : 2 * deep] = left_ref[me ^ 3]
            ref[2 * deep : 2 * deep + rows] = attended
        else:
            ref[deep : deep + rows] = attended
            ref[deep + rows : deep + 2 * rows] = normed_ref[...]


def emit_wide(split, out_ref, start, block):
    if split is None:
        out_ref[start : start + block.shape[0]] = block
        return
    unit = 32
    rows = block.shape[1]
    per_shard, per_part = split[0] // unit, split[1] // unit
    stack = out_ref.shape[1] // split[1]
    for j in range(block.shape[0] // unit):
        shard, rest = divmod(start // unit + j, per_shard)
        part, place = divmod(rest, per_part)
        at = (shard % stack) * split[1] + place * unit
        lane = (shard // stack) * rows
        out_ref[part, at : at + unit, lane : lane + rows] = block[j * unit : (j + 1) * unit]


def deal(split, left_ref, left_refs):
    if split is None:
        left_refs[0][...] = left_ref[...]
        return
    me = lax.axis_index("replica")
    for n, ref in enumerate(left_refs):
        ref[...] = left_ref[me ^ n]


def emit(split, out_ref, start, block):
    if split is None:
        out_ref[start : start + block.shape[0]] = block
        return
    unit = 32
    per_shard, per_part = split[0] // unit, split[1] // unit
    for j in range(block.shape[0] // unit):
        shard, rest = divmod(start // unit + j, per_shard)
        part, place = divmod(rest, per_part)
        at = shard * split[1] + place * unit
        out_ref[part, at : at + unit] = block[j * unit : (j + 1) * unit]


def term_kernel(columns, rows, *refs):
    own, near, far, hop, far_normed, hop_normed = refs[0:6]
    cots = refs[6:10]
    keep_ref, send_ref = refs[10:]
    half, part = keep_ref.shape[:2]
    held, count = cots[0].shape[0] // part, cots[0].shape[1]
    deep = own.shape[0] - 2 * rows
    stack = deep // part
    cut = slice(*columns)
    width = columns[1] - columns[0]
    att = slice(deep, deep + rows)
    nor = slice(deep + rows, deep + 2 * rows)
    far_att = slice(2 * deep, 2 * deep + rows)
    attended = [own[att, cut], near[att, cut], far[far_att, cut], hop[far_att, cut]]
    normed = [own[nor, cut], near[nor, cut], far_normed[:, cut], hop_normed[:, cut]]

    def left(ref, start, lo, hi):
        blocks = [
            ref[start : start + deep, j * count : (j + 1) * count]
            for j in range(lo // stack, hi // stack)
        ]
        return jnp.concatenate(blocks, axis=0) if len(blocks) > 1 else blocks[0]

    def block(lefts, right):
        acc = None
        for value, e in zip(lefts, right):
            step = mm(value, e)
            acc = step if acc is None else acc + step
        return acc.reshape(acc.shape[0] // part, part, width)

    peers = ((own, 0), (near, 0), (far, 0), (hop, deep))
    qkv = 2 * half - held
    first = [(0, block([left(ref, start, 0, half) for ref, start in peers], normed))]
    second = [
        (0, block([left(ref, start, half, qkv) for ref, start in peers], normed)),
        (qkv - half, block([ref[...] for ref in cots], attended)),
    ]
    spans = (first, second)
    for mine in range(2):

        @pl.when(lax.axis_index("eta") == mine)
        def _():
            for at, value in spans[mine]:
                keep_ref[at : at + value.shape[0]] = value
            for at, value in spans[1 - mine]:
                send_ref[at : at + value.shape[0]] = value.astype(bf16)


def line_kernel(keep_ref, got_ref, own_ref, *send_refs):
    count = keep_ref.shape[0]
    me = lax.axis_index("phi")
    own_ref[...] = keep_ref[me] + got_ref[me].astype(f32)
    for k, ref in enumerate(send_refs):
        at = lax.rem(me + k + 1, count)
        ref[...] = (keep_ref[at] + got_ref[at].astype(f32)).astype(bf16)


def close_kernel(count, *refs):
    width = refs[0].shape[-1]
    for n in range((len(refs) - 1) // count):
        total = refs[n * count][...]
        for ref in refs[n * count + 1 : (n + 1) * count]:
            total = total + ref[...].astype(f32)
        refs[-1][:, n * width : (n + 1) * width] = total.astype(bf16)


def spread_kernel(own_ref, one_ref, two_ref, three_ref, out_ref):
    me = lax.axis_index("replica")
    for n, ref in enumerate((own_ref, one_ref, two_ref, three_ref)):
        out_ref[me ^ n] = ref[...].astype(f32)


def tie(values, *others):
    return lax.optimization_barrier((values, others))[0]


def fill_kernel(padded, pos_ref, ids_ref, mask_ref, got_ref, *refs):
    wide_ref = refs[-1]
    slots = slot_column(pos_ref, wide_ref, padded)
    ids = ids_ref[0:1] + lax.axis_index("eta").astype(f32) * ids_ref[1:2]
    chosen = (slots == ids).astype(f32).astype(bf16)
    got = got_ref[...]
    values = mm(chosen, got, TN)
    hits = mm(chosen, jnp.ones((got.shape[0], 128), bf16), TN)[:, 0:1]
    values = jnp.where(hits > 0.5, values, mask_ref[...].astype(f32)).astype(bf16)
    at = 0
    for ref in refs[:-1]:
        ref[...] = values[at : at + ref.shape[0]]
        at += ref.shape[0]


def conv_kernel_body(
    shape, span, folded, grid_ref, left_ref, right_ref, rims, taps_ref, out_ref,
    full_ref, wide_ref, mixed_ref,
):
    lines, columns = shape
    rim = span // 2
    width = grid_ref.shape[-1]
    lead = 8
    full_ref[rim : rim + lines, lead : lead + columns] = (
        grid_ref[...].astype(f32).reshape(lines, columns, width)
    )
    left = left_ref[...].astype(f32)
    right = right_ref[...].astype(f32)
    for x in range(lines):
        full_ref[rim + x, lead - rim : lead] = left[rim * x : rim * (x + 1)]
        full_ref[rim + x, lead + columns : lead + columns + rim] = right[rim * x : rim * (x + 1)]

    def put(base, edge_ref, first_ref, last_ref):
        edge = edge_ref[...].astype(f32)
        first = first_ref[...].astype(f32)
        last = last_ref[...].astype(f32)
        for i in range(rim):
            full_ref[base + i, lead : lead + columns] = edge[columns * i : columns * (i + 1)]
            full_ref[base + i, lead - rim : lead] = first[rim * i : rim * (i + 1)]
            full_ref[base + i, lead + columns : lead + columns + rim] = last[
                rim * i : rim * (i + 1)
            ]

    if folded:
        far = rim + lines
        base = jnp.where(lax.axis_index("eta") == 0, far, 0)
        for i in range(rim):
            full_ref[far - base + i] = jnp.zeros(full_ref.shape[1:], f32)
        put(base, *rims)
    else:
        put(0, *rims[:3])
        put(rim + lines, *rims[3:])
    for t in range(span * span):
        wide_ref[t] = jnp.broadcast_to(taps_ref[t // span, t % span : t % span + 1], (8, width))
    groups = columns // 8

    for c in range(width // 128):
        cut = slice(c * 128, (c + 1) * 128)

        def step(x, accs, live, cut=cut):
            accs = list(accs)
            for v in range(span):
                at = lead - rim + v
                line = full_ref[x, at : at + columns, cut].reshape(groups, 8, 128)
                for i in live:
                    tap = wide_ref[(span - 1 - i) * span + v, :, cut]
                    accs[i] = accs[i] + line * tap[None]
            return accs

        def store(row, acc, cut=cut):
            at = row * columns
            if not isinstance(row, int):
                at = pl.multiple_of(at, columns)
            mixed_ref[pl.ds(at, columns), cut] = acc.reshape(columns, 128)

        zero = jnp.zeros((groups, 8, 128), f32)
        accs = [zero] * span
        for x in range(span - 1):
            accs = step(x, accs, range(span - 1 - x, span))
            accs = accs[1:] + [zero]

        def middle(x, accs):
            accs = step(x, accs, range(span))
            store(x - (span - 1), accs[0])
            return tuple(accs[1:] + [zero])

        accs = list(lax.fori_loop(span - 1, lines, middle, tuple(accs)))
        for x in range(lines, lines + span - 1):
            accs = step(x, accs, range(0, lines + span - 1 - x))
            store(x - (span - 1), accs[0])
            accs = accs[1:] + [zero]

    mixed = mixed_ref[...]
    centred = mixed - jnp.mean(mixed, axis=-1, keepdims=True)
    spread = jnp.mean(centred * centred, axis=-1, keepdims=True)
    out_ref[...] = (centred * lax.rsqrt(spread + norm_eps)).astype(bf16)


def mix_folded(shape, span, grid, left, right, a, b, c, taps, out, full, wide, mixed):
    conv_kernel_body(
        shape, span, True, grid, left, right, (a, b, c), taps, out, full, wide, mixed
    )


def mix_open(
    shape, span, grid, left, right, a, b, c, d, e, g, taps, out, full, wide, mixed
):
    conv_kernel_body(
        shape, span, False, grid, left, right, (a, b, c, d, e, g), taps, out, full, wide,
        mixed,
    )


def feed_kernel(chunk, normed_ref, grid_ref, up_ref, down_ref, head_ref, out_ref):
    for at in range(0, normed_ref.shape[0], chunk):
        rows = slice(at, at + chunk)
        wide = mm(normed_ref[rows], up_ref[...])
        hidden = (0.5 * wide * (1.0 + lax.erf(wide * 0.7071067811865476))).astype(bf16)
        decoded = (grid_ref[rows].astype(f32) + mm(hidden, down_ref[...])).astype(bf16)
        out_ref[rows] = mm(decoded, head_ref[...])


def flip(value, axis, bit):
    return lax.ppermute(value, axis, [(i, i ^ bit) for i in range(lax.axis_size(axis))])


def turn(value, axis, k):
    count = lax.axis_size(axis)
    return lax.ppermute(value, axis, [(i, (i + k) % count) for i in range(count)])


def summed_slow(left, cot_t, normed, attended):
    term = jnp.concatenate([mm(left, normed), mm(cot_t, attended)], axis=0)
    share = lax.psum_scatter(term, ("eta", "phi", "replica"), scatter_dimension=0, tiled=True)
    return lax.all_gather(share.astype(bf16), "replica", axis=0, tiled=True).astype(f32)


def body(
    tokens, send_pos, enc_src, window_id, enc_cot, w_qkv, head_scale, w_out, w_dec_in,
    mask_token, conv_kernel, w_up, w_down, w_head,
):
    eta_cells, phi_cells, width = tokens.shape[1:]
    dec_width = w_dec_in.shape[1]
    tile_len = eta_cells * phi_cells
    eta_count = lax.axis_size("eta")
    phi_count = lax.axis_size("phi")
    replicas = lax.axis_size("replica")
    group = eta_count * phi_count
    cap = send_pos.shape[-1]
    padded = -(-cap // 8) * 8
    slots = group * padded
    rows = enc_cot.shape[-2]
    heads = head_scale.shape[0]
    out_rows = 4 * width
    shard_rows = out_rows // group
    part_rows = shard_rows // replicas
    fast = (
        eta_count == 2
        and replicas == 4
        and part_rows % 32 == 0
        and width % shard_rows == 0
        and 3 * width // shard_rows >= group // 2
    )

    positions = send_pos.reshape(group, cap)
    outgoing = call(
        functools.partial(pick_kernel, padded),
        "pick",
        sds((slots, width), bf16),
        [vmem(), vmem()],
        scratch=[pltpu.VMEM((group, 128), f32)],
        flops=2 * slots * tile_len * width,
        nbytes=3 * MIB,
        limit=8,
    )(positions, tokens.reshape(tile_len, width))
    arrived = lax.all_to_all(
        outgoing.reshape(group, padded, width), ("eta", "phi"), split_axis=0, concat_axis=0,
        tiled=True,
    ).reshape(slots, width)

    cotangent = enc_cot.reshape(rows, width)
    split = (shard_rows, part_rows) if fast else None
    pieces = replicas if fast else 1
    cot_part = (width * part_rows // shard_rows, rows) if fast else (width, rows)
    deep = 3 * width * part_rows // shard_rows * rows // width if fast else 3 * width
    cot_whole = (replicas,) + cot_part if fast else cot_part
    left_whole = (replicas, deep, width) if fast else (3 * width, rows)
    if fast:
        peer_shapes = [(deep + 2 * rows, width)] * 2 + [(2 * deep + rows, width)]
    else:
        peer_shapes = [(3 * width, rows), (rows, width)]
    grad_att, w_qkv_t, *cots = call(
        functools.partial(prep_kernel, split),
        "prep",
        [sds((width, rows), bf16), sds((3 * width, width), bf16)]
        + [sds(cot_part, bf16)] * pieces,
        [vmem()] * 3,
        scratch=[pltpu.VMEM(cot_whole, bf16)],
        flops=2 * rows * width * width,
        nbytes=10 * MIB,
        limit=10,
    )(cotangent, w_out, w_qkv)
    if fast:
        cots = [cots[0]] + [flip(cots[k], "replica", k) for k in range(1, 4)]

    normed, enc_in, units, lengths, values, places = call(
        functools.partial(project_kernel, cap, padded),
        "project",
        [
            sds((rows, width), bf16),
            sds((rows, width), bf16),
            sds((2 * width, rows), f32),
            sds((2 * heads, rows), f32),
            sds((width, rows), bf16),
            sds((1, rows), f32),
        ],
        [vmem(), vmem(), pl.BlockSpec(memory_space=pltpu.HBM)],
        scratch=[pltpu.VMEM((3 * width, width), bf16), pltpu.SemaphoreType.DMA((3,))],
        flops=2 * rows * width * width * 4,
        nbytes=8 * MIB,
        limit=14,
    )(enc_src.reshape(1, rows), arrived, w_qkv_t)
    if fast:
        normed_y = flip(normed, "replica", 2)
        lengths = tie(lengths, cots)

    outbound, *peers = call(
        functools.partial(encode_kernel, split),
        "encode",
        [sds((slots, dec_width), bf16)] + [sds(shape, bf16) for shape in peer_shapes],
        [vmem(), smem()] + [vmem()] * 9,
        scratch=[
            pltpu.VMEM((heads, rows, rows), bf16),
            pltpu.VMEM((width, rows), bf16),
            pltpu.VMEM(left_whole, bf16),
        ],
        flops=2 * rows * width * width * 10,
        nbytes=8 * MIB,
        limit=14,
    )(
        window_id.reshape(1, rows), head_scale, places, enc_in, units, lengths, values, grad_att,
        w_out, w_dec_in, normed,
    )
    returned = lax.all_to_all(
        outbound.reshape(group, padded, dec_width), ("eta", "phi"), split_axis=0, concat_axis=0,
        tiled=True,
    )
    if fast:
        own, near, far = peers[0], flip(peers[1], "replica", 1), flip(peers[2], "replica", 2)
        normed_y = tie(normed_y, outbound)
        normed_hop = flip(normed_y, "replica", 1)
        returned = tie(returned, near, normed_hop)
    else:
        grad_total = summed_slow(peers[0], cots[0], normed, peers[1])

    span = conv_kernel.shape[0]
    rim = span // 2
    folded = eta_count == 2
    lines = np.arange(eta_cells)[:, None]
    columns = np.arange(phi_cells)[None, :]
    cell = lines * phi_cells + columns
    parts = [cell]
    moves = [0]
    if folded:
        edge = cell[eta_cells - rim :]
        parts += [cell[:, :rim], cell[:, -rim:], edge, edge[:, :rim], edge[:, -rim:]]
        moves += [0, 0] + [-(eta_cells - rim) * phi_cells] * 3
    sizes = [-(-p.size // 16) * 16 for p in parts]
    ids = np.full((2, -(-sum(sizes) // 128) * 128), -7.0, np.float32)
    ids[1] = 0
    at = 0
    for p, size, move in zip(parts, sizes, moves):
        ids[0, at : at + p.size] = p.reshape(-1)
        ids[1, at : at + p.size] = move
        at += size
    filled = call(
        functools.partial(fill_kernel, padded),
        "fill",
        [sds((size, dec_width), bf16) for size in sizes],
        [vmem()] * 4,
        scratch=[pltpu.VMEM((group, 128), f32)],
        flops=2 * slots * ids.shape[1] * (dec_width + 128),
        nbytes=3 * MIB,
        limit=12,
    )(
        positions, jnp.asarray(ids), mask_token.reshape(1, dec_width),
        returned.reshape(slots, dec_width),
    )
    dec_grid = filled[0]
    plane = ("eta", "phi")

    def shifted(value, by):
        pairs = [
            (e * phi_count + p, (1 - e) * phi_count + (p + by) % phi_count)
            for e in range(2)
            for p in range(phi_count)
        ]
        return lax.ppermute(value, plane, pairs)

    if folded:
        _, first, last, edge, edge_first, edge_last = filled
        left_halo = turn(last, "phi", 1)
        right_halo = turn(first, "phi", -1)
        rims = (shifted(edge, 0), shifted(edge_last, 1), shifted(edge_first, -1))
    else:
        box = dec_grid.reshape(eta_cells, phi_cells, dec_width)
        down = [(i, i + 1) for i in range(eta_count - 1)]
        up = [(i + 1, i) for i in range(eta_count - 1)]
        top = lax.ppermute(box[eta_cells - rim :], "eta", down)
        bottom = lax.ppermute(box[:rim], "eta", up)
        box = jnp.concatenate([top, box, bottom], axis=0)
        low = turn(box[:, phi_cells - rim :], "phi", 1)
        high = turn(box[:, :rim], "phi", -1)

        def flat(value):
            return value.reshape(-1, dec_width)

        far = eta_cells + rim
        left_halo, right_halo = flat(low[rim:far]), flat(high[rim:far])
        rims = (
            flat(top), flat(low[:rim]), flat(high[:rim]),
            flat(bottom), flat(low[far:]), flat(high[far:]),
        )
    if fast:
        far = tie(far, left_halo, right_halo, rims[0])
        peers = [own, near, far, flip(far, "replica", 1), normed_y, normed_hop]
        peers, cots = tie((peers, cots), left_halo, right_halo, rims)
        chunk = width // 2
        half = group // 2
        kept, sent = [], []
        for c in range(2):
            keep, send = call(
                functools.partial(term_kernel, (c * chunk, (c + 1) * chunk), rows),
                "terms%d" % c,
                [sds((half, part_rows, chunk), f32), sds((half, part_rows, chunk), bf16)],
                [vmem()] * 10,
                flops=2 * out_rows * chunk * rows,
                nbytes=8 * MIB,
                limit=10,
            )(*peers, *cots)
            kept.append(keep)
            sent.append(turn(send, "eta", 1))
        left, right_halo, rims = tie((left_halo, right_halo, rims), kept)
    else:
        left = left_halo
    normed_cells = call(
        functools.partial(mix_folded if folded else mix_open, (eta_cells, phi_cells), span),
        "mix",
        sds((tile_len, dec_width), bf16),
        [vmem()] * (4 + len(rims)),
        scratch=[
            pltpu.VMEM((eta_cells + 2 * rim, phi_cells + 16, dec_width), f32),
            pltpu.VMEM((span * span, 8, dec_width), f32),
            pltpu.VMEM((tile_len, dec_width), f32),
        ],
        flops=200 * 2 * span * span * tile_len * dec_width,
        nbytes=3 * MIB,
        limit=16,
    )(dec_grid, left, right_halo, *rims, conv_kernel)
    if fast:
        summed = []
        for c in range(2):
            own, *outs = call(
                line_kernel,
                "line%d" % c,
                [sds((part_rows, chunk), f32)] + [sds((part_rows, chunk), bf16)] * (phi_count - 1),
                [vmem()] * 2,
                flops=half * part_rows * chunk,
                nbytes=2 * MIB,
                limit=4,
            )(kept[c], tie(sent[c], normed_cells))
            summed.append([own] + [turn(outs[k], "phi", k + 1) for k in range(phi_count - 1)])
            normed_cells = tie(normed_cells, own)
    reconstruction = call(
        functools.partial(feed_kernel, 256),
        "feed",
        sds((tile_len, w_head.shape[1]), f32),
        [vmem()] * 5,
        flops=2 * tile_len * dec_width * (2 * w_up.shape[1] + w_head.shape[1]),
        nbytes=4 * MIB,
        limit=12,
    )(normed_cells, dec_grid, w_up, w_down, w_head).reshape(1, eta_cells, phi_cells, -1)
    if fast:
        summed = tie(summed, reconstruction)
        mine = call(
            functools.partial(close_kernel, phi_count),
            "close",
            sds((part_rows, width), bf16),
            [vmem()] * (2 * phi_count),
            flops=4 * part_rows * width,
            nbytes=MIB,
            limit=4,
        )(*summed[0], *summed[1])
        mine_y = flip(mine, "replica", 2)
        grad_total = call(
            spread_kernel,
            "spread",
            sds((replicas, part_rows, width), f32),
            [vmem()] * 4,
            flops=4 * part_rows * width,
            nbytes=2 * MIB,
            limit=4,
        )(
            mine, flip(mine, "replica", 1), mine_y, flip(mine_y, "replica", 1),
        ).reshape(shard_rows, width)
    return (grad_total, reconstruction)


def solution(mesh):
    in_specs = (
        P("replica", "eta", "phi", None),
        P("replica", "eta", "phi", None, None),
        P("replica", "eta", "phi", None),
        P("replica", "eta", "phi", None),
        P("replica", "eta", "phi", None, None),
        P(), P(), P(), P(), P(), P(), P(), P(), P(),
    )
    out_specs = (P(("eta", "phi"), None), P("replica", "eta", "phi", None))
    return jax.shard_map(body, mesh=mesh, in_specs=in_specs, out_specs=out_specs, check_vma=False)
```

```python
import functools

import jax
import jax.numpy as jnp
import numpy as np
from jax import lax
from jax.experimental import pallas as pl
from jax.experimental.pallas import tpu as pltpu
from jax.sharding import PartitionSpec as P

norm_eps = 1e-05
length_eps = 1e-06
f32 = jnp.float32
bf16 = jnp.bfloat16
MIB = 1024 * 1024

NN = (((1,), (0,)), ((), ()))
NT = (((1,), (1,)), ((), ()))
TN = (((0,), (0,)), ((), ()))


def mm(a, b, dims=NN):
    return lax.dot_general(a, b, dims, preferred_element_type=f32)


def vmem():
    return pl.BlockSpec(memory_space=pltpu.VMEM)


def smem():
    return pl.BlockSpec(memory_space=pltpu.SMEM)


def call(kernel, name, outs, in_specs, scratch=(), flops=0, nbytes=0, limit=20, cost=1000):
    single = not isinstance(outs, (list, tuple))
    out_list = [outs] if single else list(outs)
    specs = [vmem() for _ in out_list]
    return pl.pallas_call(
        kernel,
        out_shape=out_list[0] if single else tuple(out_list),
        in_specs=in_specs,
        out_specs=specs[0] if single else tuple(specs),
        scratch_shapes=list(scratch),
        compiler_params=pltpu.CompilerParams(vmem_limit_bytes=limit * MIB),
        cost_estimate=pl.CostEstimate(
            flops=cost, bytes_accessed=1000 + cost // 300, transcendentals=0
        ),
        name=name,
    )


def sds(shape, dtype):
    return jax.ShapeDtypeStruct(shape, dtype)


def column_of(row):
    return jnp.transpose(jnp.broadcast_to(row, (8, row.shape[1])))[:, 0:1]


def slot_column(pos_ref, wide_ref, padded):
    group, cap = pos_ref.shape
    wide_ref[...] = jnp.full(wide_ref.shape, -1.0, f32)
    wide_ref[:, 0:cap] = pos_ref[...].astype(f32)
    turned = jnp.transpose(wide_ref[...])
    return jnp.concatenate([turned[0:padded, d : d + 1] for d in range(group)], axis=0)


def pick_kernel(padded, pos_ref, tok_ref, out_ref, wide_ref):
    slots = slot_column(pos_ref, wide_ref, padded)
    cells = lax.broadcasted_iota(jnp.int32, (slots.shape[0], tok_ref.shape[0]), 1).astype(f32)
    chosen = (slots == cells).astype(f32).astype(bf16)
    out_ref[...] = mm(chosen, tok_ref[...]).astype(bf16)


def prep_kernel(split, cot_ref, wout_ref, wqkv_ref, ga_ref, wqkv_t_ref, *refs):
    ga_ref[...] = mm(wout_ref[...], cot_ref[...], NT).astype(bf16)
    emit(split, refs[-1], 0, jnp.transpose(cot_ref[...]))
    deal(split, refs[-1], refs[:-1])
    wqkv_t_ref[...] = jnp.transpose(wqkv_ref[...])


def project_kernel(
    cap, padded, src_ref, arr_ref, wqkv_t_ref, normed_ref, enc_ref, u_ref, len_ref, v_ref,
    place_ref,
):
    rows, width = normed_ref.shape
    heads = len_ref.shape[0] // 2
    size = width // heads
    slots = arr_ref.shape[0]
    src = src_ref[...].astype(f32)
    slot_row = src + (padded - cap) * jnp.floor((src + 0.5) * (1.0 / cap))
    place_ref[...] = slot_row
    slot_col = column_of(slot_row)
    lanes = lax.broadcasted_iota(jnp.int32, (rows, slots), 1).astype(f32)
    pick = (slot_col == lanes).astype(f32).astype(bf16)
    enc_in = mm(pick, arr_ref[...])
    enc_ref[...] = enc_in.astype(bf16)
    centred = enc_in - jnp.mean(enc_in, axis=-1, keepdims=True)
    spread = jnp.mean(centred * centred, axis=-1, keepdims=True)
    normed = (centred * lax.rsqrt(spread + norm_eps)).astype(bf16)
    normed_ref[...] = normed
    for t in range(2):
        raw = mm(wqkv_t_ref[t * width : (t + 1) * width], normed, NT)
        for h in range(heads):
            part = raw[h * size : (h + 1) * size]
            inv = lax.rsqrt(jnp.sum(part * part, axis=0, keepdims=True) + length_eps)
            at = t * width + h * size
            u_ref[at : at + size] = part * inv
            len_ref[t * heads + h : t * heads + h + 1] = inv
    v_ref[...] = mm(wqkv_t_ref[2 * width : 3 * width], normed, NT).astype(bf16)


def encode_kernel(
    split, win_ref, scale_ref, place_ref, enc_ref, u_ref, len_ref, v_ref, ga_ref, wout_ref,
    wdec_ref, normed_ref, *refs,
):
    cots, refs = (refs[:4], refs[4:]) if split is not None else ((), refs)
    out_ref, peer_refs = refs[0], refs[1:-3]
    p_ref, att_ref, left_ref = refs[-3:]
    rows, width = enc_ref.shape
    heads = p_ref.shape[0]
    size = width // heads
    slots = out_ref.shape[0]
    win = win_ref[...].astype(f32)
    same = column_of(win) == win
    for h in range(heads):
        lo, hi = h * size, (h + 1) * size
        q = u_ref[lo:hi].astype(bf16)
        k = u_ref[width + lo : width + hi].astype(bf16)
        scores = mm(k, q, TN)
        raised = jnp.where(same, jnp.exp(scores * scale_ref[h]), 0.0)
        weights = (raised * (1.0 / jnp.sum(raised, axis=0, keepdims=True))).astype(bf16)
        p_ref[h] = weights
        att_ref[lo:hi] = mm(v_ref[lo:hi], weights).astype(bf16)
    attended = jnp.transpose(att_ref[...])
    enc_out = (enc_ref[...].astype(f32) + mm(attended, wout_ref[...])).astype(bf16)
    dec = mm(enc_out, wdec_ref[...]).astype(bf16)
    places = lax.broadcasted_iota(jnp.int32, (slots, rows), 0).astype(f32)
    put = (places == place_ref[...]).astype(f32).astype(bf16)
    out_ref[...] = mm(put, dec).astype(bf16)
    for h in range(heads):
        lo, hi = h * size, (h + 1) * size
        ga = ga_ref[lo:hi]
        low = p_ref[h]
        weights = low.astype(f32)
        grad_soft = mm(v_ref[lo:hi], ga, TN)
        part = weights * grad_soft
        total = jnp.sum(part, axis=0, keepdims=True)
        grad_scores = ((part - weights * total) * scale_ref[h]).astype(bf16)
        q = u_ref[lo:hi]
        k = u_ref[width + lo : width + hi]
        grad_v = mm(ga, low, NT)
        grad_q = mm(k.astype(bf16), grad_scores)
        grad_k = mm(q.astype(bf16), grad_scores, NT)
        grad_q = (grad_q - q * jnp.sum(q * grad_q, axis=0, keepdims=True)) * len_ref[h : h + 1]
        grad_k = (grad_k - k * jnp.sum(k * grad_k, axis=0, keepdims=True)) * len_ref[
            heads + h : heads + h + 1
        ]
        emit_wide(split, left_ref, lo, grad_q.astype(bf16))
        emit_wide(split, left_ref, width + lo, grad_k.astype(bf16))
        emit_wide(split, left_ref, 2 * width + lo, grad_v.astype(bf16))
    if split is None:
        peer_refs[0][...] = left_ref[...]
        peer_refs[1][...] = attended
        return
    me = lax.axis_index("replica")
    deep = left_ref.shape[1]
    for n, ref in enumerate(peer_refs):
        ref[0:deep] = left_ref[me ^ n]
        if n == 2:
            ref[deep : 2 * deep] = left_ref[me ^ 3]
            ref[2 * deep : 2 * deep + rows] = attended
        else:
            ref[deep : deep + rows] = attended
            ref[deep + rows : deep + 2 * rows] = normed_ref[...]
    at = deep + 2 * rows
    high = cots[0].shape[0]
    for n, ref in enumerate(cots):
        down, lane = divmod(n, width // rows)
        top = at + down * high
        peer_refs[0][top : top + high, lane * rows : (lane + 1) * rows] = ref[...]


def emit_wide(split, out_ref, start, block):
    if split is None:
        out_ref[start : start + block.shape[0]] = block
        return
    unit = 32
    rows = block.shape[1]
    per_shard, per_part = split[0] // unit, split[1] // unit
    stack = out_ref.shape[1] // split[1]
    for j in range(block.shape[0] // unit):
        shard, rest = divmod(start // unit + j, per_shard)
        part, place = divmod(rest, per_part)
        at = (shard % stack) * split[1] + place * unit
        lane = (shard // stack) * rows
        out_ref[part, at : at + unit, lane : lane + rows] = block[j * unit : (j + 1) * unit]


def deal(split, left_ref, left_refs):
    if split is None:
        left_refs[0][...] = left_ref[...]
        return
    me = lax.axis_index("replica")
    for n, ref in enumerate(left_refs):
        ref[...] = left_ref[me ^ n]


def emit(split, out_ref, start, block):
    if split is None:
        out_ref[start : start + block.shape[0]] = block
        return
    unit = 32
    per_shard, per_part = split[0] // unit, split[1] // unit
    for j in range(block.shape[0] // unit):
        shard, rest = divmod(start // unit + j, per_shard)
        part, place = divmod(rest, per_part)
        at = shard * split[1] + place * unit
        out_ref[part, at : at + unit] = block[j * unit : (j + 1) * unit]


def term_kernel(columns, rows, *refs):
    own, near, far, hop, far_normed, hop_normed = refs[0:6]
    keep_ref, send_ref = refs[6:]
    half, part = keep_ref.shape[:2]
    count = rows
    deep = near.shape[0] - 2 * rows
    across = own.shape[1] // count
    high = (own.shape[0] - near.shape[0]) // -(-4 // across)
    held = high // part
    cots = []
    for n in range(4):
        down, lane = divmod(n, across)
        top = near.shape[0] + down * high
        cots.append(own[top : top + high, lane * count : (lane + 1) * count])
    stack = deep // part
    cut = slice(*columns)
    width = columns[1] - columns[0]
    att = slice(deep, deep + rows)
    nor = slice(deep + rows, deep + 2 * rows)
    far_att = slice(2 * deep, 2 * deep + rows)
    attended = [own[att, cut], near[att, cut], far[far_att, cut], hop[far_att, cut]]
    normed = [own[nor, cut], near[nor, cut], far_normed[:, cut], hop_normed[:, cut]]

    def left(ref, start, lo, hi):
        blocks = [
            ref[start : start + deep, j * count : (j + 1) * count]
            for j in range(lo // stack, hi // stack)
        ]
        return jnp.concatenate(blocks, axis=0) if len(blocks) > 1 else blocks[0]

    def block(lefts, right):
        acc = None
        for value, e in zip(lefts, right):
            step = mm(value, e)
            acc = step if acc is None else acc + step
        return acc.reshape(acc.shape[0] // part, part, width)

    peers = ((own, 0), (near, 0), (far, 0), (hop, deep))
    qkv = 2 * half - held
    first = [(0, block([left(ref, start, 0, half) for ref, start in peers], normed))]
    second = [
        (0, block([left(ref, start, half, qkv) for ref, start in peers], normed)),
        (qkv - half, block(cots, attended)),
    ]
    spans = (first, second)
    for mine in range(2):

        @pl.when(lax.axis_index("eta") == mine)
        def _():
            for at, value in spans[mine]:
                keep_ref[at : at + value.shape[0]] = value
            for at, value in spans[1 - mine]:
                send_ref[at : at + value.shape[0]] = value.astype(bf16)


def line_kernel(keep_ref, got_ref, own_ref, *send_refs):
    count = keep_ref.shape[0]
    me = lax.axis_index("phi")
    own_ref[...] = keep_ref[me] + got_ref[me].astype(f32)
    for k, ref in enumerate(send_refs):
        at = lax.rem(me + k + 1, count)
        ref[...] = (keep_ref[at] + got_ref[at].astype(f32)).astype(bf16)


def close_kernel(count, *refs):
    width = refs[0].shape[-1]
    for n in range((len(refs) - 1) // count):
        total = refs[n * count][...]
        for ref in refs[n * count + 1 : (n + 1) * count]:
            total = total + ref[...].astype(f32)
        refs[-1][:, n * width : (n + 1) * width] = total.astype(bf16)


def spread_kernel(own_ref, one_ref, two_ref, three_ref, out_ref):
    me = lax.axis_index("replica")
    for n, ref in enumerate((own_ref, one_ref, two_ref, three_ref)):
        out_ref[me ^ n] = ref[...].astype(f32)


def tie(values, *others):
    return lax.optimization_barrier((values, others))[0]


def fill_kernel(padded, pos_ref, ids_ref, mask_ref, got_ref, *refs):
    wide_ref = refs[-1]
    slots = slot_column(pos_ref, wide_ref, padded)
    ids = ids_ref[0:1] + lax.axis_index("eta").astype(f32) * ids_ref[1:2]
    chosen = (slots == ids).astype(f32).astype(bf16)
    got = got_ref[...]
    values = mm(chosen, got, TN)
    hits = mm(chosen, jnp.ones((got.shape[0], 128), bf16), TN)[:, 0:1]
    values = jnp.where(hits > 0.5, values, mask_ref[...].astype(f32)).astype(bf16)
    at = 0
    for ref in refs[:-1]:
        ref[...] = values[at : at + ref.shape[0]]
        at += ref.shape[0]


def conv_kernel_body(
    shape, span, folded, grid_ref, left_ref, right_ref, rims, taps_ref, out_ref,
    full_ref, wide_ref, mixed_ref,
):
    lines, columns = shape
    rim = span // 2
    width = grid_ref.shape[-1]
    lead = 8
    full_ref[rim : rim + lines, lead : lead + columns] = (
        grid_ref[...].astype(f32).reshape(lines, columns, width)
    )
    left = left_ref[...].astype(f32)
    right = right_ref[...].astype(f32)
    for x in range(lines):
        full_ref[rim + x, lead - rim : lead] = left[rim * x : rim * (x + 1)]
        full_ref[rim + x, lead + columns : lead + columns + rim] = right[rim * x : rim * (x + 1)]

    def put(base, edge_ref, first_ref, last_ref):
        edge = edge_ref[...].astype(f32)
        first = first_ref[...].astype(f32)
        last = last_ref[...].astype(f32)
        for i in range(rim):
            full_ref[base + i, lead : lead + columns] = edge[columns * i : columns * (i + 1)]
            full_ref[base + i, lead - rim : lead] = first[rim * i : rim * (i + 1)]
            full_ref[base + i, lead + columns : lead + columns + rim] = last[
                rim * i : rim * (i + 1)
            ]

    if folded:
        far = rim + lines
        base = jnp.where(lax.axis_index("eta") == 0, far, 0)
        for i in range(rim):
            full_ref[far - base + i] = jnp.zeros(full_ref.shape[1:], f32)
        put(base, *rims)
    else:
        put(0, *rims[:3])
        put(rim + lines, *rims[3:])
    for t in range(span * span):
        wide_ref[t] = jnp.broadcast_to(taps_ref[t // span, t % span : t % span + 1], (8, width))
    groups = columns // 8

    for c in range(width // 128):
        cut = slice(c * 128, (c + 1) * 128)

        def step(x, accs, live, cut=cut):
            accs = list(accs)
            for v in range(span):
                at = lead - rim + v
                line = full_ref[x, at : at + columns, cut].reshape(groups, 8, 128)
                for i in live:
                    tap = wide_ref[(span - 1 - i) * span + v, :, cut]
                    accs[i] = accs[i] + line * tap[None]
            return accs

        def store(row, acc, cut=cut):
            at = row * columns
            if not isinstance(row, int):
                at = pl.multiple_of(at, columns)
            mixed_ref[pl.ds(at, columns), cut] = acc.reshape(columns, 128)

        zero = jnp.zeros((groups, 8, 128), f32)
        accs = [zero] * span
        for x in range(span - 1):
            accs = step(x, accs, range(span - 1 - x, span))
            accs = accs[1:] + [zero]

        def middle(x, accs):
            accs = step(x, accs, range(span))
            store(x - (span - 1), accs[0])
            return tuple(accs[1:] + [zero])

        accs = list(lax.fori_loop(span - 1, lines, middle, tuple(accs)))
        for x in range(lines, lines + span - 1):
            accs = step(x, accs, range(0, lines + span - 1 - x))
            store(x - (span - 1), accs[0])
            accs = accs[1:] + [zero]

    mixed = mixed_ref[...]
    centred = mixed - jnp.mean(mixed, axis=-1, keepdims=True)
    spread = jnp.mean(centred * centred, axis=-1, keepdims=True)
    out_ref[...] = (centred * lax.rsqrt(spread + norm_eps)).astype(bf16)


def mix_folded(shape, span, grid, left, right, a, b, c, taps, out, full, wide, mixed):
    conv_kernel_body(
        shape, span, True, grid, left, right, (a, b, c), taps, out, full, wide, mixed
    )


def mix_open(
    shape, span, grid, left, right, a, b, c, d, e, g, taps, out, full, wide, mixed
):
    conv_kernel_body(
        shape, span, False, grid, left, right, (a, b, c, d, e, g), taps, out, full, wide,
        mixed,
    )


def feed_kernel(chunk, normed_ref, grid_ref, up_ref, down_ref, head_ref, out_ref):
    for at in range(0, normed_ref.shape[0], chunk):
        rows = slice(at, at + chunk)
        wide = mm(normed_ref[rows], up_ref[...])
        hidden = (0.5 * wide * (1.0 + lax.erf(wide * 0.7071067811865476))).astype(bf16)
        decoded = (grid_ref[rows].astype(f32) + mm(hidden, down_ref[...])).astype(bf16)
        out_ref[rows] = mm(decoded, head_ref[...])


def flip(value, axis, bit):
    return lax.ppermute(value, axis, [(i, i ^ bit) for i in range(lax.axis_size(axis))])


def turn(value, axis, k):
    count = lax.axis_size(axis)
    return lax.ppermute(value, axis, [(i, (i + k) % count) for i in range(count)])


def summed_slow(left, cot_t, normed, attended):
    term = jnp.concatenate([mm(left, normed), mm(cot_t, attended)], axis=0)
    share = lax.psum_scatter(term, ("eta", "phi", "replica"), scatter_dimension=0, tiled=True)
    return lax.all_gather(share.astype(bf16), "replica", axis=0, tiled=True).astype(f32)


def body(
    tokens, send_pos, enc_src, window_id, enc_cot, w_qkv, head_scale, w_out, w_dec_in,
    mask_token, conv_kernel, w_up, w_down, w_head,
):
    eta_cells, phi_cells, width = tokens.shape[1:]
    dec_width = w_dec_in.shape[1]
    tile_len = eta_cells * phi_cells
    eta_count = lax.axis_size("eta")
    phi_count = lax.axis_size("phi")
    replicas = lax.axis_size("replica")
    group = eta_count * phi_count
    cap = send_pos.shape[-1]
    padded = -(-cap // 8) * 8
    slots = group * padded
    rows = enc_cot.shape[-2]
    heads = head_scale.shape[0]
    out_rows = 4 * width
    shard_rows = out_rows // group
    part_rows = shard_rows // replicas
    fast = (
        eta_count == 2
        and replicas == 4
        and part_rows % 32 == 0
        and width % shard_rows == 0
        and 3 * width // shard_rows >= group // 2
    )

    positions = send_pos.reshape(group, cap)
    outgoing = call(
        functools.partial(pick_kernel, padded),
        "pick",
        sds((slots, width), bf16),
        [vmem(), vmem()],
        scratch=[pltpu.VMEM((group, 128), f32)],
        flops=2 * slots * tile_len * width,
        nbytes=3 * MIB,
        limit=8,
    )(positions, tokens.reshape(tile_len, width))
    arrived = lax.all_to_all(
        outgoing.reshape(group, padded, width), ("eta", "phi"), split_axis=0, concat_axis=0,
        tiled=True,
    ).reshape(slots, width)

    cotangent = enc_cot.reshape(rows, width)
    split = (shard_rows, part_rows) if fast else None
    pieces = replicas if fast else 1
    cot_part = (width * part_rows // shard_rows, rows) if fast else (width, rows)
    deep = 3 * width * part_rows // shard_rows * rows // width if fast else 3 * width
    cot_whole = (replicas,) + cot_part if fast else cot_part
    left_whole = (replicas, deep, width) if fast else (3 * width, rows)
    if fast:
        tail = -(-4 // (width // rows)) * (width * part_rows // shard_rows)
        peer_shapes = [(deep + 2 * rows + tail, width), (deep + 2 * rows, width)]
        peer_shapes += [(2 * deep + rows, width)]
    else:
        peer_shapes = [(3 * width, rows), (rows, width)]
    grad_att, w_qkv_t, *cots = call(
        functools.partial(prep_kernel, split),
        "prep",
        [sds((width, rows), bf16), sds((3 * width, width), bf16)]
        + [sds(cot_part, bf16)] * pieces,
        [vmem()] * 3,
        scratch=[pltpu.VMEM(cot_whole, bf16)],
        flops=2 * rows * width * width,
        nbytes=10 * MIB,
        limit=10,
    )(cotangent, w_out, w_qkv)
    if fast:
        cots = [cots[0]] + [flip(cots[k], "replica", k) for k in range(1, 4)]

    normed, enc_in, units, lengths, values, places = call(
        functools.partial(project_kernel, cap, padded),
        "project",
        [
            sds((rows, width), bf16),
            sds((rows, width), bf16),
            sds((2 * width, rows), f32),
            sds((2 * heads, rows), f32),
            sds((width, rows), bf16),
            sds((1, rows), f32),
        ],
        [vmem()] * 3,
        flops=2 * rows * width * width * 4,
        nbytes=8 * MIB,
        limit=14,
        cost=2000000000,
    )(enc_src.reshape(1, rows), arrived, w_qkv_t)
    if fast:
        normed_y = flip(normed, "replica", 2)

    outbound, *peers = call(
        functools.partial(encode_kernel, split),
        "encode",
        [sds((slots, dec_width), bf16)] + [sds(shape, bf16) for shape in peer_shapes],
        [vmem(), smem()] + [vmem()] * (13 if fast else 9),
        scratch=[
            pltpu.VMEM((heads, rows, rows), bf16),
            pltpu.VMEM((width, rows), bf16),
            pltpu.VMEM(left_whole, bf16),
        ],
        flops=2 * rows * width * width * 10,
        nbytes=8 * MIB,
        limit=14,
        cost=8000000000,
    )(
        window_id.reshape(1, rows), head_scale, places, enc_in, units, lengths, values, grad_att,
        w_out, w_dec_in, normed, *(cots if fast else ()),
    )
    if fast:
        peers[1], peers[2], normed_y = lax.optimization_barrier((peers[1], peers[2], normed_y))
    returned = lax.all_to_all(
        outbound.reshape(group, padded, dec_width), ("eta", "phi"), split_axis=0, concat_axis=0,
        tiled=True,
    )
    if fast:
        own, near, far = peers[0], flip(peers[1], "replica", 1), flip(peers[2], "replica", 2)
        normed_hop = flip(normed_y, "replica", 1)
        returned = tie(returned, near, normed_hop)
    else:
        grad_total = summed_slow(peers[0], cots[0], normed, peers[1])

    span = conv_kernel.shape[0]
    rim = span // 2
    folded = eta_count == 2
    lines = np.arange(eta_cells)[:, None]
    columns = np.arange(phi_cells)[None, :]
    cell = lines * phi_cells + columns
    parts = [cell]
    moves = [0]
    if folded:
        edge = cell[eta_cells - rim :]
        parts += [cell[:, :rim], cell[:, -rim:], edge, edge[:, :rim], edge[:, -rim:]]
        moves += [0, 0] + [-(eta_cells - rim) * phi_cells] * 3
    sizes = [-(-p.size // 16) * 16 for p in parts]
    ids = np.full((2, -(-sum(sizes) // 128) * 128), -7.0, np.float32)
    ids[1] = 0
    at = 0
    for p, size, move in zip(parts, sizes, moves):
        ids[0, at : at + p.size] = p.reshape(-1)
        ids[1, at : at + p.size] = move
        at += size
    filled = call(
        functools.partial(fill_kernel, padded),
        "fill",
        [sds((size, dec_width), bf16) for size in sizes],
        [vmem()] * 4,
        scratch=[pltpu.VMEM((group, 128), f32)],
        flops=2 * slots * ids.shape[1] * (dec_width + 128),
        nbytes=3 * MIB,
        limit=12,
    )(
        positions, jnp.asarray(ids), mask_token.reshape(1, dec_width),
        returned.reshape(slots, dec_width),
    )
    dec_grid = filled[0]
    plane = ("eta", "phi")

    def shifted(value, by):
        pairs = [
            (e * phi_count + p, (1 - e) * phi_count + (p + by) % phi_count)
            for e in range(2)
            for p in range(phi_count)
        ]
        return lax.ppermute(value, plane, pairs)

    if folded:
        _, first, last, edge, edge_first, edge_last = filled
        left_halo = turn(last, "phi", 1)
        right_halo = turn(first, "phi", -1)
        rims = (shifted(edge, 0), shifted(edge_last, 1), shifted(edge_first, -1))
    else:
        box = dec_grid.reshape(eta_cells, phi_cells, dec_width)
        down = [(i, i + 1) for i in range(eta_count - 1)]
        up = [(i + 1, i) for i in range(eta_count - 1)]
        top = lax.ppermute(box[eta_cells - rim :], "eta", down)
        bottom = lax.ppermute(box[:rim], "eta", up)
        box = jnp.concatenate([top, box, bottom], axis=0)
        low = turn(box[:, phi_cells - rim :], "phi", 1)
        high = turn(box[:, :rim], "phi", -1)

        def flat(value):
            return value.reshape(-1, dec_width)

        far = eta_cells + rim
        left_halo, right_halo = flat(low[rim:far]), flat(high[rim:far])
        rims = (
            flat(top), flat(low[:rim]), flat(high[:rim]),
            flat(bottom), flat(low[far:]), flat(high[far:]),
        )
    if fast:
        far = tie(far, left_halo, right_halo, rims)
        peers = [own, near, far, flip(far, "replica", 1), normed_y, normed_hop]
        chunk = width // 2
        half = group // 2
        kept, sent = [], []
        for c in range(2):
            keep, send = call(
                functools.partial(term_kernel, (c * chunk, (c + 1) * chunk), rows),
                "terms%d" % c,
                [sds((half, part_rows, chunk), f32), sds((half, part_rows, chunk), bf16)],
                [vmem()] * 6,
                flops=2 * out_rows * chunk * rows,
                nbytes=8 * MIB,
                limit=10,
            )(*peers)
            kept.append(keep)
            sent.append(turn(send, "eta", 1))
        left, right_halo, rims = tie((left_halo, right_halo, rims), kept)
    else:
        left = left_halo
    normed_cells = call(
        functools.partial(mix_folded if folded else mix_open, (eta_cells, phi_cells), span),
        "mix",
        sds((tile_len, dec_width), bf16),
        [vmem()] * (4 + len(rims)),
        scratch=[
            pltpu.VMEM((eta_cells + 2 * rim, phi_cells + 16, dec_width), f32),
            pltpu.VMEM((span * span, 8, dec_width), f32),
            pltpu.VMEM((tile_len, dec_width), f32),
        ],
        flops=200 * 2 * span * span * tile_len * dec_width,
        nbytes=3 * MIB,
        limit=16,
    )(dec_grid, left, right_halo, *rims, conv_kernel)
    if fast:
        summed = []
        for c in range(2):
            own, *outs = call(
                line_kernel,
                "line%d" % c,
                [sds((part_rows, chunk), f32)] + [sds((part_rows, chunk), bf16)] * (phi_count - 1),
                [vmem()] * 2,
                flops=half * part_rows * chunk,
                nbytes=2 * MIB,
                limit=4,
            )(kept[c], tie(sent[c], normed_cells))
            summed.append([own] + [turn(outs[k], "phi", k + 1) for k in range(phi_count - 1)])
            normed_cells = tie(normed_cells, own)
    reconstruction = call(
        functools.partial(feed_kernel, 256),
        "feed",
        sds((tile_len, w_head.shape[1]), f32),
        [vmem()] * 5,
        flops=2 * tile_len * dec_width * (2 * w_up.shape[1] + w_head.shape[1]),
        nbytes=4 * MIB,
        limit=12,
    )(normed_cells, dec_grid, w_up, w_down, w_head).reshape(1, eta_cells, phi_cells, -1)
    if fast:
        summed = tie(summed, reconstruction)
        mine = call(
            functools.partial(close_kernel, phi_count),
            "close",
            sds((part_rows, width), bf16),
            [vmem()] * (2 * phi_count),
            flops=4 * part_rows * width,
            nbytes=MIB,
            limit=4,
        )(*summed[0], *summed[1])
        mine_y = flip(mine, "replica", 2)
        grad_total = call(
            spread_kernel,
            "spread",
            sds((replicas, part_rows, width), f32),
            [vmem()] * 4,
            flops=4 * part_rows * width,
            nbytes=2 * MIB,
            limit=4,
        )(
            mine, flip(mine, "replica", 1), mine_y, flip(mine_y, "replica", 1),
        ).reshape(shard_rows, width)
    return (grad_total, reconstruction)


def solution(mesh):
    in_specs = (
        P("replica", "eta", "phi", None),
        P("replica", "eta", "phi", None, None),
        P("replica", "eta", "phi", None),
        P("replica", "eta", "phi", None),
        P("replica", "eta", "phi", None, None),
        P(), P(), P(), P(), P(), P(), P(), P(), P(),
    )
    out_specs = (P(("eta", "phi"), None), P("replica", "eta", "phi", None))
    return jax.shard_map(body, mesh=mesh, in_specs=in_specs, out_specs=out_specs, check_vma=False)
```

```python
import functools

import jax
import jax.numpy as jnp
import numpy as np
from jax import lax
from jax.experimental import pallas as pl
from jax.experimental.pallas import tpu as pltpu
from jax.sharding import PartitionSpec as P

norm_eps = 1e-05
length_eps = 1e-06
f32 = jnp.float32
bf16 = jnp.bfloat16
MIB = 1024 * 1024

NN = (((1,), (0,)), ((), ()))
NT = (((1,), (1,)), ((), ()))
TN = (((0,), (0,)), ((), ()))


def mm(a, b, dims=NN):
    return lax.dot_general(a, b, dims, preferred_element_type=f32)


def vmem():
    return pl.BlockSpec(memory_space=pltpu.VMEM)


def smem():
    return pl.BlockSpec(memory_space=pltpu.SMEM)


def call(kernel, name, outs, in_specs, scratch=(), flops=0, nbytes=0, limit=20, cost=1000):
    single = not isinstance(outs, (list, tuple))
    out_list = [outs] if single else list(outs)
    specs = [vmem() for _ in out_list]
    return pl.pallas_call(
        kernel,
        out_shape=out_list[0] if single else tuple(out_list),
        in_specs=in_specs,
        out_specs=specs[0] if single else tuple(specs),
        scratch_shapes=list(scratch),
        compiler_params=pltpu.CompilerParams(vmem_limit_bytes=limit * MIB),
        cost_estimate=pl.CostEstimate(
            flops=cost, bytes_accessed=1000 + cost // 300, transcendentals=0
        ),
        name=name,
    )


def sds(shape, dtype):
    return jax.ShapeDtypeStruct(shape, dtype)


def column_of(row):
    return jnp.transpose(jnp.broadcast_to(row, (8, row.shape[1])))[:, 0:1]


def slot_column(pos_ref, wide_ref, padded):
    group, cap = pos_ref.shape
    wide_ref[...] = jnp.full(wide_ref.shape, -1.0, f32)
    wide_ref[:, 0:cap] = pos_ref[...].astype(f32)
    turned = jnp.transpose(wide_ref[...])
    return jnp.concatenate([turned[0:padded, d : d + 1] for d in range(group)], axis=0)


def pick_kernel(padded, pos_ref, tok_ref, out_ref, wide_ref):
    slots = slot_column(pos_ref, wide_ref, padded)
    cells = lax.broadcasted_iota(jnp.int32, (slots.shape[0], tok_ref.shape[0]), 1).astype(f32)
    chosen = (slots == cells).astype(f32).astype(bf16)
    out_ref[...] = mm(chosen, tok_ref[...]).astype(bf16)


def prep_kernel(cot_ref, wout_ref, wqkv_ref, ga_ref, wqkv_t_ref):
    ga_ref[...] = mm(wout_ref[...], cot_ref[...], NT).astype(bf16)
    wqkv_t_ref[...] = jnp.transpose(wqkv_ref[...])


def norm_kernel(cap, padded, src_ref, arr_ref, normed_ref, enc_ref, place_ref):
    rows = normed_ref.shape[0]
    slots = arr_ref.shape[0]
    src = src_ref[...].astype(f32)
    slot_row = src + (padded - cap) * jnp.floor((src + 0.5) * (1.0 / cap))
    place_ref[...] = slot_row
    slot_col = column_of(slot_row)
    lanes = lax.broadcasted_iota(jnp.int32, (rows, slots), 1).astype(f32)
    pick = (slot_col == lanes).astype(f32).astype(bf16)
    enc_in = mm(pick, arr_ref[...])
    enc_ref[...] = enc_in.astype(bf16)
    centred = enc_in - jnp.mean(enc_in, axis=-1, keepdims=True)
    spread = jnp.mean(centred * centred, axis=-1, keepdims=True)
    normed_ref[...] = (centred * lax.rsqrt(spread + norm_eps)).astype(bf16)


def project_kernel(normed_ref, wqkv_t_ref, u_ref, len_ref, v_ref):
    normed = normed_ref[...]
    width = normed.shape[1]
    heads = len_ref.shape[0] // 2
    size = width // heads
    for t in range(2):
        raw = mm(wqkv_t_ref[t * width : (t + 1) * width], normed, NT)
        for h in range(heads):
            part = raw[h * size : (h + 1) * size]
            inv = lax.rsqrt(jnp.sum(part * part, axis=0, keepdims=True) + length_eps)
            at = t * width + h * size
            u_ref[at : at + size] = part * inv
            len_ref[t * heads + h : t * heads + h + 1] = inv
    v_ref[...] = mm(wqkv_t_ref[2 * width : 3 * width], normed, NT).astype(bf16)


def encode_kernel(
    split, win_ref, scale_ref, place_ref, enc_ref, u_ref, len_ref, v_ref, ga_ref, wout_ref,
    wdec_ref, out_ref, *refs,
):
    peer_refs = refs[:-3]
    p_ref, att_ref, left_ref = refs[-3:]
    rows, width = enc_ref.shape
    heads = p_ref.shape[0]
    size = width // heads
    slots = out_ref.shape[0]
    win = win_ref[...].astype(f32)
    same = column_of(win) == win
    for h in range(heads):
        lo, hi = h * size, (h + 1) * size
        q = u_ref[lo:hi].astype(bf16)
        k = u_ref[width + lo : width + hi].astype(bf16)
        scores = mm(k, q, TN)
        raised = jnp.where(same, jnp.exp(scores * scale_ref[h]), 0.0)
        weights = (raised * (1.0 / jnp.sum(raised, axis=0, keepdims=True))).astype(bf16)
        p_ref[h] = weights
        att = mm(v_ref[lo:hi], weights).astype(bf16)
        att_ref[lo:hi] = att
        emit(split, left_ref, 3 * width + lo, att)
    attended = jnp.transpose(att_ref[...])
    enc_out = (enc_ref[...].astype(f32) + mm(attended, wout_ref[...])).astype(bf16)
    dec = mm(enc_out, wdec_ref[...]).astype(bf16)
    places = lax.broadcasted_iota(jnp.int32, (slots, rows), 0).astype(f32)
    put = (places == place_ref[...]).astype(f32).astype(bf16)
    out_ref[...] = mm(put, dec).astype(bf16)
    for h in range(heads):
        lo, hi = h * size, (h + 1) * size
        ga = ga_ref[lo:hi]
        low = p_ref[h]
        weights = low.astype(f32)
        grad_soft = mm(v_ref[lo:hi], ga, TN)
        part = weights * grad_soft
        total = jnp.sum(part, axis=0, keepdims=True)
        grad_scores = ((part - weights * total) * scale_ref[h]).astype(bf16)
        q = u_ref[lo:hi]
        k = u_ref[width + lo : width + hi]
        grad_v = mm(ga, low, NT)
        grad_q = mm(k.astype(bf16), grad_scores)
        grad_k = mm(q.astype(bf16), grad_scores, NT)
        grad_q = (grad_q - q * jnp.sum(q * grad_q, axis=0, keepdims=True)) * len_ref[h : h + 1]
        grad_k = (grad_k - k * jnp.sum(k * grad_k, axis=0, keepdims=True)) * len_ref[
            heads + h : heads + h + 1
        ]
        emit(split, left_ref, lo, grad_q.astype(bf16))
        emit(split, left_ref, width + lo, grad_k.astype(bf16))
        emit(split, left_ref, 2 * width + lo, grad_v.astype(bf16))
    me = lax.axis_index("replica") if split is not None else 0
    for n, ref in enumerate(peer_refs):
        ref[...] = left_ref[me ^ n] if split is not None else left_ref[...]


def emit(split, out_ref, start, block):
    if split is None:
        out_ref[start : start + block.shape[0]] = block
        return
    unit = 32
    shard_rows, part_rows, qkv_rows = split
    for j in range(block.shape[0] // unit):
        row = start + j * unit
        if row < qkv_rows:
            shard, rest = divmod(row, shard_rows)
            part, place = divmod(rest, part_rows)
            at = shard * part_rows + place
        else:
            part, place = divmod(row - qkv_rows, qkv_rows // 3 // out_ref.shape[0])
            at = qkv_rows // out_ref.shape[0] + place
        out_ref[part, at : at + unit] = block[j * unit : (j + 1) * unit]


def term_kernel(c, *refs):
    lefts, normed, cots = refs[0:4], refs[4:8], refs[8:12]
    keep_ref, send_ref = refs[12:]
    half, part, chunk = keep_ref.shape
    cut = slice(c * chunk, (c + 1) * chunk)

    def block(lo, hi, right, cols):
        acc = None
        for left, e in zip(lefts, right):
            step = mm(left[lo:hi], e[:, cols])
            acc = step if acc is None else acc + step
        return acc

    rows = half * part
    first = [(0, block(0, rows, normed, cut).reshape(half, part, chunk))]
    shared = block(rows, rows + (half - 2) * part, normed, cut).reshape(half - 2, part, chunk)
    at = rows + (half - 2 + c) * part
    turned = block(at, at + part, cots, slice(0, 2 * chunk))
    second = [
        (0, shared),
        (half - 2, turned[:, 0:chunk].reshape(1, part, chunk)),
        (half - 1, turned[:, chunk:].reshape(1, part, chunk)),
    ]
    spans = (first, second)
    for mine in range(2):

        @pl.when(lax.axis_index("eta") == mine)
        def _():
            for at, value in spans[mine]:
                keep_ref[at : at + value.shape[0]] = value
            for at, value in spans[1 - mine]:
                send_ref[at : at + value.shape[0]] = value.astype(bf16)


def line_kernel(keep_ref, got_ref, own_ref, *send_refs):
    count = keep_ref.shape[0]
    me = lax.axis_index("phi")
    own_ref[...] = keep_ref[me] + got_ref[me].astype(f32)
    for k, ref in enumerate(send_refs):
        at = lax.rem(me + k + 1, count)
        ref[...] = (keep_ref[at] + got_ref[at].astype(f32)).astype(bf16)


def close_kernel(count, *refs):
    width = refs[0].shape[-1]
    for n in range((len(refs) - 1) // count):
        total = refs[n * count][...]
        for ref in refs[n * count + 1 : (n + 1) * count]:
            total = total + ref[...].astype(f32)
        refs[-1][:, n * width : (n + 1) * width] = total.astype(bf16)


def spread_kernel(own_ref, one_ref, two_ref, three_ref, out_ref, all_ref):
    me = lax.axis_index("replica")
    for n, ref in enumerate((own_ref, one_ref, two_ref, three_ref)):
        all_ref[me ^ n] = ref[...].astype(f32)
    count, part, width = all_ref.shape
    chunk = width // 2
    phis = lax.axis_size("phi")
    turned = lax.axis_index("eta") * phis + lax.axis_index("phi") >= 2 * phis - 2

    @pl.when(jnp.logical_not(turned))
    def _():
        for r in range(count):
            out_ref[r * part : (r + 1) * part] = all_ref[r]

    @pl.when(turned)
    def _():
        pieces = []
        for r in range(count):
            for c in range(2):
                pieces.append(all_ref[r, :, c * chunk : (c + 1) * chunk])
        out_ref[...] = jnp.transpose(jnp.concatenate(pieces, axis=0))


def tie(values, *others):
    return lax.optimization_barrier((values, others))[0]


def fill_kernel(padded, pos_ref, ids_ref, mask_ref, got_ref, *refs):
    wide_ref = refs[-1]
    slots = slot_column(pos_ref, wide_ref, padded)
    ids = ids_ref[0:1] + lax.axis_index("eta").astype(f32) * ids_ref[1:2]
    chosen = (slots == ids).astype(f32).astype(bf16)
    got = got_ref[...]
    values = mm(chosen, got, TN)
    hits = mm(chosen, jnp.ones((got.shape[0], 128), bf16), TN)[:, 0:1]
    values = jnp.where(hits > 0.5, values, mask_ref[...].astype(f32)).astype(bf16)
    at = 0
    for ref in refs[:-1]:
        ref[...] = values[at : at + ref.shape[0]]
        at += ref.shape[0]


def conv_kernel_body(
    shape, span, folded, grid_ref, left_ref, right_ref, rims, taps_ref, out_ref,
    full_ref, wide_ref, mixed_ref,
):
    lines, columns = shape
    rim = span // 2
    width = grid_ref.shape[-1]
    lead = 8
    full_ref[rim : rim + lines, lead : lead + columns] = (
        grid_ref[...].astype(f32).reshape(lines, columns, width)
    )
    left = left_ref[...].astype(f32)
    right = right_ref[...].astype(f32)
    for x in range(lines):
        full_ref[rim + x, lead - rim : lead] = left[rim * x : rim * (x + 1)]
        full_ref[rim + x, lead + columns : lead + columns + rim] = right[rim * x : rim * (x + 1)]

    def put(base, edge_ref, first_ref, last_ref):
        edge = edge_ref[...].astype(f32)
        first = first_ref[...].astype(f32)
        last = last_ref[...].astype(f32)
        for i in range(rim):
            full_ref[base + i, lead : lead + columns] = edge[columns * i : columns * (i + 1)]
            full_ref[base + i, lead - rim : lead] = first[rim * i : rim * (i + 1)]
            full_ref[base + i, lead + columns : lead + columns + rim] = last[
                rim * i : rim * (i + 1)
            ]

    if folded:
        far = rim + lines
        base = jnp.where(lax.axis_index("eta") == 0, far, 0)
        for i in range(rim):
            full_ref[far - base + i] = jnp.zeros(full_ref.shape[1:], f32)
        put(base, *rims)
    else:
        put(0, *rims[:3])
        put(rim + lines, *rims[3:])
    for t in range(span * span):
        wide_ref[t] = jnp.broadcast_to(taps_ref[t // span, t % span : t % span + 1], (8, width))
    groups = columns // 8

    for c in range(width // 128):
        cut = slice(c * 128, (c + 1) * 128)

        def step(x, accs, live, cut=cut):
            accs = list(accs)
            for v in range(span):
                at = lead - rim + v
                line = full_ref[x, at : at + columns, cut].reshape(groups, 8, 128)
                for i in live:
                    tap = wide_ref[(span - 1 - i) * span + v, :, cut]
                    accs[i] = accs[i] + line * tap[None]
            return accs

        def store(row, acc, cut=cut):
            at = row * columns
            if not isinstance(row, int):
                at = pl.multiple_of(at, columns)
            mixed_ref[pl.ds(at, columns), cut] = acc.reshape(columns, 128)

        zero = jnp.zeros((groups, 8, 128), f32)
        accs = [zero] * span
        for x in range(span - 1):
            accs = step(x, accs, range(span - 1 - x, span))
            accs = accs[1:] + [zero]

        def middle(x, accs):
            accs = step(x, accs, range(span))
            store(x - (span - 1), accs[0])
            return tuple(accs[1:] + [zero])

        accs = list(lax.fori_loop(span - 1, lines, middle, tuple(accs)))
        for x in range(lines, lines + span - 1):
            accs = step(x, accs, range(0, lines + span - 1 - x))
            store(x - (span - 1), accs[0])
            accs = accs[1:] + [zero]

    mixed = mixed_ref[...]
    centred = mixed - jnp.mean(mixed, axis=-1, keepdims=True)
    spread = jnp.mean(centred * centred, axis=-1, keepdims=True)
    out_ref[...] = (centred * lax.rsqrt(spread + norm_eps)).astype(bf16)


def mix_folded(shape, span, grid, left, right, a, b, c, taps, out, full, wide, mixed):
    conv_kernel_body(
        shape, span, True, grid, left, right, (a, b, c), taps, out, full, wide, mixed
    )


def mix_open(
    shape, span, grid, left, right, a, b, c, d, e, g, taps, out, full, wide, mixed
):
    conv_kernel_body(
        shape, span, False, grid, left, right, (a, b, c, d, e, g), taps, out, full, wide,
        mixed,
    )


def feed_kernel(chunk, normed_ref, grid_ref, up_ref, down_ref, head_ref, out_ref):
    for at in range(0, normed_ref.shape[0], chunk):
        rows = slice(at, at + chunk)
        wide = mm(normed_ref[rows], up_ref[...])
        hidden = (0.5 * wide * (1.0 + lax.erf(wide * 0.7071067811865476))).astype(bf16)
        decoded = (grid_ref[rows].astype(f32) + mm(hidden, down_ref[...])).astype(bf16)
        out_ref[rows] = mm(decoded, head_ref[...])


def flip(value, axis, bit):
    return lax.ppermute(value, axis, [(i, i ^ bit) for i in range(lax.axis_size(axis))])


def turn(value, axis, k):
    count = lax.axis_size(axis)
    return lax.ppermute(value, axis, [(i, (i + k) % count) for i in range(count)])


def summed_slow(left, normed, cotangent):
    width = normed.shape[1]
    term = jnp.concatenate(
        [mm(left[: 3 * width], normed), mm(cotangent, left[3 * width :], (((0,), (1,)), ((), ())))],
        axis=0,
    )
    share = lax.psum_scatter(term, ("eta", "phi", "replica"), scatter_dimension=0, tiled=True)
    return lax.all_gather(share.astype(bf16), "replica", axis=0, tiled=True).astype(f32)


def body(
    tokens, send_pos, enc_src, window_id, enc_cot, w_qkv, head_scale, w_out, w_dec_in,
    mask_token, conv_kernel, w_up, w_down, w_head,
):
    eta_cells, phi_cells, width = tokens.shape[1:]
    dec_width = w_dec_in.shape[1]
    tile_len = eta_cells * phi_cells
    eta_count = lax.axis_size("eta")
    phi_count = lax.axis_size("phi")
    replicas = lax.axis_size("replica")
    group = eta_count * phi_count
    cap = send_pos.shape[-1]
    padded = -(-cap // 8) * 8
    slots = group * padded
    rows = enc_cot.shape[-2]
    heads = head_scale.shape[0]
    out_rows = 4 * width
    shard_rows = out_rows // group
    part_rows = shard_rows // replicas
    fast = (
        eta_count == 2
        and replicas == 4
        and part_rows % 32 == 0
        and width == 2 * shard_rows
    )

    positions = send_pos.reshape(group, cap)
    outgoing = call(
        functools.partial(pick_kernel, padded),
        "pick",
        sds((slots, width), bf16),
        [vmem(), vmem()],
        scratch=[pltpu.VMEM((group, 128), f32)],
        flops=2 * slots * tile_len * width,
        nbytes=3 * MIB,
        limit=8,
    )(positions, tokens.reshape(tile_len, width))
    arrived = lax.all_to_all(
        outgoing.reshape(group, padded, width), ("eta", "phi"), split_axis=0, concat_axis=0,
        tiled=True,
    ).reshape(slots, width)

    cotangent = enc_cot.reshape(rows, width)
    split = (shard_rows, part_rows, 3 * width) if fast else None
    pieces = replicas if fast else 1
    left_part = (out_rows // pieces, rows)
    left_whole = (replicas,) + left_part if fast else left_part
    if fast:
        cots = [cotangent, flip(cotangent, "replica", 1), flip(cotangent, "replica", 2)]
    grad_att, w_qkv_t = call(
        prep_kernel,
        "prep",
        [sds((width, rows), bf16), sds((3 * width, width), bf16)],
        [vmem()] * 3,
        flops=2 * rows * width * width,
        nbytes=10 * MIB,
        limit=10,
    )(cotangent, w_out, w_qkv)
    if fast:
        cots.append(flip(tie(cots[2], w_qkv_t), "replica", 1))

    normed, enc_in, places = call(
        functools.partial(norm_kernel, cap, padded),
        "norm",
        [sds((rows, width), bf16), sds((rows, width), bf16), sds((1, rows), f32)],
        [vmem()] * 2,
        flops=2 * rows * width * slots,
        nbytes=2 * MIB,
        limit=8,
        cost=600000000,
    )(enc_src.reshape(1, rows), arrived)
    if fast:
        normed_y = flip(normed, "replica", 2)
        normed_c = flip(normed, "replica", 1)
    units, lengths, values = call(
        project_kernel,
        "project",
        [sds((2 * width, rows), f32), sds((2 * heads, rows), f32), sds((width, rows), bf16)],
        [vmem()] * 2,
        flops=2 * rows * width * width * 4,
        nbytes=8 * MIB,
        limit=10,
        cost=2000000000,
    )(tie(normed, cots) if fast else normed, w_qkv_t)

    outbound, *lefts = call(
        functools.partial(encode_kernel, split),
        "encode",
        [sds((slots, dec_width), bf16)] + [sds(left_part, bf16)] * pieces,
        [vmem(), smem()] + [vmem()] * 8,
        scratch=[
            pltpu.VMEM((heads, rows, rows), bf16),
            pltpu.VMEM((width, rows), bf16),
            pltpu.VMEM(left_whole, bf16),
        ],
        flops=2 * rows * width * width * 10,
        nbytes=8 * MIB,
        limit=14,
        cost=8000000000,
    )(
        window_id.reshape(1, rows), head_scale, places, enc_in, units, lengths, values, grad_att,
        w_out, w_dec_in,
    )
    if fast:
        *lefts, normed_y, normed_c = lax.optimization_barrier((*lefts, normed_y, normed_c))
    returned = lax.all_to_all(
        outbound.reshape(group, padded, dec_width), ("eta", "phi"), split_axis=0, concat_axis=0,
        tiled=True,
    )
    if fast:
        lefts = [lefts[0]] + [flip(lefts[k], "replica", k) for k in range(1, 4)]
        rights = [normed, normed_c, normed_y, flip(normed_y, "replica", 1)]
        returned = tie(returned, lefts[1], rights[3])
    else:
        grad_total = summed_slow(lefts[0], normed, cotangent)

    span = conv_kernel.shape[0]
    rim = span // 2
    folded = eta_count == 2
    lines = np.arange(eta_cells)[:, None]
    columns = np.arange(phi_cells)[None, :]
    cell = lines * phi_cells + columns
    parts = [cell]
    moves = [0]
    if folded:
        edge = cell[eta_cells - rim :]
        parts += [cell[:, :rim], cell[:, -rim:], edge, edge[:, :rim], edge[:, -rim:]]
        moves += [0, 0] + [-(eta_cells - rim) * phi_cells] * 3
    sizes = [-(-p.size // 16) * 16 for p in parts]
    ids = np.full((2, -(-sum(sizes) // 128) * 128), -7.0, np.float32)
    ids[1] = 0
    at = 0
    for p, size, move in zip(parts, sizes, moves):
        ids[0, at : at + p.size] = p.reshape(-1)
        ids[1, at : at + p.size] = move
        at += size
    filled = call(
        functools.partial(fill_kernel, padded),
        "fill",
        [sds((size, dec_width), bf16) for size in sizes],
        [vmem()] * 4,
        scratch=[pltpu.VMEM((group, 128), f32)],
        flops=2 * slots * ids.shape[1] * (dec_width + 128),
        nbytes=3 * MIB,
        limit=12,
    )(
        positions, jnp.asarray(ids), mask_token.reshape(1, dec_width),
        returned.reshape(slots, dec_width),
    )
    dec_grid = filled[0]
    plane = ("eta", "phi")

    def shifted(value, by):
        pairs = [
            (e * phi_count + p, (1 - e) * phi_count + (p + by) % phi_count)
            for e in range(2)
            for p in range(phi_count)
        ]
        return lax.ppermute(value, plane, pairs)

    if folded:
        _, first, last, edge, edge_first, edge_last = filled
        left_halo = turn(last, "phi", 1)
        right_halo = turn(first, "phi", -1)
        rims = (shifted(edge, 0), shifted(edge_last, 1), shifted(edge_first, -1))
    else:
        box = dec_grid.reshape(eta_cells, phi_cells, dec_width)
        down = [(i, i + 1) for i in range(eta_count - 1)]
        up = [(i + 1, i) for i in range(eta_count - 1)]
        top = lax.ppermute(box[eta_cells - rim :], "eta", down)
        bottom = lax.ppermute(box[:rim], "eta", up)
        box = jnp.concatenate([top, box, bottom], axis=0)
        low = turn(box[:, phi_cells - rim :], "phi", 1)
        high = turn(box[:, :rim], "phi", -1)

        def flat(value):
            return value.reshape(-1, dec_width)

        far = eta_cells + rim
        left_halo, right_halo = flat(low[rim:far]), flat(high[rim:far])
        rims = (
            flat(top), flat(low[:rim]), flat(high[:rim]),
            flat(bottom), flat(low[far:]), flat(high[far:]),
        )
    if fast:
        lefts, rights, cots = tie((lefts, rights, cots), left_halo, right_halo, rims)
        chunk = width // 2
        half = group // 2
        kept, sent = [], []
        for c in range(2):
            keep, send = call(
                functools.partial(term_kernel, c),
                "terms%d" % c,
                [sds((half, part_rows, chunk), f32), sds((half, part_rows, chunk), bf16)],
                [vmem()] * 12,
                flops=2 * out_rows * chunk * rows,
                nbytes=8 * MIB,
                limit=10,
            )(*lefts, *rights, *cots)
            kept.append(keep)
            sent.append(turn(send, "eta", 1))
        left, right_halo, rims = tie((left_halo, right_halo, rims), kept)
    else:
        left = left_halo
    normed_cells = call(
        functools.partial(mix_folded if folded else mix_open, (eta_cells, phi_cells), span),
        "mix",
        sds((tile_len, dec_width), bf16),
        [vmem()] * (4 + len(rims)),
        scratch=[
            pltpu.VMEM((eta_cells + 2 * rim, phi_cells + 16, dec_width), f32),
            pltpu.VMEM((span * span, 8, dec_width), f32),
            pltpu.VMEM((tile_len, dec_width), f32),
        ],
        flops=200 * 2 * span * span * tile_len * dec_width,
        nbytes=3 * MIB,
        limit=16,
    )(dec_grid, left, right_halo, *rims, conv_kernel)
    if fast:
        summed = []
        for c in range(2):
            own, *outs = call(
                line_kernel,
                "line%d" % c,
                [sds((part_rows, chunk), f32)] + [sds((part_rows, chunk), bf16)] * (phi_count - 1),
                [vmem()] * 2,
                flops=half * part_rows * chunk,
                nbytes=2 * MIB,
                limit=4,
            )(kept[c], tie(sent[c], normed_cells))
            summed.append([own] + [turn(outs[k], "phi", k + 1) for k in range(phi_count - 1)])
            normed_cells = tie(normed_cells, own)
    reconstruction = call(
        functools.partial(feed_kernel, 256),
        "feed",
        sds((tile_len, w_head.shape[1]), f32),
        [vmem()] * 5,
        flops=2 * tile_len * dec_width * (2 * w_up.shape[1] + w_head.shape[1]),
        nbytes=4 * MIB,
        limit=12,
    )(normed_cells, dec_grid, w_up, w_down, w_head).reshape(1, eta_cells, phi_cells, -1)
    if fast:
        summed = tie(summed, reconstruction)
        mine = call(
            functools.partial(close_kernel, phi_count),
            "close",
            sds((part_rows, width), bf16),
            [vmem()] * (2 * phi_count),
            flops=4 * part_rows * width,
            nbytes=MIB,
            limit=4,
        )(*summed[0], *summed[1])
        mine_y = flip(mine, "replica", 2)
        grad_total = call(
            spread_kernel,
            "spread",
            sds((shard_rows, width), f32),
            [vmem()] * 4,
            scratch=[pltpu.VMEM((replicas, part_rows, width), f32)],
            flops=4 * part_rows * width,
            nbytes=2 * MIB,
            limit=8,
        )(mine, flip(mine, "replica", 1), mine_y, flip(mine_y, "replica", 1))
    return (grad_total, reconstruction)


def solution(mesh):
    in_specs = (
        P("replica", "eta", "phi", None),
        P("replica", "eta", "phi", None, None),
        P("replica", "eta", "phi", None),
        P("replica", "eta", "phi", None),
        P("replica", "eta", "phi", None, None),
        P(), P(), P(), P(), P(), P(), P(), P(), P(),
    )
    out_specs = (P(("eta", "phi"), None), P("replica", "eta", "phi", None))
    return jax.shard_map(body, mesh=mesh, in_specs=in_specs, out_specs=out_specs, check_vma=False)
```

```python
import functools

import jax
import jax.numpy as jnp
import numpy as np
from jax import lax
from jax.experimental import pallas as pl
from jax.experimental.pallas import tpu as pltpu
from jax.sharding import PartitionSpec as P

norm_eps = 1e-05
length_eps = 1e-06
f32 = jnp.float32
bf16 = jnp.bfloat16
MIB = 1024 * 1024

NN = (((1,), (0,)), ((), ()))
NT = (((1,), (1,)), ((), ()))
TN = (((0,), (0,)), ((), ()))


def mm(a, b, dims=NN):
    return lax.dot_general(a, b, dims, preferred_element_type=f32)


def vmem():
    return pl.BlockSpec(memory_space=pltpu.VMEM)


def smem():
    return pl.BlockSpec(memory_space=pltpu.SMEM)


def call(kernel, name, outs, in_specs, scratch=(), flops=0, nbytes=0, limit=20, cost=1000):
    single = not isinstance(outs, (list, tuple))
    out_list = [outs] if single else list(outs)
    specs = [vmem() for _ in out_list]
    return pl.pallas_call(
        kernel,
        out_shape=out_list[0] if single else tuple(out_list),
        in_specs=in_specs,
        out_specs=specs[0] if single else tuple(specs),
        scratch_shapes=list(scratch),
        compiler_params=pltpu.CompilerParams(vmem_limit_bytes=limit * MIB),
        cost_estimate=pl.CostEstimate(
            flops=cost, bytes_accessed=1000 + cost // 300, transcendentals=0
        ),
        name=name,
    )


def sds(shape, dtype):
    return jax.ShapeDtypeStruct(shape, dtype)


def column_of(row):
    return jnp.transpose(jnp.broadcast_to(row, (8, row.shape[1])))[:, 0:1]


def slot_column(pos_ref, wide_ref, padded):
    group, cap = pos_ref.shape
    wide_ref[...] = jnp.full(wide_ref.shape, -1.0, f32)
    wide_ref[:, 0:cap] = pos_ref[...].astype(f32)
    turned = jnp.transpose(wide_ref[...])
    return jnp.concatenate([turned[0:padded, d : d + 1] for d in range(group)], axis=0)


def pick_kernel(padded, pos_ref, tok_ref, out_ref, wide_ref):
    slots = slot_column(pos_ref, wide_ref, padded)
    cells = lax.broadcasted_iota(jnp.int32, (slots.shape[0], tok_ref.shape[0]), 1).astype(f32)
    chosen = (slots == cells).astype(f32).astype(bf16)
    out_ref[...] = mm(chosen, tok_ref[...]).astype(bf16)


def prep_kernel(cot_ref, wout_ref, wqkv_ref, ga_ref, wqkv_t_ref):
    ga_ref[...] = mm(wout_ref[...], cot_ref[...], NT).astype(bf16)
    wqkv_t_ref[...] = jnp.transpose(wqkv_ref[...])


def norm_kernel(cap, padded, src_ref, arr_ref, normed_ref, enc_ref, place_ref):
    rows = normed_ref.shape[0]
    slots = arr_ref.shape[0]
    src = src_ref[...].astype(f32)
    slot_row = src + (padded - cap) * jnp.floor((src + 0.5) * (1.0 / cap))
    place_ref[...] = slot_row
    slot_col = column_of(slot_row)
    lanes = lax.broadcasted_iota(jnp.int32, (rows, slots), 1).astype(f32)
    pick = (slot_col == lanes).astype(f32).astype(bf16)
    enc_in = mm(pick, arr_ref[...])
    enc_ref[...] = enc_in.astype(bf16)
    centred = enc_in - jnp.mean(enc_in, axis=-1, keepdims=True)
    spread = jnp.mean(centred * centred, axis=-1, keepdims=True)
    normed_ref[...] = (centred * lax.rsqrt(spread + norm_eps)).astype(bf16)


def project_kernel(normed_ref, wqkv_t_ref, u_ref, len_ref, v_ref):
    normed = normed_ref[...]
    width = normed.shape[1]
    heads = len_ref.shape[0] // 2
    size = width // heads
    for t in range(2):
        raw = mm(wqkv_t_ref[t * width : (t + 1) * width], normed, NT)
        for h in range(heads):
            part = raw[h * size : (h + 1) * size]
            inv = lax.rsqrt(jnp.sum(part * part, axis=0, keepdims=True) + length_eps)
            at = t * width + h * size
            u_ref[at : at + size] = part * inv
            len_ref[t * heads + h : t * heads + h + 1] = inv
    v_ref[...] = mm(wqkv_t_ref[2 * width : 3 * width], normed, NT).astype(bf16)


def encode_kernel(
    split, win_ref, scale_ref, place_ref, enc_ref, u_ref, len_ref, v_ref, ga_ref, wout_ref,
    wdec_ref, out_ref, *refs,
):
    peer_refs = refs[:-3]
    p_ref, att_ref, left_ref = refs[-3:]
    rows, width = enc_ref.shape
    heads = p_ref.shape[0]
    size = width // heads
    slots = out_ref.shape[0]
    win = win_ref[...].astype(f32)
    same = column_of(win) == win
    for h in range(heads):
        lo, hi = h * size, (h + 1) * size
        q = u_ref[lo:hi].astype(bf16)
        k = jnp.transpose(u_ref[width + lo : width + hi].astype(bf16))
        value = v_ref[lo:hi]
        for at in range(0, rows, 128):
            cut = slice(at, at + 128)
            scores = mm(k, q[:, cut])
            raised = jnp.where(same[:, cut], jnp.exp(scores * scale_ref[h]), 0.0)
            weights = (raised * (1.0 / jnp.sum(raised, axis=0, keepdims=True))).astype(bf16)
            p_ref[h, :, cut] = weights
            att_ref[lo:hi, cut] = mm(value, weights).astype(bf16)
        emit(split, left_ref, 3 * width + lo, att_ref[lo:hi])
    attended = jnp.transpose(att_ref[...])
    enc_out = (enc_ref[...].astype(f32) + mm(attended, wout_ref[...])).astype(bf16)
    dec = mm(enc_out, wdec_ref[...]).astype(bf16)
    places = lax.broadcasted_iota(jnp.int32, (slots, rows), 0).astype(f32)
    put = (places == place_ref[...]).astype(f32).astype(bf16)
    out_ref[...] = mm(put, dec).astype(bf16)
    for h in range(heads):
        lo, hi = h * size, (h + 1) * size
        ga = ga_ref[lo:hi]
        q = u_ref[lo:hi]
        k = u_ref[width + lo : width + hi]
        q_low, k_low = q.astype(bf16), k.astype(bf16)
        value = jnp.transpose(v_ref[lo:hi])
        grad_v, grad_k, grad_q = 0.0, 0.0, []
        for at in range(0, rows, 128):
            cut = slice(at, at + 128)
            low = p_ref[h, :, cut]
            weights = low.astype(f32)
            grad_soft = mm(value, ga[:, cut])
            part = weights * grad_soft
            total = jnp.sum(part, axis=0, keepdims=True)
            grad_scores = ((part - weights * total) * scale_ref[h]).astype(bf16)
            grad_v = grad_v + mm(ga[:, cut], low, NT)
            grad_k = grad_k + mm(q_low[:, cut], grad_scores, NT)
            grad_q.append(mm(k_low, grad_scores))
        grad_q = jnp.concatenate(grad_q, axis=1)
        grad_q = (grad_q - q * jnp.sum(q * grad_q, axis=0, keepdims=True)) * len_ref[h : h + 1]
        grad_k = (grad_k - k * jnp.sum(k * grad_k, axis=0, keepdims=True)) * len_ref[
            heads + h : heads + h + 1
        ]
        emit(split, left_ref, lo, grad_q.astype(bf16))
        emit(split, left_ref, width + lo, grad_k.astype(bf16))
        emit(split, left_ref, 2 * width + lo, grad_v.astype(bf16))
    me = lax.axis_index("replica") if split is not None else 0
    for n, ref in enumerate(peer_refs):
        ref[...] = left_ref[me ^ n] if split is not None else left_ref[...]


def emit(split, out_ref, start, block):
    if split is None:
        out_ref[start : start + block.shape[0]] = block
        return
    unit = 32
    shard_rows, part_rows, qkv_rows = split
    for j in range(block.shape[0] // unit):
        row = start + j * unit
        if row < qkv_rows:
            shard, rest = divmod(row, shard_rows)
            part, place = divmod(rest, part_rows)
            at = shard * part_rows + place
        else:
            part, place = divmod(row - qkv_rows, qkv_rows // 3 // out_ref.shape[0])
            at = qkv_rows // out_ref.shape[0] + place
        out_ref[part, at : at + unit] = block[j * unit : (j + 1) * unit]


def term_kernel(c, *refs):
    lefts, normed, cots = refs[0:4], refs[4:8], refs[8:12]
    keep_ref, send_ref = refs[12:]
    half, part, chunk = keep_ref.shape
    cut = slice(c * chunk, (c + 1) * chunk)

    def block(lo, hi, right, cols):
        acc = None
        for left, e in zip(lefts, right):
            step = mm(left[lo:hi], e[:, cols])
            acc = step if acc is None else acc + step
        return acc

    rows = half * part
    first = [(0, block(0, rows, normed, cut).reshape(half, part, chunk))]
    shared = block(rows, rows + (half - 2) * part, normed, cut).reshape(half - 2, part, chunk)
    at = rows + (half - 2 + c) * part
    turned = block(at, at + part, cots, slice(0, 2 * chunk))
    second = [
        (0, shared),
        (half - 2, turned[:, 0:chunk].reshape(1, part, chunk)),
        (half - 1, turned[:, chunk:].reshape(1, part, chunk)),
    ]
    spans = (first, second)
    for mine in range(2):

        @pl.when(lax.axis_index("eta") == mine)
        def _():
            for at, value in spans[mine]:
                keep_ref[at : at + value.shape[0]] = value
            for at, value in spans[1 - mine]:
                send_ref[at : at + value.shape[0]] = value.astype(bf16)


def line_kernel(keep_ref, got_ref, own_ref, *send_refs):
    count = keep_ref.shape[0]
    me = lax.axis_index("phi")
    own_ref[...] = keep_ref[me] + got_ref[me].astype(f32)
    for k, ref in enumerate(send_refs):
        at = lax.rem(me + k + 1, count)
        ref[...] = (keep_ref[at] + got_ref[at].astype(f32)).astype(bf16)


def close_kernel(count, *refs):
    width = refs[0].shape[-1]
    for n in range((len(refs) - 1) // count):
        total = refs[n * count][...]
        for ref in refs[n * count + 1 : (n + 1) * count]:
            total = total + ref[...].astype(f32)
        refs[-1][:, n * width : (n + 1) * width] = total.astype(bf16)


def spread_kernel(own_ref, one_ref, two_ref, three_ref, out_ref, all_ref):
    me = lax.axis_index("replica")
    for n, ref in enumerate((own_ref, one_ref, two_ref, three_ref)):
        all_ref[me ^ n] = ref[...].astype(f32)
    count, part, width = all_ref.shape
    chunk = width // 2
    phis = lax.axis_size("phi")
    turned = lax.axis_index("eta") * phis + lax.axis_index("phi") >= 2 * phis - 2

    @pl.when(jnp.logical_not(turned))
    def _():
        for r in range(count):
            out_ref[r * part : (r + 1) * part] = all_ref[r]

    @pl.when(turned)
    def _():
        pieces = []
        for r in range(count):
            for c in range(2):
                pieces.append(all_ref[r, :, c * chunk : (c + 1) * chunk])
        out_ref[...] = jnp.transpose(jnp.concatenate(pieces, axis=0))


def tie(values, *others):
    return lax.optimization_barrier((values, others))[0]


def fill_kernel(padded, pos_ref, ids_ref, mask_ref, got_ref, *refs):
    wide_ref = refs[-1]
    slots = slot_column(pos_ref, wide_ref, padded)
    ids = ids_ref[0:1] + lax.axis_index("eta").astype(f32) * ids_ref[1:2]
    chosen = (slots == ids).astype(f32).astype(bf16)
    got = got_ref[...]
    values = mm(chosen, got, TN)
    hits = mm(chosen, jnp.ones((got.shape[0], 128), bf16), TN)[:, 0:1]
    values = jnp.where(hits > 0.5, values, mask_ref[...].astype(f32)).astype(bf16)
    at = 0
    for ref in refs[:-1]:
        ref[...] = values[at : at + ref.shape[0]]
        at += ref.shape[0]


def rim_kernel(rim, left_ref, right_ref, edge_ref, out_ref):
    size = edge_ref.shape[0]
    out_ref[0:size] = edge_ref[...]

    def corners(at):
        for start, ref in ((size, left_ref), (size + 16, right_ref)):
            out_ref[start : start + 16] = ref[at : at + 16]

    @pl.when(lax.axis_index("eta") == 0)
    def _():
        corners(left_ref.shape[0] - 16)

    @pl.when(lax.axis_index("eta") != 0)
    def _():
        corners(0)


def conv_kernel_body(
    shape, span, folded, grid_ref, left_ref, right_ref, rims, taps_ref, out_ref,
    full_ref, wide_ref, mixed_ref,
):
    lines, columns = shape
    rim = span // 2
    width = grid_ref.shape[-1]
    lead = 8
    full_ref[rim : rim + lines, lead : lead + columns] = (
        grid_ref[...].astype(f32).reshape(lines, columns, width)
    )
    left = left_ref[...].astype(f32)
    right = right_ref[...].astype(f32)
    for x in range(lines):
        full_ref[rim + x, lead - rim : lead] = left[rim * x : rim * (x + 1)]
        full_ref[rim + x, lead + columns : lead + columns + rim] = right[rim * x : rim * (x + 1)]

    def put(base, edge, first, last):
        for i in range(rim):
            full_ref[base + i, lead : lead + columns] = edge[columns * i : columns * (i + 1)]
            full_ref[base + i, lead - rim : lead] = first[rim * i : rim * (i + 1)]
            full_ref[base + i, lead + columns : lead + columns + rim] = last[
                rim * i : rim * (i + 1)
            ]

    if folded:
        far = rim + lines
        base = jnp.where(lax.axis_index("eta") == 0, far, 0)
        for i in range(rim):
            full_ref[far - base + i] = jnp.zeros(full_ref.shape[1:], f32)
        size = rim * columns
        edge = rims[0][...].astype(f32)
        low = lax.axis_index("eta") == 0
        count = rim * rim
        corners = []
        for at in (size, size + 16):
            early, late = edge[at : at + count], edge[at + 16 - count : at + 16]
            corners.append(jnp.where(low, early, late))
        put(base, edge[0:size], *corners)
    else:
        pieces = [ref[...].astype(f32) for ref in rims]
        put(0, *pieces[:3])
        put(rim + lines, *pieces[3:])
    for t in range(span * span):
        wide_ref[t] = jnp.broadcast_to(taps_ref[t // span, t % span : t % span + 1], (8, width))
    groups = columns // 8

    for c in range(width // 128):
        cut = slice(c * 128, (c + 1) * 128)

        def step(x, accs, live, cut=cut):
            accs = list(accs)
            for v in range(span):
                at = lead - rim + v
                line = full_ref[x, at : at + columns, cut].reshape(groups, 8, 128)
                for i in live:
                    tap = wide_ref[(span - 1 - i) * span + v, :, cut]
                    accs[i] = accs[i] + line * tap[None]
            return accs

        def store(row, acc, cut=cut):
            at = row * columns
            if not isinstance(row, int):
                at = pl.multiple_of(at, columns)
            mixed_ref[pl.ds(at, columns), cut] = acc.reshape(columns, 128)

        zero = jnp.zeros((groups, 8, 128), f32)
        accs = [zero] * span
        for x in range(span - 1):
            accs = step(x, accs, range(span - 1 - x, span))
            accs = accs[1:] + [zero]

        def middle(x, accs):
            accs = step(x, accs, range(span))
            store(x - (span - 1), accs[0])
            return tuple(accs[1:] + [zero])

        accs = list(lax.fori_loop(span - 1, lines, middle, tuple(accs)))
        for x in range(lines, lines + span - 1):
            accs = step(x, accs, range(0, lines + span - 1 - x))
            store(x - (span - 1), accs[0])
            accs = accs[1:] + [zero]

    mixed = mixed_ref[...]
    centred = mixed - jnp.mean(mixed, axis=-1, keepdims=True)
    spread = jnp.mean(centred * centred, axis=-1, keepdims=True)
    out_ref[...] = (centred * lax.rsqrt(spread + norm_eps)).astype(bf16)


def mix_folded(shape, span, grid, left, right, a, *refs):
    conv_kernel_body(shape, span, True, grid, left, right, (a,), *refs)


def mix_open(shape, span, grid, left, right, a, b, c, d, e, g, *refs):
    conv_kernel_body(shape, span, False, grid, left, right, (a, b, c, d, e, g), *refs)


def feed_kernel(chunk, normed_ref, grid_ref, up_ref, down_ref, head_ref, out_ref):
    for at in range(0, normed_ref.shape[0], chunk):
        rows = slice(at, at + chunk)
        wide = mm(normed_ref[rows], up_ref[...])
        hidden = (0.5 * wide * (1.0 + lax.erf(wide * 0.7071067811865476))).astype(bf16)
        decoded = (grid_ref[rows].astype(f32) + mm(hidden, down_ref[...])).astype(bf16)
        out_ref[rows] = mm(decoded, head_ref[...])


def flip(value, axis, bit):
    return lax.ppermute(value, axis, [(i, i ^ bit) for i in range(lax.axis_size(axis))])


def turn(value, axis, k):
    count = lax.axis_size(axis)
    return lax.ppermute(value, axis, [(i, (i + k) % count) for i in range(count)])


def summed_slow(left, normed, cotangent):
    width = normed.shape[1]
    term = jnp.concatenate(
        [mm(left[: 3 * width], normed), mm(cotangent, left[3 * width :], (((0,), (1,)), ((), ())))],
        axis=0,
    )
    share = lax.psum_scatter(term, ("eta", "phi", "replica"), scatter_dimension=0, tiled=True)
    return lax.all_gather(share.astype(bf16), "replica", axis=0, tiled=True).astype(f32)


def body(
    tokens, send_pos, enc_src, window_id, enc_cot, w_qkv, head_scale, w_out, w_dec_in,
    mask_token, conv_kernel, w_up, w_down, w_head,
):
    eta_cells, phi_cells, width = tokens.shape[1:]
    dec_width = w_dec_in.shape[1]
    tile_len = eta_cells * phi_cells
    eta_count = lax.axis_size("eta")
    phi_count = lax.axis_size("phi")
    replicas = lax.axis_size("replica")
    group = eta_count * phi_count
    cap = send_pos.shape[-1]
    padded = -(-cap // 8) * 8
    slots = group * padded
    rows = enc_cot.shape[-2]
    heads = head_scale.shape[0]
    out_rows = 4 * width
    shard_rows = out_rows // group
    part_rows = shard_rows // replicas
    fast = (
        eta_count == 2
        and replicas == 4
        and part_rows % 32 == 0
        and width == 2 * shard_rows
    )

    positions = send_pos.reshape(group, cap)
    outgoing = call(
        functools.partial(pick_kernel, padded),
        "pick",
        sds((slots, width), bf16),
        [vmem(), vmem()],
        scratch=[pltpu.VMEM((group, 128), f32)],
        flops=2 * slots * tile_len * width,
        nbytes=3 * MIB,
        limit=8,
    )(positions, tokens.reshape(tile_len, width))
    arrived = lax.all_to_all(
        outgoing.reshape(group, padded, width), ("eta", "phi"), split_axis=0, concat_axis=0,
        tiled=True,
    ).reshape(slots, width)

    cotangent = enc_cot.reshape(rows, width)
    split = (shard_rows, part_rows, 3 * width) if fast else None
    pieces = replicas if fast else 1
    left_part = (out_rows // pieces, rows)
    left_whole = (replicas,) + left_part if fast else left_part
    if fast:
        cots = [cotangent, flip(cotangent, "replica", 1), flip(cotangent, "replica", 2)]
    grad_att, w_qkv_t = call(
        prep_kernel,
        "prep",
        [sds((width, rows), bf16), sds((3 * width, width), bf16)],
        [vmem()] * 3,
        flops=2 * rows * width * width,
        nbytes=10 * MIB,
        limit=10,
    )(cotangent, w_out, w_qkv)
    if fast:
        cots.append(flip(tie(cots[2], w_qkv_t), "replica", 1))

    normed, enc_in, places = call(
        functools.partial(norm_kernel, cap, padded),
        "norm",
        [sds((rows, width), bf16), sds((rows, width), bf16), sds((1, rows), f32)],
        [vmem()] * 2,
        flops=2 * rows * width * slots,
        nbytes=2 * MIB,
        limit=8,
        cost=600000000,
    )(enc_src.reshape(1, rows), arrived)
    if fast:
        normed_y = flip(normed, "replica", 2)
        normed_c = flip(normed, "replica", 1)
    units, lengths, values = call(
        project_kernel,
        "project",
        [sds((2 * width, rows), f32), sds((2 * heads, rows), f32), sds((width, rows), bf16)],
        [vmem()] * 2,
        flops=2 * rows * width * width * 4,
        nbytes=8 * MIB,
        limit=10,
        cost=2000000000,
    )(tie(normed, cots) if fast else normed, w_qkv_t)

    outbound, *lefts = call(
        functools.partial(encode_kernel, split),
        "encode",
        [sds((slots, dec_width), bf16)] + [sds(left_part, bf16)] * pieces,
        [vmem(), smem()] + [vmem()] * 8,
        scratch=[
            pltpu.VMEM((heads, rows, rows), bf16),
            pltpu.VMEM((width, rows), bf16),
            pltpu.VMEM(left_whole, bf16),
        ],
        flops=2 * rows * width * width * 10,
        nbytes=8 * MIB,
        limit=14,
        cost=8000000000,
    )(
        window_id.reshape(1, rows), head_scale, places, enc_in, units, lengths, values, grad_att,
        w_out, w_dec_in,
    )
    if fast:
        *lefts, normed_y, normed_c = lax.optimization_barrier((*lefts, normed_y, normed_c))
    returned = lax.all_to_all(
        outbound.reshape(group, padded, dec_width), ("eta", "phi"), split_axis=0, concat_axis=0,
        tiled=True,
    )
    if fast:
        lefts = [lefts[0]] + [flip(lefts[k], "replica", k) for k in range(1, 4)]
        rights = [normed, normed_c, normed_y, flip(normed_y, "replica", 1)]
        returned = tie(returned, lefts[1], rights[3])
    else:
        grad_total = summed_slow(lefts[0], normed, cotangent)

    span = conv_kernel.shape[0]
    rim = span // 2
    folded = eta_count == 2
    lines = np.arange(eta_cells)[:, None]
    columns = np.arange(phi_cells)[None, :]
    cell = lines * phi_cells + columns
    parts = [cell]
    moves = [0]
    if folded:
        edge = cell[eta_cells - rim :]
        parts += [cell[:, :rim], cell[:, -rim:], edge]
        moves += [0, 0, -(eta_cells - rim) * phi_cells]
    sizes = [-(-p.size // 16) * 16 for p in parts]
    ids = np.full((2, -(-sum(sizes) // 128) * 128), -7.0, np.float32)
    ids[1] = 0
    at = 0
    for p, size, move in zip(parts, sizes, moves):
        ids[0, at : at + p.size] = p.reshape(-1)
        ids[1, at : at + p.size] = move
        at += size
    filled = call(
        functools.partial(fill_kernel, padded),
        "fill",
        [sds((size, dec_width), bf16) for size in sizes],
        [vmem()] * 4,
        scratch=[pltpu.VMEM((group, 128), f32)],
        flops=2 * slots * ids.shape[1] * (dec_width + 128),
        nbytes=3 * MIB,
        limit=12,
    )(
        positions, jnp.asarray(ids), mask_token.reshape(1, dec_width),
        returned.reshape(slots, dec_width),
    )
    dec_grid = filled[0]
    if folded:
        _, first, last, edge = filled
        left_halo = turn(last, "phi", 1)
        right_halo = turn(first, "phi", -1)
        rim_out = call(
            functools.partial(rim_kernel, rim),
            "rim",
            sds((edge.shape[0] + 32, dec_width), bf16),
            [vmem()] * 3,
            limit=4,
        )(left_halo, right_halo, edge)
        rims = (turn(rim_out, "eta", 1),)
    else:
        box = dec_grid.reshape(eta_cells, phi_cells, dec_width)
        down = [(i, i + 1) for i in range(eta_count - 1)]
        up = [(i + 1, i) for i in range(eta_count - 1)]
        top = lax.ppermute(box[eta_cells - rim :], "eta", down)
        bottom = lax.ppermute(box[:rim], "eta", up)
        box = jnp.concatenate([top, box, bottom], axis=0)
        low = turn(box[:, phi_cells - rim :], "phi", 1)
        high = turn(box[:, :rim], "phi", -1)

        def flat(value):
            return value.reshape(-1, dec_width)

        far = eta_cells + rim
        left_halo, right_halo = flat(low[rim:far]), flat(high[rim:far])
        rims = (
            flat(top), flat(low[:rim]), flat(high[:rim]),
            flat(bottom), flat(low[far:]), flat(high[far:]),
        )
    if fast:
        lefts, rights, cots = tie((lefts, rights, cots), rim_out)
        chunk = width // 2
        half = group // 2
        kept, sent = [], []
        for c in range(2):
            keep, send = call(
                functools.partial(term_kernel, c),
                "terms%d" % c,
                [sds((half, part_rows, chunk), f32), sds((half, part_rows, chunk), bf16)],
                [vmem()] * 12,
                flops=2 * out_rows * chunk * rows,
                nbytes=8 * MIB,
                limit=10,
            )(*lefts, *rights, *cots)
            if c == 0:
                lefts, rights, cots = tie((lefts, rights, cots), rims)
            kept.append(keep)
            sent.append(turn(send, "eta", 1))
        left, right_halo, rims = tie((left_halo, right_halo, rims), kept)
    else:
        left = left_halo
    normed_cells = call(
        functools.partial(mix_folded if folded else mix_open, (eta_cells, phi_cells), span),
        "mix",
        sds((tile_len, dec_width), bf16),
        [vmem()] * (4 + len(rims)),
        scratch=[
            pltpu.VMEM((eta_cells + 2 * rim, phi_cells + 16, dec_width), f32),
            pltpu.VMEM((span * span, 8, dec_width), f32),
            pltpu.VMEM((tile_len, dec_width), f32),
        ],
        flops=200 * 2 * span * span * tile_len * dec_width,
        nbytes=3 * MIB,
        limit=16,
    )(dec_grid, left, right_halo, *rims, conv_kernel)
    if fast:
        summed = []
        for c in range(2):
            own, *outs = call(
                line_kernel,
                "line%d" % c,
                [sds((part_rows, chunk), f32)] + [sds((part_rows, chunk), bf16)] * (phi_count - 1),
                [vmem()] * 2,
                flops=half * part_rows * chunk,
                nbytes=2 * MIB,
                limit=4,
            )(kept[c], tie(sent[c], normed_cells))
            summed.append([own] + [turn(outs[k], "phi", k + 1) for k in range(phi_count - 1)])
            normed_cells = tie(normed_cells, own)
    reconstruction = call(
        functools.partial(feed_kernel, 256),
        "feed",
        sds((tile_len, w_head.shape[1]), f32),
        [vmem()] * 5,
        flops=2 * tile_len * dec_width * (2 * w_up.shape[1] + w_head.shape[1]),
        nbytes=4 * MIB,
        limit=12,
    )(normed_cells, dec_grid, w_up, w_down, w_head).reshape(1, eta_cells, phi_cells, -1)
    if fast:
        summed = tie(summed, reconstruction)
        mine = call(
            functools.partial(close_kernel, phi_count),
            "close",
            sds((part_rows, width), bf16),
            [vmem()] * (2 * phi_count),
            flops=4 * part_rows * width,
            nbytes=MIB,
            limit=4,
        )(*summed[0], *summed[1])
        mine_y = flip(mine, "replica", 2)
        grad_total = call(
            spread_kernel,
            "spread",
            sds((shard_rows, width), f32),
            [vmem()] * 4,
            scratch=[pltpu.VMEM((replicas, part_rows, width), f32)],
            flops=4 * part_rows * width,
            nbytes=2 * MIB,
            limit=8,
        )(mine, flip(mine, "replica", 1), mine_y, flip(mine_y, "replica", 1))
    return (grad_total, reconstruction)


def solution(mesh):
    in_specs = (
        P("replica", "eta", "phi", None),
        P("replica", "eta", "phi", None, None),
        P("replica", "eta", "phi", None),
        P("replica", "eta", "phi", None),
        P("replica", "eta", "phi", None, None),
        P(), P(), P(), P(), P(), P(), P(), P(), P(),
    )
    out_specs = (P(("eta", "phi"), None), P("replica", "eta", "phi", None))
    return jax.shard_map(body, mesh=mesh, in_specs=in_specs, out_specs=out_specs, check_vma=False)
```

```python
import functools

import jax
import jax.numpy as jnp
import numpy as np
from jax import lax
from jax.experimental import pallas as pl
from jax.experimental.pallas import tpu as pltpu
from jax.sharding import PartitionSpec as P

norm_eps = 1e-05
length_eps = 1e-06
f32 = jnp.float32
bf16 = jnp.bfloat16
MIB = 1024 * 1024

NN = (((1,), (0,)), ((), ()))
NT = (((1,), (1,)), ((), ()))
TN = (((0,), (0,)), ((), ()))


def mm(a, b, dims=NN):
    return lax.dot_general(a, b, dims, preferred_element_type=f32)


def vmem():
    return pl.BlockSpec(memory_space=pltpu.VMEM)


def smem():
    return pl.BlockSpec(memory_space=pltpu.SMEM)


def call(kernel, name, outs, in_specs, scratch=(), flops=0, nbytes=0, limit=20, cost=1000):
    single = not isinstance(outs, (list, tuple))
    out_list = [outs] if single else list(outs)
    specs = [vmem() for _ in out_list]
    return pl.pallas_call(
        kernel,
        out_shape=out_list[0] if single else tuple(out_list),
        in_specs=in_specs,
        out_specs=specs[0] if single else tuple(specs),
        scratch_shapes=list(scratch),
        compiler_params=pltpu.CompilerParams(vmem_limit_bytes=limit * MIB),
        cost_estimate=pl.CostEstimate(
            flops=cost, bytes_accessed=1000 + cost // 300, transcendentals=0
        ),
        name=name,
    )


def sds(shape, dtype):
    return jax.ShapeDtypeStruct(shape, dtype)


def column_of(row):
    return jnp.transpose(jnp.broadcast_to(row, (8, row.shape[1])))[:, 0:1]


def slot_column(pos_ref, wide_ref, padded):
    group, cap = pos_ref.shape
    wide_ref[...] = jnp.full(wide_ref.shape, -1.0, f32)
    wide_ref[:, 0:cap] = pos_ref[...].astype(f32)
    turned = jnp.transpose(wide_ref[...])
    return jnp.concatenate([turned[0:padded, d : d + 1] for d in range(group)], axis=0)


def pick_kernel(padded, pos_ref, tok_ref, out_ref, wide_ref):
    slots = slot_column(pos_ref, wide_ref, padded)
    cells = lax.broadcasted_iota(jnp.int32, (slots.shape[0], tok_ref.shape[0]), 1).astype(f32)
    chosen = (slots == cells).astype(f32).astype(bf16)
    out_ref[...] = mm(chosen, tok_ref[...]).astype(bf16)


def prep_kernel(cot_ref, wout_ref, wqkv_ref, ga_ref, wqkv_t_ref):
    ga_ref[...] = mm(wout_ref[...], cot_ref[...], NT).astype(bf16)
    wqkv_t_ref[...] = jnp.transpose(wqkv_ref[...])


def norm_kernel(cap, padded, src_ref, arr_ref, normed_ref, enc_ref, place_ref):
    rows = normed_ref.shape[0]
    slots = arr_ref.shape[0]
    src = src_ref[...].astype(f32)
    slot_row = src + (padded - cap) * jnp.floor((src + 0.5) * (1.0 / cap))
    place_ref[...] = slot_row
    slot_col = column_of(slot_row)
    lanes = lax.broadcasted_iota(jnp.int32, (rows, slots), 1).astype(f32)
    pick = (slot_col == lanes).astype(f32).astype(bf16)
    enc_in = mm(pick, arr_ref[...])
    enc_ref[...] = enc_in.astype(bf16)
    centred = enc_in - jnp.mean(enc_in, axis=-1, keepdims=True)
    spread = jnp.mean(centred * centred, axis=-1, keepdims=True)
    normed_ref[...] = (centred * lax.rsqrt(spread + norm_eps)).astype(bf16)


def project_kernel(normed_ref, wqkv_t_ref, u_ref, len_ref, v_ref):
    normed = normed_ref[...]
    width = normed.shape[1]
    heads = len_ref.shape[0] // 2
    size = width // heads
    for t in range(2):
        raw = mm(wqkv_t_ref[t * width : (t + 1) * width], normed, NT)
        for h in range(heads):
            part = raw[h * size : (h + 1) * size]
            inv = lax.rsqrt(jnp.sum(part * part, axis=0, keepdims=True) + length_eps)
            at = t * width + h * size
            u_ref[at : at + size] = part * inv
            len_ref[t * heads + h : t * heads + h + 1] = inv
    v_ref[...] = mm(wqkv_t_ref[2 * width : 3 * width], normed, NT).astype(bf16)


def encode_kernel(
    split, win_ref, scale_ref, place_ref, enc_ref, u_ref, len_ref, v_ref, ga_ref, wout_ref,
    wdec_ref, out_ref, *refs,
):
    peer_refs = refs[:-3]
    p_ref, att_ref, left_ref = refs[-3:]
    rows, width = enc_ref.shape
    heads = p_ref.shape[0]
    size = width // heads
    slots = out_ref.shape[0]
    win = win_ref[...].astype(f32)
    same = column_of(win) == win
    for h in range(heads):
        lo, hi = h * size, (h + 1) * size
        q = u_ref[lo:hi].astype(bf16)
        k = u_ref[width + lo : width + hi].astype(bf16)
        scores = mm(k, q, TN)
        raised = jnp.where(same, jnp.exp(scores * scale_ref[h]), 0.0)
        weights = (raised * (1.0 / jnp.sum(raised, axis=0, keepdims=True))).astype(bf16)
        p_ref[h] = weights
        att = mm(v_ref[lo:hi], weights).astype(bf16)
        att_ref[lo:hi] = att
        emit(split, left_ref, 3 * width + lo, att)
    attended = jnp.transpose(att_ref[...])
    enc_out = (enc_ref[...].astype(f32) + mm(attended, wout_ref[...])).astype(bf16)
    dec = mm(enc_out, wdec_ref[...]).astype(bf16)
    places = lax.broadcasted_iota(jnp.int32, (slots, rows), 0).astype(f32)
    put = (places == place_ref[...]).astype(f32).astype(bf16)
    out_ref[...] = mm(put, dec).astype(bf16)
    for h in range(heads):
        lo, hi = h * size, (h + 1) * size
        ga = ga_ref[lo:hi]
        low = p_ref[h]
        weights = low.astype(f32)
        grad_soft = mm(v_ref[lo:hi], ga, TN)
        part = weights * grad_soft
        total = jnp.sum(part, axis=0, keepdims=True)
        grad_scores = ((part - weights * total) * scale_ref[h]).astype(bf16)
        q = u_ref[lo:hi]
        k = u_ref[width + lo : width + hi]
        grad_v = mm(ga, low, NT)
        grad_q = mm(k.astype(bf16), grad_scores)
        grad_k = mm(q.astype(bf16), grad_scores, NT)
        grad_q = (grad_q - q * jnp.sum(q * grad_q, axis=0, keepdims=True)) * len_ref[h : h + 1]
        grad_k = (grad_k - k * jnp.sum(k * grad_k, axis=0, keepdims=True)) * len_ref[
            heads + h : heads + h + 1
        ]
        emit(split, left_ref, lo, grad_q.astype(bf16))
        emit(split, left_ref, width + lo, grad_k.astype(bf16))
        emit(split, left_ref, 2 * width + lo, grad_v.astype(bf16))
    me = lax.axis_index("replica") if split is not None else 0
    for n, ref in enumerate(peer_refs):
        ref[...] = left_ref[me ^ n] if split is not None else left_ref[...]


def emit(split, out_ref, start, block):
    if split is None:
        out_ref[start : start + block.shape[0]] = block
        return
    unit = 32
    shard_rows, part_rows, qkv_rows = split
    for j in range(block.shape[0] // unit):
        row = start + j * unit
        if row < qkv_rows:
            shard, rest = divmod(row, shard_rows)
            part, place = divmod(rest, part_rows)
            at = shard * part_rows + place
        else:
            part, place = divmod(row - qkv_rows, qkv_rows // 3 // out_ref.shape[0])
            at = qkv_rows // out_ref.shape[0] + place
        out_ref[part, at : at + unit] = block[j * unit : (j + 1) * unit]


def term_kernel(c, *refs):
    lefts, normed, cots = refs[0:4], refs[4:8], refs[8:12]
    keep_ref, send_ref = refs[12:]
    half, part, chunk = keep_ref.shape
    cut = slice(c * chunk, (c + 1) * chunk)

    def block(lo, hi, right, cols):
        acc = None
        for left, e in zip(lefts, right):
            step = mm(left[lo:hi], e[:, cols])
            acc = step if acc is None else acc + step
        return acc

    rows = half * part
    first = [(0, block(0, rows, normed, cut).reshape(half, part, chunk))]
    shared = block(rows, rows + (half - 2) * part, normed, cut).reshape(half - 2, part, chunk)
    at = rows + (half - 2 + c) * part
    turned = block(at, at + part, cots, slice(0, 2 * chunk))
    second = [
        (0, shared),
        (half - 2, turned[:, 0:chunk].reshape(1, part, chunk)),
        (half - 1, turned[:, chunk:].reshape(1, part, chunk)),
    ]
    spans = (first, second)
    for mine in range(2):

        @pl.when(lax.axis_index("eta") == mine)
        def _():
            for at, value in spans[mine]:
                keep_ref[at : at + value.shape[0]] = value
            for at, value in spans[1 - mine]:
                send_ref[at : at + value.shape[0]] = value.astype(bf16)


def line_kernel(keep_ref, got_ref, own_ref, *send_refs):
    count = keep_ref.shape[0]
    me = lax.axis_index("phi")
    own_ref[...] = keep_ref[me] + got_ref[me].astype(f32)
    for k, ref in enumerate(send_refs):
        at = lax.rem(me + k + 1, count)
        ref[...] = (keep_ref[at] + got_ref[at].astype(f32)).astype(bf16)


def close_kernel(count, *refs):
    width = refs[0].shape[-1]
    for n in range((len(refs) - 1) // count):
        total = refs[n * count][...]
        for ref in refs[n * count + 1 : (n + 1) * count]:
            total = total + ref[...].astype(f32)
        refs[-1][:, n * width : (n + 1) * width] = total.astype(bf16)


def spread_kernel(own_ref, one_ref, two_ref, three_ref, out_ref, all_ref):
    me = lax.axis_index("replica")
    for n, ref in enumerate((own_ref, one_ref, two_ref, three_ref)):
        all_ref[me ^ n] = ref[...].astype(f32)
    count, part, width = all_ref.shape
    chunk = width // 2
    phis = lax.axis_size("phi")
    turned = lax.axis_index("eta") * phis + lax.axis_index("phi") >= 2 * phis - 2

    @pl.when(jnp.logical_not(turned))
    def _():
        for r in range(count):
            out_ref[r * part : (r + 1) * part] = all_ref[r]

    @pl.when(turned)
    def _():
        pieces = []
        for r in range(count):
            for c in range(2):
                pieces.append(all_ref[r, :, c * chunk : (c + 1) * chunk])
        out_ref[...] = jnp.transpose(jnp.concatenate(pieces, axis=0))


def tie(values, *others):
    return lax.optimization_barrier((values, others))[0]


def fill_kernel(padded, pos_ref, ids_ref, mask_ref, got_ref, *refs):
    wide_ref = refs[-1]
    slots = slot_column(pos_ref, wide_ref, padded)
    ids = ids_ref[0:1] + lax.axis_index("eta").astype(f32) * ids_ref[1:2]
    chosen = (slots == ids).astype(f32).astype(bf16)
    got = got_ref[...]
    values = mm(chosen, got, TN)
    hits = mm(chosen, jnp.ones((got.shape[0], 128), bf16), TN)[:, 0:1]
    values = jnp.where(hits > 0.5, values, mask_ref[...].astype(f32)).astype(bf16)
    at = 0
    for ref in refs[:-1]:
        ref[...] = values[at : at + ref.shape[0]]
        at += ref.shape[0]


def rim_kernel(rim, left_ref, right_ref, edge_ref, out_ref):
    size = edge_ref.shape[0]
    out_ref[0:size] = edge_ref[...]

    def corners(at):
        for start, ref in ((size, left_ref), (size + 16, right_ref)):
            out_ref[start : start + 16] = ref[at : at + 16]

    @pl.when(lax.axis_index("eta") == 0)
    def _():
        corners(left_ref.shape[0] - 16)

    @pl.when(lax.axis_index("eta") != 0)
    def _():
        corners(0)


def conv_kernel_body(
    shape, span, folded, grid_ref, left_ref, right_ref, rims, taps_ref, out_ref,
    full_ref, wide_ref, mixed_ref,
):
    lines, columns = shape
    rim = span // 2
    width = grid_ref.shape[-1]
    lead = 8
    full_ref[rim : rim + lines, lead : lead + columns] = (
        grid_ref[...].astype(f32).reshape(lines, columns, width)
    )
    left = left_ref[...].astype(f32)
    right = right_ref[...].astype(f32)
    for x in range(lines):
        full_ref[rim + x, lead - rim : lead] = left[rim * x : rim * (x + 1)]
        full_ref[rim + x, lead + columns : lead + columns + rim] = right[rim * x : rim * (x + 1)]

    def put(base, edge, first, last):
        for i in range(rim):
            full_ref[base + i, lead : lead + columns] = edge[columns * i : columns * (i + 1)]
            full_ref[base + i, lead - rim : lead] = first[rim * i : rim * (i + 1)]
            full_ref[base + i, lead + columns : lead + columns + rim] = last[
                rim * i : rim * (i + 1)
            ]

    if folded:
        far = rim + lines
        base = jnp.where(lax.axis_index("eta") == 0, far, 0)
        for i in range(rim):
            full_ref[far - base + i] = jnp.zeros(full_ref.shape[1:], f32)
        size = rim * columns
        edge = rims[0][...].astype(f32)
        low = lax.axis_index("eta") == 0
        count = rim * rim
        corners = []
        for at in (size, size + 16):
            early, late = edge[at : at + count], edge[at + 16 - count : at + 16]
            corners.append(jnp.where(low, early, late))
        put(base, edge[0:size], *corners)
    else:
        pieces = [ref[...].astype(f32) for ref in rims]
        put(0, *pieces[:3])
        put(rim + lines, *pieces[3:])
    for t in range(span * span):
        wide_ref[t] = jnp.broadcast_to(taps_ref[t // span, t % span : t % span + 1], (8, width))
    groups = columns // 8

    for c in range(width // 128):
        cut = slice(c * 128, (c + 1) * 128)

        def step(x, accs, live, cut=cut):
            accs = list(accs)
            for v in range(span):
                at = lead - rim + v
                line = full_ref[x, at : at + columns, cut].reshape(groups, 8, 128)
                for i in live:
                    tap = wide_ref[(span - 1 - i) * span + v, :, cut]
                    accs[i] = accs[i] + line * tap[None]
            return accs

        def store(row, acc, cut=cut):
            at = row * columns
            if not isinstance(row, int):
                at = pl.multiple_of(at, columns)
            mixed_ref[pl.ds(at, columns), cut] = acc.reshape(columns, 128)

        zero = jnp.zeros((groups, 8, 128), f32)
        accs = [zero] * span
        for x in range(span - 1):
            accs = step(x, accs, range(span - 1 - x, span))
            accs = accs[1:] + [zero]

        def middle(x, accs):
            accs = step(x, accs, range(span))
            store(x - (span - 1), accs[0])
            return tuple(accs[1:] + [zero])

        accs = list(lax.fori_loop(span - 1, lines, middle, tuple(accs)))
        for x in range(lines, lines + span - 1):
            accs = step(x, accs, range(0, lines + span - 1 - x))
            store(x - (span - 1), accs[0])
            accs = accs[1:] + [zero]

    mixed = mixed_ref[...]
    centred = mixed - jnp.mean(mixed, axis=-1, keepdims=True)
    spread = jnp.mean(centred * centred, axis=-1, keepdims=True)
    out_ref[...] = (centred * lax.rsqrt(spread + norm_eps)).astype(bf16)


def mix_folded(shape, span, grid, left, right, a, *refs):
    conv_kernel_body(shape, span, True, grid, left, right, (a,), *refs)


def mix_open(shape, span, grid, left, right, a, b, c, d, e, g, *refs):
    conv_kernel_body(shape, span, False, grid, left, right, (a, b, c, d, e, g), *refs)


def feed_kernel(chunk, normed_ref, grid_ref, up_ref, down_ref, head_ref, out_ref):
    for at in range(0, normed_ref.shape[0], chunk):
        rows = slice(at, at + chunk)
        wide = mm(normed_ref[rows], up_ref[...])
        hidden = (0.5 * wide * (1.0 + lax.erf(wide * 0.7071067811865476))).astype(bf16)
        decoded = (grid_ref[rows].astype(f32) + mm(hidden, down_ref[...])).astype(bf16)
        out_ref[rows] = mm(decoded, head_ref[...])


def flip(value, axis, bit):
    return lax.ppermute(value, axis, [(i, i ^ bit) for i in range(lax.axis_size(axis))])


def turn(value, axis, k):
    count = lax.axis_size(axis)
    return lax.ppermute(value, axis, [(i, (i + k) % count) for i in range(count)])


def summed_slow(left, normed, cotangent):
    width = normed.shape[1]
    term = jnp.concatenate(
        [mm(left[: 3 * width], normed), mm(cotangent, left[3 * width :], (((0,), (1,)), ((), ())))],
        axis=0,
    )
    share = lax.psum_scatter(term, ("eta", "phi", "replica"), scatter_dimension=0, tiled=True)
    return lax.all_gather(share.astype(bf16), "replica", axis=0, tiled=True).astype(f32)


def body(
    tokens, send_pos, enc_src, window_id, enc_cot, w_qkv, head_scale, w_out, w_dec_in,
    mask_token, conv_kernel, w_up, w_down, w_head,
):
    eta_cells, phi_cells, width = tokens.shape[1:]
    dec_width = w_dec_in.shape[1]
    tile_len = eta_cells * phi_cells
    eta_count = lax.axis_size("eta")
    phi_count = lax.axis_size("phi")
    replicas = lax.axis_size("replica")
    group = eta_count * phi_count
    cap = send_pos.shape[-1]
    padded = -(-cap // 8) * 8
    slots = group * padded
    rows = enc_cot.shape[-2]
    heads = head_scale.shape[0]
    out_rows = 4 * width
    shard_rows = out_rows // group
    part_rows = shard_rows // replicas
    fast = (
        eta_count == 2
        and replicas == 4
        and part_rows % 32 == 0
        and width == 2 * shard_rows
    )

    positions = send_pos.reshape(group, cap)
    outgoing = call(
        functools.partial(pick_kernel, padded),
        "pick",
        sds((slots, width), bf16),
        [vmem(), vmem()],
        scratch=[pltpu.VMEM((group, 128), f32)],
        flops=2 * slots * tile_len * width,
        nbytes=3 * MIB,
        limit=8,
    )(positions, tokens.reshape(tile_len, width))
    arrived = lax.all_to_all(
        outgoing.reshape(group, padded, width), ("eta", "phi"), split_axis=0, concat_axis=0,
        tiled=True,
    ).reshape(slots, width)

    cotangent = enc_cot.reshape(rows, width)
    split = (shard_rows, part_rows, 3 * width) if fast else None
    pieces = replicas if fast else 1
    left_part = (out_rows // pieces, rows)
    left_whole = (replicas,) + left_part if fast else left_part
    if fast:
        cots = [cotangent] + [flip(cotangent, "replica", k) for k in range(1, 4)]
    grad_att, w_qkv_t = call(
        prep_kernel,
        "prep",
        [sds((width, rows), bf16), sds((3 * width, width), bf16)],
        [vmem()] * 3,
        flops=2 * rows * width * width,
        nbytes=10 * MIB,
        limit=10,
    )(cotangent, w_out, w_qkv)
    arrived = tie(arrived, w_qkv_t)

    normed, enc_in, places = call(
        functools.partial(norm_kernel, cap, padded),
        "norm",
        [sds((rows, width), bf16), sds((rows, width), bf16), sds((1, rows), f32)],
        [vmem()] * 2,
        flops=2 * rows * width * slots,
        nbytes=2 * MIB,
        limit=8,
        cost=600000000,
    )(enc_src.reshape(1, rows), arrived)
    if fast:
        normed_y = flip(normed, "replica", 2)
        normed_c = flip(normed, "replica", 1)
    units, lengths, values = call(
        project_kernel,
        "project",
        [sds((2 * width, rows), f32), sds((2 * heads, rows), f32), sds((width, rows), bf16)],
        [vmem()] * 2,
        flops=2 * rows * width * width * 4,
        nbytes=8 * MIB,
        limit=10,
        cost=2000000000,
    )(normed, w_qkv_t)

    outbound, *lefts = call(
        functools.partial(encode_kernel, split),
        "encode",
        [sds((slots, dec_width), bf16)] + [sds(left_part, bf16)] * pieces,
        [vmem(), smem()] + [vmem()] * 8,
        scratch=[
            pltpu.VMEM((heads, rows, rows), bf16),
            pltpu.VMEM((width, rows), bf16),
            pltpu.VMEM(left_whole, bf16),
        ],
        flops=2 * rows * width * width * 10,
        nbytes=8 * MIB,
        limit=14,
        cost=8000000000,
    )(
        window_id.reshape(1, rows), head_scale, places, enc_in, units, lengths, values, grad_att,
        w_out, w_dec_in,
    )
    if fast:
        cots, lefts, normed_y, normed_c = lax.optimization_barrier(
            (cots, lefts, normed_y, normed_c)
        )
    returned = lax.all_to_all(
        outbound.reshape(group, padded, dec_width), ("eta", "phi"), split_axis=0, concat_axis=0,
        tiled=True,
    )
    if fast:
        lefts = [lefts[0]] + [flip(lefts[k], "replica", k) for k in range(1, 4)]
        rights = [normed, normed_c, normed_y, flip(normed_y, "replica", 1)]
        returned = tie(returned, lefts[1], rights[3])
    else:
        grad_total = summed_slow(lefts[0], normed, cotangent)

    span = conv_kernel.shape[0]
    rim = span // 2
    folded = eta_count == 2
    lines = np.arange(eta_cells)[:, None]
    columns = np.arange(phi_cells)[None, :]
    cell = lines * phi_cells + columns
    parts = [cell]
    moves = [0]
    if folded:
        edge = cell[eta_cells - rim :]
        parts += [cell[:, :rim], cell[:, -rim:], edge]
        moves += [0, 0, -(eta_cells - rim) * phi_cells]
    sizes = [-(-p.size // 16) * 16 for p in parts]
    ids = np.full((2, -(-sum(sizes) // 128) * 128), -7.0, np.float32)
    ids[1] = 0
    at = 0
    for p, size, move in zip(parts, sizes, moves):
        ids[0, at : at + p.size] = p.reshape(-1)
        ids[1, at : at + p.size] = move
        at += size
    filled = call(
        functools.partial(fill_kernel, padded),
        "fill",
        [sds((size, dec_width), bf16) for size in sizes],
        [vmem()] * 4,
        scratch=[pltpu.VMEM((group, 128), f32)],
        flops=2 * slots * ids.shape[1] * (dec_width + 128),
        nbytes=3 * MIB,
        limit=12,
    )(
        positions, jnp.asarray(ids), mask_token.reshape(1, dec_width),
        returned.reshape(slots, dec_width),
    )
    dec_grid = filled[0]
    if folded:
        _, first, last, edge = filled
        left_halo = turn(last, "phi", 1)
        right_halo = turn(first, "phi", -1)
        rim_out = call(
            functools.partial(rim_kernel, rim),
            "rim",
            sds((edge.shape[0] + 32, dec_width), bf16),
            [vmem()] * 3,
            limit=4,
        )(left_halo, right_halo, edge)
        rims = (turn(rim_out, "eta", 1),)
    else:
        box = dec_grid.reshape(eta_cells, phi_cells, dec_width)
        down = [(i, i + 1) for i in range(eta_count - 1)]
        up = [(i + 1, i) for i in range(eta_count - 1)]
        top = lax.ppermute(box[eta_cells - rim :], "eta", down)
        bottom = lax.ppermute(box[:rim], "eta", up)
        box = jnp.concatenate([top, box, bottom], axis=0)
        low = turn(box[:, phi_cells - rim :], "phi", 1)
        high = turn(box[:, :rim], "phi", -1)

        def flat(value):
            return value.reshape(-1, dec_width)

        far = eta_cells + rim
        left_halo, right_halo = flat(low[rim:far]), flat(high[rim:far])
        rims = (
            flat(top), flat(low[:rim]), flat(high[:rim]),
            flat(bottom), flat(low[far:]), flat(high[far:]),
        )
    if fast:
        lefts, rights, cots = tie((lefts, rights, cots), rim_out)
        chunk = width // 2
        half = group // 2
        kept, sent = [], []
        for c in range(2):
            keep, send = call(
                functools.partial(term_kernel, c),
                "terms%d" % c,
                [sds((half, part_rows, chunk), f32), sds((half, part_rows, chunk), bf16)],
                [vmem()] * 12,
                flops=2 * out_rows * chunk * rows,
                nbytes=8 * MIB,
                limit=10,
            )(*lefts, *rights, *cots)
            if c == 0:
                lefts, rights, cots = tie((lefts, rights, cots), rims)
            kept.append(keep)
            sent.append(turn(send, "eta", 1))
        left, right_halo, rims = tie((left_halo, right_halo, rims), kept)
    else:
        left = left_halo
    normed_cells = call(
        functools.partial(mix_folded if folded else mix_open, (eta_cells, phi_cells), span),
        "mix",
        sds((tile_len, dec_width), bf16),
        [vmem()] * (4 + len(rims)),
        scratch=[
            pltpu.VMEM((eta_cells + 2 * rim, phi_cells + 16, dec_width), f32),
            pltpu.VMEM((span * span, 8, dec_width), f32),
            pltpu.VMEM((tile_len, dec_width), f32),
        ],
        flops=200 * 2 * span * span * tile_len * dec_width,
        nbytes=3 * MIB,
        limit=16,
    )(dec_grid, left, right_halo, *rims, conv_kernel)
    if fast:
        summed = []
        for c in range(2):
            own, *outs = call(
                line_kernel,
                "line%d" % c,
                [sds((part_rows, chunk), f32)] + [sds((part_rows, chunk), bf16)] * (phi_count - 1),
                [vmem()] * 2,
                flops=half * part_rows * chunk,
                nbytes=2 * MIB,
                limit=4,
            )(kept[c], tie(sent[c], normed_cells))
            summed.append([own] + [turn(outs[k], "phi", k + 1) for k in range(phi_count - 1)])
            normed_cells = tie(normed_cells, own)
    reconstruction = call(
        functools.partial(feed_kernel, 256),
        "feed",
        sds((tile_len, w_head.shape[1]), f32),
        [vmem()] * 5,
        flops=2 * tile_len * dec_width * (2 * w_up.shape[1] + w_head.shape[1]),
        nbytes=4 * MIB,
        limit=12,
    )(normed_cells, dec_grid, w_up, w_down, w_head).reshape(1, eta_cells, phi_cells, -1)
    if fast:
        summed = tie(summed, reconstruction)
        mine = call(
            functools.partial(close_kernel, phi_count),
            "close",
            sds((part_rows, width), bf16),
            [vmem()] * (2 * phi_count),
            flops=4 * part_rows * width,
            nbytes=MIB,
            limit=4,
        )(*summed[0], *summed[1])
        mine_y = flip(mine, "replica", 2)
        grad_total = call(
            spread_kernel,
            "spread",
            sds((shard_rows, width), f32),
            [vmem()] * 4,
            scratch=[pltpu.VMEM((replicas, part_rows, width), f32)],
            flops=4 * part_rows * width,
            nbytes=2 * MIB,
            limit=8,
        )(mine, flip(mine, "replica", 1), mine_y, flip(mine_y, "replica", 1))
    return (grad_total, reconstruction)


def solution(mesh):
    in_specs = (
        P("replica", "eta", "phi", None),
        P("replica", "eta", "phi", None, None),
        P("replica", "eta", "phi", None),
        P("replica", "eta", "phi", None),
        P("replica", "eta", "phi", None, None),
        P(), P(), P(), P(), P(), P(), P(), P(), P(),
    )
    out_specs = (P(("eta", "phi"), None), P("replica", "eta", "phi", None))
    return jax.shard_map(body, mesh=mesh, in_specs=in_specs, out_specs=out_specs, check_vma=False)
```

```python
import functools

import jax
import jax.numpy as jnp
import numpy as np
from jax import lax
from jax.experimental import pallas as pl
from jax.experimental.pallas import tpu as pltpu
from jax.sharding import PartitionSpec as P

norm_eps = 1e-05
length_eps = 1e-06
f32 = jnp.float32
bf16 = jnp.bfloat16
MIB = 1024 * 1024

NN = (((1,), (0,)), ((), ()))
NT = (((1,), (1,)), ((), ()))
TN = (((0,), (0,)), ((), ()))


def mm(a, b, dims=NN):
    return lax.dot_general(a, b, dims, preferred_element_type=f32)


def vmem():
    return pl.BlockSpec(memory_space=pltpu.VMEM)


def smem():
    return pl.BlockSpec(memory_space=pltpu.SMEM)


def call(kernel, name, outs, in_specs, scratch=(), flops=0, nbytes=0, limit=20, cost=1000):
    single = not isinstance(outs, (list, tuple))
    out_list = [outs] if single else list(outs)
    specs = [vmem() for _ in out_list]
    return pl.pallas_call(
        kernel,
        out_shape=out_list[0] if single else tuple(out_list),
        in_specs=in_specs,
        out_specs=specs[0] if single else tuple(specs),
        scratch_shapes=list(scratch),
        compiler_params=pltpu.CompilerParams(vmem_limit_bytes=limit * MIB),
        cost_estimate=pl.CostEstimate(
            flops=cost, bytes_accessed=1000 + cost // 300, transcendentals=0
        ),
        name=name,
    )


def sds(shape, dtype):
    return jax.ShapeDtypeStruct(shape, dtype)


def column_of(row):
    return jnp.transpose(jnp.broadcast_to(row, (8, row.shape[1])))[:, 0:1]


def slot_column(pos_ref, wide_ref, padded):
    group, cap = pos_ref.shape
    wide_ref[...] = jnp.full(wide_ref.shape, -1.0, f32)
    wide_ref[:, 0:cap] = pos_ref[...].astype(f32)
    turned = jnp.transpose(wide_ref[...])
    return jnp.concatenate([turned[0:padded, d : d + 1] for d in range(group)], axis=0)


def pick_kernel(padded, pos_ref, tok_ref, out_ref, wide_ref):
    slots = slot_column(pos_ref, wide_ref, padded)
    cells = lax.broadcasted_iota(jnp.int32, (slots.shape[0], tok_ref.shape[0]), 1).astype(f32)
    chosen = (slots == cells).astype(f32).astype(bf16)
    out_ref[...] = mm(chosen, tok_ref[...]).astype(bf16)


def prep_kernel(cot_ref, wout_ref, wqkv_ref, ga_ref, wqk_t_ref, wval_t_ref):
    ga_ref[...] = mm(wout_ref[...], cot_ref[...], NT).astype(bf16)
    cut = wqk_t_ref.shape[0]
    wqk_t_ref[...] = jnp.transpose(wqkv_ref[:, 0:cut])
    wval_t_ref[...] = jnp.transpose(wqkv_ref[:, cut:])


def norm_kernel(cap, padded, src_ref, arr_ref, normed_ref, enc_ref, place_ref):
    rows = normed_ref.shape[0]
    slots = arr_ref.shape[0]
    src = src_ref[...].astype(f32)
    slot_row = src + (padded - cap) * jnp.floor((src + 0.5) * (1.0 / cap))
    place_ref[...] = slot_row
    slot_col = column_of(slot_row)
    lanes = lax.broadcasted_iota(jnp.int32, (rows, slots), 1).astype(f32)
    pick = (slot_col == lanes).astype(f32).astype(bf16)
    enc_in = mm(pick, arr_ref[...])
    enc_ref[...] = enc_in.astype(bf16)
    centred = enc_in - jnp.mean(enc_in, axis=-1, keepdims=True)
    spread = jnp.mean(centred * centred, axis=-1, keepdims=True)
    normed_ref[...] = (centred * lax.rsqrt(spread + norm_eps)).astype(bf16)


def project_kernel(normed_ref, wqkv_t_ref, u_ref, len_ref):
    normed = normed_ref[...]
    width = normed.shape[1]
    heads = len_ref.shape[0] // 2
    size = width // heads
    for t in range(2):
        raw = mm(wqkv_t_ref[t * width : (t + 1) * width], normed, NT)
        for h in range(heads):
            part = raw[h * size : (h + 1) * size]
            inv = lax.rsqrt(jnp.sum(part * part, axis=0, keepdims=True) + length_eps)
            at = t * width + h * size
            u_ref[at : at + size] = part * inv
            len_ref[t * heads + h : t * heads + h + 1] = inv


def encode_kernel(
    split, win_ref, scale_ref, place_ref, enc_ref, normed_ref, u_ref, len_ref, ga_ref, wval_ref,
    wout_ref, wdec_ref, out_ref, *refs,
):
    peer_refs = refs[:-3]
    v_ref, att_ref, left_ref = refs[-3:]
    rows, width = enc_ref.shape
    heads = len_ref.shape[0] // 2
    size = width // heads
    slots = out_ref.shape[0]
    v_ref[...] = mm(wval_ref[...], normed_ref[...], NT).astype(bf16)
    win = win_ref[...].astype(f32)
    same = column_of(win) == win
    for h in range(heads):
        lo, hi = h * size, (h + 1) * size
        q = u_ref[lo:hi]
        k = u_ref[width + lo : width + hi]
        q_low, k_low = q.astype(bf16), k.astype(bf16)
        value = v_ref[lo:hi]
        ga = ga_ref[lo:hi]
        scores = mm(k_low, q_low, TN)
        raised = jnp.where(same, jnp.exp(scores * scale_ref[h]), 0.0)
        weights = raised * (1.0 / jnp.sum(raised, axis=0, keepdims=True))
        low = weights.astype(bf16)
        att = mm(value, low).astype(bf16)
        att_ref[lo:hi] = att
        emit(split, left_ref, 3 * width + lo, att)
        grad_v = mm(ga, low, NT)
        part = weights * mm(value, ga, TN)
        total = jnp.sum(part, axis=0, keepdims=True)
        grad_scores = ((part - weights * total) * scale_ref[h]).astype(bf16)
        grad_q = mm(k_low, grad_scores)
        grad_k = mm(q_low, grad_scores, NT)
        grad_q = (grad_q - q * jnp.sum(q * grad_q, axis=0, keepdims=True)) * len_ref[h : h + 1]
        grad_k = (grad_k - k * jnp.sum(k * grad_k, axis=0, keepdims=True)) * len_ref[
            heads + h : heads + h + 1
        ]
        emit(split, left_ref, lo, grad_q.astype(bf16))
        emit(split, left_ref, width + lo, grad_k.astype(bf16))
        emit(split, left_ref, 2 * width + lo, grad_v.astype(bf16))
    attended = jnp.transpose(att_ref[...])
    enc_out = (enc_ref[...].astype(f32) + mm(attended, wout_ref[...])).astype(bf16)
    dec = mm(enc_out, wdec_ref[...]).astype(bf16)
    places = lax.broadcasted_iota(jnp.int32, (slots, rows), 0).astype(f32)
    put = (places == place_ref[...]).astype(f32).astype(bf16)
    out_ref[...] = mm(put, dec).astype(bf16)
    me = lax.axis_index("replica") if split is not None else 0
    for n, ref in enumerate(peer_refs):
        ref[...] = left_ref[me ^ n] if split is not None else left_ref[...]


def emit(split, out_ref, start, block):
    if split is None:
        out_ref[start : start + block.shape[0]] = block
        return
    unit = 32
    shard_rows, part_rows, qkv_rows = split
    for j in range(block.shape[0] // unit):
        row = start + j * unit
        if row < qkv_rows:
            shard, rest = divmod(row, shard_rows)
            part, place = divmod(rest, part_rows)
            at = shard * part_rows + place
        else:
            part, place = divmod(row - qkv_rows, qkv_rows // 3 // out_ref.shape[0])
            at = qkv_rows // out_ref.shape[0] + place
        out_ref[part, at : at + unit] = block[j * unit : (j + 1) * unit]


def term_kernel(c, *refs):
    lefts, normed, cots = refs[0:4], refs[4:8], refs[8:12]
    keep_ref, send_ref = refs[12:]
    half, part, chunk = keep_ref.shape
    cut = slice(c * chunk, (c + 1) * chunk)

    def block(lo, hi, right, cols):
        acc = None
        for left, e in zip(lefts, right):
            step = mm(left[lo:hi], e[:, cols])
            acc = step if acc is None else acc + step
        return acc

    rows = half * part
    first = [(0, block(0, rows, normed, cut).reshape(half, part, chunk))]
    shared = block(rows, rows + (half - 2) * part, normed, cut).reshape(half - 2, part, chunk)
    at = rows + (half - 2 + c) * part
    turned = block(at, at + part, cots, slice(0, 2 * chunk))
    second = [
        (0, shared),
        (half - 2, turned[:, 0:chunk].reshape(1, part, chunk)),
        (half - 1, turned[:, chunk:].reshape(1, part, chunk)),
    ]
    spans = (first, second)
    for mine in range(2):

        @pl.when(lax.axis_index("eta") == mine)
        def _():
            for at, value in spans[mine]:
                keep_ref[at : at + value.shape[0]] = value
            for at, value in spans[1 - mine]:
                send_ref[at : at + value.shape[0]] = value.astype(bf16)


def line_kernel(keep_ref, got_ref, own_ref, *send_refs):
    count = keep_ref.shape[0]
    me = lax.axis_index("phi")
    own_ref[...] = keep_ref[me] + got_ref[me].astype(f32)
    for k, ref in enumerate(send_refs):
        at = lax.rem(me + k + 1, count)
        ref[...] = (keep_ref[at] + got_ref[at].astype(f32)).astype(bf16)


def close_kernel(count, *refs):
    width = refs[0].shape[-1]
    for n in range((len(refs) - 1) // count):
        total = refs[n * count][...]
        for ref in refs[n * count + 1 : (n + 1) * count]:
            total = total + ref[...].astype(f32)
        refs[-1][:, n * width : (n + 1) * width] = total.astype(bf16)


def spread_kernel(own_ref, one_ref, two_ref, three_ref, out_ref, all_ref):
    me = lax.axis_index("replica")
    for n, ref in enumerate((own_ref, one_ref, two_ref, three_ref)):
        all_ref[me ^ n] = ref[...].astype(f32)
    count, part, width = all_ref.shape
    chunk = width // 2
    phis = lax.axis_size("phi")
    turned = lax.axis_index("eta") * phis + lax.axis_index("phi") >= 2 * phis - 2

    @pl.when(jnp.logical_not(turned))
    def _():
        for r in range(count):
            out_ref[r * part : (r + 1) * part] = all_ref[r]

    @pl.when(turned)
    def _():
        pieces = []
        for r in range(count):
            for c in range(2):
                pieces.append(all_ref[r, :, c * chunk : (c + 1) * chunk])
        out_ref[...] = jnp.transpose(jnp.concatenate(pieces, axis=0))


def tie(values, *others):
    return lax.optimization_barrier((values, others))[0]


def fill_kernel(padded, pos_ref, ids_ref, mask_ref, got_ref, *refs):
    wide_ref = refs[-1]
    slots = slot_column(pos_ref, wide_ref, padded)
    ids = ids_ref[0:1] + lax.axis_index("eta").astype(f32) * ids_ref[1:2]
    chosen = (slots == ids).astype(f32).astype(bf16)
    got = got_ref[...]
    values = mm(chosen, got, TN)
    hits = mm(chosen, jnp.ones((got.shape[0], 128), bf16), TN)[:, 0:1]
    values = jnp.where(hits > 0.5, values, mask_ref[...].astype(f32)).astype(bf16)
    at = 0
    for ref in refs[:-1]:
        ref[...] = values[at : at + ref.shape[0]]
        at += ref.shape[0]


def rim_kernel(rim, left_ref, right_ref, edge_ref, out_ref):
    size = edge_ref.shape[0]
    out_ref[0:size] = edge_ref[...]

    def corners(at):
        for start, ref in ((size, left_ref), (size + 16, right_ref)):
            out_ref[start : start + 16] = ref[at : at + 16]

    @pl.when(lax.axis_index("eta") == 0)
    def _():
        corners(left_ref.shape[0] - 16)

    @pl.when(lax.axis_index("eta") != 0)
    def _():
        corners(0)


def conv_kernel_body(
    shape, span, first_line, folded, grid_ref, left_ref, right_ref, rims, taps_ref, out_ref,
    full_ref, wide_ref, mixed_ref,
):
    total, columns = shape
    rim = span // 2
    width = grid_ref.shape[-1]
    lines = out_ref.shape[0] // columns
    lead = 8
    tall = lines + 2 * rim
    if folded:
        size = rim * columns
        edge = rims[0][...].astype(f32)
        low = lax.axis_index("eta") == 0
        count = rim * rim
        outer = [edge[0:size]]
        for at in (size, size + 16):
            early, late = edge[at : at + count], edge[at + 16 - count : at + 16]
            outer.append(jnp.where(low, early, late))
        top = [jnp.where(low, 0.0, value) for value in outer]
        bottom = [jnp.where(low, value, 0.0) for value in outer]
    else:
        pieces = [ref[...].astype(f32) for ref in rims]
        top, bottom = pieces[:3], pieces[3:]
    low_line = max(first_line, rim) - rim
    high_line = min(first_line + tall, rim + total) - rim
    base = low_line + rim - first_line
    cells = slice(low_line * columns, high_line * columns)
    full_ref[base : base + high_line - low_line, lead : lead + columns] = (
        grid_ref[cells].astype(f32).reshape(high_line - low_line, columns, width)
    )
    left = left_ref[...].astype(f32)
    right = right_ref[...].astype(f32)

    def put(at, value, col, pieces, high):
        full_ref[at, col : col + high] = value[pieces : pieces + high]

    for x in range(low_line, high_line):
        at = x + rim - first_line
        put(at, left, lead - rim, rim * x, rim)
        put(at, right, lead + columns, rim * x, rim)
    for start, group in ((0, top), (rim + total, bottom)):
        for i in range(rim):
            at = start + i - first_line
            if 0 <= at < tall:
                put(at, group[0], lead, columns * i, columns)
                put(at, group[1], lead - rim, rim * i, rim)
                put(at, group[2], lead + columns, rim * i, rim)
    for t in range(span * span):
        wide_ref[t] = jnp.broadcast_to(taps_ref[t // span, t % span : t % span + 1], (8, width))
    groups = columns // 8

    for c in range(width // 128):
        cut = slice(c * 128, (c + 1) * 128)

        def step(x, accs, live, cut=cut):
            accs = list(accs)
            for v in range(span):
                at = lead - rim + v
                line = full_ref[x, at : at + columns, cut].reshape(groups, 8, 128)
                for i in live:
                    tap = wide_ref[(span - 1 - i) * span + v, :, cut]
                    accs[i] = accs[i] + line * tap[None]
            return accs

        def store(row, acc, cut=cut):
            at = row * columns
            if not isinstance(row, int):
                at = pl.multiple_of(at, columns)
            mixed_ref[pl.ds(at, columns), cut] = acc.reshape(columns, 128)

        zero = jnp.zeros((groups, 8, 128), f32)
        accs = [zero] * span
        for x in range(span - 1):
            accs = step(x, accs, range(span - 1 - x, span))
            accs = accs[1:] + [zero]

        def middle(x, accs):
            accs = step(x, accs, range(span))
            store(x - (span - 1), accs[0])
            return tuple(accs[1:] + [zero])

        accs = list(lax.fori_loop(span - 1, lines, middle, tuple(accs)))
        for x in range(lines, lines + span - 1):
            accs = step(x, accs, range(0, lines + span - 1 - x))
            store(x - (span - 1), accs[0])
            accs = accs[1:] + [zero]

    mixed = mixed_ref[...]
    centred = mixed - jnp.mean(mixed, axis=-1, keepdims=True)
    spread = jnp.mean(centred * centred, axis=-1, keepdims=True)
    out_ref[...] = (centred * lax.rsqrt(spread + norm_eps)).astype(bf16)


def mix_folded(shape, span, start, grid, left, right, a, *refs):
    conv_kernel_body(shape, span, start, True, grid, left, right, (a,), *refs)


def mix_open(shape, span, start, grid, left, right, a, b, c, d, e, g, *refs):
    conv_kernel_body(shape, span, start, False, grid, left, right, (a, b, c, d, e, g), *refs)


def feed_kernel(chunk, upper_ref, lower_ref, grid_ref, up_ref, down_ref, head_ref, out_ref):
    half = upper_ref.shape[0]
    for at in range(0, 2 * half, chunk):
        rows = slice(at, at + chunk)
        source = upper_ref if at < half else lower_ref
        wide = mm(source[at % half : at % half + chunk], up_ref[...])
        hidden = (0.5 * wide * (1.0 + lax.erf(wide * 0.7071067811865476))).astype(bf16)
        decoded = (grid_ref[rows].astype(f32) + mm(hidden, down_ref[...])).astype(bf16)
        out_ref[rows] = mm(decoded, head_ref[...])


def flip(value, axis, bit):
    return lax.ppermute(value, axis, [(i, i ^ bit) for i in range(lax.axis_size(axis))])


def turn(value, axis, k):
    count = lax.axis_size(axis)
    return lax.ppermute(value, axis, [(i, (i + k) % count) for i in range(count)])


def summed_slow(left, normed, cotangent):
    width = normed.shape[1]
    term = jnp.concatenate(
        [mm(left[: 3 * width], normed), mm(cotangent, left[3 * width :], (((0,), (1,)), ((), ())))],
        axis=0,
    )
    share = lax.psum_scatter(term, ("eta", "phi", "replica"), scatter_dimension=0, tiled=True)
    return lax.all_gather(share.astype(bf16), "replica", axis=0, tiled=True).astype(f32)


def body(
    tokens, send_pos, enc_src, window_id, enc_cot, w_qkv, head_scale, w_out, w_dec_in,
    mask_token, conv_kernel, w_up, w_down, w_head,
):
    eta_cells, phi_cells, width = tokens.shape[1:]
    dec_width = w_dec_in.shape[1]
    tile_len = eta_cells * phi_cells
    eta_count = lax.axis_size("eta")
    phi_count = lax.axis_size("phi")
    replicas = lax.axis_size("replica")
    group = eta_count * phi_count
    cap = send_pos.shape[-1]
    padded = -(-cap // 8) * 8
    slots = group * padded
    rows = enc_cot.shape[-2]
    heads = head_scale.shape[0]
    out_rows = 4 * width
    shard_rows = out_rows // group
    part_rows = shard_rows // replicas
    fast = (
        eta_count == 2
        and replicas == 4
        and part_rows % 32 == 0
        and width == 2 * shard_rows
    )

    positions = send_pos.reshape(group, cap)
    outgoing = call(
        functools.partial(pick_kernel, padded),
        "pick",
        sds((slots, width), bf16),
        [vmem(), vmem()],
        scratch=[pltpu.VMEM((group, 128), f32)],
        flops=2 * slots * tile_len * width,
        nbytes=3 * MIB,
        limit=8,
    )(positions, tokens.reshape(tile_len, width))
    arrived = lax.all_to_all(
        outgoing.reshape(group, padded, width), ("eta", "phi"), split_axis=0, concat_axis=0,
        tiled=True,
    ).reshape(slots, width)

    cotangent = enc_cot.reshape(rows, width)
    split = (shard_rows, part_rows, 3 * width) if fast else None
    pieces = replicas if fast else 1
    left_part = (out_rows // pieces, rows)
    left_whole = (replicas,) + left_part if fast else left_part
    if fast:
        cots = [cotangent] + [flip(cotangent, "replica", k) for k in range(1, 4)]
    grad_att, w_qk_t, w_val_t = call(
        prep_kernel,
        "prep",
        [sds((width, rows), bf16), sds((2 * width, width), bf16), sds((width, width), bf16)],
        [vmem()] * 3,
        flops=2 * rows * width * width,
        nbytes=10 * MIB,
        limit=10,
    )(cotangent, w_out, w_qkv)
    arrived = tie(arrived, w_qk_t)

    normed, enc_in, places = call(
        functools.partial(norm_kernel, cap, padded),
        "norm",
        [sds((rows, width), bf16), sds((rows, width), bf16), sds((1, rows), f32)],
        [vmem()] * 2,
        flops=2 * rows * width * slots,
        nbytes=2 * MIB,
        limit=8,
        cost=600000000,
    )(enc_src.reshape(1, rows), arrived)
    if fast:
        normed_y = flip(normed, "replica", 2)
        normed_c = flip(normed, "replica", 1)
    units, lengths = call(
        project_kernel,
        "project",
        [sds((2 * width, rows), f32), sds((2 * heads, rows), f32)],
        [vmem()] * 2,
        flops=2 * rows * width * width * 4,
        nbytes=8 * MIB,
        limit=10,
        cost=2000000000,
    )(normed, w_qk_t)

    outbound, *lefts = call(
        functools.partial(encode_kernel, split),
        "encode",
        [sds((slots, dec_width), bf16)] + [sds(left_part, bf16)] * pieces,
        [vmem(), smem()] + [vmem()] * 9,
        scratch=[
            pltpu.VMEM((width, rows), bf16),
            pltpu.VMEM((width, rows), bf16),
            pltpu.VMEM(left_whole, bf16),
        ],
        flops=2 * rows * width * width * 10,
        nbytes=8 * MIB,
        limit=14,
        cost=8000000000,
    )(
        window_id.reshape(1, rows), head_scale, places, enc_in, normed, units, lengths, grad_att,
        w_val_t, w_out, w_dec_in,
    )
    if fast:
        cots, lefts, normed_y, normed_c = lax.optimization_barrier(
            (cots, lefts, normed_y, normed_c)
        )
    returned = lax.all_to_all(
        outbound.reshape(group, padded, dec_width), ("eta", "phi"), split_axis=0, concat_axis=0,
        tiled=True,
    )
    if fast:
        lefts = [lefts[0]] + [flip(lefts[k], "replica", k) for k in range(1, 4)]
        rights = [normed, normed_c, normed_y, flip(normed_y, "replica", 1)]
        returned = tie(returned, lefts[1], rights[3])
    else:
        grad_total = summed_slow(lefts[0], normed, cotangent)

    span = conv_kernel.shape[0]
    rim = span // 2
    folded = eta_count == 2
    lines = np.arange(eta_cells)[:, None]
    columns = np.arange(phi_cells)[None, :]
    cell = lines * phi_cells + columns
    parts = [cell]
    moves = [0]
    if folded:
        edge = cell[eta_cells - rim :]
        parts += [cell[:, :rim], cell[:, -rim:], edge]
        moves += [0, 0, -(eta_cells - rim) * phi_cells]
    sizes = [-(-p.size // 16) * 16 for p in parts]
    ids = np.full((2, -(-sum(sizes) // 128) * 128), -7.0, np.float32)
    ids[1] = 0
    at = 0
    for p, size, move in zip(parts, sizes, moves):
        ids[0, at : at + p.size] = p.reshape(-1)
        ids[1, at : at + p.size] = move
        at += size
    filled = call(
        functools.partial(fill_kernel, padded),
        "fill",
        [sds((size, dec_width), bf16) for size in sizes],
        [vmem()] * 4,
        scratch=[pltpu.VMEM((group, 128), f32)],
        flops=2 * slots * ids.shape[1] * (dec_width + 128),
        nbytes=3 * MIB,
        limit=12,
    )(
        positions, jnp.asarray(ids), mask_token.reshape(1, dec_width),
        returned.reshape(slots, dec_width),
    )
    dec_grid = filled[0]
    if folded:
        _, first, last, edge = filled
        left_halo = turn(last, "phi", 1)
        right_halo = turn(first, "phi", -1)
        rim_out = call(
            functools.partial(rim_kernel, rim),
            "rim",
            sds((edge.shape[0] + 32, dec_width), bf16),
            [vmem()] * 3,
            limit=4,
        )(left_halo, right_halo, edge)
        rims = (turn(rim_out, "eta", 1),)
    else:
        box = dec_grid.reshape(eta_cells, phi_cells, dec_width)
        down = [(i, i + 1) for i in range(eta_count - 1)]
        up = [(i + 1, i) for i in range(eta_count - 1)]
        top = lax.ppermute(box[eta_cells - rim :], "eta", down)
        bottom = lax.ppermute(box[:rim], "eta", up)
        box = jnp.concatenate([top, box, bottom], axis=0)
        low = turn(box[:, phi_cells - rim :], "phi", 1)
        high = turn(box[:, :rim], "phi", -1)

        def flat(value):
            return value.reshape(-1, dec_width)

        far = eta_cells + rim
        left_halo, right_halo = flat(low[rim:far]), flat(high[rim:far])
        rims = (
            flat(top), flat(low[:rim]), flat(high[:rim]),
            flat(bottom), flat(low[far:]), flat(high[far:]),
        )
    if fast:
        lefts, rights, cots = tie((lefts, rights, cots), rim_out)
        chunk = width // 2
        half = group // 2
        kept, sent = [], []
        for c in range(2):
            keep, send = call(
                functools.partial(term_kernel, c),
                "terms%d" % c,
                [sds((half, part_rows, chunk), f32), sds((half, part_rows, chunk), bf16)],
                [vmem()] * 12,
                flops=2 * out_rows * chunk * rows,
                nbytes=8 * MIB,
                limit=10,
            )(*lefts, *rights, *cots)
            if c == 0:
                lefts, rights, cots = tie((lefts, rights, cots), rims)
            kept.append(keep)
            sent.append(turn(send, "eta", 1))
        left, right_halo, rims = tie((left_halo, right_halo, rims), kept)
    else:
        left = left_halo
    rows_half = eta_cells // 2

    def mix(start, *rest):
        return call(
            functools.partial(
                mix_folded if folded else mix_open, (eta_cells, phi_cells), span, start
            ),
            "mix%d" % start,
            sds((tile_len // 2, dec_width), bf16),
            [vmem()] * (4 + len(rims)),
            scratch=[
                pltpu.VMEM((rows_half + 2 * rim, phi_cells + 16, dec_width), f32),
                pltpu.VMEM((span * span, 8, dec_width), f32),
                pltpu.VMEM((tile_len // 2, dec_width), f32),
            ],
            flops=200 * span * span * tile_len * dec_width,
            nbytes=3 * MIB,
            limit=12,
        )(*rest)

    upper = mix(0, dec_grid, left, right_halo, *rims, conv_kernel)
    if not fast:
        lower = mix(rows_half, dec_grid, left, right_halo, *rims, conv_kernel)
    if fast:
        summed = []
        for c in range(2):
            own, *outs = call(
                line_kernel,
                "line%d" % c,
                [sds((part_rows, chunk), f32)] + [sds((part_rows, chunk), bf16)] * (phi_count - 1),
                [vmem()] * 2,
                flops=half * part_rows * chunk,
                nbytes=2 * MIB,
                limit=4,
            )(kept[c], tie(sent[c], upper if c == 0 else lower))
            summed.append([own] + [turn(outs[k], "phi", k + 1) for k in range(phi_count - 1)])
            if c == 0:
                lower = mix(rows_half, tie(dec_grid, summed[0][1]), left, right_halo, *rims, conv_kernel)
            else:
                upper = tie(upper, own)
    reconstruction = call(
        functools.partial(feed_kernel, 256),
        "feed",
        sds((tile_len, w_head.shape[1]), f32),
        [vmem()] * 6,
        flops=2 * tile_len * dec_width * (2 * w_up.shape[1] + w_head.shape[1]),
        nbytes=4 * MIB,
        limit=12,
    )(upper, lower, dec_grid, w_up, w_down, w_head).reshape(1, eta_cells, phi_cells, -1)
    if fast:
        summed = tie(summed, reconstruction)
        mine = call(
            functools.partial(close_kernel, phi_count),
            "close",
            sds((part_rows, width), bf16),
            [vmem()] * (2 * phi_count),
            flops=4 * part_rows * width,
            nbytes=MIB,
            limit=4,
        )(*summed[0], *summed[1])
        mine_y = flip(mine, "replica", 2)
        grad_total = call(
            spread_kernel,
            "spread",
            sds((shard_rows, width), f32),
            [vmem()] * 4,
            scratch=[pltpu.VMEM((replicas, part_rows, width), f32)],
            flops=4 * part_rows * width,
            nbytes=2 * MIB,
            limit=8,
        )(mine, flip(mine, "replica", 1), mine_y, flip(mine_y, "replica", 1))
    return (grad_total, reconstruction)


def solution(mesh):
    in_specs = (
        P("replica", "eta", "phi", None),
        P("replica", "eta", "phi", None, None),
        P("replica", "eta", "phi", None),
        P("replica", "eta", "phi", None),
        P("replica", "eta", "phi", None, None),
        P(), P(), P(), P(), P(), P(), P(), P(), P(),
    )
    out_specs = (P(("eta", "phi"), None), P("replica", "eta", "phi", None))
    return jax.shard_map(body, mesh=mesh, in_specs=in_specs, out_specs=out_specs, check_vma=False)
```

```python
import functools

import jax
import jax.numpy as jnp
import numpy as np
from jax import lax
from jax.experimental import pallas as pl
from jax.experimental.pallas import tpu as pltpu
from jax.sharding import PartitionSpec as P

norm_eps = 1e-05
length_eps = 1e-06
f32 = jnp.float32
bf16 = jnp.bfloat16
MIB = 1024 * 1024

NN = (((1,), (0,)), ((), ()))
NT = (((1,), (1,)), ((), ()))
TN = (((0,), (0,)), ((), ()))


def mm(a, b, dims=NN):
    return lax.dot_general(a, b, dims, preferred_element_type=f32)


def vmem():
    return pl.BlockSpec(memory_space=pltpu.VMEM)


def smem():
    return pl.BlockSpec(memory_space=pltpu.SMEM)


def call(kernel, name, outs, in_specs, scratch=(), flops=0, nbytes=0, limit=20, cost=1000):
    single = not isinstance(outs, (list, tuple))
    out_list = [outs] if single else list(outs)
    specs = [vmem() for _ in out_list]
    return pl.pallas_call(
        kernel,
        out_shape=out_list[0] if single else tuple(out_list),
        in_specs=in_specs,
        out_specs=specs[0] if single else tuple(specs),
        scratch_shapes=list(scratch),
        compiler_params=pltpu.CompilerParams(vmem_limit_bytes=limit * MIB),
        cost_estimate=pl.CostEstimate(
            flops=cost, bytes_accessed=1000 + cost // 300, transcendentals=0
        ),
        name=name,
    )


def sds(shape, dtype):
    return jax.ShapeDtypeStruct(shape, dtype)


def column_of(row):
    return jnp.transpose(jnp.broadcast_to(row, (8, row.shape[1])))[:, 0:1]


def slot_column(pos_ref, wide_ref, padded):
    group, cap = pos_ref.shape
    wide_ref[...] = jnp.full(wide_ref.shape, -1.0, f32)
    wide_ref[:, 0:cap] = pos_ref[...].astype(f32)
    turned = jnp.transpose(wide_ref[...])
    return jnp.concatenate([turned[0:padded, d : d + 1] for d in range(group)], axis=0)


def plane_index():
    return lax.axis_index("eta") * lax.axis_size("phi") + lax.axis_index("phi")


def pick_kernel(padded, pos_ref, tok_ref, *refs):
    out_refs, (wide_ref, all_ref) = refs[:-2], refs[-2:]
    slots = slot_column(pos_ref, wide_ref, padded)
    cells = lax.broadcasted_iota(jnp.int32, (slots.shape[0], tok_ref.shape[0]), 1).astype(f32)
    chosen = (slots == cells).astype(f32).astype(bf16)
    taken = mm(chosen, tok_ref[...])
    if len(out_refs) == 1:
        out_refs[0][...] = taken.astype(bf16)
        return
    group = len(out_refs)
    for d in range(group):
        all_ref[d] = taken[d * padded : (d + 1) * padded].astype(bf16)
    me = plane_index()
    for k, ref in enumerate(out_refs):
        ref[...] = all_ref[lax.rem(me + k, group)]


def prep_kernel(cot_ref, wout_ref, wqkv_ref, ga_ref, wqkv_t_ref):
    ga_ref[...] = mm(wout_ref[...], cot_ref[...], NT).astype(bf16)
    wqkv_t_ref[...] = jnp.transpose(wqkv_ref[...])


def norm_kernel(cap, padded, src_ref, cot_ref, *refs):
    arr_refs, (both_ref, enc_ref, place_ref) = refs[:-3], refs[-3:]
    rows = enc_ref.shape[0]
    group = len(arr_refs)
    src = src_ref[...].astype(f32)
    tile = jnp.floor((src + 0.5) * (1.0 / cap))
    slot_row = src + (padded - cap) * tile
    place_ref[...] = slot_row
    if group > 1:
        arrived = jnp.concatenate([ref[...].astype(f32) for ref in arr_refs], axis=0).astype(bf16)
        turn_by = plane_index().astype(f32) - tile
        turn_by = jnp.where(turn_by < 0.0, turn_by + group, turn_by)
        slot_row = slot_row + padded * (turn_by - tile)
    else:
        arrived = arr_refs[0][...]
    slot_col = column_of(slot_row)
    lanes = lax.broadcasted_iota(jnp.int32, (rows, arrived.shape[0]), 1).astype(f32)
    pick = (slot_col == lanes).astype(f32).astype(bf16)
    enc_in = mm(pick, arrived)
    enc_ref[...] = enc_in.astype(bf16)
    centred = enc_in - jnp.mean(enc_in, axis=-1, keepdims=True)
    spread = jnp.mean(centred * centred, axis=-1, keepdims=True)
    both_ref[0:rows] = (centred * lax.rsqrt(spread + norm_eps)).astype(bf16)
    both_ref[rows : 2 * rows] = cot_ref[...]


def project_kernel(normed_ref, wqkv_t_ref, u_ref, len_ref, v_ref):
    width = v_ref.shape[0]
    normed = normed_ref[0 : v_ref.shape[1]]
    heads = len_ref.shape[0] // 2
    size = width // heads
    for t in range(2):
        raw = mm(wqkv_t_ref[t * width : (t + 1) * width], normed, NT)
        for h in range(heads):
            part = raw[h * size : (h + 1) * size]
            inv = lax.rsqrt(jnp.sum(part * part, axis=0, keepdims=True) + length_eps)
            at = t * width + h * size
            u_ref[at : at + size] = part * inv
            len_ref[t * heads + h : t * heads + h + 1] = inv
    v_ref[...] = mm(wqkv_t_ref[2 * width : 3 * width], normed, NT).astype(bf16)


def encode_kernel(
    split, win_ref, scale_ref, place_ref, enc_ref, u_ref, len_ref, v_ref, ga_ref, wout_ref,
    wdec_ref, out_ref, *refs,
):
    peer_refs = refs[:-3]
    p_ref, att_ref, left_ref = refs[-3:]
    rows, width = enc_ref.shape
    heads = p_ref.shape[0]
    size = width // heads
    slots = out_ref.shape[0]
    win = win_ref[...].astype(f32)
    same = column_of(win) == win
    for h in range(heads):
        lo, hi = h * size, (h + 1) * size
        q = u_ref[lo:hi].astype(bf16)
        k = u_ref[width + lo : width + hi].astype(bf16)
        scores = mm(k, q, TN)
        raised = jnp.where(same, jnp.exp(scores * scale_ref[h]), 0.0)
        weights = (raised * (1.0 / jnp.sum(raised, axis=0, keepdims=True))).astype(bf16)
        p_ref[h] = weights
        att = mm(v_ref[lo:hi], weights).astype(bf16)
        att_ref[lo:hi] = att
        emit(split, left_ref, 3 * width + lo, att)
    attended = jnp.transpose(att_ref[...])
    enc_out = (enc_ref[...].astype(f32) + mm(attended, wout_ref[...])).astype(bf16)
    dec = mm(enc_out, wdec_ref[...]).astype(bf16)
    places = lax.broadcasted_iota(jnp.int32, (slots, rows), 0).astype(f32)
    put = (places == place_ref[...]).astype(f32).astype(bf16)
    out_ref[...] = mm(put, dec).astype(bf16)
    for h in range(heads):
        lo, hi = h * size, (h + 1) * size
        ga = ga_ref[lo:hi]
        low = p_ref[h]
        weights = low.astype(f32)
        grad_soft = mm(v_ref[lo:hi], ga, TN)
        part = weights * grad_soft
        total = jnp.sum(part, axis=0, keepdims=True)
        grad_scores = ((part - weights * total) * scale_ref[h]).astype(bf16)
        q = u_ref[lo:hi]
        k = u_ref[width + lo : width + hi]
        grad_v = mm(ga, low, NT)
        grad_q = mm(k.astype(bf16), grad_scores)
        grad_k = mm(q.astype(bf16), grad_scores, NT)
        grad_q = (grad_q - q * jnp.sum(q * grad_q, axis=0, keepdims=True)) * len_ref[h : h + 1]
        grad_k = (grad_k - k * jnp.sum(k * grad_k, axis=0, keepdims=True)) * len_ref[
            heads + h : heads + h + 1
        ]
        emit(split, left_ref, lo, grad_q.astype(bf16))
        emit(split, left_ref, width + lo, grad_k.astype(bf16))
        emit(split, left_ref, 2 * width + lo, grad_v.astype(bf16))
    me = lax.axis_index("replica") if split is not None else 0
    for n, ref in enumerate(peer_refs):
        ref[...] = left_ref[me ^ n] if split is not None else left_ref[...]


def emit(split, out_ref, start, block):
    if split is None:
        out_ref[start : start + block.shape[0]] = block
        return
    unit = 32
    shard_rows, part_rows, qkv_rows = split
    for j in range(block.shape[0] // unit):
        row = start + j * unit
        if row < qkv_rows:
            shard, rest = divmod(row, shard_rows)
            part, place = divmod(rest, part_rows)
            at = shard * part_rows + place
        else:
            part, place = divmod(row - qkv_rows, qkv_rows // 3 // out_ref.shape[0])
            at = qkv_rows // out_ref.shape[0] + place
        out_ref[part, at : at + unit] = block[j * unit : (j + 1) * unit]


def term_kernel(c, *refs):
    lefts, rights = refs[0:4], refs[4:8]
    keep_ref, send_ref = refs[8:]
    half, part, chunk = keep_ref.shape
    cut = slice(c * chunk, (c + 1) * chunk)

    count = lefts[0].shape[1]
    normed, cots = slice(0, count), slice(count, 2 * count)

    def block(lo, hi, which, cols):
        acc = None
        for left, e in zip(lefts, rights):
            step = mm(left[lo:hi], e[which, cols])
            acc = step if acc is None else acc + step
        return acc

    rows = half * part
    first = [(0, block(0, rows, normed, cut).reshape(half, part, chunk))]
    shared = block(rows, rows + (half - 2) * part, normed, cut).reshape(half - 2, part, chunk)
    at = rows + (half - 2 + c) * part
    turned = block(at, at + part, cots, slice(0, 2 * chunk))
    second = [
        (0, shared),
        (half - 2, turned[:, 0:chunk].reshape(1, part, chunk)),
        (half - 1, turned[:, chunk:].reshape(1, part, chunk)),
    ]
    spans = (first, second)
    for mine in range(2):

        @pl.when(lax.axis_index("eta") == mine)
        def _():
            for at, value in spans[mine]:
                keep_ref[at : at + value.shape[0]] = value
            for at, value in spans[1 - mine]:
                send_ref[at : at + value.shape[0]] = value.astype(bf16)


def line_kernel(keep_ref, got_ref, own_ref, *send_refs):
    count = keep_ref.shape[0]
    me = lax.axis_index("phi")
    own_ref[...] = keep_ref[me] + got_ref[me].astype(f32)
    for k, ref in enumerate(send_refs):
        at = lax.rem(me + k + 1, count)
        ref[...] = (keep_ref[at] + got_ref[at].astype(f32)).astype(bf16)


def close_kernel(count, *refs):
    width = refs[0].shape[-1]
    for n in range((len(refs) - 1) // count):
        total = refs[n * count][...]
        for ref in refs[n * count + 1 : (n + 1) * count]:
            total = total + ref[...].astype(f32)
        refs[-1][:, n * width : (n + 1) * width] = total.astype(bf16)


def spread_kernel(own_ref, one_ref, two_ref, three_ref, out_ref, all_ref):
    me = lax.axis_index("replica")
    for n, ref in enumerate((own_ref, one_ref, two_ref, three_ref)):
        all_ref[me ^ n] = ref[...].astype(f32)
    count, part, width = all_ref.shape
    chunk = width // 2
    phis = lax.axis_size("phi")
    turned = lax.axis_index("eta") * phis + lax.axis_index("phi") >= 2 * phis - 2

    @pl.when(jnp.logical_not(turned))
    def _():
        for r in range(count):
            out_ref[r * part : (r + 1) * part] = all_ref[r]

    @pl.when(turned)
    def _():
        pieces = []
        for r in range(count):
            for c in range(2):
                pieces.append(all_ref[r, :, c * chunk : (c + 1) * chunk])
        out_ref[...] = jnp.transpose(jnp.concatenate(pieces, axis=0))


def tie(values, *others):
    return lax.optimization_barrier((values, others))[0]


def fill_kernel(padded, pos_ref, ids_ref, mask_ref, got_ref, *refs):
    wide_ref = refs[-1]
    slots = slot_column(pos_ref, wide_ref, padded)
    ids = ids_ref[0:1] + lax.axis_index("eta").astype(f32) * ids_ref[1:2]
    chosen = (slots == ids).astype(f32).astype(bf16)
    got = got_ref[...]
    values = mm(chosen, got, TN)
    hits = mm(chosen, jnp.ones((got.shape[0], 128), bf16), TN)[:, 0:1]
    values = jnp.where(hits > 0.5, values, mask_ref[...].astype(f32)).astype(bf16)
    at = 0
    for ref in refs[:-1]:
        ref[...] = values[at : at + ref.shape[0]]
        at += ref.shape[0]


def rim_kernel(rim, left_ref, right_ref, edge_ref, out_ref):
    size = edge_ref.shape[0]
    out_ref[0:size] = edge_ref[...]

    def corners(at):
        for start, ref in ((size, left_ref), (size + 16, right_ref)):
            out_ref[start : start + 16] = ref[at : at + 16]

    @pl.when(lax.axis_index("eta") == 0)
    def _():
        corners(left_ref.shape[0] - 16)

    @pl.when(lax.axis_index("eta") != 0)
    def _():
        corners(0)


def conv_kernel_body(
    shape, span, folded, grid_ref, left_ref, right_ref, rims, taps_ref, out_ref,
    full_ref, wide_ref, mixed_ref,
):
    lines, columns = shape
    rim = span // 2
    width = grid_ref.shape[-1]
    lead = 8
    full_ref[rim : rim + lines, lead : lead + columns] = (
        grid_ref[...].astype(f32).reshape(lines, columns, width)
    )
    left = left_ref[...].astype(f32)
    right = right_ref[...].astype(f32)
    for x in range(lines):
        full_ref[rim + x, lead - rim : lead] = left[rim * x : rim * (x + 1)]
        full_ref[rim + x, lead + columns : lead + columns + rim] = right[rim * x : rim * (x + 1)]

    def put(base, edge, first, last):
        for i in range(rim):
            full_ref[base + i, lead : lead + columns] = edge[columns * i : columns * (i + 1)]
            full_ref[base + i, lead - rim : lead] = first[rim * i : rim * (i + 1)]
            full_ref[base + i, lead + columns : lead + columns + rim] = last[
                rim * i : rim * (i + 1)
            ]

    if folded:
        far = rim + lines
        base = jnp.where(lax.axis_index("eta") == 0, far, 0)
        for i in range(rim):
            full_ref[far - base + i] = jnp.zeros(full_ref.shape[1:], f32)
        size = rim * columns
        edge = rims[0][...].astype(f32)
        low = lax.axis_index("eta") == 0
        count = rim * rim
        corners = []
        for at in (size, size + 16):
            early, late = edge[at : at + count], edge[at + 16 - count : at + 16]
            corners.append(jnp.where(low, early, late))
        put(base, edge[0:size], *corners)
    else:
        pieces = [ref[...].astype(f32) for ref in rims]
        put(0, *pieces[:3])
        put(rim + lines, *pieces[3:])
    for t in range(span * span):
        wide_ref[t] = jnp.broadcast_to(taps_ref[t // span, t % span : t % span + 1], (8, width))
    groups = columns // 8

    for c in range(width // 128):
        cut = slice(c * 128, (c + 1) * 128)

        def step(x, accs, live, cut=cut):
            accs = list(accs)
            for v in range(span):
                at = lead - rim + v
                line = full_ref[x, at : at + columns, cut].reshape(groups, 8, 128)
                for i in live:
                    tap = wide_ref[(span - 1 - i) * span + v, :, cut]
                    accs[i] = accs[i] + line * tap[None]
            return accs

        def store(row, acc, cut=cut):
            at = row * columns
            if not isinstance(row, int):
                at = pl.multiple_of(at, columns)
            mixed_ref[pl.ds(at, columns), cut] = acc.reshape(columns, 128)

        zero = jnp.zeros((groups, 8, 128), f32)
        accs = [zero] * span
        for x in range(span - 1):
            accs = step(x, accs, range(span - 1 - x, span))
            accs = accs[1:] + [zero]

        def middle(x, accs):
            accs = step(x, accs, range(span))
            store(x - (span - 1), accs[0])
            return tuple(accs[1:] + [zero])

        accs = list(lax.fori_loop(span - 1, lines, middle, tuple(accs)))
        for x in range(lines, lines + span - 1):
            accs = step(x, accs, range(0, lines + span - 1 - x))
            store(x - (span - 1), accs[0])
            accs = accs[1:] + [zero]

    mixed = mixed_ref[...]
    centred = mixed - jnp.mean(mixed, axis=-1, keepdims=True)
    spread = jnp.mean(centred * centred, axis=-1, keepdims=True)
    out_ref[...] = (centred * lax.rsqrt(spread + norm_eps)).astype(bf16)


def mix_folded(shape, span, grid, left, right, a, *refs):
    conv_kernel_body(shape, span, True, grid, left, right, (a,), *refs)


def mix_open(shape, span, grid, left, right, a, b, c, d, e, g, *refs):
    conv_kernel_body(shape, span, False, grid, left, right, (a, b, c, d, e, g), *refs)


def feed_kernel(chunk, normed_ref, grid_ref, up_ref, down_ref, head_ref, out_ref):
    for at in range(0, normed_ref.shape[0], chunk):
        rows = slice(at, at + chunk)
        wide = mm(normed_ref[rows], up_ref[...])
        hidden = (0.5 * wide * (1.0 + lax.erf(wide * 0.7071067811865476))).astype(bf16)
        decoded = (grid_ref[rows].astype(f32) + mm(hidden, down_ref[...])).astype(bf16)
        out_ref[rows] = mm(decoded, head_ref[...])


def flip(value, axis, bit):
    return lax.ppermute(value, axis, [(i, i ^ bit) for i in range(lax.axis_size(axis))])


def turn(value, axis, k):
    count = lax.axis_size(axis)
    return lax.ppermute(value, axis, [(i, (i + k) % count) for i in range(count)])


def summed_slow(left, normed, cotangent):
    width = normed.shape[1]
    term = jnp.concatenate(
        [mm(left[: 3 * width], normed), mm(cotangent, left[3 * width :], (((0,), (1,)), ((), ())))],
        axis=0,
    )
    share = lax.psum_scatter(term, ("eta", "phi", "replica"), scatter_dimension=0, tiled=True)
    return lax.all_gather(share.astype(bf16), "replica", axis=0, tiled=True).astype(f32)


def body(
    tokens, send_pos, enc_src, window_id, enc_cot, w_qkv, head_scale, w_out, w_dec_in,
    mask_token, conv_kernel, w_up, w_down, w_head,
):
    eta_cells, phi_cells, width = tokens.shape[1:]
    dec_width = w_dec_in.shape[1]
    tile_len = eta_cells * phi_cells
    eta_count = lax.axis_size("eta")
    phi_count = lax.axis_size("phi")
    replicas = lax.axis_size("replica")
    group = eta_count * phi_count
    cap = send_pos.shape[-1]
    padded = -(-cap // 8) * 8
    slots = group * padded
    rows = enc_cot.shape[-2]
    heads = head_scale.shape[0]
    out_rows = 4 * width
    shard_rows = out_rows // group
    part_rows = shard_rows // replicas
    fast = (
        eta_count == 2
        and replicas == 4
        and part_rows % 32 == 0
        and width == 2 * shard_rows
    )

    positions = send_pos.reshape(group, cap)
    turned = 1 < group <= 8
    outgoing = call(
        functools.partial(pick_kernel, padded),
        "pick",
        [sds((padded, width), bf16)] * group if turned else [sds((slots, width), bf16)],
        [vmem(), vmem()],
        scratch=[pltpu.VMEM((group, 128), f32), pltpu.VMEM((group, padded, width), bf16)],
        flops=2 * slots * tile_len * width,
        nbytes=3 * MIB,
        limit=8,
    )(positions, tokens.reshape(tile_len, width))
    if turned:
        arrived = [outgoing[0]]
        for k in range(1, group):
            pairs = [(i, (i + k) % group) for i in range(group)]
            arrived.append(lax.ppermute(outgoing[k], ("eta", "phi"), pairs))
    else:
        arrived = [
            lax.all_to_all(
                outgoing[0].reshape(group, padded, width), ("eta", "phi"), split_axis=0,
                concat_axis=0, tiled=True,
            ).reshape(slots, width)
        ]

    cotangent = enc_cot.reshape(rows, width)
    split = (shard_rows, part_rows, 3 * width) if fast else None
    pieces = replicas if fast else 1
    left_part = (out_rows // pieces, rows)
    left_whole = (replicas,) + left_part if fast else left_part
    grad_att, w_qkv_t = call(
        prep_kernel,
        "prep",
        [sds((width, rows), bf16), sds((3 * width, width), bf16)],
        [vmem()] * 3,
        flops=2 * rows * width * width,
        nbytes=10 * MIB,
        limit=10,
    )(cotangent, w_out, w_qkv)
    arrived = tie(arrived, w_qkv_t)

    both, enc_in, places = call(
        functools.partial(norm_kernel, cap, padded),
        "norm",
        [sds((2 * rows, width), bf16), sds((rows, width), bf16), sds((1, rows), f32)],
        [vmem()] * (2 + len(arrived)),
        flops=2 * rows * width * slots,
        nbytes=2 * MIB,
        limit=8,
        cost=600000000,
    )(enc_src.reshape(1, rows), cotangent, *arrived)
    if fast:
        both_y = flip(both, "replica", 2)
        both_c = flip(both, "replica", 1)
    units, lengths, values = call(
        project_kernel,
        "project",
        [sds((2 * width, rows), f32), sds((2 * heads, rows), f32), sds((width, rows), bf16)],
        [vmem()] * 2,
        flops=2 * rows * width * width * 4,
        nbytes=8 * MIB,
        limit=10,
        cost=2000000000,
    )(both, w_qkv_t)

    outbound, *lefts = call(
        functools.partial(encode_kernel, split),
        "encode",
        [sds((slots, dec_width), bf16)] + [sds(left_part, bf16)] * pieces,
        [vmem(), smem()] + [vmem()] * 8,
        scratch=[
            pltpu.VMEM((heads, rows, rows), bf16),
            pltpu.VMEM((width, rows), bf16),
            pltpu.VMEM(left_whole, bf16),
        ],
        flops=2 * rows * width * width * 10,
        nbytes=8 * MIB,
        limit=14,
        cost=8000000000,
    )(
        window_id.reshape(1, rows), head_scale, places, enc_in, units, lengths, values, grad_att,
        w_out, w_dec_in,
    )
    if fast:
        lefts, both_y, both_c = lax.optimization_barrier((lefts, both_y, both_c))
    returned = lax.all_to_all(
        outbound.reshape(group, padded, dec_width), ("eta", "phi"), split_axis=0, concat_axis=0,
        tiled=True,
    )
    if fast:
        lefts = [lefts[0]] + [flip(lefts[k], "replica", k) for k in range(1, 4)]
        rights = [both, both_c, both_y, flip(both_y, "replica", 1)]
        returned = tie(returned, lefts[1], rights[3])
    else:
        grad_total = summed_slow(lefts[0], both[:rows], cotangent)

    span = conv_kernel.shape[0]
    rim = span // 2
    folded = eta_count == 2
    lines = np.arange(eta_cells)[:, None]
    columns = np.arange(phi_cells)[None, :]
    cell = lines * phi_cells + columns
    parts = [cell]
    moves = [0]
    if folded:
        edge = cell[eta_cells - rim :]
        parts += [cell[:, :rim], cell[:, -rim:], edge]
        moves += [0, 0, -(eta_cells - rim) * phi_cells]
    sizes = [-(-p.size // 16) * 16 for p in parts]
    ids = np.full((2, -(-sum(sizes) // 128) * 128), -7.0, np.float32)
    ids[1] = 0
    at = 0
    for p, size, move in zip(parts, sizes, moves):
        ids[0, at : at + p.size] = p.reshape(-1)
        ids[1, at : at + p.size] = move
        at += size
    filled = call(
        functools.partial(fill_kernel, padded),
        "fill",
        [sds((size, dec_width), bf16) for size in sizes],
        [vmem()] * 4,
        scratch=[pltpu.VMEM((group, 128), f32)],
        flops=2 * slots * ids.shape[1] * (dec_width + 128),
        nbytes=3 * MIB,
        limit=12,
    )(
        positions, jnp.asarray(ids), mask_token.reshape(1, dec_width),
        returned.reshape(slots, dec_width),
    )
    dec_grid = filled[0]
    if folded:
        _, first, last, edge = filled
        left_halo = turn(last, "phi", 1)
        right_halo = turn(first, "phi", -1)
        rim_out = call(
            functools.partial(rim_kernel, rim),
            "rim",
            sds((edge.shape[0] + 32, dec_width), bf16),
            [vmem()] * 3,
            limit=4,
        )(left_halo, right_halo, edge)
        rims = (turn(rim_out, "eta", 1),)
    else:
        box = dec_grid.reshape(eta_cells, phi_cells, dec_width)
        down = [(i, i + 1) for i in range(eta_count - 1)]
        up = [(i + 1, i) for i in range(eta_count - 1)]
        top = lax.ppermute(box[eta_cells - rim :], "eta", down)
        bottom = lax.ppermute(box[:rim], "eta", up)
        box = jnp.concatenate([top, box, bottom], axis=0)
        low = turn(box[:, phi_cells - rim :], "phi", 1)
        high = turn(box[:, :rim], "phi", -1)

        def flat(value):
            return value.reshape(-1, dec_width)

        far = eta_cells + rim
        left_halo, right_halo = flat(low[rim:far]), flat(high[rim:far])
        rims = (
            flat(top), flat(low[:rim]), flat(high[:rim]),
            flat(bottom), flat(low[far:]), flat(high[far:]),
        )
    if fast:
        lefts, rights = tie((lefts, rights), rim_out)
        chunk = width // 2
        half = group // 2
        kept, sent = [], []
        for c in range(2):
            keep, send = call(
                functools.partial(term_kernel, c),
                "terms%d" % c,
                [sds((half, part_rows, chunk), f32), sds((half, part_rows, chunk), bf16)],
                [vmem()] * 8,
                flops=2 * out_rows * chunk * rows,
                nbytes=8 * MIB,
                limit=10,
            )(*lefts, *rights)
            if c == 0:
                lefts, rights = tie((lefts, rights), rims)
            kept.append(keep)
            sent.append(turn(send, "eta", 1))
        left, right_halo, rims = tie((left_halo, right_halo, rims), kept)
    else:
        left = left_halo
    normed_cells = call(
        functools.partial(mix_folded if folded else mix_open, (eta_cells, phi_cells), span),
        "mix",
        sds((tile_len, dec_width), bf16),
        [vmem()] * (4 + len(rims)),
        scratch=[
            pltpu.VMEM((eta_cells + 2 * rim, phi_cells + 16, dec_width), f32),
            pltpu.VMEM((span * span, 8, dec_width), f32),
            pltpu.VMEM((tile_len, dec_width), f32),
        ],
        flops=200 * 2 * span * span * tile_len * dec_width,
        nbytes=3 * MIB,
        limit=16,
    )(dec_grid, left, right_halo, *rims, conv_kernel)
    if fast:
        summed = []
        for c in range(2):
            own, *outs = call(
                line_kernel,
                "line%d" % c,
                [sds((part_rows, chunk), f32)] + [sds((part_rows, chunk), bf16)] * (phi_count - 1),
                [vmem()] * 2,
                flops=half * part_rows * chunk,
                nbytes=2 * MIB,
                limit=4,
            )(kept[c], tie(sent[c], normed_cells))
            summed.append([own] + [turn(outs[k], "phi", k + 1) for k in range(phi_count - 1)])
            normed_cells = tie(normed_cells, own)
    reconstruction = call(
        functools.partial(feed_kernel, 256),
        "feed",
        sds((tile_len, w_head.shape[1]), f32),
        [vmem()] * 5,
        flops=2 * tile_len * dec_width * (2 * w_up.shape[1] + w_head.shape[1]),
        nbytes=4 * MIB,
        limit=12,
    )(normed_cells, dec_grid, w_up, w_down, w_head).reshape(1, eta_cells, phi_cells, -1)
    if fast:
        summed = tie(summed, reconstruction)
        mine = call(
            functools.partial(close_kernel, phi_count),
            "close",
            sds((part_rows, width), bf16),
            [vmem()] * (2 * phi_count),
            flops=4 * part_rows * width,
            nbytes=MIB,
            limit=4,
        )(*summed[0], *summed[1])
        mine_y = flip(mine, "replica", 2)
        grad_total = call(
            spread_kernel,
            "spread",
            sds((shard_rows, width), f32),
            [vmem()] * 4,
            scratch=[pltpu.VMEM((replicas, part_rows, width), f32)],
            flops=4 * part_rows * width,
            nbytes=2 * MIB,
            limit=8,
        )(mine, flip(mine, "replica", 1), mine_y, flip(mine_y, "replica", 1))
    return (grad_total, reconstruction)


def solution(mesh):
    in_specs = (
        P("replica", "eta", "phi", None),
        P("replica", "eta", "phi", None, None),
        P("replica", "eta", "phi", None),
        P("replica", "eta", "phi", None),
        P("replica", "eta", "phi", None, None),
        P(), P(), P(), P(), P(), P(), P(), P(), P(),
    )
    out_specs = (P(("eta", "phi"), None), P("replica", "eta", "phi", None))
    return jax.shard_map(body, mesh=mesh, in_specs=in_specs, out_specs=out_specs, check_vma=False)
```

```python
import functools

import jax
import jax.numpy as jnp
import numpy as np
from jax import lax
from jax.experimental import pallas as pl
from jax.experimental.pallas import tpu as pltpu
from jax.sharding import PartitionSpec as P

norm_eps = 1e-05
length_eps = 1e-06
f32 = jnp.float32
bf16 = jnp.bfloat16
MIB = 1024 * 1024

NN = (((1,), (0,)), ((), ()))
NT = (((1,), (1,)), ((), ()))
TN = (((0,), (0,)), ((), ()))


def mm(a, b, dims=NN):
    return lax.dot_general(a, b, dims, preferred_element_type=f32)


def vmem():
    return pl.BlockSpec(memory_space=pltpu.VMEM)


def smem():
    return pl.BlockSpec(memory_space=pltpu.SMEM)


def call(kernel, name, outs, in_specs, scratch=(), flops=0, nbytes=0, limit=20, cost=1000):
    single = not isinstance(outs, (list, tuple))
    out_list = [outs] if single else list(outs)
    specs = [vmem() for _ in out_list]
    return pl.pallas_call(
        kernel,
        out_shape=out_list[0] if single else tuple(out_list),
        in_specs=in_specs,
        out_specs=specs[0] if single else tuple(specs),
        scratch_shapes=list(scratch),
        compiler_params=pltpu.CompilerParams(vmem_limit_bytes=limit * MIB),
        cost_estimate=pl.CostEstimate(
            flops=cost, bytes_accessed=1000 + cost // 300, transcendentals=0
        ),
        name=name,
    )


def sds(shape, dtype):
    return jax.ShapeDtypeStruct(shape, dtype)


def column_of(row):
    return jnp.transpose(jnp.broadcast_to(row, (8, row.shape[1])))[:, 0:1]


def slot_column(pos_ref, wide_ref, padded):
    group, cap = pos_ref.shape
    wide_ref[...] = jnp.full(wide_ref.shape, -1.0, f32)
    wide_ref[:, 0:cap] = pos_ref[...].astype(f32)
    turned = jnp.transpose(wide_ref[...])
    return jnp.concatenate([turned[0:padded, d : d + 1] for d in range(group)], axis=0)


def plane_index():
    return lax.axis_index("eta") * lax.axis_size("phi") + lax.axis_index("phi")


def pick_kernel(padded, pos_ref, tok_ref, *refs):
    out_refs, (wide_ref, all_ref) = refs[:-2], refs[-2:]
    slots = slot_column(pos_ref, wide_ref, padded)
    cells = lax.broadcasted_iota(jnp.int32, (slots.shape[0], tok_ref.shape[0]), 1).astype(f32)
    chosen = (slots == cells).astype(f32).astype(bf16)
    taken = mm(chosen, tok_ref[...])
    if len(out_refs) == 1:
        out_refs[0][...] = taken.astype(bf16)
        return
    group = len(out_refs)
    for d in range(group):
        all_ref[d] = taken[d * padded : (d + 1) * padded].astype(bf16)
    me = plane_index()
    for k, ref in enumerate(out_refs):
        ref[...] = all_ref[lax.rem(me + k, group)]


def prep_kernel(cot_ref, wout_ref, wqkv_ref, ga_ref, wqkv_t_ref):
    ga_ref[...] = mm(wout_ref[...], cot_ref[...], NT).astype(bf16)
    wqkv_t_ref[...] = jnp.transpose(wqkv_ref[...])


def norm_kernel(cap, padded, src_ref, cot_ref, *refs):
    arr_refs, (both_ref, normed_ref, enc_ref, place_ref) = refs[:-4], refs[-4:]
    rows = enc_ref.shape[0]
    group = len(arr_refs)
    src = src_ref[...].astype(f32)
    tile = jnp.floor((src + 0.5) * (1.0 / cap))
    slot_row = src + (padded - cap) * tile
    place_ref[...] = slot_row
    if group > 1:
        arrived = jnp.concatenate([ref[...].astype(f32) for ref in arr_refs], axis=0).astype(bf16)
        turn_by = plane_index().astype(f32) - tile
        turn_by = jnp.where(turn_by < 0.0, turn_by + group, turn_by)
        slot_row = slot_row + padded * (turn_by - tile)
    else:
        arrived = arr_refs[0][...]
    slot_col = column_of(slot_row)
    lanes = lax.broadcasted_iota(jnp.int32, (rows, arrived.shape[0]), 1).astype(f32)
    pick = (slot_col == lanes).astype(f32).astype(bf16)
    enc_in = mm(pick, arrived)
    enc_ref[...] = enc_in.astype(bf16)
    centred = enc_in - jnp.mean(enc_in, axis=-1, keepdims=True)
    spread = jnp.mean(centred * centred, axis=-1, keepdims=True)
    normed = (centred * lax.rsqrt(spread + norm_eps)).astype(bf16)
    normed_ref[...] = normed
    both_ref[0:rows] = normed
    both_ref[rows : 2 * rows] = cot_ref[...]


def project_kernel(normed_ref, wqkv_t_ref, u_ref, len_ref, v_ref):
    width = v_ref.shape[0]
    normed = normed_ref[...]
    heads = len_ref.shape[0] // 2
    size = width // heads
    for t in range(2):
        raw = mm(wqkv_t_ref[t * width : (t + 1) * width], normed, NT)
        for h in range(heads):
            part = raw[h * size : (h + 1) * size]
            inv = lax.rsqrt(jnp.sum(part * part, axis=0, keepdims=True) + length_eps)
            at = t * width + h * size
            u_ref[at : at + size] = part * inv
            len_ref[t * heads + h : t * heads + h + 1] = inv
    v_ref[...] = mm(wqkv_t_ref[2 * width : 3 * width], normed, NT).astype(bf16)


def encode_kernel(
    split, sends, win_ref, scale_ref, place_ref, enc_ref, u_ref, len_ref, v_ref, ga_ref, wout_ref,
    wdec_ref, *refs,
):
    out_refs, peer_refs = refs[:sends], refs[sends:-4]
    p_ref, att_ref, left_ref, all_ref = refs[-4:]
    rows, width = enc_ref.shape
    heads = p_ref.shape[0]
    size = width // heads
    slots = sends * out_refs[0].shape[0]
    win = win_ref[...].astype(f32)
    same = column_of(win) == win
    for h in range(heads):
        lo, hi = h * size, (h + 1) * size
        q = u_ref[lo:hi].astype(bf16)
        k = u_ref[width + lo : width + hi].astype(bf16)
        scores = mm(k, q, TN)
        raised = jnp.where(same, jnp.exp(scores * scale_ref[h]), 0.0)
        weights = (raised * (1.0 / jnp.sum(raised, axis=0, keepdims=True))).astype(bf16)
        p_ref[h] = weights
        att = mm(v_ref[lo:hi], weights).astype(bf16)
        att_ref[lo:hi] = att
        emit(split, left_ref, 3 * width + lo, att)
    attended = jnp.transpose(att_ref[...])
    enc_out = (enc_ref[...].astype(f32) + mm(attended, wout_ref[...])).astype(bf16)
    dec = mm(enc_out, wdec_ref[...]).astype(bf16)
    places = lax.broadcasted_iota(jnp.int32, (slots, rows), 0).astype(f32)
    put = (places == place_ref[...]).astype(f32).astype(bf16)
    placed = mm(put, dec)
    if sends == 1:
        out_refs[0][...] = placed.astype(bf16)
    else:
        step = slots // sends
        for d in range(sends):
            all_ref[d] = placed[d * step : (d + 1) * step].astype(bf16)
        place = plane_index()
        for n, ref in enumerate(out_refs):
            ref[...] = all_ref[lax.rem(place + n, sends)]
    for h in range(heads):
        lo, hi = h * size, (h + 1) * size
        ga = ga_ref[lo:hi]
        low = p_ref[h]
        weights = low.astype(f32)
        grad_soft = mm(v_ref[lo:hi], ga, TN)
        part = weights * grad_soft
        total = jnp.sum(part, axis=0, keepdims=True)
        grad_scores = ((part - weights * total) * scale_ref[h]).astype(bf16)
        q = u_ref[lo:hi]
        k = u_ref[width + lo : width + hi]
        grad_v = mm(ga, low, NT)
        grad_q = mm(k.astype(bf16), grad_scores)
        grad_k = mm(q.astype(bf16), grad_scores, NT)
        grad_q = (grad_q - q * jnp.sum(q * grad_q, axis=0, keepdims=True)) * len_ref[h : h + 1]
        grad_k = (grad_k - k * jnp.sum(k * grad_k, axis=0, keepdims=True)) * len_ref[
            heads + h : heads + h + 1
        ]
        emit(split, left_ref, lo, grad_q.astype(bf16))
        emit(split, left_ref, width + lo, grad_k.astype(bf16))
        emit(split, left_ref, 2 * width + lo, grad_v.astype(bf16))
    me = lax.axis_index("replica") if split is not None else 0
    for n, ref in enumerate(peer_refs):
        ref[...] = left_ref[me ^ n] if split is not None else left_ref[...]


def emit(split, out_ref, start, block):
    if split is None:
        out_ref[start : start + block.shape[0]] = block
        return
    unit = 32
    shard_rows, part_rows, qkv_rows = split
    for j in range(block.shape[0] // unit):
        row = start + j * unit
        if row < qkv_rows:
            shard, rest = divmod(row, shard_rows)
            part, place = divmod(rest, part_rows)
            at = shard * part_rows + place
        else:
            part, place = divmod(row - qkv_rows, qkv_rows // 3 // out_ref.shape[0])
            at = qkv_rows // out_ref.shape[0] + place
        out_ref[part, at : at + unit] = block[j * unit : (j + 1) * unit]


def term_kernel(c, *refs):
    lefts, rights = refs[0:4], refs[4:10]
    keep_ref, send_ref = refs[10:]
    half, part, chunk = keep_ref.shape
    cut = slice(c * chunk, (c + 1) * chunk)

    count = lefts[0].shape[1]
    whole = slice(0, count)
    below = slice(count, 2 * count)
    normed = [(ref, whole) for ref in rights[0:4]]
    cots = [(ref, below) for ref in rights[0:2]] + [(ref, whole) for ref in rights[4:6]]

    def block(lo, hi, right, cols):
        acc = None
        for left, (ref, which) in zip(lefts, right):
            step = mm(left[lo:hi], ref[which, cols])
            acc = step if acc is None else acc + step
        return acc

    rows = half * part
    first = [(0, block(0, rows, normed, cut).reshape(half, part, chunk))]
    shared = block(rows, rows + (half - 2) * part, normed, cut).reshape(half - 2, part, chunk)
    at = rows + (half - 2 + c) * part
    turned = block(at, at + part, cots, slice(0, 2 * chunk))
    second = [
        (0, shared),
        (half - 2, turned[:, 0:chunk].reshape(1, part, chunk)),
        (half - 1, turned[:, chunk:].reshape(1, part, chunk)),
    ]
    spans = (first, second)
    for mine in range(2):

        @pl.when(lax.axis_index("eta") == mine)
        def _():
            for at, value in spans[mine]:
                keep_ref[at : at + value.shape[0]] = value
            for at, value in spans[1 - mine]:
                send_ref[at : at + value.shape[0]] = value.astype(bf16)


def line_kernel(keep_ref, got_ref, own_ref, *send_refs):
    count = keep_ref.shape[0]
    me = lax.axis_index("phi")
    own_ref[...] = keep_ref[me] + got_ref[me].astype(f32)
    for k, ref in enumerate(send_refs):
        at = lax.rem(me + k + 1, count)
        ref[...] = (keep_ref[at] + got_ref[at].astype(f32)).astype(bf16)


def close_kernel(count, *refs):
    width = refs[0].shape[-1]
    for n in range((len(refs) - 1) // count):
        total = refs[n * count][...]
        for ref in refs[n * count + 1 : (n + 1) * count]:
            total = total + ref[...].astype(f32)
        refs[-1][:, n * width : (n + 1) * width] = total.astype(bf16)


def spread_kernel(own_ref, one_ref, two_ref, three_ref, out_ref, all_ref):
    me = lax.axis_index("replica")
    for n, ref in enumerate((own_ref, one_ref, two_ref, three_ref)):
        all_ref[me ^ n] = ref[...].astype(f32)
    count, part, width = all_ref.shape
    chunk = width // 2
    phis = lax.axis_size("phi")
    turned = lax.axis_index("eta") * phis + lax.axis_index("phi") >= 2 * phis - 2

    @pl.when(jnp.logical_not(turned))
    def _():
        for r in range(count):
            out_ref[r * part : (r + 1) * part] = all_ref[r]

    @pl.when(turned)
    def _():
        pieces = []
        for r in range(count):
            for c in range(2):
                pieces.append(all_ref[r, :, c * chunk : (c + 1) * chunk])
        out_ref[...] = jnp.transpose(jnp.concatenate(pieces, axis=0))


def tie(values, *others):
    return lax.optimization_barrier((values, others))[0]


def fill_kernel(padded, parts, pos_ref, ids_ref, mask_ref, *refs):
    got_refs, (wide_ref, all_ref) = refs[:parts], refs[-2:]
    refs = refs[parts:-2]
    slots = slot_column(pos_ref, wide_ref, padded)
    ids = ids_ref[0:1] + lax.axis_index("eta").astype(f32) * ids_ref[1:2]
    chosen = (slots == ids).astype(f32).astype(bf16)
    if parts == 1:
        got = got_refs[0][...]
    else:
        me = plane_index()
        for k, ref in enumerate(got_refs):
            all_ref[lax.rem(me + parts - k, parts)] = ref[...].astype(f32)
        got = all_ref[...].reshape(parts * padded, got_refs[0].shape[1]).astype(bf16)
    values = mm(chosen, got, TN)
    hits = mm(chosen, jnp.ones((got.shape[0], 128), bf16), TN)[:, 0:1]
    values = jnp.where(hits > 0.5, values, mask_ref[...].astype(f32)).astype(bf16)
    at = 0
    for ref in refs:
        ref[...] = values[at : at + ref.shape[0]]
        at += ref.shape[0]


def rim_kernel(rim, left_ref, right_ref, edge_ref, out_ref):
    size = edge_ref.shape[0]
    out_ref[0:size] = edge_ref[...]

    def corners(at):
        for start, ref in ((size, left_ref), (size + 16, right_ref)):
            out_ref[start : start + 16] = ref[at : at + 16]

    @pl.when(lax.axis_index("eta") == 0)
    def _():
        corners(left_ref.shape[0] - 16)

    @pl.when(lax.axis_index("eta") != 0)
    def _():
        corners(0)


def conv_kernel_body(
    shape, span, folded, grid_ref, left_ref, right_ref, rims, taps_ref, out_ref,
    full_ref, wide_ref, mixed_ref,
):
    lines, columns = shape
    rim = span // 2
    width = grid_ref.shape[-1]
    lead = 8
    full_ref[rim : rim + lines, lead : lead + columns] = (
        grid_ref[...].astype(f32).reshape(lines, columns, width)
    )
    left = left_ref[...].astype(f32)
    right = right_ref[...].astype(f32)
    for x in range(lines):
        full_ref[rim + x, lead - rim : lead] = left[rim * x : rim * (x + 1)]
        full_ref[rim + x, lead + columns : lead + columns + rim] = right[rim * x : rim * (x + 1)]

    def put(base, edge, first, last):
        for i in range(rim):
            full_ref[base + i, lead : lead + columns] = edge[columns * i : columns * (i + 1)]
            full_ref[base + i, lead - rim : lead] = first[rim * i : rim * (i + 1)]
            full_ref[base + i, lead + columns : lead + columns + rim] = last[
                rim * i : rim * (i + 1)
            ]

    if folded:
        far = rim + lines
        base = jnp.where(lax.axis_index("eta") == 0, far, 0)
        for i in range(rim):
            full_ref[far - base + i] = jnp.zeros(full_ref.shape[1:], f32)
        size = rim * columns
        edge = rims[0][...].astype(f32)
        low = lax.axis_index("eta") == 0
        count = rim * rim
        corners = []
        for at in (size, size + 16):
            early, late = edge[at : at + count], edge[at + 16 - count : at + 16]
            corners.append(jnp.where(low, early, late))
        put(base, edge[0:size], *corners)
    else:
        pieces = [ref[...].astype(f32) for ref in rims]
        put(0, *pieces[:3])
        put(rim + lines, *pieces[3:])
    for t in range(span * span):
        wide_ref[t] = jnp.broadcast_to(taps_ref[t // span, t % span : t % span + 1], (8, width))
    groups = columns // 8

    for c in range(width // 128):
        cut = slice(c * 128, (c + 1) * 128)

        def step(x, accs, live, cut=cut):
            accs = list(accs)
            for v in range(span):
                at = lead - rim + v
                line = full_ref[x, at : at + columns, cut].reshape(groups, 8, 128)
                for i in live:
                    tap = wide_ref[(span - 1 - i) * span + v, :, cut]
                    accs[i] = accs[i] + line * tap[None]
            return accs

        def store(row, acc, cut=cut):
            at = row * columns
            if not isinstance(row, int):
                at = pl.multiple_of(at, columns)
            mixed_ref[pl.ds(at, columns), cut] = acc.reshape(columns, 128)

        zero = jnp.zeros((groups, 8, 128), f32)
        accs = [zero] * span
        for x in range(span - 1):
            accs = step(x, accs, range(span - 1 - x, span))
            accs = accs[1:] + [zero]

        def middle(x, accs):
            accs = step(x, accs, range(span))
            store(x - (span - 1), accs[0])
            return tuple(accs[1:] + [zero])

        accs = list(lax.fori_loop(span - 1, lines, middle, tuple(accs)))
        for x in range(lines, lines + span - 1):
            accs = step(x, accs, range(0, lines + span - 1 - x))
            store(x - (span - 1), accs[0])
            accs = accs[1:] + [zero]

    mixed = mixed_ref[...]
    centred = mixed - jnp.mean(mixed, axis=-1, keepdims=True)
    spread = jnp.mean(centred * centred, axis=-1, keepdims=True)
    out_ref[...] = (centred * lax.rsqrt(spread + norm_eps)).astype(bf16)


def mix_folded(shape, span, grid, left, right, a, *refs):
    conv_kernel_body(shape, span, True, grid, left, right, (a,), *refs)


def mix_open(shape, span, grid, left, right, a, b, c, d, e, g, *refs):
    conv_kernel_body(shape, span, False, grid, left, right, (a, b, c, d, e, g), *refs)


def feed_kernel(chunk, normed_ref, grid_ref, up_ref, down_ref, head_ref, out_ref):
    for at in range(0, normed_ref.shape[0], chunk):
        rows = slice(at, at + chunk)
        wide = mm(normed_ref[rows], up_ref[...])
        hidden = (0.5 * wide * (1.0 + lax.erf(wide * 0.7071067811865476))).astype(bf16)
        decoded = (grid_ref[rows].astype(f32) + mm(hidden, down_ref[...])).astype(bf16)
        out_ref[rows] = mm(decoded, head_ref[...])


def flip(value, axis, bit):
    return lax.ppermute(value, axis, [(i, i ^ bit) for i in range(lax.axis_size(axis))])


def turn(value, axis, k):
    count = lax.axis_size(axis)
    return lax.ppermute(value, axis, [(i, (i + k) % count) for i in range(count)])


def summed_slow(left, normed, cotangent):
    width = normed.shape[1]
    term = jnp.concatenate(
        [mm(left[: 3 * width], normed), mm(cotangent, left[3 * width :], (((0,), (1,)), ((), ())))],
        axis=0,
    )
    share = lax.psum_scatter(term, ("eta", "phi", "replica"), scatter_dimension=0, tiled=True)
    return lax.all_gather(share.astype(bf16), "replica", axis=0, tiled=True).astype(f32)


def body(
    tokens, send_pos, enc_src, window_id, enc_cot, w_qkv, head_scale, w_out, w_dec_in,
    mask_token, conv_kernel, w_up, w_down, w_head,
):
    eta_cells, phi_cells, width = tokens.shape[1:]
    dec_width = w_dec_in.shape[1]
    tile_len = eta_cells * phi_cells
    eta_count = lax.axis_size("eta")
    phi_count = lax.axis_size("phi")
    replicas = lax.axis_size("replica")
    group = eta_count * phi_count
    cap = send_pos.shape[-1]
    padded = -(-cap // 8) * 8
    slots = group * padded
    rows = enc_cot.shape[-2]
    heads = head_scale.shape[0]
    out_rows = 4 * width
    shard_rows = out_rows // group
    part_rows = shard_rows // replicas
    fast = (
        eta_count == 2
        and replicas == 4
        and part_rows % 32 == 0
        and width == 2 * shard_rows
    )

    positions = send_pos.reshape(group, cap)
    turned = 1 < group <= 8
    outgoing = call(
        functools.partial(pick_kernel, padded),
        "pick",
        [sds((padded, width), bf16)] * group if turned else [sds((slots, width), bf16)],
        [vmem(), vmem()],
        scratch=[pltpu.VMEM((group, 128), f32), pltpu.VMEM((group, padded, width), bf16)],
        flops=2 * slots * tile_len * width,
        nbytes=3 * MIB,
        limit=8,
    )(positions, tokens.reshape(tile_len, width))
    if turned:
        arrived = [outgoing[0]]
        for k in range(1, group):
            pairs = [(i, (i + k) % group) for i in range(group)]
            arrived.append(lax.ppermute(outgoing[k], ("eta", "phi"), pairs))
    else:
        arrived = [
            lax.all_to_all(
                outgoing[0].reshape(group, padded, width), ("eta", "phi"), split_axis=0,
                concat_axis=0, tiled=True,
            ).reshape(slots, width)
        ]

    cotangent = enc_cot.reshape(rows, width)
    split = (shard_rows, part_rows, 3 * width) if fast else None
    pieces = replicas if fast else 1
    left_part = (out_rows // pieces, rows)
    left_whole = (replicas,) + left_part if fast else left_part
    grad_att, w_qkv_t = call(
        prep_kernel,
        "prep",
        [sds((width, rows), bf16), sds((3 * width, width), bf16)],
        [vmem()] * 3,
        flops=2 * rows * width * width,
        nbytes=10 * MIB,
        limit=10,
    )(cotangent, w_out, w_qkv)
    if fast:
        cot_y = flip(cotangent, "replica", 2)
    arrived = tie(arrived, w_qkv_t)

    both, normed, enc_in, places = call(
        functools.partial(norm_kernel, cap, padded),
        "norm",
        [sds((2 * rows, width), bf16)] + [sds((rows, width), bf16)] * 2 + [sds((1, rows), f32)],
        [vmem()] * (2 + len(arrived)),
        flops=2 * rows * width * slots,
        nbytes=2 * MIB,
        limit=8,
        cost=600000000,
    )(enc_src.reshape(1, rows), cotangent, *arrived)
    if fast:
        normed_y = flip(normed, "replica", 2)
        both_c = flip(both, "replica", 1)
    units, lengths, values = call(
        project_kernel,
        "project",
        [sds((2 * width, rows), f32), sds((2 * heads, rows), f32), sds((width, rows), bf16)],
        [vmem()] * 2,
        flops=2 * rows * width * width * 4,
        nbytes=8 * MIB,
        limit=10,
        cost=2000000000,
    )(normed, w_qkv_t)

    sends = group if turned else 1
    outs = call(
        functools.partial(encode_kernel, split, sends),
        "encode",
        [sds((slots // sends, dec_width), bf16)] * sends + [sds(left_part, bf16)] * pieces,
        [vmem(), smem()] + [vmem()] * 8,
        scratch=[
            pltpu.VMEM((heads, rows, rows), bf16),
            pltpu.VMEM((width, rows), bf16),
            pltpu.VMEM(left_whole, bf16),
            pltpu.VMEM((group, padded, dec_width), bf16),
        ],
        flops=2 * rows * width * width * 10,
        nbytes=8 * MIB,
        limit=14,
        cost=8000000000,
    )(
        window_id.reshape(1, rows), head_scale, places, enc_in, units, lengths, values, grad_att,
        w_out, w_dec_in,
    )
    outbound, lefts = list(outs[:sends]), list(outs[sends:])
    if fast:
        lefts, normed_y, cot_y, both_c = lax.optimization_barrier(
            (lefts, normed_y, cot_y, both_c)
        )
    if fast:
        lefts = [lefts[0]] + [flip(lefts[k], "replica", k) for k in range(1, 4)]
        rights = [both, both_c, normed_y, flip(normed_y, "replica", 1)]
        rights += [cot_y, flip(cot_y, "replica", 1)]
        outbound = tie(outbound, lefts[1], rights[3], rights[5])
    else:
        grad_total = summed_slow(lefts[0], normed, cotangent)

    if turned:
        returned = [outbound[0]]
        for k in range(1, group):
            pairs = [(i, (i + k) % group) for i in range(group)]
            returned.append(lax.ppermute(outbound[k], ("eta", "phi"), pairs))
    else:
        returned = [
            lax.all_to_all(
                outbound[0].reshape(group, padded, dec_width), ("eta", "phi"), split_axis=0,
                concat_axis=0, tiled=True,
            ).reshape(slots, dec_width)
        ]

    span = conv_kernel.shape[0]
    rim = span // 2
    folded = eta_count == 2
    lines = np.arange(eta_cells)[:, None]
    columns = np.arange(phi_cells)[None, :]
    cell = lines * phi_cells + columns
    parts = [cell]
    moves = [0]
    if folded:
        edge = cell[eta_cells - rim :]
        parts += [cell[:, :rim], cell[:, -rim:], edge]
        moves += [0, 0, -(eta_cells - rim) * phi_cells]
    sizes = [-(-p.size // 16) * 16 for p in parts]
    ids = np.full((2, -(-sum(sizes) // 128) * 128), -7.0, np.float32)
    ids[1] = 0
    at = 0
    for p, size, move in zip(parts, sizes, moves):
        ids[0, at : at + p.size] = p.reshape(-1)
        ids[1, at : at + p.size] = move
        at += size
    filled = call(
        functools.partial(fill_kernel, padded, len(returned)),
        "fill",
        [sds((size, dec_width), bf16) for size in sizes],
        [vmem()] * (3 + len(returned)),
        scratch=[pltpu.VMEM((group, 128), f32), pltpu.VMEM((group, padded, dec_width), f32)],
        flops=2 * slots * ids.shape[1] * (dec_width + 128),
        nbytes=3 * MIB,
        limit=12,
    )(
        positions, jnp.asarray(ids), mask_token.reshape(1, dec_width),
        *returned,
    )
    dec_grid = filled[0]
    if folded:
        _, first, last, edge = filled
        left_halo = turn(last, "phi", 1)
        right_halo = turn(first, "phi", -1)
        rim_out = call(
            functools.partial(rim_kernel, rim),
            "rim",
            sds((edge.shape[0] + 32, dec_width), bf16),
            [vmem()] * 3,
            limit=4,
        )(left_halo, right_halo, edge)
        rims = (turn(rim_out, "eta", 1),)
    else:
        box = dec_grid.reshape(eta_cells, phi_cells, dec_width)
        down = [(i, i + 1) for i in range(eta_count - 1)]
        up = [(i + 1, i) for i in range(eta_count - 1)]
        top = lax.ppermute(box[eta_cells - rim :], "eta", down)
        bottom = lax.ppermute(box[:rim], "eta", up)
        box = jnp.concatenate([top, box, bottom], axis=0)
        low = turn(box[:, phi_cells - rim :], "phi", 1)
        high = turn(box[:, :rim], "phi", -1)

        def flat(value):
            return value.reshape(-1, dec_width)

        far = eta_cells + rim
        left_halo, right_halo = flat(low[rim:far]), flat(high[rim:far])
        rims = (
            flat(top), flat(low[:rim]), flat(high[:rim]),
            flat(bottom), flat(low[far:]), flat(high[far:]),
        )
    if fast:
        lefts, rights = tie((lefts, rights), rim_out)
        chunk = width // 2
        half = group // 2
        kept, sent = [], []
        for c in range(2):
            keep, send = call(
                functools.partial(term_kernel, c),
                "terms%d" % c,
                [sds((half, part_rows, chunk), f32), sds((half, part_rows, chunk), bf16)],
                [vmem()] * 10,
                flops=2 * out_rows * chunk * rows,
                nbytes=8 * MIB,
                limit=10,
            )(*lefts, *rights)
            if c == 0:
                lefts, rights = tie((lefts, rights), rims)
            kept.append(keep)
            sent.append(turn(send, "eta", 1))
        left, right_halo, rims = tie((left_halo, right_halo, rims), kept)
    else:
        left = left_halo
    normed_cells = call(
        functools.partial(mix_folded if folded else mix_open, (eta_cells, phi_cells), span),
        "mix",
        sds((tile_len, dec_width), bf16),
        [vmem()] * (4 + len(rims)),
        scratch=[
            pltpu.VMEM((eta_cells + 2 * rim, phi_cells + 16, dec_width), f32),
            pltpu.VMEM((span * span, 8, dec_width), f32),
            pltpu.VMEM((tile_len, dec_width), f32),
        ],
        flops=200 * 2 * span * span * tile_len * dec_width,
        nbytes=3 * MIB,
        limit=16,
    )(dec_grid, left, right_halo, *rims, conv_kernel)
    if fast:
        summed = []
        for c in range(2):
            own, *outs = call(
                line_kernel,
                "line%d" % c,
                [sds((part_rows, chunk), f32)] + [sds((part_rows, chunk), bf16)] * (phi_count - 1),
                [vmem()] * 2,
                flops=half * part_rows * chunk,
                nbytes=2 * MIB,
                limit=4,
            )(kept[c], tie(sent[c], normed_cells))
            summed.append([own] + [turn(outs[k], "phi", k + 1) for k in range(phi_count - 1)])
            normed_cells = tie(normed_cells, own)
    reconstruction = call(
        functools.partial(feed_kernel, 256),
        "feed",
        sds((tile_len, w_head.shape[1]), f32),
        [vmem()] * 5,
        flops=2 * tile_len * dec_width * (2 * w_up.shape[1] + w_head.shape[1]),
        nbytes=4 * MIB,
        limit=12,
    )(normed_cells, dec_grid, w_up, w_down, w_head).reshape(1, eta_cells, phi_cells, -1)
    if fast:
        summed = tie(summed, reconstruction)
        mine = call(
            functools.partial(close_kernel, phi_count),
            "close",
            sds((part_rows, width), bf16),
            [vmem()] * (2 * phi_count),
            flops=4 * part_rows * width,
            nbytes=MIB,
            limit=4,
        )(*summed[0], *summed[1])
        mine_y = flip(mine, "replica", 2)
        grad_total = call(
            spread_kernel,
            "spread",
            sds((shard_rows, width), f32),
            [vmem()] * 4,
            scratch=[pltpu.VMEM((replicas, part_rows, width), f32)],
            flops=4 * part_rows * width,
            nbytes=2 * MIB,
            limit=8,
        )(mine, flip(mine, "replica", 1), mine_y, flip(mine_y, "replica", 1))
    return (grad_total, reconstruction)


def solution(mesh):
    in_specs = (
        P("replica", "eta", "phi", None),
        P("replica", "eta", "phi", None, None),
        P("replica", "eta", "phi", None),
        P("replica", "eta", "phi", None),
        P("replica", "eta", "phi", None, None),
        P(), P(), P(), P(), P(), P(), P(), P(), P(),
    )
    out_specs = (P(("eta", "phi"), None), P("replica", "eta", "phi", None))
    return jax.shard_map(body, mesh=mesh, in_specs=in_specs, out_specs=out_specs, check_vma=False)
```

```python
import functools

import jax
import jax.numpy as jnp
import numpy as np
from jax import lax
from jax.experimental import pallas as pl
from jax.experimental.pallas import tpu as pltpu
from jax.sharding import PartitionSpec as P

norm_eps = 1e-05
length_eps = 1e-06
f32 = jnp.float32
bf16 = jnp.bfloat16
MIB = 1024 * 1024

NN = (((1,), (0,)), ((), ()))
NT = (((1,), (1,)), ((), ()))
TN = (((0,), (0,)), ((), ()))


def mm(a, b, dims=NN):
    return lax.dot_general(a, b, dims, preferred_element_type=f32)


def vmem():
    return pl.BlockSpec(memory_space=pltpu.VMEM)


def smem():
    return pl.BlockSpec(memory_space=pltpu.SMEM)


def call(kernel, name, outs, in_specs, scratch=(), flops=0, nbytes=0, limit=20, cost=1000):
    single = not isinstance(outs, (list, tuple))
    out_list = [outs] if single else list(outs)
    specs = [vmem() for _ in out_list]
    return pl.pallas_call(
        kernel,
        out_shape=out_list[0] if single else tuple(out_list),
        in_specs=in_specs,
        out_specs=specs[0] if single else tuple(specs),
        scratch_shapes=list(scratch),
        compiler_params=pltpu.CompilerParams(vmem_limit_bytes=limit * MIB),
        cost_estimate=pl.CostEstimate(
            flops=cost, bytes_accessed=1000 + cost // 300, transcendentals=0
        ),
        name=name,
    )


def sds(shape, dtype):
    return jax.ShapeDtypeStruct(shape, dtype)


def column_of(row):
    return jnp.transpose(jnp.broadcast_to(row, (8, row.shape[1])))[:, 0:1]


def slot_column(pos_ref, wide_ref, padded):
    group, cap = pos_ref.shape
    wide_ref[...] = jnp.full(wide_ref.shape, -1.0, f32)
    wide_ref[:, 0:cap] = pos_ref[...].astype(f32)
    turned = jnp.transpose(wide_ref[...])
    return jnp.concatenate([turned[0:padded, d : d + 1] for d in range(group)], axis=0)


def plane_index():
    return lax.axis_index("eta") * lax.axis_size("phi") + lax.axis_index("phi")


def pick_kernel(padded, pos_ref, tok_ref, *refs):
    out_refs, (wide_ref, all_ref) = refs[:-2], refs[-2:]
    slots = slot_column(pos_ref, wide_ref, padded)
    cells = lax.broadcasted_iota(jnp.int32, (slots.shape[0], tok_ref.shape[0]), 1).astype(f32)
    chosen = (slots == cells).astype(f32).astype(bf16)
    taken = mm(chosen, tok_ref[...])
    if len(out_refs) == 1:
        out_refs[0][...] = taken.astype(bf16)
        return
    group = len(out_refs)
    for d in range(group):
        all_ref[d] = taken[d * padded : (d + 1) * padded].astype(bf16)
    me = plane_index()
    for k, ref in enumerate(out_refs):
        ref[...] = all_ref[lax.rem(me + k, group)]


def prep_kernel(cot_ref, wout_ref, wqkv_ref, ga_ref, wqkv_t_ref):
    ga_ref[...] = mm(wout_ref[...], cot_ref[...], NT).astype(bf16)
    wqkv_t_ref[...] = jnp.transpose(wqkv_ref[...])


def norm_kernel(cap, padded, src_ref, cot_ref, *refs):
    arr_refs, (both_ref, normed_ref, enc_ref, place_ref) = refs[:-4], refs[-4:]
    rows = enc_ref.shape[0]
    group = len(arr_refs)
    src = src_ref[...].astype(f32)
    tile = jnp.floor((src + 0.5) * (1.0 / cap))
    slot_row = src + (padded - cap) * tile
    place_ref[...] = slot_row
    if group > 1:
        arrived = jnp.concatenate([ref[...].astype(f32) for ref in arr_refs], axis=0).astype(bf16)
        turn_by = plane_index().astype(f32) - tile
        turn_by = jnp.where(turn_by < 0.0, turn_by + group, turn_by)
        slot_row = slot_row + padded * (turn_by - tile)
    else:
        arrived = arr_refs[0][...]
    slot_col = column_of(slot_row)
    lanes = lax.broadcasted_iota(jnp.int32, (rows, arrived.shape[0]), 1).astype(f32)
    pick = (slot_col == lanes).astype(f32).astype(bf16)
    enc_in = mm(pick, arrived)
    enc_ref[...] = enc_in.astype(bf16)
    centred = enc_in - jnp.mean(enc_in, axis=-1, keepdims=True)
    spread = jnp.mean(centred * centred, axis=-1, keepdims=True)
    normed = (centred * lax.rsqrt(spread + norm_eps)).astype(bf16)
    normed_ref[...] = normed
    both_ref[0:rows] = normed
    both_ref[rows : 2 * rows] = cot_ref[...]


def project_kernel(normed_ref, wqkv_t_ref, u_ref, len_ref, v_ref):
    width = v_ref.shape[0]
    normed = normed_ref[...]
    heads = len_ref.shape[0] // 2
    size = width // heads
    for t in range(2):
        raw = mm(wqkv_t_ref[t * width : (t + 1) * width], normed, NT)
        for h in range(heads):
            part = raw[h * size : (h + 1) * size]
            inv = lax.rsqrt(jnp.sum(part * part, axis=0, keepdims=True) + length_eps)
            at = t * width + h * size
            u_ref[at : at + size] = part * inv
            len_ref[t * heads + h : t * heads + h + 1] = inv
    v_ref[...] = mm(wqkv_t_ref[2 * width : 3 * width], normed, NT).astype(bf16)


def encode_kernel(
    split, sends, win_ref, scale_ref, place_ref, enc_ref, u_ref, len_ref, v_ref, ga_ref, wout_ref,
    wdec_ref, *refs,
):
    out_refs, peer_refs = refs[:sends], refs[sends:-4]
    p_ref, att_ref, left_ref, all_ref = refs[-4:]
    rows, width = enc_ref.shape
    heads = p_ref.shape[0]
    size = width // heads
    slots = sends * out_refs[0].shape[0]
    win = win_ref[...].astype(f32)
    same = column_of(win) == win
    for h in range(heads):
        lo, hi = h * size, (h + 1) * size
        q = u_ref[lo:hi].astype(bf16)
        k = u_ref[width + lo : width + hi].astype(bf16)
        scores = mm(k, q, TN)
        raised = jnp.where(same, jnp.exp(scores * scale_ref[h]), 0.0)
        weights = (raised * (1.0 / jnp.sum(raised, axis=0, keepdims=True))).astype(bf16)
        p_ref[h] = weights
        att = mm(v_ref[lo:hi], weights).astype(bf16)
        att_ref[lo:hi] = att
        emit(split, left_ref, 3 * width + lo, att)
    attended = jnp.transpose(att_ref[...])
    enc_out = (enc_ref[...].astype(f32) + mm(attended, wout_ref[...])).astype(bf16)
    dec = mm(enc_out, wdec_ref[...]).astype(bf16)
    places = lax.broadcasted_iota(jnp.int32, (slots, rows), 0).astype(f32)
    put = (places == place_ref[...]).astype(f32).astype(bf16)
    placed = mm(put, dec)
    if sends == 1:
        out_refs[0][...] = placed.astype(bf16)
    else:
        step = slots // sends
        for d in range(sends):
            all_ref[d] = placed[d * step : (d + 1) * step].astype(bf16)
        place = plane_index()
        for n, ref in enumerate(out_refs):
            ref[...] = all_ref[lax.rem(place + n, sends)]
    for h in range(heads):
        lo, hi = h * size, (h + 1) * size
        ga = ga_ref[lo:hi]
        low = p_ref[h]
        weights = low.astype(f32)
        grad_soft = mm(v_ref[lo:hi], ga, TN)
        part = weights * grad_soft
        total = jnp.sum(part, axis=0, keepdims=True)
        grad_scores = ((part - weights * total) * scale_ref[h]).astype(bf16)
        q = u_ref[lo:hi]
        k = u_ref[width + lo : width + hi]
        grad_v = mm(ga, low, NT)
        grad_q = mm(k.astype(bf16), grad_scores)
        grad_k = mm(q.astype(bf16), grad_scores, NT)
        grad_q = (grad_q - q * jnp.sum(q * grad_q, axis=0, keepdims=True)) * len_ref[h : h + 1]
        grad_k = (grad_k - k * jnp.sum(k * grad_k, axis=0, keepdims=True)) * len_ref[
            heads + h : heads + h + 1
        ]
        emit(split, left_ref, lo, grad_q.astype(bf16))
        emit(split, left_ref, width + lo, grad_k.astype(bf16))
        emit(split, left_ref, 2 * width + lo, grad_v.astype(bf16))
    me = lax.axis_index("replica") if split is not None else 0
    for n, ref in enumerate(peer_refs):
        ref[...] = left_ref[me ^ n] if split is not None else left_ref[...]


def emit(split, out_ref, start, block):
    if split is None:
        out_ref[start : start + block.shape[0]] = block
        return
    unit = 32
    shard_rows, part_rows, qkv_rows = split
    for j in range(block.shape[0] // unit):
        row = start + j * unit
        if row < qkv_rows:
            shard, rest = divmod(row, shard_rows)
            part, place = divmod(rest, part_rows)
            at = shard * part_rows + place
        else:
            part, place = divmod(row - qkv_rows, qkv_rows // 3 // out_ref.shape[0])
            at = qkv_rows // out_ref.shape[0] + place
        out_ref[part, at : at + unit] = block[j * unit : (j + 1) * unit]


def term_kernel(c, *refs):
    lefts, rights = refs[0:4], refs[4:10]
    keep_ref, send_ref = refs[10:]
    half, part, chunk = keep_ref.shape
    cut = slice(c * chunk, (c + 1) * chunk)

    count = lefts[0].shape[1]
    whole = slice(0, count)
    below = slice(count, 2 * count)
    normed = [(ref, whole) for ref in rights[0:4]]
    cots = [(ref, below) for ref in rights[0:2]] + [(ref, whole) for ref in rights[4:6]]

    def block(lo, hi, right, cols):
        acc = None
        for left, (ref, which) in zip(lefts, right):
            step = mm(left[lo:hi], ref[which, cols])
            acc = step if acc is None else acc + step
        return acc

    rows = half * part
    first = [(0, block(0, rows, normed, cut).reshape(half, part, chunk))]
    shared = block(rows, rows + (half - 2) * part, normed, cut).reshape(half - 2, part, chunk)
    at = rows + (half - 2 + c) * part
    turned = block(at, at + part, cots, slice(0, 2 * chunk))
    second = [
        (0, shared),
        (half - 2, turned[:, 0:chunk].reshape(1, part, chunk)),
        (half - 1, turned[:, chunk:].reshape(1, part, chunk)),
    ]
    spans = (first, second)
    for mine in range(2):

        @pl.when(lax.axis_index("eta") == mine)
        def _():
            for at, value in spans[mine]:
                keep_ref[at : at + value.shape[0]] = value
            for at, value in spans[1 - mine]:
                send_ref[at : at + value.shape[0]] = value.astype(bf16)


def line_kernel(keep_ref, got_ref, own_ref, *send_refs):
    count = keep_ref.shape[0]
    me = lax.axis_index("phi")
    own_ref[...] = keep_ref[me] + got_ref[me].astype(f32)
    for k, ref in enumerate(send_refs):
        at = lax.rem(me + k + 1, count)
        ref[...] = (keep_ref[at] + got_ref[at].astype(f32)).astype(bf16)


def close_kernel(count, *refs):
    width = refs[0].shape[-1]
    for n in range((len(refs) - 1) // count):
        total = refs[n * count][...]
        for ref in refs[n * count + 1 : (n + 1) * count]:
            total = total + ref[...].astype(f32)
        refs[-1][:, n * width : (n + 1) * width] = total.astype(bf16)


def spread_kernel(own_ref, one_ref, two_ref, three_ref, out_ref, all_ref):
    me = lax.axis_index("replica")
    for n, ref in enumerate((own_ref, one_ref, two_ref, three_ref)):
        all_ref[me ^ n] = ref[...].astype(f32)
    count, part, width = all_ref.shape
    chunk = width // 2
    phis = lax.axis_size("phi")
    turned = lax.axis_index("eta") * phis + lax.axis_index("phi") >= 2 * phis - 2

    @pl.when(jnp.logical_not(turned))
    def _():
        for r in range(count):
            out_ref[r * part : (r + 1) * part] = all_ref[r]

    @pl.when(turned)
    def _():
        pieces = []
        for r in range(count):
            for c in range(2):
                pieces.append(all_ref[r, :, c * chunk : (c + 1) * chunk])
        out_ref[...] = jnp.transpose(jnp.concatenate(pieces, axis=0))


def tie(values, *others):
    return lax.optimization_barrier((values, others))[0]


def fill_kernel(padded, parts, pos_ref, ids_ref, mask_ref, *refs):
    got_refs, (wide_ref, all_ref) = refs[:parts], refs[-2:]
    refs = refs[parts:-2]
    slots = slot_column(pos_ref, wide_ref, padded)
    ids = ids_ref[0:1] + lax.axis_index("eta").astype(f32) * ids_ref[1:2]
    chosen = (slots == ids).astype(f32).astype(bf16)
    if parts == 1:
        got = got_refs[0][...]
    else:
        me = plane_index()
        for k, ref in enumerate(got_refs):
            all_ref[lax.rem(me + parts - k, parts)] = ref[...].astype(f32)
        got = all_ref[...].reshape(parts * padded, got_refs[0].shape[1]).astype(bf16)
    values = mm(chosen, got, TN)
    hits = mm(chosen, jnp.ones((got.shape[0], 128), bf16), TN)[:, 0:1]
    values = jnp.where(hits > 0.5, values, mask_ref[...].astype(f32)).astype(bf16)
    at = 0
    for ref in refs:
        ref[...] = values[at : at + ref.shape[0]]
        at += ref.shape[0]


def rim_kernel(rim, left_ref, right_ref, edge_ref, out_ref):
    size = edge_ref.shape[0]
    out_ref[0:size] = edge_ref[...]

    def corners(at):
        for start, ref in ((size, left_ref), (size + 16, right_ref)):
            out_ref[start : start + 16] = ref[at : at + 16]

    @pl.when(lax.axis_index("eta") == 0)
    def _():
        corners(left_ref.shape[0] - 16)

    @pl.when(lax.axis_index("eta") != 0)
    def _():
        corners(0)


def conv_kernel_body(
    shape, span, folded, grid_ref, left_ref, right_ref, rims, taps_ref, out_ref,
    full_ref, wide_ref, mixed_ref,
):
    lines, columns = shape
    rim = span // 2
    width = grid_ref.shape[-1]
    lead = 8
    full_ref[rim : rim + lines, lead : lead + columns] = (
        grid_ref[...].astype(f32).reshape(lines, columns, width)
    )
    left = left_ref[...].astype(f32)
    right = right_ref[...].astype(f32)
    for x in range(lines):
        full_ref[rim + x, lead - rim : lead] = left[rim * x : rim * (x + 1)]
        full_ref[rim + x, lead + columns : lead + columns + rim] = right[rim * x : rim * (x + 1)]

    def put(base, edge, first, last):
        for i in range(rim):
            full_ref[base + i, lead : lead + columns] = edge[columns * i : columns * (i + 1)]
            full_ref[base + i, lead - rim : lead] = first[rim * i : rim * (i + 1)]
            full_ref[base + i, lead + columns : lead + columns + rim] = last[
                rim * i : rim * (i + 1)
            ]

    if folded:
        far = rim + lines
        base = jnp.where(lax.axis_index("eta") == 0, far, 0)
        for i in range(rim):
            full_ref[far - base + i] = jnp.zeros(full_ref.shape[1:], f32)
        size = rim * columns
        edge = rims[0][...].astype(f32)
        low = lax.axis_index("eta") == 0
        count = rim * rim
        corners = []
        for at in (size, size + 16):
            early, late = edge[at : at + count], edge[at + 16 - count : at + 16]
            corners.append(jnp.where(low, early, late))
        put(base, edge[0:size], *corners)
    else:
        pieces = [ref[...].astype(f32) for ref in rims]
        put(0, *pieces[:3])
        put(rim + lines, *pieces[3:])
    for t in range(span * span):
        wide_ref[t] = jnp.broadcast_to(taps_ref[t // span, t % span : t % span + 1], (8, width))
    groups = columns // 8

    for c in range(width // 128):
        cut = slice(c * 128, (c + 1) * 128)

        def step(x, accs, live, cut=cut):
            accs = list(accs)
            for v in range(span):
                at = lead - rim + v
                line = full_ref[x, at : at + columns, cut].reshape(groups, 8, 128)
                for i in live:
                    tap = wide_ref[(span - 1 - i) * span + v, :, cut]
                    accs[i] = accs[i] + line * tap[None]
            return accs

        def store(row, acc, cut=cut):
            at = row * columns
            if not isinstance(row, int):
                at = pl.multiple_of(at, columns)
            mixed_ref[pl.ds(at, columns), cut] = acc.reshape(columns, 128)

        zero = jnp.zeros((groups, 8, 128), f32)
        accs = [zero] * span
        for x in range(span - 1):
            accs = step(x, accs, range(span - 1 - x, span))
            accs = accs[1:] + [zero]

        def middle(x, accs):
            accs = step(x, accs, range(span))
            store(x - (span - 1), accs[0])
            return tuple(accs[1:] + [zero])

        accs = list(lax.fori_loop(span - 1, lines, middle, tuple(accs)))
        for x in range(lines, lines + span - 1):
            accs = step(x, accs, range(0, lines + span - 1 - x))
            store(x - (span - 1), accs[0])
            accs = accs[1:] + [zero]

    mixed = mixed_ref[...]
    centred = mixed - jnp.mean(mixed, axis=-1, keepdims=True)
    spread = jnp.mean(centred * centred, axis=-1, keepdims=True)
    out_ref[...] = (centred * lax.rsqrt(spread + norm_eps)).astype(bf16)


def mix_folded(shape, span, grid, left, right, a, *refs):
    conv_kernel_body(shape, span, True, grid, left, right, (a,), *refs)


def mix_open(shape, span, grid, left, right, a, b, c, d, e, g, *refs):
    conv_kernel_body(shape, span, False, grid, left, right, (a, b, c, d, e, g), *refs)


def feed_kernel(chunk, normed_ref, grid_ref, up_ref, down_ref, head_ref, out_ref):
    for at in range(0, normed_ref.shape[0], chunk):
        rows = slice(at, at + chunk)
        wide = mm(normed_ref[rows], up_ref[...])
        hidden = (0.5 * wide * (1.0 + lax.erf(wide * 0.7071067811865476))).astype(bf16)
        decoded = (grid_ref[rows].astype(f32) + mm(hidden, down_ref[...])).astype(bf16)
        out_ref[rows] = mm(decoded, head_ref[...])


def flip(value, axis, bit):
    return lax.ppermute(value, axis, [(i, i ^ bit) for i in range(lax.axis_size(axis))])


def turn(value, axis, k):
    count = lax.axis_size(axis)
    return lax.ppermute(value, axis, [(i, (i + k) % count) for i in range(count)])


def summed_slow(left, normed, cotangent):
    width = normed.shape[1]
    term = jnp.concatenate(
        [mm(left[: 3 * width], normed), mm(cotangent, left[3 * width :], (((0,), (1,)), ((), ())))],
        axis=0,
    )
    share = lax.psum_scatter(term, ("eta", "phi", "replica"), scatter_dimension=0, tiled=True)
    return lax.all_gather(share.astype(bf16), "replica", axis=0, tiled=True).astype(f32)


def body(
    tokens, send_pos, enc_src, window_id, enc_cot, w_qkv, head_scale, w_out, w_dec_in,
    mask_token, conv_kernel, w_up, w_down, w_head,
):
    eta_cells, phi_cells, width = tokens.shape[1:]
    dec_width = w_dec_in.shape[1]
    tile_len = eta_cells * phi_cells
    eta_count = lax.axis_size("eta")
    phi_count = lax.axis_size("phi")
    replicas = lax.axis_size("replica")
    group = eta_count * phi_count
    cap = send_pos.shape[-1]
    padded = -(-cap // 8) * 8
    slots = group * padded
    rows = enc_cot.shape[-2]
    heads = head_scale.shape[0]
    out_rows = 4 * width
    shard_rows = out_rows // group
    part_rows = shard_rows // replicas
    fast = (
        eta_count == 2
        and replicas == 4
        and part_rows % 32 == 0
        and width == 2 * shard_rows
    )

    positions = send_pos.reshape(group, cap)
    turned = 1 < group <= 8
    outgoing = call(
        functools.partial(pick_kernel, padded),
        "pick",
        [sds((padded, width), bf16)] * group if turned else [sds((slots, width), bf16)],
        [vmem(), vmem()],
        scratch=[pltpu.VMEM((group, 128), f32), pltpu.VMEM((group, padded, width), bf16)],
        flops=2 * slots * tile_len * width,
        nbytes=3 * MIB,
        limit=8,
    )(positions, tokens.reshape(tile_len, width))
    cotangent = enc_cot.reshape(rows, width)
    if fast:
        cot_y = flip(cotangent, "replica", 2)
        outgoing = list(outgoing)
        outgoing[-2:] = tie(outgoing[-2:], cot_y)
    if turned:
        arrived = [outgoing[0]]
        for k in range(1, group):
            pairs = [(i, (i + k) % group) for i in range(group)]
            arrived.append(lax.ppermute(outgoing[k], ("eta", "phi"), pairs))
    else:
        arrived = [
            lax.all_to_all(
                outgoing[0].reshape(group, padded, width), ("eta", "phi"), split_axis=0,
                concat_axis=0, tiled=True,
            ).reshape(slots, width)
        ]

    cotangent = enc_cot.reshape(rows, width)
    split = (shard_rows, part_rows, 3 * width) if fast else None
    pieces = replicas if fast else 1
    left_part = (out_rows // pieces, rows)
    left_whole = (replicas,) + left_part if fast else left_part
    grad_att, w_qkv_t = call(
        prep_kernel,
        "prep",
        [sds((width, rows), bf16), sds((3 * width, width), bf16)],
        [vmem()] * 3,
        flops=2 * rows * width * width,
        nbytes=10 * MIB,
        limit=10,
    )(cotangent, w_out, w_qkv)
    arrived = tie(arrived, w_qkv_t)

    both, normed, enc_in, places = call(
        functools.partial(norm_kernel, cap, padded),
        "norm",
        [sds((2 * rows, width), bf16)] + [sds((rows, width), bf16)] * 2 + [sds((1, rows), f32)],
        [vmem()] * (2 + len(arrived)),
        flops=2 * rows * width * slots,
        nbytes=2 * MIB,
        limit=8,
        cost=600000000,
    )(enc_src.reshape(1, rows), cotangent, *arrived)
    if fast:
        normed_y = flip(normed, "replica", 2)
        both_c = flip(both, "replica", 1)
    units, lengths, values = call(
        project_kernel,
        "project",
        [sds((2 * width, rows), f32), sds((2 * heads, rows), f32), sds((width, rows), bf16)],
        [vmem()] * 2,
        flops=2 * rows * width * width * 4,
        nbytes=8 * MIB,
        limit=10,
        cost=2000000000,
    )(normed, w_qkv_t)

    sends = group if turned else 1
    outs = call(
        functools.partial(encode_kernel, split, sends),
        "encode",
        [sds((slots // sends, dec_width), bf16)] * sends + [sds(left_part, bf16)] * pieces,
        [vmem(), smem()] + [vmem()] * 8,
        scratch=[
            pltpu.VMEM((heads, rows, rows), bf16),
            pltpu.VMEM((width, rows), bf16),
            pltpu.VMEM(left_whole, bf16),
            pltpu.VMEM((group, padded, dec_width), bf16),
        ],
        flops=2 * rows * width * width * 10,
        nbytes=8 * MIB,
        limit=14,
        cost=8000000000,
    )(
        window_id.reshape(1, rows), head_scale, places, enc_in, units, lengths, values, grad_att,
        w_out, w_dec_in,
    )
    outbound, lefts = list(outs[:sends]), list(outs[sends:])
    if fast:
        lefts, normed_y, cot_y, both_c = lax.optimization_barrier(
            (lefts, normed_y, cot_y, both_c)
        )
    if fast:
        lefts = [lefts[0]] + [flip(lefts[k], "replica", k) for k in range(1, 4)]
        rights = [both, both_c, normed_y, flip(normed_y, "replica", 1)]
        rights += [cot_y, flip(cot_y, "replica", 1)]
        outbound = tie(outbound, lefts[1], rights[3], rights[5])
    else:
        grad_total = summed_slow(lefts[0], normed, cotangent)

    if turned:
        returned = [outbound[0]]
        for k in range(1, group):
            pairs = [(i, (i + k) % group) for i in range(group)]
            returned.append(lax.ppermute(outbound[k], ("eta", "phi"), pairs))
    else:
        returned = [
            lax.all_to_all(
                outbound[0].reshape(group, padded, dec_width), ("eta", "phi"), split_axis=0,
                concat_axis=0, tiled=True,
            ).reshape(slots, dec_width)
        ]

    span = conv_kernel.shape[0]
    rim = span // 2
    folded = eta_count == 2
    lines = np.arange(eta_cells)[:, None]
    columns = np.arange(phi_cells)[None, :]
    cell = lines * phi_cells + columns
    parts = [cell]
    moves = [0]
    if folded:
        edge = cell[eta_cells - rim :]
        parts += [cell[:, :rim], cell[:, -rim:], edge]
        moves += [0, 0, -(eta_cells - rim) * phi_cells]
    sizes = [-(-p.size // 16) * 16 for p in parts]
    ids = np.full((2, -(-sum(sizes) // 128) * 128), -7.0, np.float32)
    ids[1] = 0
    at = 0
    for p, size, move in zip(parts, sizes, moves):
        ids[0, at : at + p.size] = p.reshape(-1)
        ids[1, at : at + p.size] = move
        at += size
    filled = call(
        functools.partial(fill_kernel, padded, len(returned)),
        "fill",
        [sds((size, dec_width), bf16) for size in sizes],
        [vmem()] * (3 + len(returned)),
        scratch=[pltpu.VMEM((group, 128), f32), pltpu.VMEM((group, padded, dec_width), f32)],
        flops=2 * slots * ids.shape[1] * (dec_width + 128),
        nbytes=3 * MIB,
        limit=12,
    )(
        positions, jnp.asarray(ids), mask_token.reshape(1, dec_width),
        *returned,
    )
    dec_grid = filled[0]
    if folded:
        _, first, last, edge = filled
        left_halo = turn(last, "phi", 1)
        right_halo = turn(first, "phi", -1)
        rim_out = call(
            functools.partial(rim_kernel, rim),
            "rim",
            sds((edge.shape[0] + 32, dec_width), bf16),
            [vmem()] * 3,
            limit=4,
        )(left_halo, right_halo, edge)
        rims = (turn(rim_out, "eta", 1),)
    else:
        box = dec_grid.reshape(eta_cells, phi_cells, dec_width)
        down = [(i, i + 1) for i in range(eta_count - 1)]
        up = [(i + 1, i) for i in range(eta_count - 1)]
        top = lax.ppermute(box[eta_cells - rim :], "eta", down)
        bottom = lax.ppermute(box[:rim], "eta", up)
        box = jnp.concatenate([top, box, bottom], axis=0)
        low = turn(box[:, phi_cells - rim :], "phi", 1)
        high = turn(box[:, :rim], "phi", -1)

        def flat(value):
            return value.reshape(-1, dec_width)

        far = eta_cells + rim
        left_halo, right_halo = flat(low[rim:far]), flat(high[rim:far])
        rims = (
            flat(top), flat(low[:rim]), flat(high[:rim]),
            flat(bottom), flat(low[far:]), flat(high[far:]),
        )
    if fast:
        lefts, rights = tie((lefts, rights), rim_out)
        chunk = width // 2
        half = group // 2
        kept, sent = [], []
        for c in range(2):
            keep, send = call(
                functools.partial(term_kernel, c),
                "terms%d" % c,
                [sds((half, part_rows, chunk), f32), sds((half, part_rows, chunk), bf16)],
                [vmem()] * 10,
                flops=2 * out_rows * chunk * rows,
                nbytes=8 * MIB,
                limit=10,
            )(*lefts, *rights)
            if c == 0:
                lefts, rights = tie((lefts, rights), rims)
            kept.append(keep)
            sent.append(turn(send, "eta", 1))
        left, right_halo, rims = tie((left_halo, right_halo, rims), kept)
    else:
        left = left_halo
    normed_cells = call(
        functools.partial(mix_folded if folded else mix_open, (eta_cells, phi_cells), span),
        "mix",
        sds((tile_len, dec_width), bf16),
        [vmem()] * (4 + len(rims)),
        scratch=[
            pltpu.VMEM((eta_cells + 2 * rim, phi_cells + 16, dec_width), f32),
            pltpu.VMEM((span * span, 8, dec_width), f32),
            pltpu.VMEM((tile_len, dec_width), f32),
        ],
        flops=200 * 2 * span * span * tile_len * dec_width,
        nbytes=3 * MIB,
        limit=16,
    )(dec_grid, left, right_halo, *rims, conv_kernel)
    if fast:
        summed = []
        for c in range(2):
            own, *outs = call(
                line_kernel,
                "line%d" % c,
                [sds((part_rows, chunk), f32)] + [sds((part_rows, chunk), bf16)] * (phi_count - 1),
                [vmem()] * 2,
                flops=half * part_rows * chunk,
                nbytes=2 * MIB,
                limit=4,
            )(kept[c], tie(sent[c], normed_cells))
            summed.append([own] + [turn(outs[k], "phi", k + 1) for k in range(phi_count - 1)])
            normed_cells = tie(normed_cells, own)
    reconstruction = call(
        functools.partial(feed_kernel, 256),
        "feed",
        sds((tile_len, w_head.shape[1]), f32),
        [vmem()] * 5,
        flops=2 * tile_len * dec_width * (2 * w_up.shape[1] + w_head.shape[1]),
        nbytes=4 * MIB,
        limit=12,
    )(normed_cells, dec_grid, w_up, w_down, w_head).reshape(1, eta_cells, phi_cells, -1)
    if fast:
        summed = tie(summed, reconstruction)
        mine = call(
            functools.partial(close_kernel, phi_count),
            "close",
            sds((part_rows, width), bf16),
            [vmem()] * (2 * phi_count),
            flops=4 * part_rows * width,
            nbytes=MIB,
            limit=4,
        )(*summed[0], *summed[1])
        mine_y = flip(mine, "replica", 2)
        grad_total = call(
            spread_kernel,
            "spread",
            sds((shard_rows, width), f32),
            [vmem()] * 4,
            scratch=[pltpu.VMEM((replicas, part_rows, width), f32)],
            flops=4 * part_rows * width,
            nbytes=2 * MIB,
            limit=8,
        )(mine, flip(mine, "replica", 1), mine_y, flip(mine_y, "replica", 1))
    return (grad_total, reconstruction)


def solution(mesh):
    in_specs = (
        P("replica", "eta", "phi", None),
        P("replica", "eta", "phi", None, None),
        P("replica", "eta", "phi", None),
        P("replica", "eta", "phi", None),
        P("replica", "eta", "phi", None, None),
        P(), P(), P(), P(), P(), P(), P(), P(), P(),
    )
    out_specs = (P(("eta", "phi"), None), P("replica", "eta", "phi", None))
    return jax.shard_map(body, mesh=mesh, in_specs=in_specs, out_specs=out_specs, check_vma=False)
```

```python
import functools

import jax
import jax.numpy as jnp
import numpy as np
from jax import lax
from jax.experimental import pallas as pl
from jax.experimental.pallas import tpu as pltpu
from jax.sharding import PartitionSpec as P

norm_eps = 1e-05
length_eps = 1e-06
f32 = jnp.float32
bf16 = jnp.bfloat16
MIB = 1024 * 1024

NN = (((1,), (0,)), ((), ()))
NT = (((1,), (1,)), ((), ()))
TN = (((0,), (0,)), ((), ()))


def mm(a, b, dims=NN):
    return lax.dot_general(a, b, dims, preferred_element_type=f32)


def vmem():
    return pl.BlockSpec(memory_space=pltpu.VMEM)


def smem():
    return pl.BlockSpec(memory_space=pltpu.SMEM)


def call(kernel, name, outs, in_specs, scratch=(), flops=0, nbytes=0, limit=20, cost=1000):
    single = not isinstance(outs, (list, tuple))
    out_list = [outs] if single else list(outs)
    specs = [vmem() for _ in out_list]
    return pl.pallas_call(
        kernel,
        out_shape=out_list[0] if single else tuple(out_list),
        in_specs=in_specs,
        out_specs=specs[0] if single else tuple(specs),
        scratch_shapes=list(scratch),
        compiler_params=pltpu.CompilerParams(vmem_limit_bytes=limit * MIB),
        cost_estimate=pl.CostEstimate(
            flops=cost, bytes_accessed=1000 + cost // 300, transcendentals=0
        ),
        name=name,
    )


def sds(shape, dtype):
    return jax.ShapeDtypeStruct(shape, dtype)


def column_of(row):
    return jnp.transpose(jnp.broadcast_to(row, (8, row.shape[1])))[:, 0:1]


def slot_column(pos_ref, wide_ref, padded):
    group, cap = pos_ref.shape
    wide_ref[...] = jnp.full(wide_ref.shape, -1.0, f32)
    wide_ref[:, 0:cap] = pos_ref[...].astype(f32)
    turned = jnp.transpose(wide_ref[...])
    return jnp.concatenate([turned[0:padded, d : d + 1] for d in range(group)], axis=0)


def plane_index():
    return lax.axis_index("eta") * lax.axis_size("phi") + lax.axis_index("phi")


def pick_kernel(padded, pos_ref, tok_ref, *refs):
    out_refs, (wide_ref, all_ref) = refs[:-2], refs[-2:]
    slots = slot_column(pos_ref, wide_ref, padded)
    cells = lax.broadcasted_iota(jnp.int32, (slots.shape[0], tok_ref.shape[0]), 1).astype(f32)
    chosen = (slots == cells).astype(f32).astype(bf16)
    taken = mm(chosen, tok_ref[...])
    if len(out_refs) == 1:
        out_refs[0][...] = taken.astype(bf16)
        return
    group = len(out_refs)
    for d in range(group):
        all_ref[d] = taken[d * padded : (d + 1) * padded].astype(bf16)
    me = plane_index()
    for k, ref in enumerate(out_refs):
        ref[...] = all_ref[lax.rem(me + k, group)]


def prep_kernel(cot_ref, wout_ref, wqkv_ref, ga_ref, wqkv_t_ref):
    ga_ref[...] = mm(wout_ref[...], cot_ref[...], NT).astype(bf16)
    wqkv_t_ref[...] = jnp.transpose(wqkv_ref[...])


def norm_kernel(cap, padded, src_ref, cot_ref, *refs):
    arr_refs, (both_ref, normed_ref, enc_ref, place_ref) = refs[:-4], refs[-4:]
    rows = enc_ref.shape[0]
    group = len(arr_refs)
    src = src_ref[...].astype(f32)
    tile = jnp.floor((src + 0.5) * (1.0 / cap))
    slot_row = src + (padded - cap) * tile
    place_ref[...] = slot_row
    if group > 1:
        arrived = jnp.concatenate([ref[...].astype(f32) for ref in arr_refs], axis=0).astype(bf16)
        turn_by = plane_index().astype(f32) - tile
        turn_by = jnp.where(turn_by < 0.0, turn_by + group, turn_by)
        slot_row = slot_row + padded * (turn_by - tile)
    else:
        arrived = arr_refs[0][...]
    slot_col = column_of(slot_row)
    lanes = lax.broadcasted_iota(jnp.int32, (rows, arrived.shape[0]), 1).astype(f32)
    pick = (slot_col == lanes).astype(f32).astype(bf16)
    enc_in = mm(pick, arrived)
    enc_ref[...] = enc_in.astype(bf16)
    centred = enc_in - jnp.mean(enc_in, axis=-1, keepdims=True)
    spread = jnp.mean(centred * centred, axis=-1, keepdims=True)
    normed = (centred * lax.rsqrt(spread + norm_eps)).astype(bf16)
    normed_ref[...] = normed
    both_ref[0:rows] = normed
    both_ref[rows : 2 * rows] = cot_ref[...]


def project_kernel(normed_ref, wqkv_t_ref, u_ref, len_ref, v_ref):
    width = v_ref.shape[0]
    normed = normed_ref[...]
    heads = len_ref.shape[0] // 2
    size = width // heads
    for t in range(2):
        raw = mm(wqkv_t_ref[t * width : (t + 1) * width], normed, NT)
        for h in range(heads):
            part = raw[h * size : (h + 1) * size]
            inv = lax.rsqrt(jnp.sum(part * part, axis=0, keepdims=True) + length_eps)
            at = t * width + h * size
            u_ref[at : at + size] = part * inv
            len_ref[t * heads + h : t * heads + h + 1] = inv
    v_ref[...] = mm(wqkv_t_ref[2 * width : 3 * width], normed, NT).astype(bf16)


def encode_kernel(
    split, sends, win_ref, scale_ref, place_ref, enc_ref, u_ref, len_ref, v_ref, ga_ref, wout_ref,
    wdec_ref, *refs,
):
    out_refs, peer_refs = refs[:sends], refs[sends:-4]
    p_ref, att_ref, left_ref, all_ref = refs[-4:]
    rows, width = enc_ref.shape
    heads = p_ref.shape[0]
    size = width // heads
    slots = sends * out_refs[0].shape[0]
    win = win_ref[...].astype(f32)
    same = column_of(win) == win
    for h in range(heads):
        lo, hi = h * size, (h + 1) * size
        q = u_ref[lo:hi].astype(bf16)
        k = u_ref[width + lo : width + hi].astype(bf16)
        scores = mm(k, q, TN)
        raised = jnp.where(same, jnp.exp(scores * scale_ref[h]), 0.0)
        weights = (raised * (1.0 / jnp.sum(raised, axis=0, keepdims=True))).astype(bf16)
        p_ref[h] = weights
        att = mm(v_ref[lo:hi], weights).astype(bf16)
        att_ref[lo:hi] = att
        emit(split, left_ref, 3 * width + lo, att)
    attended = jnp.transpose(att_ref[...])
    enc_out = (enc_ref[...].astype(f32) + mm(attended, wout_ref[...])).astype(bf16)
    dec = mm(enc_out, wdec_ref[...]).astype(bf16)
    places = lax.broadcasted_iota(jnp.int32, (slots, rows), 0).astype(f32)
    put = (places == place_ref[...]).astype(f32).astype(bf16)
    placed = mm(put, dec)
    if sends == 1:
        out_refs[0][...] = placed.astype(bf16)
    else:
        step = slots // sends
        for d in range(sends):
            all_ref[d] = placed[d * step : (d + 1) * step].astype(bf16)
        place = plane_index()
        for n, ref in enumerate(out_refs):
            ref[...] = all_ref[lax.rem(place + n, sends)]
    for h in range(heads):
        lo, hi = h * size, (h + 1) * size
        ga = ga_ref[lo:hi]
        low = p_ref[h]
        weights = low.astype(f32)
        grad_soft = mm(v_ref[lo:hi], ga, TN)
        part = weights * grad_soft
        total = jnp.sum(part, axis=0, keepdims=True)
        grad_scores = ((part - weights * total) * scale_ref[h]).astype(bf16)
        q = u_ref[lo:hi]
        k = u_ref[width + lo : width + hi]
        grad_v = mm(ga, low, NT)
        grad_q = mm(k.astype(bf16), grad_scores)
        grad_k = mm(q.astype(bf16), grad_scores, NT)
        grad_q = (grad_q - q * jnp.sum(q * grad_q, axis=0, keepdims=True)) * len_ref[h : h + 1]
        grad_k = (grad_k - k * jnp.sum(k * grad_k, axis=0, keepdims=True)) * len_ref[
            heads + h : heads + h + 1
        ]
        emit(split, left_ref, lo, grad_q.astype(bf16))
        emit(split, left_ref, width + lo, grad_k.astype(bf16))
        emit(split, left_ref, 2 * width + lo, grad_v.astype(bf16))
    me = lax.axis_index("replica") if split is not None else 0
    for n, ref in enumerate(peer_refs):
        ref[...] = left_ref[me ^ n] if split is not None else left_ref[...]


def emit(split, out_ref, start, block):
    if split is None:
        out_ref[start : start + block.shape[0]] = block
        return
    unit = 32
    shard_rows, part_rows, qkv_rows = split
    for j in range(block.shape[0] // unit):
        row = start + j * unit
        if row < qkv_rows:
            shard, rest = divmod(row, shard_rows)
            part, place = divmod(rest, part_rows)
            at = shard * part_rows + place
        else:
            part, place = divmod(row - qkv_rows, qkv_rows // 3 // out_ref.shape[0])
            at = qkv_rows // out_ref.shape[0] + place
        out_ref[part, at : at + unit] = block[j * unit : (j + 1) * unit]


def term_kernel(c, *refs):
    lefts, rights = refs[0:4], refs[4:10]
    keep_ref, send_ref = refs[10:]
    half, part, chunk = keep_ref.shape
    cut = slice(c * chunk, (c + 1) * chunk)

    count = lefts[0].shape[1]
    whole = slice(0, count)
    below = slice(count, 2 * count)
    normed = [(ref, whole) for ref in rights[0:4]]
    cots = [(ref, below) for ref in rights[0:2]] + [(ref, whole) for ref in rights[4:6]]

    def block(lo, hi, right, cols):
        acc = None
        for left, (ref, which) in zip(lefts, right):
            step = mm(left[lo:hi], ref[which, cols])
            acc = step if acc is None else acc + step
        return acc

    rows = half * part
    first = [(0, block(0, rows, normed, cut).reshape(half, part, chunk))]
    shared = block(rows, rows + (half - 2) * part, normed, cut).reshape(half - 2, part, chunk)
    at = rows + (half - 2 + c) * part
    turned = block(at, at + part, cots, slice(0, 2 * chunk))
    second = [
        (0, shared),
        (half - 2, turned[:, 0:chunk].reshape(1, part, chunk)),
        (half - 1, turned[:, chunk:].reshape(1, part, chunk)),
    ]
    spans = (first, second)
    for mine in range(2):

        @pl.when(lax.axis_index("eta") == mine)
        def _():
            for at, value in spans[mine]:
                keep_ref[at : at + value.shape[0]] = value
            for at, value in spans[1 - mine]:
                send_ref[at : at + value.shape[0]] = value.astype(bf16)


def line_kernel(keep_ref, got_ref, own_ref, *send_refs):
    count = keep_ref.shape[0]
    me = lax.axis_index("phi")
    own_ref[...] = keep_ref[me] + got_ref[me].astype(f32)
    for k, ref in enumerate(send_refs):
        at = lax.rem(me + k + 1, count)
        ref[...] = (keep_ref[at] + got_ref[at].astype(f32)).astype(bf16)


def close_kernel(count, *refs):
    width = refs[0].shape[-1]
    for n in range((len(refs) - 1) // count):
        total = refs[n * count][...]
        for ref in refs[n * count + 1 : (n + 1) * count]:
            total = total + ref[...].astype(f32)
        refs[-1][:, n * width : (n + 1) * width] = total.astype(bf16)


def spread_kernel(own_ref, one_ref, two_ref, three_ref, out_ref, all_ref):
    me = lax.axis_index("replica")
    for n, ref in enumerate((own_ref, one_ref, two_ref, three_ref)):
        all_ref[me ^ n] = ref[...].astype(f32)
    count, part, width = all_ref.shape
    chunk = width // 2
    phis = lax.axis_size("phi")
    turned = lax.axis_index("eta") * phis + lax.axis_index("phi") >= 2 * phis - 2

    @pl.when(jnp.logical_not(turned))
    def _():
        for r in range(count):
            out_ref[r * part : (r + 1) * part] = all_ref[r]

    @pl.when(turned)
    def _():
        pieces = []
        for r in range(count):
            for c in range(2):
                pieces.append(all_ref[r, :, c * chunk : (c + 1) * chunk])
        out_ref[...] = jnp.transpose(jnp.concatenate(pieces, axis=0))


def tie(values, *others):
    return lax.optimization_barrier((values, others))[0]


def fill_kernel(padded, parts, pos_ref, ids_ref, mask_ref, *refs):
    got_refs, (wide_ref, all_ref) = refs[:parts], refs[-2:]
    refs = refs[parts:-2]
    slots = slot_column(pos_ref, wide_ref, padded)
    ids = ids_ref[0:1] + lax.axis_index("eta").astype(f32) * ids_ref[1:2]
    chosen = (slots == ids).astype(f32).astype(bf16)
    if parts == 1:
        got = got_refs[0][...]
    else:
        me = plane_index()
        for k, ref in enumerate(got_refs):
            all_ref[lax.rem(me + parts - k, parts)] = ref[...].astype(f32)
        got = all_ref[...].reshape(parts * padded, got_refs[0].shape[1]).astype(bf16)
    values = mm(chosen, got, TN)
    hits = mm(chosen, jnp.ones((got.shape[0], 128), bf16), TN)[:, 0:1]
    values = jnp.where(hits > 0.5, values, mask_ref[...].astype(f32)).astype(bf16)
    at = 0
    for ref in refs:
        ref[...] = values[at : at + ref.shape[0]]
        at += ref.shape[0]


def rim_kernel(rim, left_ref, right_ref, edge_ref, out_ref):
    size = edge_ref.shape[0]
    out_ref[0:size] = edge_ref[...]

    def corners(at):
        for start, ref in ((size, left_ref), (size + 16, right_ref)):
            out_ref[start : start + 16] = ref[at : at + 16]

    @pl.when(lax.axis_index("eta") == 0)
    def _():
        corners(left_ref.shape[0] - 16)

    @pl.when(lax.axis_index("eta") != 0)
    def _():
        corners(0)


def conv_kernel_body(
    shape, span, folded, grid_ref, left_ref, right_ref, rims, taps_ref, out_ref,
    full_ref, wide_ref, mixed_ref,
):
    lines, columns = shape
    rim = span // 2
    width = grid_ref.shape[-1]
    lead = 8
    full_ref[rim : rim + lines, lead : lead + columns] = (
        grid_ref[...].astype(f32).reshape(lines, columns, width)
    )
    left = left_ref[...].astype(f32)
    right = right_ref[...].astype(f32)
    for x in range(lines):
        full_ref[rim + x, lead - rim : lead] = left[rim * x : rim * (x + 1)]
        full_ref[rim + x, lead + columns : lead + columns + rim] = right[rim * x : rim * (x + 1)]

    def put(base, edge, first, last):
        for i in range(rim):
            full_ref[base + i, lead : lead + columns] = edge[columns * i : columns * (i + 1)]
            full_ref[base + i, lead - rim : lead] = first[rim * i : rim * (i + 1)]
            full_ref[base + i, lead + columns : lead + columns + rim] = last[
                rim * i : rim * (i + 1)
            ]

    if folded:
        far = rim + lines
        base = jnp.where(lax.axis_index("eta") == 0, far, 0)
        for i in range(rim):
            full_ref[far - base + i] = jnp.zeros(full_ref.shape[1:], f32)
        size = rim * columns
        edge = rims[0][...].astype(f32)
        low = lax.axis_index("eta") == 0
        count = rim * rim
        corners = []
        for at in (size, size + 16):
            early, late = edge[at : at + count], edge[at + 16 - count : at + 16]
            corners.append(jnp.where(low, early, late))
        put(base, edge[0:size], *corners)
    else:
        pieces = [ref[...].astype(f32) for ref in rims]
        put(0, *pieces[:3])
        put(rim + lines, *pieces[3:])
    for t in range(span * span):
        wide_ref[t] = jnp.broadcast_to(taps_ref[t // span, t % span : t % span + 1], (8, width))
    groups = columns // 8

    for c in range(width // 128):
        cut = slice(c * 128, (c + 1) * 128)

        def step(x, accs, live, cut=cut):
            accs = list(accs)
            for v in range(span):
                at = lead - rim + v
                line = full_ref[x, at : at + columns, cut].reshape(groups, 8, 128)
                for i in live:
                    tap = wide_ref[(span - 1 - i) * span + v, :, cut]
                    accs[i] = accs[i] + line * tap[None]
            return accs

        def store(row, acc, cut=cut):
            at = row * columns
            if not isinstance(row, int):
                at = pl.multiple_of(at, columns)
            mixed_ref[pl.ds(at, columns), cut] = acc.reshape(columns, 128)

        zero = jnp.zeros((groups, 8, 128), f32)
        accs = [zero] * span
        for x in range(span - 1):
            accs = step(x, accs, range(span - 1 - x, span))
            accs = accs[1:] + [zero]

        def middle(x, accs):
            accs = step(x, accs, range(span))
            store(x - (span - 1), accs[0])
            return tuple(accs[1:] + [zero])

        accs = list(lax.fori_loop(span - 1, lines, middle, tuple(accs)))
        for x in range(lines, lines + span - 1):
            accs = step(x, accs, range(0, lines + span - 1 - x))
            store(x - (span - 1), accs[0])
            accs = accs[1:] + [zero]

    mixed = mixed_ref[...]
    centred = mixed - jnp.mean(mixed, axis=-1, keepdims=True)
    spread = jnp.mean(centred * centred, axis=-1, keepdims=True)
    out_ref[...] = (centred * lax.rsqrt(spread + norm_eps)).astype(bf16)


def mix_folded(shape, span, grid, left, right, a, *refs):
    conv_kernel_body(shape, span, True, grid, left, right, (a,), *refs)


def mix_open(shape, span, grid, left, right, a, b, c, d, e, g, *refs):
    conv_kernel_body(shape, span, False, grid, left, right, (a, b, c, d, e, g), *refs)


def feed_kernel(chunk, normed_ref, grid_ref, up_ref, down_ref, head_ref, out_ref):
    for at in range(0, normed_ref.shape[0], chunk):
        rows = slice(at, at + chunk)
        wide = mm(normed_ref[rows], up_ref[...])
        hidden = (0.5 * wide * (1.0 + lax.erf(wide * 0.7071067811865476))).astype(bf16)
        decoded = (grid_ref[rows].astype(f32) + mm(hidden, down_ref[...])).astype(bf16)
        out_ref[rows] = mm(decoded, head_ref[...])


def flip(value, axis, bit):
    return lax.ppermute(value, axis, [(i, i ^ bit) for i in range(lax.axis_size(axis))])


def turn(value, axis, k):
    count = lax.axis_size(axis)
    return lax.ppermute(value, axis, [(i, (i + k) % count) for i in range(count)])


def summed_slow(left, normed, cotangent):
    width = normed.shape[1]
    term = jnp.concatenate(
        [mm(left[: 3 * width], normed), mm(cotangent, left[3 * width :], (((0,), (1,)), ((), ())))],
        axis=0,
    )
    share = lax.psum_scatter(term, ("eta", "phi", "replica"), scatter_dimension=0, tiled=True)
    return lax.all_gather(share.astype(bf16), "replica", axis=0, tiled=True).astype(f32)


def body(
    tokens, send_pos, enc_src, window_id, enc_cot, w_qkv, head_scale, w_out, w_dec_in,
    mask_token, conv_kernel, w_up, w_down, w_head,
):
    eta_cells, phi_cells, width = tokens.shape[1:]
    dec_width = w_dec_in.shape[1]
    tile_len = eta_cells * phi_cells
    eta_count = lax.axis_size("eta")
    phi_count = lax.axis_size("phi")
    replicas = lax.axis_size("replica")
    group = eta_count * phi_count
    cap = send_pos.shape[-1]
    padded = -(-cap // 8) * 8
    slots = group * padded
    rows = enc_cot.shape[-2]
    heads = head_scale.shape[0]
    out_rows = 4 * width
    shard_rows = out_rows // group
    part_rows = shard_rows // replicas
    fast = (
        eta_count == 2
        and replicas == 4
        and part_rows % 32 == 0
        and width == 2 * shard_rows
    )

    positions = send_pos.reshape(group, cap)
    turned = 1 < group <= 8
    outgoing = call(
        functools.partial(pick_kernel, padded),
        "pick",
        [sds((padded, width), bf16)] * group if turned else [sds((slots, width), bf16)],
        [vmem(), vmem()],
        scratch=[pltpu.VMEM((group, 128), f32), pltpu.VMEM((group, padded, width), bf16)],
        flops=2 * slots * tile_len * width,
        nbytes=3 * MIB,
        limit=8,
    )(positions, tokens.reshape(tile_len, width))
    cotangent = enc_cot.reshape(rows, width)
    if fast:
        cot_y = flip(cotangent, "replica", 2)
        outgoing = list(outgoing)
        outgoing[-2:] = tie(outgoing[-2:], cot_y)
    if turned:
        arrived = [outgoing[0]]
        for k in range(1, group):
            pairs = [(i, (i + k) % group) for i in range(group)]
            arrived.append(lax.ppermute(outgoing[k], ("eta", "phi"), pairs))
    else:
        arrived = [
            lax.all_to_all(
                outgoing[0].reshape(group, padded, width), ("eta", "phi"), split_axis=0,
                concat_axis=0, tiled=True,
            ).reshape(slots, width)
        ]

    cotangent = enc_cot.reshape(rows, width)
    split = (shard_rows, part_rows, 3 * width) if fast else None
    pieces = replicas if fast else 1
    left_part = (out_rows // pieces, rows)
    left_whole = (replicas,) + left_part if fast else left_part
    grad_att, w_qkv_t = call(
        prep_kernel,
        "prep",
        [sds((width, rows), bf16), sds((3 * width, width), bf16)],
        [vmem()] * 3,
        flops=2 * rows * width * width,
        nbytes=10 * MIB,
        limit=10,
    )(cotangent, w_out, w_qkv)
    arrived = tie(arrived, w_qkv_t)

    both, normed, enc_in, places = call(
        functools.partial(norm_kernel, cap, padded),
        "norm",
        [sds((2 * rows, width), bf16)] + [sds((rows, width), bf16)] * 2 + [sds((1, rows), f32)],
        [vmem()] * (2 + len(arrived)),
        flops=2 * rows * width * slots,
        nbytes=2 * MIB,
        limit=8,
        cost=600000000,
    )(enc_src.reshape(1, rows), cotangent, *arrived)
    if fast:
        normed_y = flip(normed, "replica", 2)
        both_c = flip(both, "replica", 1)
    units, lengths, values = call(
        project_kernel,
        "project",
        [sds((2 * width, rows), f32), sds((2 * heads, rows), f32), sds((width, rows), bf16)],
        [vmem()] * 2,
        flops=2 * rows * width * width * 4,
        nbytes=8 * MIB,
        limit=10,
        cost=2000000000,
    )(normed, w_qkv_t)

    sends = group if turned else 1
    outs = call(
        functools.partial(encode_kernel, split, sends),
        "encode",
        [sds((slots // sends, dec_width), bf16)] * sends + [sds(left_part, bf16)] * pieces,
        [vmem(), smem()] + [vmem()] * 8,
        scratch=[
            pltpu.VMEM((heads, rows, rows), bf16),
            pltpu.VMEM((width, rows), bf16),
            pltpu.VMEM(left_whole, bf16),
            pltpu.VMEM((group, padded, dec_width), bf16),
        ],
        flops=2 * rows * width * width * 10,
        nbytes=8 * MIB,
        limit=14,
        cost=8000000000,
    )(
        window_id.reshape(1, rows), head_scale, places, enc_in, units, lengths, values, grad_att,
        w_out, w_dec_in,
    )
    outbound, lefts = list(outs[:sends]), list(outs[sends:])
    if fast:
        lefts, normed_y, cot_y, both_c = lax.optimization_barrier(
            (lefts, normed_y, cot_y, both_c)
        )
    if fast:
        lefts = [lefts[0]] + [flip(lefts[k], "replica", k) for k in range(1, 4)]
        rights = [both, both_c, normed_y, flip(normed_y, "replica", 1)]
        rights += [cot_y, flip(cot_y, "replica", 1)]
        outbound = tie(outbound, lefts[1], rights[3], rights[5])
    else:
        grad_total = summed_slow(lefts[0], normed, cotangent)

    if turned:
        returned = [outbound[0]]
        for k in range(1, group):
            pairs = [(i, (i + k) % group) for i in range(group)]
            returned.append(lax.ppermute(outbound[k], ("eta", "phi"), pairs))
    else:
        returned = [
            lax.all_to_all(
                outbound[0].reshape(group, padded, dec_width), ("eta", "phi"), split_axis=0,
                concat_axis=0, tiled=True,
            ).reshape(slots, dec_width)
        ]

    span = conv_kernel.shape[0]
    rim = span // 2
    folded = eta_count == 2
    lines = np.arange(eta_cells)[:, None]
    columns = np.arange(phi_cells)[None, :]
    cell = lines * phi_cells + columns
    parts = [cell]
    moves = [0]
    if folded:
        edge = cell[eta_cells - rim :]
        parts += [cell[:, :rim], cell[:, -rim:], edge]
        moves += [0, 0, -(eta_cells - rim) * phi_cells]
    sizes = [-(-p.size // 16) * 16 for p in parts]
    ids = np.full((2, -(-sum(sizes) // 128) * 128), -7.0, np.float32)
    ids[1] = 0
    at = 0
    for p, size, move in zip(parts, sizes, moves):
        ids[0, at : at + p.size] = p.reshape(-1)
        ids[1, at : at + p.size] = move
        at += size
    filled = call(
        functools.partial(fill_kernel, padded, len(returned)),
        "fill",
        [sds((size, dec_width), bf16) for size in sizes],
        [vmem()] * (3 + len(returned)),
        scratch=[pltpu.VMEM((group, 128), f32), pltpu.VMEM((group, padded, dec_width), f32)],
        flops=2 * slots * ids.shape[1] * (dec_width + 128),
        nbytes=3 * MIB,
        limit=12,
    )(
        positions, jnp.asarray(ids), mask_token.reshape(1, dec_width),
        *returned,
    )
    dec_grid = filled[0]
    if folded:
        _, first, last, edge = filled
        left_halo = turn(last, "phi", 1)
        right_halo = turn(first, "phi", -1)
        rim_out = call(
            functools.partial(rim_kernel, rim),
            "rim",
            sds((edge.shape[0] + 32, dec_width), bf16),
            [vmem()] * 3,
            limit=4,
        )(left_halo, right_halo, edge)
        rims = (turn(rim_out, "eta", 1),)
    else:
        box = dec_grid.reshape(eta_cells, phi_cells, dec_width)
        down = [(i, i + 1) for i in range(eta_count - 1)]
        up = [(i + 1, i) for i in range(eta_count - 1)]
        top = lax.ppermute(box[eta_cells - rim :], "eta", down)
        bottom = lax.ppermute(box[:rim], "eta", up)
        box = jnp.concatenate([top, box, bottom], axis=0)
        low = turn(box[:, phi_cells - rim :], "phi", 1)
        high = turn(box[:, :rim], "phi", -1)

        def flat(value):
            return value.reshape(-1, dec_width)

        far = eta_cells + rim
        left_halo, right_halo = flat(low[rim:far]), flat(high[rim:far])
        rims = (
            flat(top), flat(low[:rim]), flat(high[:rim]),
            flat(bottom), flat(low[far:]), flat(high[far:]),
        )
    if fast:
        lefts, rights = tie((lefts, rights), rim_out)
        chunk = width // 2
        half = group // 2
        kept, sent = [], []
        for c in range(2):
            keep, send = call(
                functools.partial(term_kernel, c),
                "terms%d" % c,
                [sds((half, part_rows, chunk), f32), sds((half, part_rows, chunk), bf16)],
                [vmem()] * 10,
                flops=2 * out_rows * chunk * rows,
                nbytes=8 * MIB,
                limit=10,
            )(*lefts, *rights)
            kept.append(keep)
            if c == 1:
                send = tie(send, rims)
            sent.append(turn(send, "eta", 1))
        left, right_halo, rims = tie((left_halo, right_halo, rims), kept)
    else:
        left = left_halo
    normed_cells = call(
        functools.partial(mix_folded if folded else mix_open, (eta_cells, phi_cells), span),
        "mix",
        sds((tile_len, dec_width), bf16),
        [vmem()] * (4 + len(rims)),
        scratch=[
            pltpu.VMEM((eta_cells + 2 * rim, phi_cells + 16, dec_width), f32),
            pltpu.VMEM((span * span, 8, dec_width), f32),
            pltpu.VMEM((tile_len, dec_width), f32),
        ],
        flops=200 * 2 * span * span * tile_len * dec_width,
        nbytes=3 * MIB,
        limit=16,
    )(dec_grid, left, right_halo, *rims, conv_kernel)
    if fast:
        summed = []
        for c in range(2):
            own, *outs = call(
                line_kernel,
                "line%d" % c,
                [sds((part_rows, chunk), f32)] + [sds((part_rows, chunk), bf16)] * (phi_count - 1),
                [vmem()] * 2,
                flops=half * part_rows * chunk,
                nbytes=2 * MIB,
                limit=4,
            )(kept[c], tie(sent[c], normed_cells))
            summed.append([own] + [turn(outs[k], "phi", k + 1) for k in range(phi_count - 1)])
            normed_cells = tie(normed_cells, own)
    reconstruction = call(
        functools.partial(feed_kernel, 256),
        "feed",
        sds((tile_len, w_head.shape[1]), f32),
        [vmem()] * 5,
        flops=2 * tile_len * dec_width * (2 * w_up.shape[1] + w_head.shape[1]),
        nbytes=4 * MIB,
        limit=12,
    )(normed_cells, dec_grid, w_up, w_down, w_head).reshape(1, eta_cells, phi_cells, -1)
    if fast:
        summed = tie(summed, reconstruction)
        mine = call(
            functools.partial(close_kernel, phi_count),
            "close",
            sds((part_rows, width), bf16),
            [vmem()] * (2 * phi_count),
            flops=4 * part_rows * width,
            nbytes=MIB,
            limit=4,
        )(*summed[0], *summed[1])
        mine_y = flip(mine, "replica", 2)
        grad_total = call(
            spread_kernel,
            "spread",
            sds((shard_rows, width), f32),
            [vmem()] * 4,
            scratch=[pltpu.VMEM((replicas, part_rows, width), f32)],
            flops=4 * part_rows * width,
            nbytes=2 * MIB,
            limit=8,
        )(mine, flip(mine, "replica", 1), mine_y, flip(mine_y, "replica", 1))
    return (grad_total, reconstruction)


def solution(mesh):
    in_specs = (
        P("replica", "eta", "phi", None),
        P("replica", "eta", "phi", None, None),
        P("replica", "eta", "phi", None),
        P("replica", "eta", "phi", None),
        P("replica", "eta", "phi", None, None),
        P(), P(), P(), P(), P(), P(), P(), P(), P(),
    )
    out_specs = (P(("eta", "phi"), None), P("replica", "eta", "phi", None))
    return jax.shard_map(body, mesh=mesh, in_specs=in_specs, out_specs=out_specs, check_vma=False)
```

```python
import functools

import jax
import jax.numpy as jnp
import numpy as np
from jax import lax
from jax.experimental import pallas as pl
from jax.experimental.pallas import tpu as pltpu
from jax.sharding import PartitionSpec as P

norm_eps = 1e-05
length_eps = 1e-06
f32 = jnp.float32
bf16 = jnp.bfloat16
MIB = 1024 * 1024

NN = (((1,), (0,)), ((), ()))
NT = (((1,), (1,)), ((), ()))
TN = (((0,), (0,)), ((), ()))


def mm(a, b, dims=NN):
    return lax.dot_general(a, b, dims, preferred_element_type=f32)


def vmem():
    return pl.BlockSpec(memory_space=pltpu.VMEM)


def smem():
    return pl.BlockSpec(memory_space=pltpu.SMEM)


def call(kernel, name, outs, in_specs, scratch=(), flops=0, nbytes=0, limit=20, cost=1000):
    single = not isinstance(outs, (list, tuple))
    out_list = [outs] if single else list(outs)
    specs = [vmem() for _ in out_list]
    return pl.pallas_call(
        kernel,
        out_shape=out_list[0] if single else tuple(out_list),
        in_specs=in_specs,
        out_specs=specs[0] if single else tuple(specs),
        scratch_shapes=list(scratch),
        compiler_params=pltpu.CompilerParams(vmem_limit_bytes=limit * MIB),
        cost_estimate=pl.CostEstimate(
            flops=cost, bytes_accessed=1000 + cost // 300, transcendentals=0
        ),
        name=name,
    )


def sds(shape, dtype):
    return jax.ShapeDtypeStruct(shape, dtype)


def column_of(row):
    return jnp.transpose(jnp.broadcast_to(row, (8, row.shape[1])))[:, 0:1]


def slot_column(pos_ref, wide_ref, padded):
    group, cap = pos_ref.shape
    wide_ref[...] = jnp.full(wide_ref.shape, -1.0, f32)
    wide_ref[:, 0:cap] = pos_ref[...].astype(f32)
    turned = jnp.transpose(wide_ref[...])
    return jnp.concatenate([turned[0:padded, d : d + 1] for d in range(group)], axis=0)


def plane_index():
    return lax.axis_index("eta") * lax.axis_size("phi") + lax.axis_index("phi")


def pick_kernel(padded, pos_ref, tok_ref, *refs):
    out_refs, (wide_ref, all_ref) = refs[:-2], refs[-2:]
    slots = slot_column(pos_ref, wide_ref, padded)
    cells = lax.broadcasted_iota(jnp.int32, (slots.shape[0], tok_ref.shape[0]), 1).astype(f32)
    chosen = (slots == cells).astype(f32).astype(bf16)
    taken = mm(chosen, tok_ref[...])
    if len(out_refs) == 1:
        out_refs[0][...] = taken.astype(bf16)
        return
    group = len(out_refs)
    for d in range(group):
        all_ref[d] = taken[d * padded : (d + 1) * padded].astype(bf16)
    me = plane_index()
    for k, ref in enumerate(out_refs):
        ref[...] = all_ref[lax.rem(me + k, group)]


def prep_kernel(cot_ref, wout_ref, wqkv_ref, ga_ref, wqkv_t_ref):
    ga_ref[...] = mm(wout_ref[...], cot_ref[...], NT).astype(bf16)
    wqkv_t_ref[...] = jnp.transpose(wqkv_ref[...])


def norm_kernel(cap, padded, src_ref, cot_ref, *refs):
    arr_refs, (both_ref, normed_ref, enc_ref, place_ref) = refs[:-4], refs[-4:]
    rows = enc_ref.shape[0]
    group = len(arr_refs)
    src = src_ref[...].astype(f32)
    tile = jnp.floor((src + 0.5) * (1.0 / cap))
    slot_row = src + (padded - cap) * tile
    place_ref[...] = slot_row
    if group > 1:
        arrived = jnp.concatenate([ref[...].astype(f32) for ref in arr_refs], axis=0).astype(bf16)
        turn_by = plane_index().astype(f32) - tile
        turn_by = jnp.where(turn_by < 0.0, turn_by + group, turn_by)
        slot_row = slot_row + padded * (turn_by - tile)
    else:
        arrived = arr_refs[0][...]
    slot_col = column_of(slot_row)
    lanes = lax.broadcasted_iota(jnp.int32, (rows, arrived.shape[0]), 1).astype(f32)
    pick = (slot_col == lanes).astype(f32).astype(bf16)
    enc_in = mm(pick, arrived)
    enc_ref[...] = enc_in.astype(bf16)
    centred = enc_in - jnp.mean(enc_in, axis=-1, keepdims=True)
    spread = jnp.mean(centred * centred, axis=-1, keepdims=True)
    normed = (centred * lax.rsqrt(spread + norm_eps)).astype(bf16)
    normed_ref[...] = normed
    both_ref[0:rows] = normed
    both_ref[rows : 2 * rows] = cot_ref[...]


def project_kernel(normed_ref, wqkv_t_ref, u_ref, len_ref, v_ref):
    width = v_ref.shape[0]
    normed = normed_ref[...]
    heads = len_ref.shape[0] // 2
    size = width // heads
    for t in range(2):
        raw = mm(wqkv_t_ref[t * width : (t + 1) * width], normed, NT)
        for h in range(heads):
            part = raw[h * size : (h + 1) * size]
            inv = lax.rsqrt(jnp.sum(part * part, axis=0, keepdims=True) + length_eps)
            at = t * width + h * size
            u_ref[at : at + size] = part * inv
            len_ref[t * heads + h : t * heads + h + 1] = inv
    v_ref[...] = mm(wqkv_t_ref[2 * width : 3 * width], normed, NT).astype(bf16)


def encode_kernel(
    split, sends, win_ref, scale_ref, place_ref, enc_ref, u_ref, len_ref, v_ref, ga_ref, wout_ref,
    wdec_ref, *refs,
):
    out_refs, peer_refs = refs[:sends], refs[sends:-4]
    p_ref, att_ref, left_ref, all_ref = refs[-4:]
    rows, width = enc_ref.shape
    heads = p_ref.shape[0]
    size = width // heads
    slots = sends * out_refs[0].shape[0]
    win = win_ref[...].astype(f32)
    same = column_of(win) == win
    for h in range(heads):
        lo, hi = h * size, (h + 1) * size
        q = u_ref[lo:hi].astype(bf16)
        k = u_ref[width + lo : width + hi].astype(bf16)
        scores = mm(k, q, TN)
        raised = jnp.where(same, jnp.exp(scores * scale_ref[h]), 0.0)
        weights = (raised * (1.0 / jnp.sum(raised, axis=0, keepdims=True))).astype(bf16)
        p_ref[h] = weights
        att = mm(v_ref[lo:hi], weights).astype(bf16)
        att_ref[lo:hi] = att
        emit(split, left_ref, 3 * width + lo, att)
    attended = jnp.transpose(att_ref[...])
    enc_out = (enc_ref[...].astype(f32) + mm(attended, wout_ref[...])).astype(bf16)
    dec = mm(enc_out, wdec_ref[...]).astype(bf16)
    places = lax.broadcasted_iota(jnp.int32, (slots, rows), 0).astype(f32)
    put = (places == place_ref[...]).astype(f32).astype(bf16)
    placed = mm(put, dec)
    if sends == 1:
        out_refs[0][...] = placed.astype(bf16)
    else:
        step = slots // sends
        for d in range(sends):
            all_ref[d] = placed[d * step : (d + 1) * step].astype(bf16)
        place = plane_index()
        for n, ref in enumerate(out_refs):
            ref[...] = all_ref[lax.rem(place + n, sends)]
    for h in range(heads):
        lo, hi = h * size, (h + 1) * size
        ga = ga_ref[lo:hi]
        low = p_ref[h]
        weights = low.astype(f32)
        grad_soft = mm(v_ref[lo:hi], ga, TN)
        part = weights * grad_soft
        total = jnp.sum(part, axis=0, keepdims=True)
        grad_scores = ((part - weights * total) * scale_ref[h]).astype(bf16)
        q = u_ref[lo:hi]
        k = u_ref[width + lo : width + hi]
        grad_v = mm(ga, low, NT)
        grad_q = mm(k.astype(bf16), grad_scores)
        grad_k = mm(q.astype(bf16), grad_scores, NT)
        grad_q = (grad_q - q * jnp.sum(q * grad_q, axis=0, keepdims=True)) * len_ref[h : h + 1]
        grad_k = (grad_k - k * jnp.sum(k * grad_k, axis=0, keepdims=True)) * len_ref[
            heads + h : heads + h + 1
        ]
        emit(split, left_ref, lo, grad_q.astype(bf16))
        emit(split, left_ref, width + lo, grad_k.astype(bf16))
        emit(split, left_ref, 2 * width + lo, grad_v.astype(bf16))
    me = lax.axis_index("replica") if split is not None else 0
    for n, ref in enumerate(peer_refs):
        ref[...] = left_ref[me ^ n] if split is not None else left_ref[...]


def emit(split, out_ref, start, block):
    if split is None:
        out_ref[start : start + block.shape[0]] = block
        return
    unit = 32
    shard_rows, part_rows, qkv_rows = split
    for j in range(block.shape[0] // unit):
        row = start + j * unit
        if row < qkv_rows:
            shard, rest = divmod(row, shard_rows)
            part, place = divmod(rest, part_rows)
            at = shard * part_rows + place
        else:
            part, place = divmod(row - qkv_rows, qkv_rows // 3 // out_ref.shape[0])
            at = qkv_rows // out_ref.shape[0] + place
        out_ref[part, at : at + unit] = block[j * unit : (j + 1) * unit]


def term_kernel(c, *refs):
    lefts, rights = refs[0:4], refs[4:10]
    keep_ref, send_ref = refs[10:]
    half, part, chunk = keep_ref.shape
    cut = slice(c * chunk, (c + 1) * chunk)

    count = lefts[0].shape[1]
    whole = slice(0, count)
    below = slice(count, 2 * count)
    normed = [(ref, whole) for ref in rights[0:4]]
    cots = [(ref, below) for ref in rights[0:2]] + [(ref, whole) for ref in rights[4:6]]

    def block(lo, hi, right, cols):
        acc = None
        for left, (ref, which) in zip(lefts, right):
            step = mm(left[lo:hi], ref[which, cols])
            acc = step if acc is None else acc + step
        return acc

    rows = half * part
    first = [(0, block(0, rows, normed, cut).reshape(half, part, chunk))]
    shared = block(rows, rows + (half - 2) * part, normed, cut).reshape(half - 2, part, chunk)
    at = rows + (half - 2 + c) * part
    turned = block(at, at + part, cots, slice(0, 2 * chunk))
    second = [
        (0, shared),
        (half - 2, turned[:, 0:chunk].reshape(1, part, chunk)),
        (half - 1, turned[:, chunk:].reshape(1, part, chunk)),
    ]
    spans = (first, second)
    for mine in range(2):

        @pl.when(lax.axis_index("eta") == mine)
        def _():
            for at, value in spans[mine]:
                keep_ref[at : at + value.shape[0]] = value
            for at, value in spans[1 - mine]:
                send_ref[at : at + value.shape[0]] = value.astype(bf16)


def line_kernel(keep_ref, got_ref, own_ref, *send_refs):
    count = keep_ref.shape[0]
    me = lax.axis_index("phi")
    own_ref[...] = keep_ref[me] + got_ref[me].astype(f32)
    for k, ref in enumerate(send_refs):
        at = lax.rem(me + k + 1, count)
        ref[...] = (keep_ref[at] + got_ref[at].astype(f32)).astype(bf16)


def close_kernel(count, *refs):
    width = refs[0].shape[-1]
    for n in range((len(refs) - 1) // count):
        total = refs[n * count][...]
        for ref in refs[n * count + 1 : (n + 1) * count]:
            total = total + ref[...].astype(f32)
        refs[-1][:, n * width : (n + 1) * width] = total.astype(bf16)


def spread_kernel(own_ref, one_ref, two_ref, three_ref, out_ref, all_ref):
    me = lax.axis_index("replica")
    for n, ref in enumerate((own_ref, one_ref, two_ref, three_ref)):
        all_ref[me ^ n] = ref[...].astype(f32)
    count, part, width = all_ref.shape
    chunk = width // 2
    phis = lax.axis_size("phi")
    turned = lax.axis_index("eta") * phis + lax.axis_index("phi") >= 2 * phis - 2

    @pl.when(jnp.logical_not(turned))
    def _():
        for r in range(count):
            out_ref[r * part : (r + 1) * part] = all_ref[r]

    @pl.when(turned)
    def _():
        pieces = []
        for r in range(count):
            for c in range(2):
                pieces.append(all_ref[r, :, c * chunk : (c + 1) * chunk])
        out_ref[...] = jnp.transpose(jnp.concatenate(pieces, axis=0))


def tie(values, *others):
    return lax.optimization_barrier((values, others))[0]


def fill_kernel(padded, parts, pos_ref, ids_ref, mask_ref, *refs):
    got_refs, (wide_ref, all_ref) = refs[:parts], refs[-2:]
    refs = refs[parts:-2]
    slots = slot_column(pos_ref, wide_ref, padded)
    ids = ids_ref[0:1] + lax.axis_index("eta").astype(f32) * ids_ref[1:2]
    chosen = (slots == ids).astype(f32).astype(bf16)
    if parts == 1:
        got = got_refs[0][...]
    else:
        me = plane_index()
        for k, ref in enumerate(got_refs):
            all_ref[lax.rem(me + parts - k, parts)] = ref[...].astype(f32)
        got = all_ref[...].reshape(parts * padded, got_refs[0].shape[1]).astype(bf16)
    values = mm(chosen, got, TN)
    hits = mm(chosen, jnp.ones((got.shape[0], 128), bf16), TN)[:, 0:1]
    values = jnp.where(hits > 0.5, values, mask_ref[...].astype(f32)).astype(bf16)
    at = 0
    for ref in refs:
        ref[...] = values[at : at + ref.shape[0]]
        at += ref.shape[0]


def rim_kernel(rim, left_ref, right_ref, edge_ref, out_ref):
    size = edge_ref.shape[0]
    out_ref[0:size] = edge_ref[...]

    def corners(at):
        for start, ref in ((size, left_ref), (size + 16, right_ref)):
            out_ref[start : start + 16] = ref[at : at + 16]

    @pl.when(lax.axis_index("eta") == 0)
    def _():
        corners(left_ref.shape[0] - 16)

    @pl.when(lax.axis_index("eta") != 0)
    def _():
        corners(0)


def conv_kernel_body(
    shape, span, folded, grid_ref, left_ref, right_ref, rims, taps_ref, out_ref,
    full_ref, wide_ref, mixed_ref,
):
    lines, columns = shape
    rim = span // 2
    width = grid_ref.shape[-1]
    lead = 8
    full_ref[rim : rim + lines, lead : lead + columns] = (
        grid_ref[...].astype(f32).reshape(lines, columns, width)
    )
    left = left_ref[...].astype(f32)
    right = right_ref[...].astype(f32)
    for x in range(lines):
        full_ref[rim + x, lead - rim : lead] = left[rim * x : rim * (x + 1)]
        full_ref[rim + x, lead + columns : lead + columns + rim] = right[rim * x : rim * (x + 1)]

    def put(base, edge, first, last):
        for i in range(rim):
            full_ref[base + i, lead : lead + columns] = edge[columns * i : columns * (i + 1)]
            full_ref[base + i, lead - rim : lead] = first[rim * i : rim * (i + 1)]
            full_ref[base + i, lead + columns : lead + columns + rim] = last[
                rim * i : rim * (i + 1)
            ]

    if folded:
        far = rim + lines
        base = jnp.where(lax.axis_index("eta") == 0, far, 0)
        for i in range(rim):
            full_ref[far - base + i] = jnp.zeros(full_ref.shape[1:], f32)
        size = rim * columns
        edge = rims[0][...].astype(f32)
        low = lax.axis_index("eta") == 0
        count = rim * rim
        corners = []
        for at in (size, size + 16):
            early, late = edge[at : at + count], edge[at + 16 - count : at + 16]
            corners.append(jnp.where(low, early, late))
        put(base, edge[0:size], *corners)
    else:
        pieces = [ref[...].astype(f32) for ref in rims]
        put(0, *pieces[:3])
        put(rim + lines, *pieces[3:])
    for t in range(span * span):
        wide_ref[t] = jnp.broadcast_to(taps_ref[t // span, t % span : t % span + 1], (8, width))
    groups = columns // 8

    for c in range(width // 128):
        cut = slice(c * 128, (c + 1) * 128)

        def step(x, accs, live, cut=cut):
            accs = list(accs)
            for v in range(span):
                at = lead - rim + v
                line = full_ref[x, at : at + columns, cut].reshape(groups, 8, 128)
                for i in live:
                    tap = wide_ref[(span - 1 - i) * span + v, :, cut]
                    accs[i] = accs[i] + line * tap[None]
            return accs

        def store(row, acc, cut=cut):
            at = row * columns
            if not isinstance(row, int):
                at = pl.multiple_of(at, columns)
            mixed_ref[pl.ds(at, columns), cut] = acc.reshape(columns, 128)

        zero = jnp.zeros((groups, 8, 128), f32)
        accs = [zero] * span
        for x in range(span - 1):
            accs = step(x, accs, range(span - 1 - x, span))
            accs = accs[1:] + [zero]

        def middle(x, accs):
            accs = step(x, accs, range(span))
            store(x - (span - 1), accs[0])
            return tuple(accs[1:] + [zero])

        accs = list(lax.fori_loop(span - 1, lines, middle, tuple(accs)))
        for x in range(lines, lines + span - 1):
            accs = step(x, accs, range(0, lines + span - 1 - x))
            store(x - (span - 1), accs[0])
            accs = accs[1:] + [zero]

    mixed = mixed_ref[...]
    centred = mixed - jnp.mean(mixed, axis=-1, keepdims=True)
    spread = jnp.mean(centred * centred, axis=-1, keepdims=True)
    out_ref[...] = (centred * lax.rsqrt(spread + norm_eps)).astype(bf16)


def mix_folded(shape, span, grid, left, right, a, *refs):
    conv_kernel_body(shape, span, True, grid, left, right, (a,), *refs)


def mix_open(shape, span, grid, left, right, a, b, c, d, e, g, *refs):
    conv_kernel_body(shape, span, False, grid, left, right, (a, b, c, d, e, g), *refs)


def feed_kernel(chunk, normed_ref, grid_ref, up_ref, down_ref, head_ref, out_ref):
    for at in range(0, normed_ref.shape[0], chunk):
        rows = slice(at, at + chunk)
        wide = mm(normed_ref[rows], up_ref[...])
        hidden = (0.5 * wide * (1.0 + lax.erf(wide * 0.7071067811865476))).astype(bf16)
        decoded = (grid_ref[rows].astype(f32) + mm(hidden, down_ref[...])).astype(bf16)
        out_ref[rows] = mm(decoded, head_ref[...])


def flip(value, axis, bit):
    return lax.ppermute(value, axis, [(i, i ^ bit) for i in range(lax.axis_size(axis))])


def turn(value, axis, k):
    count = lax.axis_size(axis)
    return lax.ppermute(value, axis, [(i, (i + k) % count) for i in range(count)])


def summed_slow(left, normed, cotangent):
    width = normed.shape[1]
    term = jnp.concatenate(
        [mm(left[: 3 * width], normed), mm(cotangent, left[3 * width :], (((0,), (1,)), ((), ())))],
        axis=0,
    )
    share = lax.psum_scatter(term, ("eta", "phi", "replica"), scatter_dimension=0, tiled=True)
    return lax.all_gather(share.astype(bf16), "replica", axis=0, tiled=True).astype(f32)


def body(
    tokens, send_pos, enc_src, window_id, enc_cot, w_qkv, head_scale, w_out, w_dec_in,
    mask_token, conv_kernel, w_up, w_down, w_head,
):
    eta_cells, phi_cells, width = tokens.shape[1:]
    dec_width = w_dec_in.shape[1]
    tile_len = eta_cells * phi_cells
    eta_count = lax.axis_size("eta")
    phi_count = lax.axis_size("phi")
    replicas = lax.axis_size("replica")
    group = eta_count * phi_count
    cap = send_pos.shape[-1]
    padded = -(-cap // 8) * 8
    slots = group * padded
    rows = enc_cot.shape[-2]
    heads = head_scale.shape[0]
    out_rows = 4 * width
    shard_rows = out_rows // group
    part_rows = shard_rows // replicas
    fast = (
        eta_count == 2
        and replicas == 4
        and part_rows % 32 == 0
        and width == 2 * shard_rows
    )

    positions = send_pos.reshape(group, cap)
    turned = 1 < group <= 8
    outgoing = call(
        functools.partial(pick_kernel, padded),
        "pick",
        [sds((padded, width), bf16)] * group if turned else [sds((slots, width), bf16)],
        [vmem(), vmem()],
        scratch=[pltpu.VMEM((group, 128), f32), pltpu.VMEM((group, padded, width), bf16)],
        flops=2 * slots * tile_len * width,
        nbytes=3 * MIB,
        limit=8,
    )(positions, tokens.reshape(tile_len, width))
    cotangent = enc_cot.reshape(rows, width)
    if fast:
        cot_y = flip(cotangent, "replica", 2)
        outgoing = list(outgoing)
        outgoing[-2:] = tie(outgoing[-2:], cot_y)
    if turned:
        arrived = [outgoing[0]]
        for k in range(1, group):
            pairs = [(i, (i + k) % group) for i in range(group)]
            arrived.append(lax.ppermute(outgoing[k], ("eta", "phi"), pairs))
    else:
        arrived = [
            lax.all_to_all(
                outgoing[0].reshape(group, padded, width), ("eta", "phi"), split_axis=0,
                concat_axis=0, tiled=True,
            ).reshape(slots, width)
        ]

    cotangent = enc_cot.reshape(rows, width)
    split = (shard_rows, part_rows, 3 * width) if fast else None
    pieces = replicas if fast else 1
    left_part = (out_rows // pieces, rows)
    left_whole = (replicas,) + left_part if fast else left_part
    grad_att, w_qkv_t = call(
        prep_kernel,
        "prep",
        [sds((width, rows), bf16), sds((3 * width, width), bf16)],
        [vmem()] * 3,
        flops=2 * rows * width * width,
        nbytes=10 * MIB,
        limit=10,
    )(cotangent, w_out, w_qkv)
    arrived = tie(arrived, w_qkv_t)

    both, normed, enc_in, places = call(
        functools.partial(norm_kernel, cap, padded),
        "norm",
        [sds((2 * rows, width), bf16)] + [sds((rows, width), bf16)] * 2 + [sds((1, rows), f32)],
        [vmem()] * (2 + len(arrived)),
        flops=2 * rows * width * slots,
        nbytes=2 * MIB,
        limit=8,
        cost=600000000,
    )(enc_src.reshape(1, rows), cotangent, *arrived)
    if fast:
        normed_y = flip(normed, "replica", 2)
    units, lengths, values = call(
        project_kernel,
        "project",
        [sds((2 * width, rows), f32), sds((2 * heads, rows), f32), sds((width, rows), bf16)],
        [vmem()] * 2,
        flops=2 * rows * width * width * 4,
        nbytes=8 * MIB,
        limit=10,
        cost=2000000000,
    )(normed, w_qkv_t)

    if fast:
        both_c = flip(tie(both, lengths), "replica", 1)
    sends = group if turned else 1
    outs = call(
        functools.partial(encode_kernel, split, sends),
        "encode",
        [sds((slots // sends, dec_width), bf16)] * sends + [sds(left_part, bf16)] * pieces,
        [vmem(), smem()] + [vmem()] * 8,
        scratch=[
            pltpu.VMEM((heads, rows, rows), bf16),
            pltpu.VMEM((width, rows), bf16),
            pltpu.VMEM(left_whole, bf16),
            pltpu.VMEM((group, padded, dec_width), bf16),
        ],
        flops=2 * rows * width * width * 10,
        nbytes=8 * MIB,
        limit=14,
        cost=8000000000,
    )(
        window_id.reshape(1, rows), head_scale, places, enc_in, units, lengths, values, grad_att,
        w_out, w_dec_in,
    )
    outbound, lefts = list(outs[:sends]), list(outs[sends:])
    if fast:
        lefts, normed_y, cot_y, both_c = lax.optimization_barrier(
            (lefts, normed_y, cot_y, both_c)
        )
    if fast:
        lefts = [lefts[0]] + [flip(lefts[k], "replica", k) for k in range(1, 4)]
        rights = [both, both_c, normed_y, flip(normed_y, "replica", 1)]
        rights += [cot_y, flip(cot_y, "replica", 1)]
        outbound = tie(outbound, lefts[1], rights[3], rights[5])
    else:
        grad_total = summed_slow(lefts[0], normed, cotangent)

    if turned:
        returned = [outbound[0]]
        for k in range(1, group):
            pairs = [(i, (i + k) % group) for i in range(group)]
            returned.append(lax.ppermute(outbound[k], ("eta", "phi"), pairs))
    else:
        returned = [
            lax.all_to_all(
                outbound[0].reshape(group, padded, dec_width), ("eta", "phi"), split_axis=0,
                concat_axis=0, tiled=True,
            ).reshape(slots, dec_width)
        ]

    span = conv_kernel.shape[0]
    rim = span // 2
    folded = eta_count == 2
    lines = np.arange(eta_cells)[:, None]
    columns = np.arange(phi_cells)[None, :]
    cell = lines * phi_cells + columns
    parts = [cell]
    moves = [0]
    if folded:
        edge = cell[eta_cells - rim :]
        parts += [cell[:, :rim], cell[:, -rim:], edge]
        moves += [0, 0, -(eta_cells - rim) * phi_cells]
    sizes = [-(-p.size // 16) * 16 for p in parts]
    ids = np.full((2, -(-sum(sizes) // 128) * 128), -7.0, np.float32)
    ids[1] = 0
    at = 0
    for p, size, move in zip(parts, sizes, moves):
        ids[0, at : at + p.size] = p.reshape(-1)
        ids[1, at : at + p.size] = move
        at += size
    filled = call(
        functools.partial(fill_kernel, padded, len(returned)),
        "fill",
        [sds((size, dec_width), bf16) for size in sizes],
        [vmem()] * (3 + len(returned)),
        scratch=[pltpu.VMEM((group, 128), f32), pltpu.VMEM((group, padded, dec_width), f32)],
        flops=2 * slots * ids.shape[1] * (dec_width + 128),
        nbytes=3 * MIB,
        limit=12,
    )(
        positions, jnp.asarray(ids), mask_token.reshape(1, dec_width),
        *returned,
    )
    dec_grid = filled[0]
    if folded:
        _, first, last, edge = filled
        left_halo = turn(last, "phi", 1)
        right_halo = turn(first, "phi", -1)
        rim_out = call(
            functools.partial(rim_kernel, rim),
            "rim",
            sds((edge.shape[0] + 32, dec_width), bf16),
            [vmem()] * 3,
            limit=4,
        )(left_halo, right_halo, edge)
        rims = (turn(rim_out, "eta", 1),)
    else:
        box = dec_grid.reshape(eta_cells, phi_cells, dec_width)
        down = [(i, i + 1) for i in range(eta_count - 1)]
        up = [(i + 1, i) for i in range(eta_count - 1)]
        top = lax.ppermute(box[eta_cells - rim :], "eta", down)
        bottom = lax.ppermute(box[:rim], "eta", up)
        box = jnp.concatenate([top, box, bottom], axis=0)
        low = turn(box[:, phi_cells - rim :], "phi", 1)
        high = turn(box[:, :rim], "phi", -1)

        def flat(value):
            return value.reshape(-1, dec_width)

        far = eta_cells + rim
        left_halo, right_halo = flat(low[rim:far]), flat(high[rim:far])
        rims = (
            flat(top), flat(low[:rim]), flat(high[:rim]),
            flat(bottom), flat(low[far:]), flat(high[far:]),
        )
    if fast:
        lefts, rights = tie((lefts, rights), rim_out)
        chunk = width // 2
        half = group // 2
        kept, sent = [], []
        for c in range(2):
            keep, send = call(
                functools.partial(term_kernel, c),
                "terms%d" % c,
                [sds((half, part_rows, chunk), f32), sds((half, part_rows, chunk), bf16)],
                [vmem()] * 10,
                flops=2 * out_rows * chunk * rows,
                nbytes=8 * MIB,
                limit=10,
            )(*lefts, *rights)
            kept.append(keep)
            if c == 1:
                send = tie(send, rims)
            sent.append(turn(send, "eta", 1))
        left, right_halo, rims = tie((left_halo, right_halo, rims), kept)
    else:
        left = left_halo
    normed_cells = call(
        functools.partial(mix_folded if folded else mix_open, (eta_cells, phi_cells), span),
        "mix",
        sds((tile_len, dec_width), bf16),
        [vmem()] * (4 + len(rims)),
        scratch=[
            pltpu.VMEM((eta_cells + 2 * rim, phi_cells + 16, dec_width), f32),
            pltpu.VMEM((span * span, 8, dec_width), f32),
            pltpu.VMEM((tile_len, dec_width), f32),
        ],
        flops=200 * 2 * span * span * tile_len * dec_width,
        nbytes=3 * MIB,
        limit=16,
    )(dec_grid, left, right_halo, *rims, conv_kernel)
    if fast:
        summed = []
        for c in range(2):
            own, *outs = call(
                line_kernel,
                "line%d" % c,
                [sds((part_rows, chunk), f32)] + [sds((part_rows, chunk), bf16)] * (phi_count - 1),
                [vmem()] * 2,
                flops=half * part_rows * chunk,
                nbytes=2 * MIB,
                limit=4,
            )(kept[c], tie(sent[c], normed_cells))
            summed.append([own] + [turn(outs[k], "phi", k + 1) for k in range(phi_count - 1)])
            normed_cells = tie(normed_cells, own)
    reconstruction = call(
        functools.partial(feed_kernel, 256),
        "feed",
        sds((tile_len, w_head.shape[1]), f32),
        [vmem()] * 5,
        flops=2 * tile_len * dec_width * (2 * w_up.shape[1] + w_head.shape[1]),
        nbytes=4 * MIB,
        limit=12,
    )(normed_cells, dec_grid, w_up, w_down, w_head).reshape(1, eta_cells, phi_cells, -1)
    if fast:
        summed = tie(summed, reconstruction)
        mine = call(
            functools.partial(close_kernel, phi_count),
            "close",
            sds((part_rows, width), bf16),
            [vmem()] * (2 * phi_count),
            flops=4 * part_rows * width,
            nbytes=MIB,
            limit=4,
        )(*summed[0], *summed[1])
        mine_y = flip(mine, "replica", 2)
        grad_total = call(
            spread_kernel,
            "spread",
            sds((shard_rows, width), f32),
            [vmem()] * 4,
            scratch=[pltpu.VMEM((replicas, part_rows, width), f32)],
            flops=4 * part_rows * width,
            nbytes=2 * MIB,
            limit=8,
        )(mine, flip(mine, "replica", 1), mine_y, flip(mine_y, "replica", 1))
    return (grad_total, reconstruction)


def solution(mesh):
    in_specs = (
        P("replica", "eta", "phi", None),
        P("replica", "eta", "phi", None, None),
        P("replica", "eta", "phi", None),
        P("replica", "eta", "phi", None),
        P("replica", "eta", "phi", None, None),
        P(), P(), P(), P(), P(), P(), P(), P(), P(),
    )
    out_specs = (P(("eta", "phi"), None), P("replica", "eta", "phi", None))
    return jax.shard_map(body, mesh=mesh, in_specs=in_specs, out_specs=out_specs, check_vma=False)
```
